32 devices in a mesh: rep: 2 (over y), fsdp: 16 (over z, x, core).
Axes of the slice: x: 2, y: 2, z: 4, core: 2. Of those that a mesh axis runs over, the one named last changes fastest.
Arguments:
- tokens: float32 [32768, 768], P(('rep', 'fsdp')), may hold values from -6 to 6
- pre_gain: bfloat16 [768], P('fsdp'), may hold values from 0.5 to 1.5
- pre_shift: bfloat16 [768], P('fsdp'), may hold values from -2 to 2
- inward_weight: bfloat16 [768, 2304], P('fsdp'), may hold values from -0.21875 to 0.21875
- inward_bias: bfloat16 [2304], P('fsdp'), may hold values from -3 to 3
- rotary_freqs: bfloat16 [768], P('fsdp'), may hold values from 0.019897461 to 1
- outward_weight: bfloat16 [768, 768], P('fsdp'), may hold values from -0.875 to 0.875
- outward_bias: bfloat16 [768], P('fsdp'), may hold values from -2 to 2
- mlp_gain: bfloat16 [768], P('fsdp'), may hold values from 0.5 to 1.5
- mlp_shift: bfloat16 [768], P('fsdp'), may hold values from -2 to 2
- up_weight: bfloat16 [768, 3072], P('fsdp'), may hold values from -0.21875 to 0.21875
- up_bias: bfloat16 [3072], P('fsdp'), may hold values from -3 to 3
- down_weight: bfloat16 [3072, 768], P('fsdp'), may hold values from -0.109375 to 0.109375
- down_bias: bfloat16 [768], P('fsdp'), may hold values from -2 to 2
- keep_mask: int32 [32, 1024], P(('rep', 'fsdp')), may hold values 0 or 1
- kept_counts: int32 [32], P(('rep', 'fsdp')), may hold values from 1 to 1024, 26624 in all
- patch_rows: int32 [32, 1024], P(('rep', 'fsdp')), may hold values from 0 to 31
- patch_cols: int32 [32, 1024], P(('rep', 'fsdp')), may hold values from 0 to 31
- cotangent: float32 [32768, 768], P(('rep', 'fsdp')), may hold values from -6 to 6
Outputs:
- outputs: float32 [32768, 768], P(('rep', 'fsdp'))
- grad_tokens: float32 [32768, 768], P(('rep', 'fsdp'))
- grad_pre_gain: float32 [768], P('fsdp')
- grad_pre_shift: float32 [768], P('fsdp')
- grad_inward_weight: float32 [768, 2304], P('fsdp')
- grad_inward_bias: float32 [1536], P('fsdp')
- grad_value_bias: float32 [768], P('fsdp')
- grad_freqs: float32 [768], P('fsdp')
- grad_outward_weight: float32 [768, 768], P('fsdp')
- grad_outward_bias: float32 [768], P('fsdp')
- grad_mlp_gain: float32 [768], P('fsdp')
- grad_mlp_shift: float32 [768], P('fsdp')
- grad_up_weight: float32 [768, 3072], P('fsdp')
- grad_up_bias: float32 [3072], P('fsdp')
- grad_down_weight: float32 [3072, 768], P('fsdp')
- grad_down_bias: float32 [768], P('fsdp')
The draws below stay inside these ranges and needn't reach their ends.
Inputs may be any that keep to these rules, and one draw needn't show every extreme that they name: `kept_counts`: the counts add up to 26624 and some image keeps all 1024 slots.
All inputs are finite; a program needn't handle non-finite values. No bound on the sum of `keep_mask` or of `kept_counts` on one device may be relied on, other than what follows from the above.
Results may differ from the reference program's by a relative error of at most 0.013.
Values may be sent and summed in bfloat16 or wider, within the bound.
No kernel may reach another device: no remote copies, remote signals or barrier semaphores. Data moves between devices by JAX's collectives and lax.ppermute only.
A program may use at most 192 MiB of HBM per device.

```python
import math
import jax
import jax.numpy as jnp
import numpy as np
from jax import lax

D = 768
HEADS = 12
HD = 64
FF = 3072
GRID = 32
SLOTS = 1024
IMAGES = 32
TOKENS = 32768
PAIRS = 384


def place_ends(values, own_key, least, high):
    place = [jax.random.randint(jax.random.fold_in(own_key, axis), (), 0, length) for axis, length in enumerate(values.shape)]
    widest = values.shape.index(max(values.shape))
    beside = place[:widest] + [(place[widest] + 1) % values.shape[widest]] + place[widest + 1:]
    return values.at[tuple(place)].set(least).at[tuple(beside)].set(high)


def shard_levels(rng, shape, cuts, low, high):
    def one(axis_at, shards_of):
        draws = jax.random.uniform(jax.random.fold_in(jax.random.fold_in(rng, 6), axis_at), (shards_of,), jnp.float32, low / len(cuts), high / len(cuts))
        return jnp.repeat(jnp.exp(draws), shape[axis_at] // shards_of).reshape((-1,) + (1,) * (len(shape) - axis_at - 1))

    factor_of = one(*cuts[0])
    for cut in cuts[1:]:
        factor_of = factor_of * one(*cut)
    return factor_of


def split_up(amount, total, most, slope):
    weights = [(1 << 20) // math.isqrt(rank ** slope) + 1 for rank in range(2, amount + 1)]
    spare, counts = total - most - (amount - 1), [1] * (amount - 1)
    while spare > 0:
        free = [i for i in range(amount - 1) if counts[i] < most]
        pool, remaining = sum([weights[i] for i in free]), spare
        for i in free:
            addition = min(most - counts[i], max(1, remaining * weights[i] // pool), spare)
            counts[i] = counts[i] + addition
            spare = spare - addition
    return np.array([most] + counts)


def uneven(key, count, total, bound, lean):
    if count == 2:
        one = jax.random.randint(key, (), max(1, total - bound), min(bound, total - 1) + 1)
        return jnp.stack([one, total - one])
    lengths = jnp.asarray(split_up(count, total, bound, lean), jnp.int32)
    pairs = (count - 1) // 2
    donor, receiver = lengths[1:1 + 2 * pairs:2], lengths[2:2 + 2 * pairs:2]
    margin = jnp.minimum(donor - 1, bound - receiver)
    shifted = jax.random.randint(jax.random.fold_in(key, 1), (pairs,), 0, 1 << 20) % (margin + 1)
    lengths = lengths.at[1:1 + 2 * pairs:2].set(donor - shifted).at[2:2 + 2 * pairs:2].set(receiver + shifted)
    return lengths[jax.random.permutation(jax.random.fold_in(key, 2), count)]


def gaussian(own_key, extent, scale, bound, cuts=(), kind=jnp.bfloat16):
    factor_of = shard_levels(own_key, extent, cuts, -0.22, 0.18) if cuts else 1.0
    result = jax.random.normal(own_key, extent, jnp.float32) * scale * factor_of
    return jnp.minimum(jnp.maximum(result, -bound), bound).astype(kind)


def setup_inputs(seed: int = 0) -> dict:
    arg_keys = jax.random.split(jax.random.key(seed), 20)
    tokens = gaussian(arg_keys[0], (TOKENS, D), 1.0, 6.0, ((0, 32),), jnp.float32)
    pre_gain = jnp.clip(1.0 + 0.1 * jax.random.normal(arg_keys[1], (D,), jnp.float32), 0.5, 1.5).astype(jnp.bfloat16)
    pre_shift = gaussian(arg_keys[2], (D,), 0.3, 2.0, ((0, 16),))
    inward_weight = gaussian(arg_keys[3], (D, 3 * D), D ** -0.5, 0.21875, ((0, 16),))
    inward_bias = gaussian(arg_keys[4], (3 * D,), 0.5, 3.0, ((0, 16),))
    rotary_freqs = jnp.clip(jnp.exp(math.log(1.0) - 3.9171631 * jax.random.uniform(arg_keys[5], (2 * PAIRS,), jnp.float32) ** shard_levels(arg_keys[5], (2 * PAIRS,), ((0, 16),), -0.2, 0.2)), 0.019897461, 1.0).astype(jnp.bfloat16)
    outward_weight = gaussian(arg_keys[6], (D, D), (D // 16) ** -0.5, 0.875, ((0, 16),))
    outward_bias = gaussian(arg_keys[7], (D,), 0.3, 2.0, ((0, 16),))
    mlp_gain = jnp.clip(1.0 + 0.1 * jax.random.normal(arg_keys[8], (D,), jnp.float32), 0.5, 1.5).astype(jnp.bfloat16)
    mlp_shift = gaussian(arg_keys[9], (D,), 0.3, 2.0, ((0, 16),))
    up_weight = gaussian(arg_keys[10], (D, FF), D ** -0.5, 0.21875, ((0, 16),))
    up_bias = gaussian(arg_keys[11], (FF,), 0.5, 3.0, ((0, 16),))
    down_weight = gaussian(arg_keys[12], (FF, D), FF ** -0.5, 0.109375, ((0, 16),))
    down_bias = gaussian(arg_keys[13], (D,), 0.3, 2.0, ((0, 16),))
    keep_mask = place_ends((jax.random.randint(arg_keys[14], (IMAGES, SLOTS), 0, 4) < 3).astype(jnp.int32), jax.random.fold_in(arg_keys[14], 1), 0, 1)
    kept_counts = uneven(arg_keys[15], IMAGES, 13 * IMAGES * SLOTS // 16, SLOTS, 2).astype(jnp.int32)
    patch_rows = place_ends(jax.random.randint(arg_keys[16], (IMAGES, SLOTS), 0, GRID), jax.random.fold_in(arg_keys[16], 1), 0, GRID - 1).astype(jnp.int32)
    patch_cols = place_ends(jax.random.randint(arg_keys[17], (IMAGES, SLOTS), 0, GRID), jax.random.fold_in(arg_keys[17], 1), 0, GRID - 1).astype(jnp.int32)
    cotangent = gaussian(arg_keys[18], (TOKENS, D), 1.0, 6.0, ((0, 32),), jnp.float32)
    return dict(tokens=tokens, pre_gain=pre_gain, pre_shift=pre_shift, inward_weight=inward_weight, inward_bias=inward_bias, rotary_freqs=rotary_freqs, outward_weight=outward_weight, outward_bias=outward_bias, mlp_gain=mlp_gain, mlp_shift=mlp_shift, up_weight=up_weight, up_bias=up_bias, down_weight=down_weight, down_bias=down_bias, keep_mask=keep_mask, kept_counts=kept_counts, patch_rows=patch_rows, patch_cols=patch_cols, cotangent=cotangent)


@jax.custom_vjp
def low(v):
    return lax.optimization_barrier(v.astype(jnp.bfloat16)).astype(jnp.float32)

@jax.custom_vjp
def low_back(v):
    return v

def low_keep(v):
    return (low(v), None)

def low_pass(kept, grad):
    return (grad,)

def back_keep(v):
    return (v, None)

def back_low(kept, grad):
    return (low(grad),)
low.defvjp(low_keep, low_pass)
low_back.defvjp(back_keep, back_low)
highest = lax.Precision.HIGHEST
epsilon = 1e-06
masked_score = -1e+30

def layer_norm(values, gain_vec, shift_vec):
    center = values - lax.optimization_barrier(jnp.mean(values, axis=-1, keepdims=True))
    spread = lax.optimization_barrier(jnp.mean(center * center, axis=-1, keepdims=True))
    return center * lax.rsqrt(spread + epsilon) * gain_vec + shift_vec

def rotate(vectors, cosine, sine_part):
    half_dim = vectors.shape[-1] // 2
    first_half = vectors[..., :half_dim]
    second_half = vectors[..., half_dim:]
    return jnp.concatenate([first_half * cosine - second_half * sine_part, first_half * sine_part + second_half * cosine], axis=-1)

def image_attention(packed):
    query_rot, key_rot, value_low, key_ok = packed
    positions = jnp.arange(key_ok.shape[0], dtype=jnp.int32)
    allowed = key_ok[None, :] | (positions[:, None] == positions[None, :])
    scores = low_back(jnp.einsum('qhd,khd->hqk', query_rot, key_rot, precision=highest) * HD ** (-0.5))
    scores = jnp.where(allowed[None], scores, masked_score)
    row_max = lax.optimization_barrier(jnp.max(scores, axis=-1, keepdims=True))
    exp_scores = jnp.exp(scores - row_max)
    probability = low(exp_scores / lax.optimization_barrier(jnp.sum(exp_scores, axis=-1, keepdims=True)))
    return jnp.einsum('hqk,khd->qhd', probability, value_low, precision=highest)

def forward(tokens, pre_gain, pre_shift, inward_weight, inward_bias, rotary_freqs, outward_weight, outward_bias, mlp_gain, mlp_shift, up_weight, up_bias, down_weight, down_bias, valid_rows, key_ok, rows_f, cols_f):
    total_rows = tokens.shape[0]
    norm_one = low(layer_norm(tokens, pre_gain, pre_shift))
    mixed = low_back(jnp.dot(norm_one, inward_weight, precision=highest) + inward_bias)
    freq_pairs = rotary_freqs.reshape(PAIRS, 2)
    angles = cols_f[:, None] * freq_pairs[:, 0] + rows_f[:, None] * freq_pairs[:, 1]
    angles = angles.reshape(total_rows, HEADS, HD // 2)
    cosine = jnp.cos(angles)
    sine_part = jnp.sin(angles)
    query_rot = low(rotate(mixed[:, :D].reshape(total_rows, HEADS, HD), cosine, sine_part))
    key_rot = low(rotate(mixed[:, D:2 * D].reshape(total_rows, HEADS, HD), cosine, sine_part))
    value_low = low(mixed[:, 2 * D:].reshape(total_rows, HEADS, HD))
    stacked = (query_rot.reshape(IMAGES, SLOTS, HEADS, HD), key_rot.reshape(IMAGES, SLOTS, HEADS, HD), value_low.reshape(IMAGES, SLOTS, HEADS, HD), key_ok)
    attended = lax.map(jax.checkpoint(image_attention), stacked)
    attended = low_back(low(attended.reshape(total_rows, D)))
    branch = low_back(jnp.dot(attended, outward_weight, precision=highest) + outward_bias)
    middle = tokens + valid_rows[:, None] * branch
    norm_two = low(layer_norm(middle, mlp_gain, mlp_shift))
    hidden_up = low_back(jnp.dot(norm_two, up_weight, precision=highest) + up_bias)
    activ = low(jax.nn.gelu(hidden_up, approximate=False))
    lowered = low_back(jnp.dot(activ, down_weight, precision=highest) + down_bias)
    return middle + valid_rows[:, None] * lowered

def reference(tokens, pre_gain, pre_shift, inward_weight, inward_bias, rotary_freqs, outward_weight, outward_bias, mlp_gain, mlp_shift, up_weight, up_bias, down_weight, down_bias, keep_mask, kept_counts, patch_rows, patch_cols, cotangent):
    slot_index = jnp.arange(SLOTS, dtype=jnp.int32)
    valid_slot = slot_index[None, :] < kept_counts[:, None]
    key_ok = valid_slot & (keep_mask == 1)
    valid_rows = valid_slot.astype(jnp.float32).reshape(-1)
    rows_f = patch_rows.astype(jnp.float32).reshape(-1)
    cols_f = patch_cols.astype(jnp.float32).reshape(-1)
    params = (pre_gain.astype(jnp.float32), pre_shift.astype(jnp.float32), inward_weight.astype(jnp.float32), inward_bias.astype(jnp.float32), rotary_freqs.astype(jnp.float32), outward_weight.astype(jnp.float32), outward_bias.astype(jnp.float32), mlp_gain.astype(jnp.float32), mlp_shift.astype(jnp.float32), up_weight.astype(jnp.float32), up_bias.astype(jnp.float32), down_weight.astype(jnp.float32), down_bias.astype(jnp.float32))

    def layer_run(tokens_in, *weights):
        return forward(tokens_in, *weights, valid_rows, key_ok, rows_f, cols_f)
    outputs, pullback = jax.vjp(layer_run, tokens, *params)
    gradients = pullback(cotangent)
    bias_grad = gradients[4]
    return (outputs, gradients[0], gradients[1], gradients[2], gradients[3], bias_grad[:2 * D], bias_grad[2 * D:], gradients[5], gradients[6], gradients[7], gradients[8], gradients[9], gradients[10], gradients[11], gradients[12], gradients[13])
```

```python
import functools
import math

import jax
import jax.numpy as jnp
from jax import lax
from jax.experimental import pallas as pl
from jax.experimental.pallas import tpu as pltpu
from jax.sharding import PartitionSpec as P

HD = 64
EPS = 1e-06
NEG = -1e30
F32 = jnp.float32
BF16 = jnp.bfloat16
GH = 4
GW = GH * HD
HALF = GW // 2
VMEM_CAP = 63 * 2**20


def dims(lhs, rhs, lhs_axis, rhs_axis):
    return lax.dot_general(
        lhs, rhs, (((lhs_axis,), (rhs_axis,)), ((), ())), preferred_element_type=F32
    )


def nn(lhs, rhs):
    return dims(lhs, rhs, 1, 0)


def nt(lhs, rhs):
    return dims(lhs, rhs, 1, 1)


def tn(lhs, rhs):
    return dims(lhs, rhs, 0, 0)


def params(grid, vmem=VMEM_CAP):
    return pltpu.CompilerParams(
        dimension_semantics=("arbitrary",) * len(grid), vmem_limit_bytes=vmem
    )


def whole(shape):
    return pl.BlockSpec(shape, lambda *idx: (0,) * len(shape))


ANY = pl.BlockSpec(memory_space=pl.ANY)
SMEM = pl.BlockSpec(memory_space=pltpu.SMEM)


def cost(flops, bytes_moved, transcendental=0):
    return pl.CostEstimate(
        flops=int(flops), bytes_accessed=int(bytes_moved), transcendentals=int(transcendental)
    )


def group_perm(transposed):
    row = lax.broadcasted_iota(jnp.int32, (GW, GW), 0)
    col = lax.broadcasted_iota(jnp.int32, (GW, GW), 1)
    packed, natural = (row, col) if transposed else (col, row)
    half = packed // HALF
    head = (packed % HALF) // (HD // 2)
    source = head * HD + half * (HD // 2) + packed % (HD // 2)
    return jnp.where(source == natural, 1.0, 0.0).astype(BF16)


def packed_head_mask(head):
    lane = lax.broadcasted_iota(jnp.int32, (1, GW), 1)
    return (lane % HALF) // (HD // 2) == head


def natural_head_mask(head):
    lane = lax.broadcasted_iota(jnp.int32, (1, GW), 1)
    return lane // HD == head


def normalize(values):
    center = values - jnp.mean(values, axis=-1, keepdims=True)
    spread = jnp.mean(center * center, axis=-1, keepdims=True)
    inverse = lax.rsqrt(spread + EPS)
    return center * inverse, inverse


def load_pieces(table, sources, target, sem):
    copies = []
    slots = table.shape[0] // 2
    for source in sources:
        rows, width = source.shape[-2:]
        for one in range(source.shape[0]):
            for two in range(source.shape[1]):
                number = len(copies)
                row = pl.multiple_of(table[number] * rows, rows)
                col = pl.multiple_of(table[slots + number] * width, width)
                copies.append(
                    pltpu.make_async_copy(
                        source.at[one, two], target.at[pl.ds(row, rows), pl.ds(col, width)], sem.at[number]
                    )
                )
    return copies


def piece_count(sources):
    return sum(s.shape[0] * s.shape[1] for s in sources)


def prologue_kernel(x_ref, gain_ref, shift_ref, fc_ref, fr_ref, col_ref, row_ref, n1_ref, cos_ref, sin_ref):
    xhat, _ = normalize(x_ref[...])
    n1_ref[...] = (xhat * gain_ref[...] + shift_ref[...]).astype(BF16)
    angle = col_ref[...] * fc_ref[...] + row_ref[...] * fr_ref[...]
    cosine, sine = cos_sin(angle)
    cos_ref[...] = cosine
    sin_ref[...] = sine


QUARTER = (1.5703125, 4.837512969970703125e-4, 7.549789948768648e-8)


def cos_sin(angle):
    turns = jnp.floor(angle * 0.6366197723675814 + 0.5)
    r = ((angle - turns * QUARTER[0]) - turns * QUARTER[1]) - turns * QUARTER[2]
    r2 = r * r
    s = r + r * r2 * (-1.6666654611e-1 + r2 * (8.3321608736e-3 - 1.9515295891e-4 * r2))
    c = 1.0 - 0.5 * r2 + r2 * r2 * (4.166664568298827e-2 + r2 * (-1.388731625493765e-3 + 2.443315711809948e-5 * r2))
    quad = turns.astype(jnp.int32)
    odd = (quad & 1) == 1
    cosine = jnp.where(odd, s, c)
    sine = jnp.where(odd, c, s)
    cosine = jnp.where(((quad + 1) & 2) == 2, -cosine, cosine)
    sine = jnp.where((quad & 2) == 2, -sine, sine)
    return cosine, sine


def prologue(x, gain, shift, fc, fr, cols, rows, rb=256):
    total, width = x.shape
    pairs = width // 2
    grid = (total // rb,)
    blk = lambda w: pl.BlockSpec((rb, w), lambda i: (i, 0))
    return pl.pallas_call(
        prologue_kernel,
        grid=grid,
        in_specs=[blk(width), whole((1, width)), whole((1, width)), whole((1, pairs)), whole((1, pairs)), blk(1), blk(1)],
        out_specs=[blk(width), blk(pairs), blk(pairs)],
        out_shape=[
            jax.ShapeDtypeStruct((total, width), BF16),
            jax.ShapeDtypeStruct((total, pairs), F32),
            jax.ShapeDtypeStruct((total, pairs), F32),
        ],
        compiler_params=params(grid),
        cost_estimate=cost(total * width * 40, total * width * 10),
        name="prologue",
    )(x, gain, shift, fc, fr, cols, rows)


def qkv_kernel(g0, npieces, table, n1_ref, bias_ref, cos_ref, sin_ref, *rest):
    pieces = rest[:npieces]
    q_ref, k_ref, v_ref, w, wp, bp, sem = rest[npieces:]
    width = n1_ref.shape[1]
    groups = w.shape[1] // (3 * GW)

    @pl.when(pl.program_id(0) == 0)
    def _():
        copies = load_pieces(table, pieces, w, sem)
        for copy in copies:
            copy.start()
        perm = group_perm(False)
        for copy in copies:
            copy.wait()
        for g in range(groups):
            for part in range(2):
                packed = pl.ds((g * 2 + part) * GW, GW)
                wp[:, packed] = nn(w[:, pl.ds((g * 3 + part) * GW, GW)], perm).astype(BF16)
                natural = pl.ds(part * width + (g0 + g) * GW, GW)
                spread = jnp.broadcast_to(bias_ref[:, natural].astype(BF16), (16, GW))
                bp[:, packed] = nn(spread, perm)[:8]

    n1 = n1_ref[...]
    for g in range(groups):
        cosine = cos_ref[:, pl.ds((g0 + g) * HALF, HALF)]
        sine = sin_ref[:, pl.ds((g0 + g) * HALF, HALF)]
        for part, out, scale in ((0, q_ref, HD**-0.5), (1, k_ref, 1.0)):
            packed = pl.ds((g * 2 + part) * GW, GW)
            mixed = nn(n1, wp[:, packed]) + bp[0:1, packed]
            a, b = mixed[:, :HALF], mixed[:, HALF:]
            first = a * cosine - b * sine
            second = a * sine + b * cosine
            if scale != 1.0:
                first = first * scale
                second = second * scale
            out[:, pl.ds(g * GW, HALF)] = first.astype(BF16)
            out[:, pl.ds(g * GW + HALF, HALF)] = second.astype(BF16)
        bias = bias_ref[:, pl.ds(2 * width + (g0 + g) * GW, GW)]
        v_ref[:, pl.ds(g * GW, GW)] = (nn(n1, w[:, pl.ds((g * 3 + 2) * GW, GW)]) + bias).astype(BF16)


def qkv(g0, groups, table, n1, bias, cosine, sine, pieces, rb=256):
    total, width = n1.shape
    pairs = width // 2
    grid = (total // rb,)
    blk = lambda w: pl.BlockSpec((rb, w), lambda i: (i, 0))
    out = jax.ShapeDtypeStruct((total, groups * GW), BF16)
    copies = piece_count(pieces)
    return pl.pallas_call(
        functools.partial(qkv_kernel, g0, len(pieces)),
        grid=grid,
        in_specs=[SMEM, blk(width), whole((1, 3 * width)), blk(pairs), blk(pairs)] + [ANY] * len(pieces),
        out_specs=[blk(groups * GW)] * 3,
        out_shape=[out] * 3,
        scratch_shapes=[
            pltpu.VMEM((width, 3 * groups * GW), BF16),
            pltpu.VMEM((width, 2 * groups * GW), BF16),
            pltpu.VMEM((8, 2 * groups * GW), F32),
            pltpu.SemaphoreType.DMA((copies,)),
        ],
        compiler_params=params(grid),
        cost_estimate=cost(total * width * groups * GW * 6, total * width * 8 + width * groups * GW * 6),
        name="qkv",
    )(table, n1, bias, cosine, sine, *pieces)


def attend_kernel(q_ref, k_ref, v_ref, kb_ref, att_ref, lse_ref, mask):
    g, r = pl.program_id(0), pl.program_id(1)
    rb, keys = q_ref.shape[0], k_ref.shape[0]
    here = pl.ds(pl.multiple_of(r * rb, rb), rb)

    @pl.when(g == 0)
    def _():
        row = lax.broadcasted_iota(jnp.int32, (rb, keys), 0) + r * rb
        col = lax.broadcasted_iota(jnp.int32, (rb, keys), 1)
        mask[here, :] = jnp.where(row == col, 0.0, jnp.broadcast_to(kb_ref[...], (rb, keys)))

    q = q_ref[...]
    k = k_ref[...]
    v = v_ref[...]
    total = jnp.zeros((rb, GW), F32)
    lane = lax.broadcasted_iota(jnp.int32, (rb, 128), 1)
    logs = jnp.zeros((rb, 128), F32)
    for h in range(GH):
        qm = jnp.where(packed_head_mask(h), q, jnp.zeros_like(q))
        scores = nt(qm, k) + mask[here, :]
        top = jnp.max(scores, axis=-1, keepdims=True)
        weight = jnp.exp(scores - top)
        norm = jnp.sum(weight, axis=-1, keepdims=True)
        vm = jnp.where(natural_head_mask(h), v, jnp.zeros_like(v))
        total = total + nn(weight.astype(BF16), vm) * (1.0 / norm)
        logs = jnp.where(lane == h, top + jnp.log(norm), logs)
    att_ref[...] = total.astype(BF16)
    lse_ref[...] = jnp.transpose(logs)[:8, :]


def attend(q, k, v, kb, rb=256):
    total, width = q.shape
    groups = width // GW
    grid = (groups, total // rb)
    return pl.pallas_call(
        attend_kernel,
        grid=grid,
        in_specs=[
            pl.BlockSpec((rb, GW), lambda g, r: (r, g)),
            pl.BlockSpec((total, GW), lambda g, r: (0, g)),
            pl.BlockSpec((total, GW), lambda g, r: (0, g)),
            whole((1, total)),
        ],
        out_specs=[
            pl.BlockSpec((rb, GW), lambda g, r: (r, g)),
            pl.BlockSpec((None, 8, rb), lambda g, r: (g, 0, r)),
        ],
        out_shape=[
            jax.ShapeDtypeStruct((total, width), BF16),
            jax.ShapeDtypeStruct((groups, 8, total), F32),
        ],
        scratch_shapes=[pltpu.VMEM((total, total), F32)],
        compiler_params=params(grid),
        cost_estimate=cost(total * total * width * 16, total * width * 8, total * total * 12),
        name="attend",
    )(q, k, v, kb)


PHI_SCALE = 0.3989422804014327
TAIL_SCALE = 0.44 * 0.7071067811865476
TAIL = (
    0.12411047596471954,
    0.12443560910041027,
    0.10865662380098591,
    0.10790671631036299,
    -0.010091621907114547,
    0.14834527631989725,
    -0.13897496529649409,
    0.03561197654899638,
)


def gelu_parts(h):
    t = 1.0 / (1.0 + TAIL_SCALE * jnp.abs(h))
    poly = TAIL[-1]
    for coefficient in TAIL[-2::-1]:
        poly = poly * t + coefficient
    bell = jnp.exp(-0.5 * h * h)
    tail = poly * t * bell
    phi = jnp.where(h < 0, tail, 1.0 - tail)
    return h * phi, phi + h * (bell * PHI_SCALE)


def up_kernel(npieces, table, count, att_ref, x_ref, small_ref, ub_ref, *rest):
    pieces = rest[:npieces]
    mid_ref, n2_ref, act_ref, gp_ref, w, sem = rest[npieces:]
    rb, width = x_ref.shape
    wide = act_ref.shape[1]

    @pl.when(pl.program_id(0) == 0)
    def _():
        copies = load_pieces(table, pieces, w, sem)
        for copy in copies:
            copy.start()
        for copy in copies:
            copy.wait()

    slot = lax.broadcasted_iota(jnp.int32, (rb, 1), 0) + pl.program_id(0) * rb
    valid = jnp.where(slot < count[0], 1.0, 0.0)
    branch = nn(att_ref[...], w[:, pl.ds(0, width)]) + small_ref[0:1, :]
    middle = x_ref[...] + valid * branch
    mid_ref[...] = middle
    xhat, _ = normalize(middle)
    n2 = (xhat * small_ref[1:2, :] + small_ref[2:3, :]).astype(BF16)
    n2_ref[...] = n2
    step = 512
    for c in range(wide // step):
        cut = pl.ds(c * step, step)
        hidden = nn(n2, w[:, pl.ds(width + c * step, step)]) + ub_ref[:, cut]
        act, slope = gelu_parts(hidden)
        act_ref[:, cut] = act.astype(BF16)
        gp_ref[:, cut] = slope.astype(BF16)


def up(table, count, att, x, small, ub, pieces, rb=256):
    total, width = x.shape
    wide = ub.shape[1]
    grid = (total // rb,)
    blk = lambda w: pl.BlockSpec((rb, w), lambda i: (i, 0))
    copies = piece_count(pieces)
    return pl.pallas_call(
        functools.partial(up_kernel, len(pieces)),
        grid=grid,
        in_specs=[SMEM, SMEM, blk(width), blk(width), whole(small.shape), whole((1, wide))] + [ANY] * len(pieces),
        out_specs=[blk(width), blk(width), blk(wide), blk(wide)],
        out_shape=[
            jax.ShapeDtypeStruct((total, width), F32),
            jax.ShapeDtypeStruct((total, width), BF16),
            jax.ShapeDtypeStruct((total, wide), BF16),
            jax.ShapeDtypeStruct((total, wide), BF16),
        ],
        scratch_shapes=[
            pltpu.VMEM((width, width + wide), BF16),
            pltpu.SemaphoreType.DMA((copies,)),
        ],
        compiler_params=params(grid),
        cost_estimate=cost(total * width * (width + wide) * 2, total * (width * 12 + wide * 4), total * wide * 2),
        name="up",
    )(table, count, att, x, small, ub, *pieces)


def down_kernel(nup, ndown, table, count, act_ref, gp_ref, mid_ref, cot_ref, gd_ref, small_ref, *rest):
    ups = rest[:nup]
    downs = rest[nup : nup + ndown]
    (out_ref, gm_ref, gb_ref, ga_ref, gu_ref, sums_ref, ubsum_ref, w, wd, sem, sem_d) = rest[nup + ndown :]
    i = pl.program_id(0)
    rb, width = mid_ref.shape
    wide = act_ref.shape[1]

    @pl.when(i == 0)
    def _():
        first = load_pieces(table, downs, wd, sem_d)
        second = load_pieces(table, ups, w, sem)
        for copy in first + second:
            copy.start()
        for copy in first + second:
            copy.wait()
        sums_ref[...] = jnp.zeros_like(sums_ref)
        ubsum_ref[...] = jnp.zeros_like(ubsum_ref)

    slot = lax.broadcasted_iota(jnp.int32, (rb, 1), 0) + i * rb
    valid = jnp.where(slot < count[0], 1.0, 0.0)
    middle = mid_ref[...]
    cot = cot_ref[...]
    gd = gd_ref[...]
    lowered = nn(act_ref[...], wd[...]) + small_ref[0:1, :]
    out_ref[...] = middle + valid * lowered
    step = 512
    gn2 = jnp.zeros((rb, width), F32)
    for c in range(wide // step):
        cut = pl.ds(c * step, step)
        g = nt(gd, wd[cut, :]) * gp_ref[:, cut].astype(F32)
        g_low = g.astype(BF16)
        gu_ref[:, cut] = g_low
        ubsum_ref[0:1, cut] += jnp.sum(g_low.astype(F32), axis=0, keepdims=True)
        gn2 = gn2 + nt(g_low, w[:, pl.ds(width + c * step, step)])
    xhat, inverse = normalize(middle)
    sums_ref[0:1, :] += jnp.sum(gn2 * xhat, axis=0, keepdims=True)
    sums_ref[1:2, :] += jnp.sum(gn2, axis=0, keepdims=True)
    e = gn2 * small_ref[1:2, :]
    back = (e - jnp.mean(e, axis=-1, keepdims=True) - xhat * jnp.mean(e * xhat, axis=-1, keepdims=True)) * inverse
    gmid = cot + back
    gm_ref[...] = gmid
    gb = (valid * gmid).astype(BF16)
    gb_ref[...] = gb
    sums_ref[2:3, :] += jnp.sum(gb.astype(F32), axis=0, keepdims=True)
    sums_ref[3:4, :] += jnp.sum(gd.astype(F32), axis=0, keepdims=True)
    ga_ref[...] = nt(gb, w[:, pl.ds(0, width)]).astype(BF16)


def down(table, count, act, gp, mid, cot, gd, small, ups, downs, rb=256):
    total, width = mid.shape
    wide = act.shape[1]
    grid = (total // rb,)
    blk = lambda w: pl.BlockSpec((rb, w), lambda i: (i, 0))
    return pl.pallas_call(
        functools.partial(down_kernel, len(ups), len(downs)),
        grid=grid,
        in_specs=[SMEM, SMEM, blk(wide), blk(wide), blk(width), blk(width), blk(width), whole(small.shape)]
        + [ANY] * (len(ups) + len(downs)),
        out_specs=[blk(width), blk(width), blk(width), blk(width), blk(wide), whole((8, width)), whole((8, wide))],
        out_shape=[
            jax.ShapeDtypeStruct((total, width), F32),
            jax.ShapeDtypeStruct((total, width), F32),
            jax.ShapeDtypeStruct((total, width), BF16),
            jax.ShapeDtypeStruct((total, width), BF16),
            jax.ShapeDtypeStruct((total, wide), BF16),
            jax.ShapeDtypeStruct((8, width), F32),
            jax.ShapeDtypeStruct((8, wide), F32),
        ],
        scratch_shapes=[
            pltpu.VMEM((width, width + wide), BF16),
            pltpu.VMEM((wide, width), BF16),
            pltpu.SemaphoreType.DMA((piece_count(ups),)),
            pltpu.SemaphoreType.DMA((piece_count(downs),)),
        ],
        compiler_params=params(grid),
        cost_estimate=cost(total * width * (width + 3 * wide) * 2, total * (width * 20 + wide * 6)),
        name="down",
    )(table, count, act, gp, mid, cot, gd, small, *ups, *downs)


def grad_kernel(nb, mids, reps, rows, cols_each, core, a_ref, *rest):
    b_refs = rest[:nb]
    keep_ref, send_ref = rest[nb:]
    part = core[0]
    a = a_ref[...]

    def spot(parity, mid, rep):
        return jnp.where(parity == 0, mid, rep), jnp.where(parity == 0, rep, mid)

    width = sum(b.shape[1] for b in b_refs)
    each = width // reps
    offset = 0
    for b_ref in b_refs:
        begin = 0
        while begin < b_ref.shape[1]:
            column = offset + begin
            step = min(b_ref.shape[1] - begin, each - column % each, cols_each)
            result = tn(a, b_ref[:, pl.ds(begin, step)])
            rep, cut = column // each, pl.ds(column % each, step)
            for pair in range(a.shape[1] // (2 * rows)):
                low = result[pair * 2 * rows : pair * 2 * rows + rows]
                high = result[pair * 2 * rows + rows : (pair + 1) * 2 * rows]
                zz, mid = pair // mids, pair % mids
                one, two = spot(part, mid, rep)
                keep_ref[one, two, zz, :, cut] = jnp.where(part == 0, low, high).astype(BF16)
                one, two = spot(1 - part, mid, rep)
                send_ref[one, two, zz, :, cut] = jnp.where(part == 0, high, low).astype(BF16)
            begin += step
        offset += b_ref.shape[1]


def weight_grad(core, a, bs, layout, name, block_of=None):
    slow, mids, reps = layout
    total, height = a.shape
    width = sum(w for _, w, _ in bs)
    rows = height // (slow * mids * 2)
    chunk = 384 if height % 384 == 0 and 384 % (2 * mids * rows) == 0 else 2 * mids * rows
    slows = chunk // (2 * mids * rows)
    grid = (height // chunk,)
    cols_each = min(width // reps, 768)
    out = jax.ShapeDtypeStruct((mids, reps, slow, rows, width // reps), BF16)
    spec = pl.BlockSpec((mids, reps, slows, rows, width // reps), lambda i: (0, 0, i, 0, 0))
    return pl.pallas_call(
        functools.partial(grad_kernel, len(bs), mids, reps, rows, cols_each),
        grid=grid,
        in_specs=[SMEM, pl.BlockSpec((total, chunk), lambda i: (0, i))]
        + [pl.BlockSpec((total, w), functools.partial(lambda at, i: (0, at), at)) for _, w, at in bs],
        out_specs=[spec, spec],
        out_shape=[out, out],
        compiler_params=params(grid),
        cost_estimate=cost(total * height * width * 2, total * (height + width) * 2 + height * width * 2),
        name=name,
    )(core, a, *[b for b, _, _ in bs])


def plain_grad_kernel(nb, a_ref, *rest):
    b_refs, out_ref = rest[:nb], rest[nb]
    a = a_ref[...]
    offset = 0
    for b_ref in b_refs:
        step = min(b_ref.shape[1], 768)
        for c in range(b_ref.shape[1] // step):
            out_ref[:, pl.ds(offset + c * step, step)] = tn(a, b_ref[:, pl.ds(c * step, step)])
        offset += b_ref.shape[1]


def plain_grad(a, bs, name):
    total, height = a.shape
    width = sum(w for _, w, _ in bs)
    chunk = 384
    grid = (height // chunk,)
    return pl.pallas_call(
        functools.partial(plain_grad_kernel, len(bs)),
        grid=grid,
        in_specs=[pl.BlockSpec((total, chunk), lambda i: (0, i))]
        + [pl.BlockSpec((total, w), functools.partial(lambda at, i: (0, at), at)) for _, w, at in bs],
        out_specs=pl.BlockSpec((chunk, width), lambda i: (i, 0)),
        out_shape=jax.ShapeDtypeStruct((height, width), F32),
        compiler_params=params(grid),
        cost_estimate=cost(total * height * width * 2, total * (height + width) * 2 + height * width * 4),
        name=name,
    )(a, *[b for b, _, _ in bs])


def unrotate(grad, cosine, sine):
    first, second = grad[:, :HALF], grad[:, HALF:]
    return first * cosine + second * sine, second * cosine - first * sine


def angle_grad(grad, rotated):
    return grad[:, HALF:] * rotated[:, :HALF] - grad[:, :HALF] * rotated[:, HALF:]


def back_kernel(g0, q_ref, k_ref, v_ref, do_ref, lse_ref, kb_ref, cos_ref, sin_ref, col_ref, row_ref,
                gq_ref, gk_ref, gv_ref, fsum_ref, bsum_ref, ds_s, p_s, dk_s, dv_s):
    g, r = pl.program_id(0), pl.program_id(1)
    rb, keys = q_ref.shape[0], k_ref.shape[0]
    here = pl.ds(pl.multiple_of(r * rb, rb), rb)
    q = q_ref[...]
    k = k_ref[...]
    v = v_ref[...]
    do = do_ref[...]
    zero = jnp.zeros_like(q)
    key = lax.broadcasted_iota(jnp.int32, (keys, rb), 0)
    query = lax.broadcasted_iota(jnp.int32, (keys, rb), 1) + r * rb
    mask = jnp.where(key == query, 0.0, jnp.broadcast_to(kb_ref[...], (keys, rb)))
    dq = jnp.zeros((rb, GW), F32)
    qms, doms = [], []
    for h in range(GH):
        qm = jnp.where(packed_head_mask(h), q, zero)
        dom = jnp.where(natural_head_mask(h), do, zero)
        qms.append(qm)
        doms.append(dom)
        soft = jnp.exp(nt(k, qm) + mask - lse_ref[h : h + 1, :])
        gp = nt(v, dom)
        inner = jnp.sum(soft * gp, axis=0, keepdims=True)
        ds = (soft * (gp - inner)).astype(BF16)
        cut = pl.ds(h * rb, rb)
        ds_s[:, cut] = ds
        p_s[:, cut] = soft.astype(BF16)
        km = jnp.where(packed_head_mask(h), k, jnp.zeros_like(k))
        dq = dq + tn(ds, km)
    dk = nn(ds_s[...], jnp.concatenate(qms, axis=0))
    dv = nn(p_s[...], jnp.concatenate(doms, axis=0))

    perm = group_perm(True)
    cosine, sine = cos_ref[here, :], sin_ref[here, :]
    dq = dq * (HD**-0.5)
    ang = angle_grad(dq, q.astype(F32) * (HD**0.5))
    first, second = unrotate(dq, cosine, sine)
    gq = nn(jnp.concatenate([first.astype(BF16), second.astype(BF16)], axis=1), perm)
    gq_ref[...] = gq.astype(BF16)
    col, row = col_ref[here, :], row_ref[here, :]
    fcol = jnp.sum(ang * col, axis=0, keepdims=True)
    frow = jnp.sum(ang * row, axis=0, keepdims=True)
    qsum = jnp.sum(gq, axis=0, keepdims=True)

    @pl.when(r == 0)
    def _():
        dk_s[...] = dk
        dv_s[...] = dv
        fsum_ref[0:1, :] = fcol
        fsum_ref[1:2, :] = frow
        bsum_ref[0:1, :] = qsum

    @pl.when(r > 0)
    def _():
        dk_s[...] += dk
        dv_s[...] += dv
        fsum_ref[0:1, :] += fcol
        fsum_ref[1:2, :] += frow
        bsum_ref[0:1, :] += qsum

    @pl.when(r == pl.num_programs(1) - 1)
    def _():
        dkf = dk_s[...]
        angk = angle_grad(dkf, k.astype(F32))
        fsum_ref[0:1, :] += jnp.sum(angk * col_ref[...], axis=0, keepdims=True)
        fsum_ref[1:2, :] += jnp.sum(angk * row_ref[...], axis=0, keepdims=True)
        one, two = unrotate(dkf, cos_ref[...], sin_ref[...])
        gk = nn(jnp.concatenate([one.astype(BF16), two.astype(BF16)], axis=1), perm)
        gk_ref[...] = gk.astype(BF16)
        bsum_ref[1:2, :] = jnp.sum(gk, axis=0, keepdims=True)
        gv = dv_s[...].astype(BF16)
        gv_ref[...] = gv
        bsum_ref[2:3, :] = jnp.sum(gv.astype(F32), axis=0, keepdims=True)


def attend_back(g0, l0, ng, q, k, v, do, lse, kb, cosine, sine, cols, rows, rb=256):
    total = q.shape[0]
    grid = (ng, total // rb)
    out = jax.ShapeDtypeStruct((total, ng * GW), BF16)
    rowblk = lambda g, r: (r, g + g0)
    colblk = lambda g, r: (0, g + g0)
    return pl.pallas_call(
        functools.partial(back_kernel, g0),
        grid=grid,
        in_specs=[
            pl.BlockSpec((rb, GW), lambda g, r: (r, g + l0)),
            pl.BlockSpec((total, GW), lambda g, r: (0, g + l0)),
            pl.BlockSpec((total, GW), lambda g, r: (0, g + l0)),
            pl.BlockSpec((rb, GW), rowblk),
            pl.BlockSpec((None, 8, rb), lambda g, r: (g + l0, 0, r)),
            whole((total, 1)),
            pl.BlockSpec((total, HALF), colblk),
            pl.BlockSpec((total, HALF), colblk),
            whole((total, 1)),
            whole((total, 1)),
        ],
        out_specs=[
            pl.BlockSpec((rb, GW), lambda g, r: (r, g)),
            pl.BlockSpec((total, GW), lambda g, r: (0, g)),
            pl.BlockSpec((total, GW), lambda g, r: (0, g)),
            pl.BlockSpec((None, 8, HALF), lambda g, r: (g, 0, 0)),
            pl.BlockSpec((None, 8, GW), lambda g, r: (g, 0, 0)),
        ],
        out_shape=[
            out,
            out,
            out,
            jax.ShapeDtypeStruct((ng, 8, HALF), F32),
            jax.ShapeDtypeStruct((ng, 8, GW), F32),
        ],
        scratch_shapes=[
            pltpu.VMEM((total, GH * rb), BF16),
            pltpu.VMEM((total, GH * rb), BF16),
            pltpu.VMEM((total, GW), F32),
            pltpu.VMEM((total, GW), F32),
        ],
        compiler_params=params(grid),
        cost_estimate=cost(total * total * GW * ng * 40, total * GW * ng * 16, total * total * GH * ng),
        name="attend_back",
    )(q, k, v, do, lse, kb, cosine, sine, cols, rows)


def final_kernel(grad_groups, counts, table, x_ref, gm_ref, gain_ref, *rest):
    grads, pieces, place = [], [], 0
    for groups in grad_groups:
        for g in range(groups):
            grads.append([rest[place + part][:, pl.ds(g * GW, GW)] for part in range(3)])
        place += 3
    for count in counts:
        pieces.append(rest[place : place + count])
        place += count
    out_ref, sums_ref = rest[place : place + 2]
    weights = rest[place + 2 : place + 2 + len(counts)]
    sems = rest[place + 2 + len(counts) :]

    @pl.when(pl.program_id(0) == 0)
    def _():
        copies = []
        for p, w, sem in zip(pieces, weights, sems):
            copies += load_pieces(table, p, w, sem)
        for copy in copies:
            copy.start()
        for copy in copies:
            copy.wait()
        sums_ref[...] = jnp.zeros_like(sums_ref)

    e = jnp.zeros(x_ref.shape, F32)
    group = 0
    for w in weights:
        for g in range(w.shape[1] // (3 * GW)):
            for part in range(3):
                e = e + nt(grads[group][part], w[:, pl.ds((g * 3 + part) * GW, GW)])
            group += 1
    xhat, inverse = normalize(x_ref[...])
    sums_ref[0:1, :] += jnp.sum(e * xhat, axis=0, keepdims=True)
    sums_ref[1:2, :] += jnp.sum(e, axis=0, keepdims=True)
    eg = e * gain_ref[...]
    back = (eg - jnp.mean(eg, axis=-1, keepdims=True) - xhat * jnp.mean(eg * xhat, axis=-1, keepdims=True)) * inverse
    out_ref[...] = gm_ref[...] + back


def final(table, x, gmid, gain, grad_sets, piece_sets, widths, rb=256):
    total, width = x.shape
    grid = (total // rb,)
    blk = lambda w: pl.BlockSpec((rb, w), lambda i: (i, 0))
    grads = [g for gs in grad_sets for g in gs]
    pieces = [p for ps in piece_sets for p in ps]
    return pl.pallas_call(
        functools.partial(final_kernel, [gs[0].shape[1] // GW for gs in grad_sets], [len(ps) for ps in piece_sets]),
        grid=grid,
        in_specs=[SMEM, blk(width), blk(width), whole((1, width))]
        + [blk(g.shape[1]) for g in grads]
        + [ANY] * len(pieces),
        out_specs=[blk(width), whole((8, width))],
        out_shape=[jax.ShapeDtypeStruct((total, width), F32), jax.ShapeDtypeStruct((8, width), F32)],
        scratch_shapes=[pltpu.VMEM((width, w), BF16) for w in widths]
        + [pltpu.SemaphoreType.DMA((piece_count(ps),)) for ps in piece_sets],
        compiler_params=params(grid),
        cost_estimate=cost(total * width * width * 6, total * width * 20 + width * width * 6),
        name="final",
    )(table, x, gmid, gain, *grads, *pieces)


def place():
    me = lax.axis_index("fsdp")
    return lax.axis_index("rep"), me // 4, (me // 2) % 2, me % 2


def move(value, step):
    moves = []
    for i in range(32):
        y, z, x, c = step(i // 16, (i // 4) % 4, (i // 2) % 2, i % 2)
        moves.append((i, y * 16 + z * 4 + x * 2 + c))
    return lax.ppermute(value, ("rep", "fsdp"), moves)


def across_core(value):
    return move(value, lambda y, z, x, c: (y, z, x, 1 - c))


def across_x(value):
    return move(value, lambda y, z, x, c: (y, z, 1 - x, c))


def across_rep(value):
    return move(value, lambda y, z, x, c: (1 - y, z, x, c))


def across_near(value):
    return move(value, lambda y, z, x, c: (y, z ^ 1, x, c))


def across_far(value):
    return move(value, lambda y, z, x, c: (y, z ^ 2, x, c))


def across_one(value):
    return move(value, lambda y, z, x, c: (y, z, 1 - x, c) if c == 0 else (1 - y, z, x, c))


def across_two(value):
    return move(value, lambda y, z, x, c: (1 - y, z, x, c) if c == 0 else (y, z, 1 - x, c))


def pick(array, index):
    return lax.dynamic_index_in_dim(array, index, 0, keepdims=False)


def pick_two(array, index):
    return lax.dynamic_slice_in_dim(array, 2 * index, 2, 0)


def own_half(shard):
    half = shard.shape[1] // 2
    return lax.dynamic_slice_in_dim(shard, lax.axis_index("rep") * half, half, 1)


def piece_table():
    y, z, x, c = place()
    slot = jnp.arange(4, dtype=jnp.int32)
    owners, halves = [], []

    def add(mid, core, half):
        owners.append((z ^ slot) * 4 + mid * 2 + core)
        halves.append(jnp.broadcast_to(half, (4,)))

    for core in (c, 1 - c):
        add(x, core, y)
        add(jnp.where(core == 0, x, 1 - x), core, jnp.where(core == 0, 1 - y, y))
        add(jnp.where(core == 0, 1 - x, x), core, jnp.where(core == 0, y, 1 - y))
        add(1 - x, core, 1 - y)
    return jnp.concatenate(owners + halves).astype(jnp.int32)


def gather_small(small):
    pair = jnp.stack([small, across_near(small)])
    column = jnp.concatenate([pair, across_far(pair)])
    both = jnp.stack([column, across_x(column)])
    every = jnp.stack([both, across_core(both)]).reshape(16, -1)
    _, z, x, c = place()
    slot = jnp.arange(16, dtype=jnp.int32)
    owner = (z ^ (slot & 3)) * 4 + (x ^ ((slot >> 2) & 1)) * 2 + (c ^ (slot >> 3))
    where = (slot[:, None] == owner[None, :]).astype(BF16)
    return jnp.dot(where, every, preferred_element_type=F32)


class Reduce:
    stages = (across_core, across_one, across_two, across_far, across_near, across_rep)

    def __init__(self, keep, send):
        self.keep, self.first, self.got, self.stage = keep, send, [], 0
        self.out = None

    def base(self, count, one, two=None, cut=None):
        step = lambda a, i: a if i is None else pick(a, i)
        total = None
        for source, used in ((self.keep, 0), (self.got[0], 0), *((g, n + 1) for n, g in enumerate(self.got[1:count]))):
            value = source
            if used < 1:
                value = step(value, one)
            if used < 2:
                value = step(value, two)
            if cut is not None:
                value = cut(value)
            value = value.astype(F32)
            total = value if total is None else total + value
        return total

    def level(self, index):
        return self.base(3, self.i1, self.i2, lambda a: pick(a, index)) + pick(self.got[3], index % 2).astype(F32)

    def send(self):
        y, z, x, c = place()
        self.i1, self.i2 = jnp.where(c == 0, x, y), jnp.where(c == 0, y, x)
        if self.stage == 0:
            return self.first
        if self.stage == 1:
            return self.base(1, 1 - self.i1).astype(BF16)
        if self.stage == 2:
            return self.base(2, self.i1, 1 - self.i2).astype(BF16)
        if self.stage == 3:
            return self.base(3, self.i1, self.i2, lambda a: pick_two(a, 1 - z // 2)).astype(BF16)
        if self.stage == 4:
            return self.level(z ^ 1).astype(BF16)
        self.total = self.level(z) + self.got[4].astype(F32)
        return self.total

    def take(self, value):
        self.stage += 1
        if self.stage == 6:
            y = lax.axis_index("rep")
            first = jnp.where(y == 0, self.total, value)
            second = jnp.where(y == 0, value, self.total)
            self.out = jnp.concatenate([first, second], axis=1)
        else:
            self.got.append(value)


class SmallReduce:
    stages = (across_core, across_x, across_far, across_near, across_rep)

    def __init__(self, rows):
        self.part, self.stage = rows.reshape(4, 2, 2, rows.shape[1]).transpose(2, 1, 0, 3), 0

    def send(self):
        y, z, x, c = place()
        if self.stage == 4:
            self.kept = self.part
            return self.part
        cut = pick_two if self.stage == 2 else pick
        index = (c, x, z // 2, z % 2)[self.stage]
        self.kept = cut(self.part, index)
        return cut(self.part, 1 - index)

    def take(self, value):
        self.stage += 1
        self.part = self.kept + value
        self.out = self.part


class Gather:
    stages = (across_near, across_far, across_two, across_one, across_core)

    def __init__(self, shard):
        self.part, self.stage, self.early = own_half(shard), 0, None

    def send(self):
        return self.part

    def take(self, value):
        self.stage += 1
        if self.stage == 1 or self.stage == 3:
            self.part = jnp.stack([self.part, value])
        elif self.stage == 2:
            self.part = jnp.concatenate([self.part, value])
        elif self.stage == 4:
            self.quad = jnp.stack([self.part, value]).reshape(4, *value.shape[1:])
            self.part = self.quad
        else:
            self.out = [self.quad, value]


def step(movers, kernel=None, *inputs):
    sends = [m.send() for m in movers]
    inputs, sends = lax.optimization_barrier((inputs, sends))
    got = [m.stages[m.stage](s) for m, s in zip(movers, sends)]
    outs = kernel(*inputs) if kernel is not None else ()
    outs, got = lax.optimization_barrier((outs, got))
    for m, g in zip(movers, got):
        m.take(g)
    return outs


def small_rows(parts, n):
    return jnp.concatenate([p.astype(F32).reshape(n, -1) for p in parts], axis=1)


def unpack(small_full, lengths, n):
    vectors = []
    offset = 0
    for length in lengths:
        vectors.append(small_full[:, offset : offset + length].reshape(1, n * length))
        offset += length
    return vectors


def group_columns(weight, g0, ng, width):
    cuts = []
    for g in range(g0, g0 + ng):
        cuts += [weight[:, part * width + g * GW : part * width + (g + 1) * GW] for part in range(3)]
    return jnp.concatenate(cuts, axis=1)


def local(tuned, n, tokens, pre_gain, pre_shift, inward_weight, inward_bias, rotary_freqs, outward_weight,
          outward_bias, mlp_gain, mlp_shift, up_weight, up_bias, down_weight, down_bias, keep_mask, kept_counts,
          patch_rows, patch_cols, cotangent):
    total, width = tokens.shape
    groups = width // GW
    wide = up_weight.shape[1]
    smalls = [pre_gain, pre_shift, inward_bias, rotary_freqs, outward_bias, mlp_gain, mlp_shift, up_bias, down_bias]
    lengths = [s.shape[0] for s in smalls]
    small = jnp.concatenate(smalls)[None, :]
    out_up = jnp.concatenate([outward_weight, up_weight], axis=1)
    splits = [(0, 1), (1, groups - 1)]
    inward_parts = [group_columns(inward_weight, g0, ng, width) for g0, ng in splits]

    slot = jnp.arange(total, dtype=jnp.int32)
    count = kept_counts
    valid = slot < count[0]
    key_bias = jnp.where(valid & (keep_mask[0] == 1), 0.0, NEG).astype(F32)
    rows_f = patch_rows.astype(F32).reshape(total, 1)
    cols_f = patch_cols.astype(F32).reshape(total, 1)
    gd = (valid.astype(F32)[:, None] * cotangent).astype(BF16)
    core = (lax.axis_index("fsdp") % 2).astype(jnp.int32)[None]

    if tuned:
        table = piece_table()
        first, second = Gather(inward_parts[0]), Gather(inward_parts[1])
        outup, downs = Gather(out_up), Gather(down_weight)
        small_full = gather_small(small)
        step([first, second])
        step([first])
        step([first, second])
        step([first, outup])
        step([first, second])
    else:
        gather = lambda a: lax.all_gather(a, "fsdp", axis=0, tiled=True)
        table = jnp.zeros((2,), jnp.int32)
        small_full = gather(small).astype(F32)

        class Whole:
            def __init__(self, shard):
                self.out = [gather(shard)[None, None]]

        first, second = Whole(inward_parts[0]), Whole(inward_parts[1])
        outup, downs = Whole(out_up), Whole(down_weight)

    def run(movers, kernel, *inputs):
        return step(movers, kernel, *inputs) if tuned else kernel(*inputs)

    f_gain, f_shift, f_bias, f_freqs, f_obias, f_mgain, f_mshift, f_ubias, f_dbias = unpack(small_full, lengths, n)
    pairs = f_freqs.reshape(-1, 2)
    fc, fr = pairs[:, 0][None, :], pairs[:, 1][None, :]
    small_up = jnp.concatenate([f_obias, f_mgain, f_mshift, jnp.zeros((5, width), F32)], axis=0)
    small_down = jnp.concatenate([f_dbias, f_mgain, jnp.zeros((6, width), F32)], axis=0)

    n1, cosine, sine = run([second], prologue, tokens, f_gain, f_shift, fc, fr, cols_f, rows_f)

    def attention(g0, ng):
        def both(*args):
            q, k, v = qkv(g0, ng, *args)
            return (q, k, v) + tuple(attend(q, k, v, key_bias[None, :]))
        return both

    q0, k0, v0, att0, lse0 = run([second, outup], attention(0, 1), table, n1, f_bias, cosine, sine, first.out)
    q1, k1, v1 = run([outup, downs], functools.partial(qkv, 1, groups - 1), table, n1, f_bias, cosine, sine, second.out)
    att1, lse1 = run([outup, downs], attend, q1, k1, v1, key_bias[None, :])
    if tuned:
        step([outup])
    att = jnp.concatenate([att0, att1], axis=1)
    middle, n2, act, slope = run([downs], up, table, count, att, tokens, small_up, f_ubias, outup.out)

    layout = (n // 4, 2, 2)

    def gradient(name, a, bs):
        if tuned:
            return weight_grad(core, a, [(b, b.shape[1], 0) for b in bs], layout, name)
        full = plain_grad(a, [(b, b.shape[1], 0) for b in bs], name)
        return lax.psum(lax.psum_scatter(full, "fsdp", scatter_dimension=0, tiled=True), "rep")

    class Done:
        def __init__(self, out):
            self.out = out

    def reduction(parts):
        return Reduce(*parts) if tuned else Done(parts)

    r_down = reduction(run([downs], functools.partial(gradient, "down_grad"), act, [gd]))
    if tuned:
        step([downs])
    outputs, gmid, gb, ga, gu, sums, ubsum = run(
        [r_down], down, table, count, act, slope, middle, cotangent, gd, small_down, outup.out, downs.out
    )
    r_up = reduction(run([r_down], functools.partial(gradient, "up_grad"), n2, [gu]))
    r_out = reduction(run([r_down, r_up], functools.partial(gradient, "out_grad"), att, [gb]))
    if tuned:
        step([r_out])
    backs = []
    heads = ((0, 0, q0, k0, v0, lse0), (1, 0, q1, k1, v1, lse1), (2, 1, q1, k1, v1, lse1))

    def back(movers, which):
        g0, l0, q, k, v, lse = heads[which]
        outs = run(movers, functools.partial(attend_back, g0, l0, 1), q, k, v, ga, lse, key_bias[:, None], cosine,
                   sine, cols_f, rows_f)
        backs.append(outs)

    def in_gradient(movers, name, which):
        bs = [backs[g][part] for g in which for part in range(3)]
        return reduction(run(movers, functools.partial(gradient, name), n1, bs))

    back([r_down, r_up, r_out], 0)
    back([r_down, r_up, r_out], 1)
    r_in0 = in_gradient([r_down], "in_grad0", (0, 1))
    if tuned:
        step([r_in0])
    back([r_up, r_out, r_in0], 2)
    r_in1 = in_gradient([r_up, r_out, r_in0], "in_grad1", (2,))
    if tuned:
        step([r_in1])
    grad_tokens, first_sums = run(
        [r_up, r_out, r_in0, r_in1], functools.partial(final, widths=[3 * GW, 6 * GW]),
        table, tokens, gmid, f_gain, [b[:3] for b in backs], [first.out, second.out]
    )
    fsum = jnp.concatenate([b[3] for b in backs], axis=0)
    bsum = jnp.concatenate([b[4] for b in backs], axis=0)
    d_freqs = jnp.stack([fsum[:, 0].reshape(-1), fsum[:, 1].reshape(-1)], axis=1).reshape(-1)
    small_grads = [
        bsum[:, :2].transpose(1, 0, 2),
        first_sums[0],
        first_sums[1],
        bsum[:, 2],
        d_freqs,
        sums[2],
        sums[0],
        sums[1],
        ubsum[0],
        sums[3],
    ]
    rows = small_rows(small_grads, n)
    if tuned:
        r_small = SmallReduce(rows)
        step([r_small, r_in0, r_in1])
        step([r_small, r_in0, r_in1])
        step([r_small, r_in1])
        step([r_small, r_in1])
        step([r_small])
        mine = r_small.out
    else:
        mine = lax.psum(lax.psum_scatter(rows, "fsdp", scatter_dimension=0, tiled=True), "rep")[0]
    pieces = []
    for r, ng in ((r_in0, 2), (r_in1, 1)):
        block = r.out.reshape(-1, ng, 3, GW)
        pieces += [block[:, g] for g in range(ng)]
    d_inward = jnp.stack(pieces, axis=2).reshape(-1, 3 * width)
    each = width // n
    cuts = []
    offset = 0
    for length in (2 * each, each, each, each, each, each, each, each, wide // n, each):
        cuts.append(lax.slice_in_dim(mine, offset, offset + length))
        offset += length
    o_bias, o_gain, o_shift, o_vbias, o_freqs, o_obias, o_mgain, o_mshift, o_ubias, o_dbias = cuts
    return (outputs, grad_tokens, o_gain, o_shift, d_inward, o_bias, o_vbias, o_freqs, r_out.out, o_obias,
            o_mgain, o_mshift, r_up.out, o_ubias, r_down.out, o_dbias)


def solution(mesh):
    n = mesh.shape["fsdp"]
    tuned = mesh.shape["rep"] == 2 and n == 16
    row = P(("rep", "fsdp"), None)
    vec, mat = P("fsdp"), P("fsdp", None)
    return jax.shard_map(
        functools.partial(local, tuned, n),
        mesh=mesh,
        in_specs=(row, vec, vec, mat, vec, vec, mat, vec, vec, vec, mat, vec, mat, vec, row,
                  P(("rep", "fsdp")), row, row, row),
        out_specs=(row, row, vec, vec, mat, vec, vec, vec, mat, vec, vec, vec, mat, vec, mat, vec),
        check_vma=False,
    )
```

```python
import functools
import math

import jax
import jax.numpy as jnp
from jax import lax
from jax.experimental import pallas as pl
from jax.experimental.pallas import tpu as pltpu
from jax.sharding import PartitionSpec as P

HD = 64
LOG2E = 1.4426950408889634
EPS = 1e-06
NEG = -1e30
F32 = jnp.float32
BF16 = jnp.bfloat16
GH = 4
GW = GH * HD
HALF = GW // 2


def dims(lhs, rhs, lhs_axis, rhs_axis):
    return lax.dot_general(
        lhs, rhs, (((lhs_axis,), (rhs_axis,)), ((), ())), preferred_element_type=F32
    )


def nn(lhs, rhs):
    return dims(lhs, rhs, 1, 0)


def nt(lhs, rhs):
    return dims(lhs, rhs, 1, 1)


def tn(lhs, rhs):
    return dims(lhs, rhs, 0, 0)


def params(grid, mib):
    return pltpu.CompilerParams(
        dimension_semantics=("arbitrary",) * len(grid), vmem_limit_bytes=mib * 2**20
    )


def whole(shape):
    return pl.BlockSpec(shape, lambda *idx: (0,) * len(shape))


ANY = pl.BlockSpec(memory_space=pl.ANY)
SMEM = pl.BlockSpec(memory_space=pltpu.SMEM)


def kept(shape, dtype):
    return pltpu.HBM(shape, dtype)


def far(*arrays):
    return [pltpu.with_memory_space_constraint(a, pltpu.HBM) for a in arrays]


def cost(flops, bytes_moved, transcendental=0):
    return pl.CostEstimate(
        flops=int(flops), bytes_accessed=int(bytes_moved), transcendentals=int(transcendental)
    )


def group_perm(transposed):
    row = lax.broadcasted_iota(jnp.int32, (GW, GW), 0)
    col = lax.broadcasted_iota(jnp.int32, (GW, GW), 1)
    packed, natural = (row, col) if transposed else (col, row)
    half = packed // HALF
    head = (packed % HALF) // (HD // 2)
    source = head * HD + half * (HD // 2) + packed % (HD // 2)
    return jnp.where(source == natural, 1.0, 0.0).astype(BF16)


def packed_head_mask(head):
    lane = lax.broadcasted_iota(jnp.int32, (1, GW), 1)
    return (lane % HALF) // (HD // 2) == head


def natural_head_mask(head):
    lane = lax.broadcasted_iota(jnp.int32, (1, GW), 1)
    return lane // HD == head


def normalize(values):
    center = values - jnp.mean(values, axis=-1, keepdims=True)
    spread = jnp.mean(center * center, axis=-1, keepdims=True)
    inverse = lax.rsqrt(spread + EPS)
    return center * inverse, inverse


def load_pieces(table, sources, target, sem, rows):
    copies = []
    slots = table.shape[0] // 2
    for source in sources:
        width = source.shape[2]
        for slot in range(source.shape[0]):
            number = len(copies)
            row = pl.multiple_of(table[number] * rows, rows)
            col = pl.multiple_of(table[slots + number] * width, width)
            copies.append(
                pltpu.make_async_copy(
                    source.at[slot, pl.ds(0, rows)], target.at[pl.ds(row, rows), pl.ds(col, width)], sem.at[number]
                )
            )
    return copies


def piece_count(sources):
    return sum(s.shape[0] for s in sources)


SMALL_ROWS = 16


def pack_kernel(rep, in_ref, out_ref, up_ref, down_ref, small_ref, one_ref, two_ref, three_ref, four_ref):
    def write(y):
        rows, third = in_ref.shape[0], in_ref.shape[1] // 3
        groups = third // GW
        cuts = [in_ref[:, pl.ds(part * third + g * GW, GW)] for g in range(groups) for part in range(3)]
        first = jnp.concatenate(cuts[:3], axis=1)
        half = first.shape[1] // 2
        one_ref[0, pl.ds(0, rows), :] = first[:, y * half : (y + 1) * half]
        one_ref[0, pl.ds(rows, SMALL_ROWS), :] = small_ref[...]
        rest = jnp.concatenate(cuts[3:], axis=1)
        half = rest.shape[1] // 2
        two_ref[0] = rest[:, y * half : (y + 1) * half]
        both = jnp.concatenate([out_ref[...], up_ref[...]], axis=1)
        half = both.shape[1] // 2
        three_ref[0] = both[:, y * half : (y + 1) * half]
        half = down_ref.shape[1] // 2
        four_ref[0] = down_ref[:, pl.ds(y * half, half)]

    @pl.when(rep[0] == 0)
    def _():
        write(0)

    @pl.when(rep[0] == 1)
    def _():
        write(1)


def pack(rep, inward, outward, upward, downward, small):
    rows, wide = inward.shape
    width = wide // 3
    shapes = [
        (1, rows + SMALL_ROWS, 3 * GW // 2),
        (1, rows, (wide - 3 * GW) // 2),
        (1, rows, (width + upward.shape[1]) // 2),
        (1, downward.shape[0], width // 2),
    ]
    return pl.pallas_call(
        pack_kernel,
        in_specs=[SMEM] + [pl.BlockSpec(memory_space=pltpu.VMEM)] * 5,
        out_specs=[pl.BlockSpec(memory_space=pltpu.VMEM)] * 4,
        out_shape=[jax.ShapeDtypeStruct(shape, BF16) for shape in shapes],
        cost_estimate=cost(0, 2 * rows * width * 24),
        name="pack",
    )(rep, inward, outward, upward, downward, small)


V_GAIN, V_SHIFT, V_BIAS, V_FREQ, V_OBIAS, V_MGAIN, V_MSHIFT, V_UBIAS, V_DBIAS = range(9)


def prologue_kernel(lengths, owners, rows, npieces, order, x_ref, pos_ref, *rest):
    pieces = rest[:npieces]
    n1_ref, cos_ref, sin_ref, vec_ref, aux_ref, got, fc, fr, sem = rest[npieces:]
    width = x_ref.shape[1]

    @pl.when(pl.program_id(0) == 0)
    def _():
        copies = []
        for number, piece in enumerate(pieces):
            slots = piece.shape[0]
            copies.append(
                pltpu.make_async_copy(
                    piece.at[:, pl.ds(rows, SMALL_ROWS)], got.at[pl.ds(number * slots, slots)], sem.at[number]
                )
            )
        for copy in copies:
            copy.start()
        for copy in copies:
            copy.wait()
        vec_ref[...] = jnp.zeros_like(vec_ref)
        for owner in range(owners):
            tile = got[order[owner]].astype(F32)
            for row, length in enumerate(lengths):
                vec_ref[row : row + 1, owner * length : (owner + 1) * length] = tile[row : row + 1, :length]
        freq = jnp.broadcast_to(vec_ref[V_FREQ : V_FREQ + 1, :width], (16, width)).astype(BF16)
        source = lax.broadcasted_iota(jnp.int32, (width, width // 2), 0)
        target = lax.broadcasted_iota(jnp.int32, (width, width // 2), 1)
        fc[...] = nn(freq, jnp.where(source == 2 * target, 1.0, 0.0).astype(BF16))[:8]
        fr[...] = nn(freq, jnp.where(source == 2 * target + 1, 1.0, 0.0).astype(BF16))[:8]

    xhat, _ = normalize(x_ref[...])
    n1_ref[...] = (xhat * vec_ref[V_GAIN : V_GAIN + 1, :width] + vec_ref[V_SHIFT : V_SHIFT + 1, :width]).astype(BF16)
    pos = pos_ref[...]
    aux = jnp.transpose(jnp.concatenate([pos, jnp.zeros((120, pos.shape[1]), F32)], axis=0))
    aux_ref[...] = aux
    angle = aux[:, 0:1] * fc[0:1, :] + aux[:, 1:2] * fr[0:1, :]
    cosine, sine = cos_sin(angle)
    cos_ref[...] = cosine
    sin_ref[...] = sine


def prologue(lengths, owners, rows, order, x, pos, pieces, rb=256):
    total, width = x.shape
    pairs = width // 2
    grid = (total // rb,)
    blk = lambda w: pl.BlockSpec((rb, w), lambda i: (i, 0))
    wide = max(lengths) * owners
    return pl.pallas_call(
        functools.partial(prologue_kernel, lengths, owners, rows, len(pieces)),
        grid=grid,
        in_specs=[SMEM, blk(width), pl.BlockSpec((8, rb), lambda i: (0, i))] + [ANY] * len(pieces),
        out_specs=[blk(width), blk(pairs), blk(pairs), whole((16, wide)), blk(128)],
        out_shape=[
            kept((total, width), BF16),
            kept((total, pairs), F32),
            kept((total, pairs), F32),
            kept((16, wide), F32),
            kept((total, 128), F32),
        ],
        scratch_shapes=[
            pltpu.VMEM((piece_count(pieces), SMALL_ROWS, pieces[0].shape[2]), BF16),
            pltpu.VMEM((8, pairs), F32),
            pltpu.VMEM((8, pairs), F32),
            pltpu.SemaphoreType.DMA((len(pieces),)),
        ],
        compiler_params=params(grid, 24),
        cost_estimate=cost(total * width * 40, total * width * 10),
        name="prologue",
    )(order, *far(x), pos, *far(*pieces))


QUARTER = (1.5703125, 4.837512969970703125e-4, 7.549789948768648e-8)


def cos_sin(angle):
    turns = jnp.floor(angle * 0.6366197723675814 + 0.5)
    r = ((angle - turns * QUARTER[0]) - turns * QUARTER[1]) - turns * QUARTER[2]
    r2 = r * r
    s = r + r * r2 * (-1.6666654611e-1 + r2 * (8.3321608736e-3 - 1.9515295891e-4 * r2))
    c = 1.0 - 0.5 * r2 + r2 * r2 * (4.166664568298827e-2 + r2 * (-1.388731625493765e-3 + 2.443315711809948e-5 * r2))
    quad = turns.astype(jnp.int32)
    odd = (quad & 1) == 1
    cosine = jnp.where(odd, s, c)
    sine = jnp.where(odd, c, s)
    cosine = jnp.where(((quad + 1) & 2) == 2, -cosine, cosine)
    sine = jnp.where((quad & 2) == 2, -sine, sine)
    return cosine, sine


def qkv_kernel(g0, npieces, rows, table, n1_ref, vec_ref, cos_ref, sin_ref, *rest):
    pieces = rest[:npieces]
    q_ref, k_ref, v_ref, w, wp, bp, sem = rest[npieces:]
    width = n1_ref.shape[1]
    groups = w.shape[1] // (3 * GW)
    bias_ref = vec_ref.at[V_BIAS : V_BIAS + 1, :]

    @pl.when(pl.program_id(0) == 0)
    def _():
        copies = load_pieces(table, pieces, w, sem, rows)
        for copy in copies:
            copy.start()
        perm = group_perm(False)
        for copy in copies:
            copy.wait()
        for g in range(groups):
            for part in range(2):
                packed = pl.ds((g * 2 + part) * GW, GW)
                wp[:, packed] = nn(w[:, pl.ds((g * 3 + part) * GW, GW)], perm).astype(BF16)
                natural = pl.ds(part * width + (g0 + g) * GW, GW)
                spread = jnp.broadcast_to(bias_ref[:, natural].astype(BF16), (16, GW))
                bp[:, packed] = nn(spread, perm)[:8]

    n1 = n1_ref[...]
    for g in range(groups):
        cosine = cos_ref[:, pl.ds((g0 + g) * HALF, HALF)]
        sine = sin_ref[:, pl.ds((g0 + g) * HALF, HALF)]
        for part, out, scale in ((0, q_ref, HD**-0.5 * LOG2E), (1, k_ref, 1.0)):
            packed = pl.ds((g * 2 + part) * GW, GW)
            mixed = nn(n1, wp[:, packed]) + bp[0:1, packed]
            a, b = mixed[:, :HALF], mixed[:, HALF:]
            first = a * cosine - b * sine
            second = a * sine + b * cosine
            if scale != 1.0:
                first = first * scale
                second = second * scale
            out[:, pl.ds(g * GW, HALF)] = first.astype(BF16)
            out[:, pl.ds(g * GW + HALF, HALF)] = second.astype(BF16)
        bias = bias_ref[:, pl.ds(2 * width + (g0 + g) * GW, GW)]
        v_ref[:, pl.ds(g * GW, GW)] = (nn(n1, w[:, pl.ds((g * 3 + 2) * GW, GW)]) + bias).astype(BF16)


def qkv(g0, groups, rows, table, n1, vec, cosine, sine, pieces, rb=256):
    total, width = n1.shape
    pairs = width // 2
    grid = (total // rb,)
    blk = lambda w: pl.BlockSpec((rb, w), lambda i: (i, 0))
    out = kept((total, groups * GW), BF16)
    copies = piece_count(pieces)
    return pl.pallas_call(
        functools.partial(qkv_kernel, g0, len(pieces), rows),
        grid=grid,
        in_specs=[SMEM, blk(width), whole(vec.shape), blk(pairs), blk(pairs)] + [ANY] * len(pieces),
        out_specs=[blk(groups * GW)] * 3,
        out_shape=[out] * 3,
        scratch_shapes=[
            pltpu.VMEM((width, 3 * groups * GW), BF16),
            pltpu.VMEM((width, 2 * groups * GW), BF16),
            pltpu.VMEM((8, 2 * groups * GW), F32),
            pltpu.SemaphoreType.DMA((copies,)),
        ],
        compiler_params=params(grid, 24),
        cost_estimate=cost(total * width * groups * GW * 6, total * width * 8 + width * groups * GW * 6),
        name="qkv",
    )(table, *far(n1, vec, cosine, sine, *pieces))


def attend_kernel(q_ref, k_ref, v_ref, pos_ref, att_in, att_ref, lse_ref, wide_ref, mask):
    g, r = pl.program_id(0), pl.program_id(1)
    rb, keys = q_ref.shape[0], k_ref.shape[0]
    here = pl.ds(pl.multiple_of(r * rb, rb), rb)

    @pl.when(g == 0)
    def _():
        row = lax.broadcasted_iota(jnp.int32, (rb, keys), 0) + r * rb
        col = lax.broadcasted_iota(jnp.int32, (rb, keys), 1)
        mask[here, :] = jnp.where(row == col, 0.0, jnp.broadcast_to(pos_ref[2:3, :], (rb, keys)))

    q = q_ref[...]
    k = k_ref[...]
    v = v_ref[...]
    total = jnp.zeros((rb, GW), F32)
    lane = lax.broadcasted_iota(jnp.int32, (rb, 128), 1)
    logs = jnp.zeros((rb, 128), F32)
    for h in range(GH):
        qm = jnp.where(packed_head_mask(h), q, jnp.zeros_like(q))
        scores = nt(qm, k) + mask[here, :]
        top = jnp.max(scores, axis=-1, keepdims=True)
        weight = jnp.exp2(scores - top)
        norm = jnp.sum(weight, axis=-1, keepdims=True)
        vm = jnp.where(natural_head_mask(h), v, jnp.zeros_like(v))
        total = total + nn(weight.astype(BF16), vm) * (1.0 / norm)
        logs = jnp.where(lane == h, top + jnp.log2(norm), logs)
    att_ref[...] = total.astype(BF16)
    wide_ref[...] = total
    lse_ref[...] = jnp.transpose(logs)[:8, :]


def attend(g0, q, k, v, pos, att, rb=512):
    total, width = q.shape
    groups = width // GW
    grid = (groups, total // rb)
    return pl.pallas_call(
        attend_kernel,
        grid=grid,
        in_specs=[
            pl.BlockSpec((rb, GW), lambda g, r: (r, g)),
            pl.BlockSpec((total, GW), lambda g, r: (0, g)),
            pl.BlockSpec((total, GW), lambda g, r: (0, g)),
            whole((8, total)),
            ANY,
        ],
        out_specs=[
            pl.BlockSpec((rb, GW), lambda g, r: (r, g + g0)),
            pl.BlockSpec((None, 8, rb), lambda g, r: (g, 0, r)),
            pl.BlockSpec((rb, GW), lambda g, r: (r, g)),
        ],
        out_shape=[
            kept(att.shape, BF16),
            kept((groups, 8, total), F32),
            kept((total, width), F32),
        ],
        input_output_aliases={4: 0},
        scratch_shapes=[pltpu.VMEM((total, total), F32)],
        compiler_params=params(grid, 32),
        cost_estimate=cost(total * total * width * 16, total * width * 8, total * total * 12),
        name="attend",
    )(*far(q, k, v, pos, att))


PHI_SCALE = 0.3989422804014327
TAIL_SCALE = 0.44 * 0.7071067811865476
TAIL = (
    0.12411047596471954,
    0.12443560910041027,
    0.10865662380098591,
    0.10790671631036299,
    -0.010091621907114547,
    0.14834527631989725,
    -0.13897496529649409,
    0.03561197654899638,
)


def gelu_parts(h):
    t = 1.0 / (1.0 + TAIL_SCALE * jnp.abs(h))
    poly = TAIL[-1]
    for coefficient in TAIL[-2::-1]:
        poly = poly * t + coefficient
    bell = jnp.exp(-0.5 * h * h)
    tail = poly * t * bell
    phi = jnp.where(h < 0, tail, 1.0 - tail)
    return h * phi, phi + h * (bell * PHI_SCALE)


def up_kernel(npieces, rows, table, count, att_ref, x_ref, cot_ref, vec_ref, *rest):
    pieces = rest[:npieces]
    mid_ref, n2_ref, act_ref, gp_ref, gd_ref, w, sem = rest[npieces:]
    rb, width = x_ref.shape
    wide = act_ref.shape[1]

    @pl.when(pl.program_id(0) == 0)
    def _():
        copies = load_pieces(table, pieces, w, sem, rows)
        for copy in copies:
            copy.start()
        for copy in copies:
            copy.wait()

    slot = lax.broadcasted_iota(jnp.int32, (rb, 1), 0) + pl.program_id(0) * rb
    valid = jnp.where(slot < count[0], 1.0, 0.0)
    gd_ref[...] = (valid * cot_ref[...]).astype(BF16)
    branch = nn(att_ref[...], w[:, pl.ds(0, width)]) + vec_ref[V_OBIAS : V_OBIAS + 1, :width]
    middle = x_ref[...] + valid * branch
    mid_ref[...] = middle
    xhat, _ = normalize(middle)
    n2 = (xhat * vec_ref[V_MGAIN : V_MGAIN + 1, :width] + vec_ref[V_MSHIFT : V_MSHIFT + 1, :width]).astype(BF16)
    n2_ref[...] = n2
    step = 512
    for c in range(wide // step):
        cut = pl.ds(c * step, step)
        hidden = nn(n2, w[:, pl.ds(width + c * step, step)]) + vec_ref[V_UBIAS : V_UBIAS + 1, cut]
        act, slope = gelu_parts(hidden)
        act_ref[:, cut] = act.astype(BF16)
        gp_ref[:, cut] = slope.astype(BF16)


def up(rows, wide, table, count, att, x, cot, vec, pieces, rb=256):
    total, width = x.shape
    grid = (total // rb,)
    blk = lambda w: pl.BlockSpec((rb, w), lambda i: (i, 0))
    copies = piece_count(pieces)
    return pl.pallas_call(
        functools.partial(up_kernel, len(pieces), rows),
        grid=grid,
        in_specs=[SMEM, SMEM, blk(width), blk(width), blk(width), whole(vec.shape)] + [ANY] * len(pieces),
        out_specs=[blk(width), blk(width), blk(wide), blk(wide), blk(width)],
        out_shape=[
            kept((total, width), F32),
            kept((total, width), BF16),
            kept((total, wide), BF16),
            kept((total, wide), BF16),
            kept((total, width), BF16),
        ],
        scratch_shapes=[
            pltpu.VMEM((width, width + wide), BF16),
            pltpu.SemaphoreType.DMA((copies,)),
        ],
        compiler_params=params(grid, 32),
        cost_estimate=cost(total * width * (width + wide) * 2, total * (width * 12 + wide * 4), total * wide * 2),
        name="up",
    )(table, count, *far(att, x, cot, vec, *pieces))


def down_kernel(nup, ndown, rows, table, count, act_ref, gp_ref, mid_ref, cot_ref, gd_ref, vec_ref, *rest):
    ups = rest[:nup]
    downs = rest[nup : nup + ndown]
    (out_ref, gm_ref, gb_ref, ga_ref, gu_ref, sums_ref, ubsum_ref, w, wd, sem, sem_d) = rest[nup + ndown :]
    i = pl.program_id(0)
    rb, width = mid_ref.shape
    wide = act_ref.shape[1]

    @pl.when(i == 0)
    def _():
        first = load_pieces(table, downs, wd, sem_d, rows * (wide // width))
        second = load_pieces(table, ups, w, sem, rows)
        for copy in first + second:
            copy.start()
        for copy in first + second:
            copy.wait()
        sums_ref[...] = jnp.zeros_like(sums_ref)
        ubsum_ref[...] = jnp.zeros_like(ubsum_ref)

    slot = lax.broadcasted_iota(jnp.int32, (rb, 1), 0) + i * rb
    valid = jnp.where(slot < count[0], 1.0, 0.0)
    middle = mid_ref[...]
    cot = cot_ref[...]
    gd = gd_ref[...]
    lowered = nn(act_ref[...], wd[...]) + vec_ref[V_DBIAS : V_DBIAS + 1, :width]
    out_ref[...] = middle + valid * lowered
    step = 512
    gn2 = jnp.zeros((rb, width), F32)
    for c in range(wide // step):
        cut = pl.ds(c * step, step)
        g = nt(gd, wd[cut, :]) * gp_ref[:, cut].astype(F32)
        g_low = g.astype(BF16)
        gu_ref[:, cut] = g_low
        ubsum_ref[0:1, cut] += jnp.sum(g_low.astype(F32), axis=0, keepdims=True)
        gn2 = gn2 + nt(g_low, w[:, pl.ds(width + c * step, step)])
    xhat, inverse = normalize(middle)
    sums_ref[0:1, :] += jnp.sum(gn2 * xhat, axis=0, keepdims=True)
    sums_ref[1:2, :] += jnp.sum(gn2, axis=0, keepdims=True)
    e = gn2 * vec_ref[V_MGAIN : V_MGAIN + 1, :width]
    back = (e - jnp.mean(e, axis=-1, keepdims=True) - xhat * jnp.mean(e * xhat, axis=-1, keepdims=True)) * inverse
    gmid = cot + back
    gm_ref[...] = gmid
    gb = (valid * gmid).astype(BF16)
    gb_ref[...] = gb
    sums_ref[2:3, :] += jnp.sum(gb.astype(F32), axis=0, keepdims=True)
    sums_ref[3:4, :] += jnp.sum(gd.astype(F32), axis=0, keepdims=True)
    ga_ref[...] = nt(gb, w[:, pl.ds(0, width)]).astype(BF16)


def down(rows, table, count, act, gp, mid, cot, gd, vec, ups, downs, rb=256):
    total, width = mid.shape
    wide = act.shape[1]
    grid = (total // rb,)
    blk = lambda w: pl.BlockSpec((rb, w), lambda i: (i, 0))
    return pl.pallas_call(
        functools.partial(down_kernel, len(ups), len(downs), rows),
        grid=grid,
        in_specs=[SMEM, SMEM, blk(wide), blk(wide), blk(width), blk(width), blk(width), whole(vec.shape)]
        + [ANY] * (len(ups) + len(downs)),
        out_specs=[blk(width), blk(width), blk(width), blk(width), blk(wide), whole((8, width)), whole((8, wide))],
        out_shape=[
            kept((total, width), F32),
            kept((total, width), F32),
            kept((total, width), BF16),
            kept((total, width), BF16),
            kept((total, wide), BF16),
            kept((8, width), F32),
            kept((8, wide), F32),
        ],
        scratch_shapes=[
            pltpu.VMEM((width, width + wide), BF16),
            pltpu.VMEM((wide, width), BF16),
            pltpu.SemaphoreType.DMA((piece_count(ups),)),
            pltpu.SemaphoreType.DMA((piece_count(downs),)),
        ],
        compiler_params=params(grid, 44),
        cost_estimate=cost(total * width * (width + 3 * wide) * 2, total * (width * 20 + wide * 6)),
        name="down",
    )(table, count, *far(act, gp, mid, cot, gd, vec, *ups, *downs))


def grad_kernel(pairs, mids, reps, rows, core, *rest):
    keep_ref, send_ref = rest[-2:]
    part = core[0]

    def spot(parity, mid, rep):
        return jnp.where(parity == 0, mid, rep), jnp.where(parity == 0, rep, mid)

    each = keep_ref.shape[-1]
    offset = 0
    for at, bt in pairs:
        a, b_ref = rest[at][...], rest[bt]
        begin = 0
        while begin < b_ref.shape[1]:
            column = offset + begin
            step = min(b_ref.shape[1] - begin, each - column % each, 768)
            result = tn(a, b_ref[:, pl.ds(begin, step)])
            rep, cut = column // each, pl.ds(column % each, step)
            for pair in range(a.shape[1] // (2 * rows)):
                low = result[pair * 2 * rows : pair * 2 * rows + rows]
                high = result[pair * 2 * rows + rows : (pair + 1) * 2 * rows]
                zz, mid = pair // mids, pair % mids
                one, two = spot(part, mid, rep)
                keep_ref[one, two, zz, :, cut] = jnp.where(part == 0, low, high).astype(BF16)
                one, two = spot(1 - part, mid, rep)
                send_ref[one, two, zz, :, cut] = jnp.where(part == 0, high, low).astype(BF16)
            begin += step
        offset += b_ref.shape[1]


def operands(pairs):
    arrays, index = [], []
    for pair in pairs:
        spots = []
        for array in pair:
            if not any(array is other for other in arrays):
                arrays.append(array)
            spots.append([array is other for other in arrays].index(True))
        index.append(spots)
    lefts = {one for one, _ in index}
    return arrays, index, lefts


def weight_grad(core, pairs, layout, name):
    slow, mids, reps = layout
    arrays, index, lefts = operands(pairs)
    total, height = pairs[0][0].shape
    width = sum(b.shape[1] for _, b in pairs)
    rows = height // (slow * mids * 2)
    chunk = 384 if 384 % (2 * mids * rows) == 0 else 2 * mids * rows
    slows = chunk // (2 * mids * rows)
    grid = (height // chunk,)
    out = jax.ShapeDtypeStruct((mids, reps, slow, rows, width // reps), BF16)
    spec = pl.BlockSpec((mids, reps, slows, rows, width // reps), lambda i: (0, 0, i, 0, 0))
    return pl.pallas_call(
        functools.partial(grad_kernel, index, mids, reps, rows),
        grid=grid,
        in_specs=[SMEM]
        + [
            pl.BlockSpec((total, chunk), lambda i: (0, i)) if n in lefts else whole(a.shape)
            for n, a in enumerate(arrays)
        ],
        out_specs=[spec, spec],
        out_shape=[out, out],
        compiler_params=params(grid, 40),
        cost_estimate=cost(total * height * width * 2, total * (height + width) * 2 + height * width * 2),
        name=name,
    )(core, *far(*arrays))


def plain_grad_kernel(pairs, *rest):
    out_ref = rest[-1]
    offset = 0
    for at, bt in pairs:
        a, b_ref = rest[at][...], rest[bt]
        step = min(b_ref.shape[1], 768)
        for c in range(b_ref.shape[1] // step):
            out_ref[:, pl.ds(offset + c * step, step)] = tn(a, b_ref[:, pl.ds(c * step, step)])
        offset += b_ref.shape[1]


def plain_grad(pairs, name):
    arrays, index, lefts = operands(pairs)
    total, height = pairs[0][0].shape
    width = sum(b.shape[1] for _, b in pairs)
    chunk = 384
    grid = (height // chunk,)
    return pl.pallas_call(
        functools.partial(plain_grad_kernel, index),
        grid=grid,
        in_specs=[
            pl.BlockSpec((total, chunk), lambda i: (0, i)) if n in lefts else whole(a.shape)
            for n, a in enumerate(arrays)
        ],
        out_specs=pl.BlockSpec((chunk, width), lambda i: (i, 0)),
        out_shape=jax.ShapeDtypeStruct((height, width), F32),
        compiler_params=params(grid, 63),
        cost_estimate=cost(total * height * width * 2, total * (height + width) * 2 + height * width * 4),
        name=name,
    )(*arrays)


def unrotate(grad, cosine, sine):
    first, second = grad[:, :HALF], grad[:, HALF:]
    return first * cosine + second * sine, second * cosine - first * sine


def angle_grad(grad, rotated):
    return grad[:, HALF:] * rotated[:, :HALF] - grad[:, :HALF] * rotated[:, HALF:]


def back_kernel(q_ref, k_ref, v_ref, do_ref, lse_ref, wide_ref, aux_ref, cos_ref, sin_ref,
                g_ref, fsum_ref, bsum_ref, ds_s, p_s, dk_s, dv_s):
    r = pl.program_id(0)
    rb, keys = q_ref.shape[0], k_ref.shape[0]
    here = pl.ds(pl.multiple_of(r * rb, rb), rb)
    q = q_ref[...]
    k = k_ref[...]
    v = v_ref[...]
    do = do_ref[...]
    zero = jnp.zeros_like(q)
    product = do.astype(F32) * wide_ref[...]
    high = product.astype(BF16)
    low = (product - high.astype(F32)).astype(BF16)
    lane = lax.broadcasted_iota(jnp.int32, (16, GW), 1)
    pick_head = jnp.where(lane // HD == lax.broadcasted_iota(jnp.int32, (16, GW), 0), 1.0, 0.0).astype(BF16)
    inner = nt(pick_head, high) + nt(pick_head, low)
    key = lax.broadcasted_iota(jnp.int32, (keys, rb), 0)
    query = lax.broadcasted_iota(jnp.int32, (keys, rb), 1) + r * rb
    mask = jnp.where(key == query, 0.0, jnp.broadcast_to(aux_ref[:, 2:3], (keys, rb)))
    dq = jnp.zeros((rb, GW), F32)
    qms, doms = [], []
    for h in range(GH):
        qm = jnp.where(packed_head_mask(h), q, zero)
        dom = jnp.where(natural_head_mask(h), do, zero)
        qms.append(qm)
        doms.append(dom)
        soft = jnp.exp2(nt(k, qm) + mask - lse_ref[h : h + 1, :])
        ds = (soft * (nt(v, dom) - inner[h : h + 1, :])).astype(BF16)
        cut = pl.ds(h * rb, rb)
        ds_s[:, cut] = ds
        p_s[:, cut] = soft.astype(BF16)
        km = jnp.where(packed_head_mask(h), k, jnp.zeros_like(k))
        dq = dq + tn(ds, km)
    dk = nn(ds_s[...], jnp.concatenate(qms, axis=0)) * (1.0 / LOG2E)
    dv = nn(p_s[...], jnp.concatenate(doms, axis=0))

    perm = group_perm(True)
    cosine, sine = cos_ref[here, :], sin_ref[here, :]
    dq = dq * (HD**-0.5)
    ang = angle_grad(dq, q.astype(F32) * (HD**0.5 / LOG2E))
    first, second = unrotate(dq, cosine, sine)
    gq = nn(jnp.concatenate([first.astype(BF16), second.astype(BF16)], axis=1), perm)
    g_ref[here, pl.ds(0, GW)] = gq.astype(BF16)
    col, row = aux_ref[here, 0:1], aux_ref[here, 1:2]
    fcol = jnp.sum(ang * col, axis=0, keepdims=True)
    frow = jnp.sum(ang * row, axis=0, keepdims=True)
    qsum = jnp.sum(gq, axis=0, keepdims=True)

    @pl.when(r == 0)
    def _():
        dk_s[...] = dk
        dv_s[...] = dv
        fsum_ref[0:1, :] = fcol
        fsum_ref[1:2, :] = frow
        bsum_ref[0:1, pl.ds(0, GW)] = qsum

    @pl.when(r > 0)
    def _():
        dk_s[...] += dk
        dv_s[...] += dv
        fsum_ref[0:1, :] += fcol
        fsum_ref[1:2, :] += frow
        bsum_ref[0:1, pl.ds(0, GW)] += qsum

    @pl.when(r == pl.num_programs(0) - 1)
    def _():
        dkf = dk_s[...]
        angk = angle_grad(dkf, k.astype(F32))
        fsum_ref[0:1, :] += jnp.sum(angk * aux_ref[:, 0:1], axis=0, keepdims=True)
        fsum_ref[1:2, :] += jnp.sum(angk * aux_ref[:, 1:2], axis=0, keepdims=True)
        one, two = unrotate(dkf, cos_ref[...], sin_ref[...])
        gk = nn(jnp.concatenate([one.astype(BF16), two.astype(BF16)], axis=1), perm)
        g_ref[:, pl.ds(GW, GW)] = gk.astype(BF16)
        bsum_ref[0:1, pl.ds(GW, GW)] = jnp.sum(gk, axis=0, keepdims=True)
        gv = dv_s[...].astype(BF16)
        g_ref[:, pl.ds(2 * GW, GW)] = gv
        bsum_ref[0:1, pl.ds(2 * GW, GW)] = jnp.sum(gv.astype(F32), axis=0, keepdims=True)


def attend_back(g0, l0, q, k, v, do, lse, wide, aux, cosine, sine, rb=512):
    total = q.shape[0]
    grid = (total // rb,)
    return pl.pallas_call(
        back_kernel,
        grid=grid,
        in_specs=[
            pl.BlockSpec((rb, GW), lambda r: (r, l0)),
            pl.BlockSpec((total, GW), lambda r: (0, l0)),
            pl.BlockSpec((total, GW), lambda r: (0, l0)),
            pl.BlockSpec((rb, GW), lambda r: (r, g0)),
            pl.BlockSpec((None, 8, rb), lambda r: (l0, 0, r)),
            pl.BlockSpec((rb, GW), lambda r: (r, l0)),
            whole((total, 128)),
            pl.BlockSpec((total, HALF), lambda r: (0, g0)),
            pl.BlockSpec((total, HALF), lambda r: (0, g0)),
        ],
        out_specs=[whole((total, 3 * GW)), whole((8, HALF)), whole((8, 3 * GW))],
        out_shape=[
            kept((total, 3 * GW), BF16),
            jax.ShapeDtypeStruct((8, HALF), F32),
            jax.ShapeDtypeStruct((8, 3 * GW), F32),
        ],
        scratch_shapes=[
            pltpu.VMEM((total, GH * rb), BF16),
            pltpu.VMEM((total, GH * rb), BF16),
            pltpu.VMEM((total, GW), F32),
            pltpu.VMEM((total, GW), F32),
        ],
        compiler_params=params(grid, 48),
        cost_estimate=cost(total * total * GW * 40, total * GW * 20, total * total * GH),
        name="attend_back",
    )(*far(q, k, v, do, lse, wide, aux, cosine, sine))


def final_kernel(count, counts, rows, table, x_ref, gm_ref, vec_ref, *rest):
    grads, place = rest[:count], count
    pieces = []
    for number in counts:
        pieces.append(rest[place : place + number])
        place += number
    out_ref, sums_ref = rest[place : place + 2]
    weights = rest[place + 2 : place + 2 + len(counts)]
    sems = rest[place + 2 + len(counts) :]

    @pl.when(pl.program_id(0) == 0)
    def _():
        copies = []
        for p, w, sem in zip(pieces, weights, sems):
            copies += load_pieces(table, p, w, sem, rows)
        for copy in copies:
            copy.start()
        for copy in copies:
            copy.wait()
        sums_ref[...] = jnp.zeros_like(sums_ref)

    e = jnp.zeros(x_ref.shape, F32)
    group = 0
    for w in weights:
        for g in range(w.shape[1] // (3 * GW)):
            e = e + nt(grads[group][...], w[:, pl.ds(g * 3 * GW, 3 * GW)])
            group += 1
    xhat, inverse = normalize(x_ref[...])
    sums_ref[0:1, :] += jnp.sum(e * xhat, axis=0, keepdims=True)
    sums_ref[1:2, :] += jnp.sum(e, axis=0, keepdims=True)
    eg = e * vec_ref[V_GAIN : V_GAIN + 1, : x_ref.shape[1]]
    back = (eg - jnp.mean(eg, axis=-1, keepdims=True) - xhat * jnp.mean(eg * xhat, axis=-1, keepdims=True)) * inverse
    out_ref[...] = gm_ref[...] + back


def final(rows, widths, table, x, gmid, vec, grads, piece_sets, rb=256):
    total, width = x.shape
    grid = (total // rb,)
    blk = lambda w: pl.BlockSpec((rb, w), lambda i: (i, 0))
    pieces = [p for ps in piece_sets for p in ps]
    return pl.pallas_call(
        functools.partial(final_kernel, len(grads), [len(ps) for ps in piece_sets], rows),
        grid=grid,
        in_specs=[SMEM, blk(width), blk(width), whole(vec.shape)]
        + [blk(g.shape[1]) for g in grads]
        + [ANY] * len(pieces),
        out_specs=[blk(width), whole((8, width))],
        out_shape=[kept((total, width), F32), jax.ShapeDtypeStruct((8, width), F32)],
        scratch_shapes=[pltpu.VMEM((width, w), BF16) for w in widths]
        + [pltpu.SemaphoreType.DMA((piece_count(ps),)) for ps in piece_sets],
        compiler_params=params(grid, 32),
        cost_estimate=cost(total * width * width * 6, total * width * 20 + width * width * 6),
        name="final",
    )(table, *far(x, gmid, vec), *far(*grads), *far(*pieces))


def place():
    me = lax.axis_index("fsdp")
    return lax.axis_index("rep"), me // 4, (me // 2) % 2, me % 2


def move(value, step):
    moves = []
    for i in range(32):
        y, z, x, c = step(i // 16, (i // 4) % 4, (i // 2) % 2, i % 2)
        moves.append((i, y * 16 + z * 4 + x * 2 + c))
    return lax.ppermute(value, ("rep", "fsdp"), moves)


def across_core(value):
    return move(value, lambda y, z, x, c: (y, z, x, 1 - c))


def across_x(value):
    return move(value, lambda y, z, x, c: (y, z, 1 - x, c))


def across_rep(value):
    return move(value, lambda y, z, x, c: (1 - y, z, x, c))


def across_near(value):
    return move(value, lambda y, z, x, c: (y, z ^ 1, x, c))


def across_far(value):
    return move(value, lambda y, z, x, c: (y, z ^ 2, x, c))


def across_one(value):
    return move(value, lambda y, z, x, c: (y, z, 1 - x, c) if c == 0 else (1 - y, z, x, c))


def across_two(value):
    return move(value, lambda y, z, x, c: (1 - y, z, x, c) if c == 0 else (y, z, 1 - x, c))


def pick(array, index):
    return lax.dynamic_index_in_dim(array, index, 0, keepdims=False)


def pick_two(array, index):
    return lax.dynamic_slice_in_dim(array, 2 * index, 2, 0)


def piece_table():
    y, z, x, c = place()
    slot = jnp.arange(4, dtype=jnp.int32)
    owners, halves = [], []

    def add(mid, core, half):
        owners.append((z ^ slot) * 4 + mid * 2 + core)
        halves.append(jnp.broadcast_to(half, (4,)))

    for core in (c, 1 - c):
        add(x, core, y)
        add(jnp.where(core == 0, x, 1 - x), core, jnp.where(core == 0, 1 - y, y))
        add(jnp.where(core == 0, 1 - x, x), core, jnp.where(core == 0, y, 1 - y))
        add(1 - x, core, 1 - y)
    return jnp.concatenate(owners + halves).astype(jnp.int32)


def first_of_owner(table, n):
    slots = table.shape[0] // 2
    match = table[None, :slots] == jnp.arange(n, dtype=jnp.int32)[:, None]
    return jnp.min(jnp.where(match, jnp.arange(slots, dtype=jnp.int32)[None, :], slots), axis=1)


class Reduce:
    stages = (across_core, across_one, across_two, across_far, across_near, across_rep)

    def __init__(self, keep, send):
        self.keep, self.first, self.got, self.stage = keep, send, [], 0
        self.out = None

    def sends(self):
        return [(self.stages[self.stage], self.send())]

    def takes(self, values):
        self.take(values[0])

    def base(self, count, one, two=None, cut=None):
        step = lambda a, i: a if i is None else pick(a, i)
        total = None
        for source, used in ((self.keep, 0), (self.got[0], 0), *((g, n + 1) for n, g in enumerate(self.got[1:count]))):
            value = source
            if used < 1:
                value = step(value, one)
            if used < 2:
                value = step(value, two)
            if cut is not None:
                value = cut(value)
            value = value.astype(F32)
            total = value if total is None else total + value
        return total

    def level(self, index):
        return self.base(3, self.i1, self.i2, lambda a: pick(a, index)) + pick(self.got[3], index % 2).astype(F32)

    def send(self):
        y, z, x, c = place()
        self.i1, self.i2 = jnp.where(c == 0, x, y), jnp.where(c == 0, y, x)
        if self.stage == 0:
            return self.first
        if self.stage == 1:
            return self.base(1, 1 - self.i1).astype(BF16)
        if self.stage == 2:
            return self.base(2, self.i1, 1 - self.i2).astype(BF16)
        if self.stage == 3:
            return self.base(3, self.i1, self.i2, lambda a: pick_two(a, 1 - z // 2)).astype(BF16)
        if self.stage == 4:
            return self.level(z ^ 1).astype(BF16)
        self.total = self.level(z) + self.got[4].astype(F32)
        return self.total

    def take(self, value):
        self.stage += 1
        if self.stage == 6:
            y = lax.axis_index("rep")
            first = jnp.where(y == 0, self.total, value)
            second = jnp.where(y == 0, value, self.total)
            self.out = jnp.concatenate([first, second], axis=1)
        else:
            self.got.append(value)


class SmallReduce:
    stages = (across_core, across_x, across_far, across_near, across_rep)

    def __init__(self, rows):
        self.part, self.stage = rows.reshape(4, 2, 2, rows.shape[1]).transpose(2, 1, 0, 3), 0

    sends, takes = Reduce.sends, Reduce.takes

    def send(self):
        y, z, x, c = place()
        if self.stage == 4:
            self.kept = self.part
            return self.part
        cut = pick_two if self.stage == 2 else pick
        index = (c, x, z // 2, z % 2)[self.stage]
        self.kept = cut(self.part, index)
        return cut(self.part, 1 - index)

    def take(self, value):
        self.stage += 1
        self.part = self.kept + value
        self.out = self.part


class Gather:
    def __init__(self, half):
        self.part, self.stage = half, 0

    def sends(self):
        if self.stage < 3:
            return [((across_near, across_far, across_two)[self.stage], self.part)]
        if self.stage == 3:
            return [(across_one, self.part), (across_one, self.two), (across_core, self.part), (across_core, self.two)]
        return [(across_core, part) for part in self.one]

    def takes(self, values):
        self.stage += 1
        if self.stage < 3:
            self.part = jnp.concatenate([self.part, values[0]])
        elif self.stage == 3:
            self.two = values[0]
        elif self.stage == 4:
            self.one, self.other = values[:2], values[2:]
        else:
            self.out = [self.part, self.two, *self.one, *self.other, *values]


def step(movers, kernel=None, *inputs):
    sends = [m.sends() for m in movers]
    inputs, arrays = lax.optimization_barrier((inputs, [[a for _, a in s] for s in sends]))
    got = [[f(a) for (f, _), a in zip(s, each)] for s, each in zip(sends, arrays)]
    outs = kernel(*inputs) if kernel is not None else ()
    outs, got = lax.optimization_barrier((outs, got))
    for m, g in zip(movers, got):
        m.takes(g)
    return outs


def small_rows(parts, n):
    return jnp.concatenate([p.astype(F32).reshape(n, -1) for p in parts], axis=1)


def group_columns(weight, g0, ng, width):
    cuts = []
    for g in range(g0, g0 + ng):
        cuts += [weight[:, part * width + g * GW : part * width + (g + 1) * GW] for part in range(3)]
    return jnp.concatenate(cuts, axis=1)


def small_block(smalls, lanes):
    total = None
    for row, vector in enumerate(smalls):
        block = jnp.pad(vector[None, :], ((row, SMALL_ROWS - 1 - row), (0, lanes - vector.shape[0])))
        total = block if total is None else total + block
    return total


class Done:
    def __init__(self, out):
        self.out = out


def local(tuned, n, tokens, pre_gain, pre_shift, inward_weight, inward_bias, rotary_freqs, outward_weight,
          outward_bias, mlp_gain, mlp_shift, up_weight, up_bias, down_weight, down_bias, keep_mask, kept_counts,
          patch_rows, patch_cols, cotangent):
    total, width = tokens.shape
    groups = width // GW
    wide = up_weight.shape[1]
    rows = width // n
    smalls = [pre_gain, pre_shift, inward_bias, rotary_freqs, outward_bias, mlp_gain, mlp_shift, up_bias, down_bias]
    lengths = [s.shape[0] for s in smalls]
    small = small_block(smalls, 3 * GW // 2)
    slot = jnp.arange(total, dtype=jnp.int32)
    count = kept_counts
    key_bias = jnp.where((slot < count[0]) & (keep_mask[0] == 1), 0.0, NEG).astype(F32)
    lines = [patch_cols[0].astype(F32), patch_rows[0].astype(F32), key_bias]
    pos = jnp.stack(lines + [jnp.zeros_like(key_bias)] * 5)
    core = (lax.axis_index("fsdp") % 2).astype(jnp.int32)[None]
    rep = lax.axis_index("rep").astype(jnp.int32)[None]

    if tuned:
        shards = pack(rep, inward_weight, outward_weight, up_weight, down_weight, small)
        first, second, outup, downs = [Gather(shard) for shard in shards]
        table = piece_table()
        order = first_of_owner(table, n)
        step([first, second])
        step([first])
        step([first, second])
        step([first])
        step([first, second, outup])
        load = skip = rows
        small_pieces = first.out
    else:
        gather = lambda a: lax.all_gather(a, "fsdp", axis=0, tiled=True)
        table = jnp.zeros((2,), jnp.int32)
        order = jnp.arange(n, dtype=jnp.int32)
        load, skip = width, SMALL_ROWS
        small_pieces = [jnp.pad(gather(small[None]), ((0, 0), (skip, 0), (0, 0)))]
        weights = [group_columns(inward_weight, 0, 1, width), group_columns(inward_weight, 1, groups - 1, width),
                   jnp.concatenate([outward_weight, up_weight], axis=1), down_weight]
        first, second, outup, downs = [Done([gather(w)[None]]) for w in weights]

    def run(movers, kernel, *inputs):
        return step(movers, kernel, *inputs) if tuned else kernel(*inputs)

    part = functools.partial
    n1, cosine, sine, vec, aux = run([second], part(prologue, lengths, n, skip), order, tokens, pos, small_pieces)

    def attention(table, n1, vec, cosine, sine, pieces, pos):
        q, k, v = qkv(0, 1, load, table, n1, vec, cosine, sine, pieces)
        return (q, k, v) + tuple(attend(0, q, k, v, pos, jnp.zeros((total, width), BF16)))

    q0, k0, v0, att, lse0, wide0 = run([second, outup], attention, table, n1, vec, cosine, sine, first.out, pos)
    q1, k1, v1 = run([outup, downs], part(qkv, 1, groups - 1, load), table, n1, vec, cosine, sine, second.out)
    att, lse1, wide1 = run([outup, downs], part(attend, 1), q1, k1, v1, pos, att)
    if tuned:
        step([outup])
    middle, n2, act, slope, gd = run([downs], part(up, load, wide), table, count, att, tokens, cotangent, vec, outup.out)

    layout = (n // 4, 2, 2)

    def gradient(name, pairs):
        if tuned:
            return weight_grad(core, pairs, layout, name)
        return lax.psum(lax.psum_scatter(plain_grad(pairs, name), "fsdp", scatter_dimension=0, tiled=True), "rep")

    def reduction(movers, name, pairs):
        out = run(movers, part(gradient, name), pairs)
        return Reduce(*out) if tuned else Done(out)

    r_down = reduction([downs], "down_grad", [(act, gd)])
    if tuned:
        step([downs])
    outputs, gmid, gb, ga, gu, sums, ubsum = run(
        [r_down], part(down, load), table, count, act, slope, middle, cotangent, gd, vec, outup.out, downs.out
    )
    r_up = reduction([r_down], "up_grad", [(att, gb), (n2, gu)])
    if tuned:
        step([r_down, r_up])
    backs = []
    heads = ((0, 0, q0, k0, v0, lse0, wide0), (1, 0, q1, k1, v1, lse1, wide1), (2, 1, q1, k1, v1, lse1, wide1))

    def back(movers, which):
        g0, l0, q, k, v, lse, att_wide = heads[which]
        backs.append(run(movers, part(attend_back, g0, l0), q, k, v, ga, lse, att_wide, aux, cosine, sine))

    def in_gradient(movers, name, which):
        return reduction(movers, name, [(n1, backs[g][0]) for g in which])

    back([r_down, r_up], 0)
    back([r_down, r_up], 1)
    r_in0 = in_gradient([r_down], "in_grad0", (0, 1))
    if tuned:
        step([r_in0])
    back([r_up, r_in0], 2)
    r_in1 = in_gradient([r_up, r_in0], "in_grad1", (2,))
    if tuned:
        step([r_in1])
    grad_tokens, first_sums = run(
        [r_up, r_in0, r_in1], part(final, load, [3 * GW, 3 * GW * (groups - 1)]),
        table, tokens, gmid, vec, [b[0] for b in backs], [first.out, second.out]
    )
    fsum = jnp.stack([b[1][:2] for b in backs])
    bsum = jnp.stack([b[2][0].reshape(3, GW) for b in backs], axis=1)
    d_freqs = fsum.transpose(0, 2, 1).reshape(-1)
    small_grads = [
        bsum[:2],
        first_sums[0],
        first_sums[1],
        bsum[2],
        d_freqs,
        sums[2],
        sums[0],
        sums[1],
        ubsum[0],
        sums[3],
    ]
    rows = small_rows(small_grads, n)
    if tuned:
        r_small = SmallReduce(rows)
        step([r_small, r_in0, r_in1])
        step([r_small, r_in0, r_in1])
        step([r_small, r_in1])
        step([r_small, r_in1])
        step([r_small])
        mine = r_small.out
    else:
        mine = lax.psum(lax.psum_scatter(rows, "fsdp", scatter_dimension=0, tiled=True), "rep")[0]
    pieces = []
    for r, ng in ((r_in0, 2), (r_in1, 1)):
        block = r.out.reshape(-1, ng, 3, GW)
        pieces += [block[:, g] for g in range(ng)]
    d_inward = jnp.stack(pieces, axis=2).reshape(-1, 3 * width)
    d_out, d_up = r_up.out[:, :width], r_up.out[:, width:]
    each = width // n
    cuts = []
    offset = 0
    for length in (2 * each, each, each, each, each, each, each, each, wide // n, each):
        cuts.append(lax.slice_in_dim(mine, offset, offset + length))
        offset += length
    o_bias, o_gain, o_shift, o_vbias, o_freqs, o_obias, o_mgain, o_mshift, o_ubias, o_dbias = cuts
    return (outputs, grad_tokens, o_gain, o_shift, d_inward, o_bias, o_vbias, o_freqs, d_out, o_obias,
            o_mgain, o_mshift, d_up, o_ubias, r_down.out, o_dbias)


def solution(mesh):
    n = mesh.shape["fsdp"]
    tuned = mesh.shape["rep"] == 2 and n == 16
    row = P(("rep", "fsdp"), None)
    vec, mat = P("fsdp"), P("fsdp", None)
    return jax.shard_map(
        functools.partial(local, tuned, n),
        mesh=mesh,
        in_specs=(row, vec, vec, mat, vec, vec, mat, vec, vec, vec, mat, vec, mat, vec, row,
                  P(("rep", "fsdp")), row, row, row),
        out_specs=(row, row, vec, vec, mat, vec, vec, vec, mat, vec, vec, vec, mat, vec, mat, vec),
        check_vma=False,
    )
```

```python
import functools
import math

import jax
import jax.numpy as jnp
from jax import lax
from jax.experimental import pallas as pl
from jax.experimental.pallas import tpu as pltpu
from jax.sharding import PartitionSpec as P

HD = 64
LOG2E = 1.4426950408889634
EPS = 1e-06
NEG = -1e30
F32 = jnp.float32
BF16 = jnp.bfloat16
GH = 4
GW = GH * HD
HALF = GW // 2


def dims(lhs, rhs, lhs_axis, rhs_axis):
    return lax.dot_general(
        lhs, rhs, (((lhs_axis,), (rhs_axis,)), ((), ())), preferred_element_type=F32
    )


def nn(lhs, rhs):
    return dims(lhs, rhs, 1, 0)


def nt(lhs, rhs):
    return dims(lhs, rhs, 1, 1)


def tn(lhs, rhs):
    return dims(lhs, rhs, 0, 0)


def params(grid, mib):
    return pltpu.CompilerParams(
        dimension_semantics=("arbitrary",) * len(grid), vmem_limit_bytes=mib * 2**20
    )


def whole(shape):
    return pl.BlockSpec(shape, lambda *idx: (0,) * len(shape))


ANY = pl.BlockSpec(memory_space=pl.ANY)
SMEM = pl.BlockSpec(memory_space=pltpu.SMEM)


def kept(shape, dtype):
    return pltpu.HBM(shape, dtype)


def far(*arrays):
    return [pltpu.with_memory_space_constraint(a, pltpu.HBM) for a in arrays]


def cost(flops, bytes_moved, transcendental=0):
    return pl.CostEstimate(
        flops=int(flops), bytes_accessed=int(bytes_moved), transcendentals=int(transcendental)
    )


def group_perm(transposed):
    row = lax.broadcasted_iota(jnp.int32, (GW, GW), 0)
    col = lax.broadcasted_iota(jnp.int32, (GW, GW), 1)
    packed, natural = (row, col) if transposed else (col, row)
    half = packed // HALF
    head = (packed % HALF) // (HD // 2)
    source = head * HD + half * (HD // 2) + packed % (HD // 2)
    return jnp.where(source == natural, 1.0, 0.0).astype(BF16)


def packed_head_mask(head):
    lane = lax.broadcasted_iota(jnp.int32, (1, GW), 1)
    return (lane % HALF) // (HD // 2) == head


def natural_head_mask(head):
    lane = lax.broadcasted_iota(jnp.int32, (1, GW), 1)
    return lane // HD == head


def normalize(values):
    center = values - jnp.mean(values, axis=-1, keepdims=True)
    spread = jnp.mean(center * center, axis=-1, keepdims=True)
    inverse = lax.rsqrt(spread + EPS)
    return center * inverse, inverse


def load_pieces(table, sources, target, sem, rows):
    copies = []
    slots = table.shape[0] // 2
    for source in sources:
        width = source.shape[2]
        for slot in range(source.shape[0]):
            number = len(copies)
            row = pl.multiple_of(table[number] * rows, rows)
            col = pl.multiple_of(table[slots + number] * width, width)
            copies.append(
                pltpu.make_async_copy(
                    source.at[slot, pl.ds(0, rows)], target.at[pl.ds(row, rows), pl.ds(col, width)], sem.at[number]
                )
            )
    return copies


def piece_count(sources):
    return sum(s.shape[0] for s in sources)


SMALL_ROWS = 16


def pack_kernel(rep, in_ref, out_ref, up_ref, down_ref, small_ref, one_ref, two_ref, three_ref, four_ref):
    def write(y):
        rows, third = in_ref.shape[0], in_ref.shape[1] // 3
        groups = third // GW
        cuts = [in_ref[:, pl.ds(part * third + g * GW, GW)] for g in range(groups) for part in range(3)]
        first = jnp.concatenate(cuts[:3], axis=1)
        half = first.shape[1] // 2
        one_ref[0, pl.ds(0, rows), :] = first[:, y * half : (y + 1) * half]
        one_ref[0, pl.ds(rows, SMALL_ROWS), :] = small_ref[...]
        rest = jnp.concatenate(cuts[3:], axis=1)
        half = rest.shape[1] // 2
        two_ref[0] = rest[:, y * half : (y + 1) * half]
        both = jnp.concatenate([out_ref[...], up_ref[...]], axis=1)
        half = both.shape[1] // 2
        three_ref[0] = both[:, y * half : (y + 1) * half]
        half = down_ref.shape[1] // 2
        four_ref[0] = down_ref[:, pl.ds(y * half, half)]

    @pl.when(rep[0] == 0)
    def _():
        write(0)

    @pl.when(rep[0] == 1)
    def _():
        write(1)


def pack(rep, inward, outward, upward, downward, small):
    rows, wide = inward.shape
    width = wide // 3
    shapes = [
        (1, rows + SMALL_ROWS, 3 * GW // 2),
        (1, rows, (wide - 3 * GW) // 2),
        (1, rows, (width + upward.shape[1]) // 2),
        (1, downward.shape[0], width // 2),
    ]
    return pl.pallas_call(
        pack_kernel,
        in_specs=[SMEM] + [pl.BlockSpec(memory_space=pltpu.VMEM)] * 5,
        out_specs=[pl.BlockSpec(memory_space=pltpu.VMEM)] * 4,
        out_shape=[jax.ShapeDtypeStruct(shape, BF16) for shape in shapes],
        cost_estimate=cost(0, 2 * rows * width * 24),
        name="pack",
    )(rep, inward, outward, upward, downward, small)


V_GAIN, V_SHIFT, V_BIAS, V_FREQ, V_OBIAS, V_MGAIN, V_MSHIFT, V_UBIAS, V_DBIAS = range(9)


def prologue_kernel(lengths, owners, rows, npieces, order, x_ref, pos_ref, *rest):
    pieces = rest[:npieces]
    n1_ref, cos_ref, sin_ref, vec_ref, aux_ref, got, fc, fr, sem = rest[npieces:]
    width = x_ref.shape[1]

    @pl.when(pl.program_id(0) == 0)
    def _():
        copies = []
        for number, piece in enumerate(pieces):
            slots = piece.shape[0]
            copies.append(
                pltpu.make_async_copy(
                    piece.at[:, pl.ds(rows, SMALL_ROWS)], got.at[pl.ds(number * slots, slots)], sem.at[number]
                )
            )
        for copy in copies:
            copy.start()
        for copy in copies:
            copy.wait()
        vec_ref[...] = jnp.zeros_like(vec_ref)
        for owner in range(owners):
            tile = got[order[owner]].astype(F32)
            for row, length in enumerate(lengths):
                vec_ref[row : row + 1, owner * length : (owner + 1) * length] = tile[row : row + 1, :length]
        freq = jnp.broadcast_to(vec_ref[V_FREQ : V_FREQ + 1, :width], (16, width)).astype(BF16)
        source = lax.broadcasted_iota(jnp.int32, (width, width // 2), 0)
        target = lax.broadcasted_iota(jnp.int32, (width, width // 2), 1)
        fc[...] = nn(freq, jnp.where(source == 2 * target, 1.0, 0.0).astype(BF16))[:8]
        fr[...] = nn(freq, jnp.where(source == 2 * target + 1, 1.0, 0.0).astype(BF16))[:8]

    xhat, _ = normalize(x_ref[...])
    n1_ref[...] = (xhat * vec_ref[V_GAIN : V_GAIN + 1, :width] + vec_ref[V_SHIFT : V_SHIFT + 1, :width]).astype(BF16)
    pos = pos_ref[...]
    aux = jnp.transpose(jnp.concatenate([pos, jnp.zeros((120, pos.shape[1]), F32)], axis=0))
    aux_ref[...] = aux
    angle = aux[:, 0:1] * fc[0:1, :] + aux[:, 1:2] * fr[0:1, :]
    cosine, sine = cos_sin(angle)
    cos_ref[...] = cosine
    sin_ref[...] = sine


def prologue(lengths, owners, rows, order, x, pos, pieces, rb=256):
    total, width = x.shape
    pairs = width // 2
    grid = (total // rb,)
    blk = lambda w: pl.BlockSpec((rb, w), lambda i: (i, 0))
    wide = max(lengths) * owners
    return pl.pallas_call(
        functools.partial(prologue_kernel, lengths, owners, rows, len(pieces)),
        grid=grid,
        in_specs=[SMEM, blk(width), pl.BlockSpec((8, rb), lambda i: (0, i))] + [ANY] * len(pieces),
        out_specs=[blk(width), blk(pairs), blk(pairs), whole((16, wide)), blk(128)],
        out_shape=[
            kept((total, width), BF16),
            kept((total, pairs), F32),
            kept((total, pairs), F32),
            kept((16, wide), F32),
            kept((total, 128), F32),
        ],
        scratch_shapes=[
            pltpu.VMEM((piece_count(pieces), SMALL_ROWS, pieces[0].shape[2]), BF16),
            pltpu.VMEM((8, pairs), F32),
            pltpu.VMEM((8, pairs), F32),
            pltpu.SemaphoreType.DMA((len(pieces),)),
        ],
        compiler_params=params(grid, 24),
        cost_estimate=cost(total * width * 40, total * width * 10),
        name="prologue",
    )(order, *far(x), pos, *far(*pieces))


QUARTER = (1.5703125, 4.837512969970703125e-4, 7.549789948768648e-8)


def cos_sin(angle):
    turns = jnp.floor(angle * 0.6366197723675814 + 0.5)
    r = ((angle - turns * QUARTER[0]) - turns * QUARTER[1]) - turns * QUARTER[2]
    r2 = r * r
    s = r + r * r2 * (-1.6666654611e-1 + r2 * (8.3321608736e-3 - 1.9515295891e-4 * r2))
    c = 1.0 - 0.5 * r2 + r2 * r2 * (4.166664568298827e-2 + r2 * (-1.388731625493765e-3 + 2.443315711809948e-5 * r2))
    quad = turns.astype(jnp.int32)
    odd = (quad & 1) == 1
    cosine = jnp.where(odd, s, c)
    sine = jnp.where(odd, c, s)
    cosine = jnp.where(((quad + 1) & 2) == 2, -cosine, cosine)
    sine = jnp.where((quad & 2) == 2, -sine, sine)
    return cosine, sine


def qkv_kernel(g0, npieces, rows, table, n1_ref, vec_ref, cos_ref, sin_ref, *rest):
    pieces = rest[:npieces]
    q_ref, k_ref, v_ref, w, wp, bp, sem = rest[npieces:]
    width = n1_ref.shape[1]
    groups = w.shape[1] // (3 * GW)
    bias_ref = vec_ref.at[V_BIAS : V_BIAS + 1, :]

    @pl.when(pl.program_id(0) == 0)
    def _():
        copies = load_pieces(table, pieces, w, sem, rows)
        for copy in copies:
            copy.start()
        perm = group_perm(False)
        for copy in copies:
            copy.wait()
        for g in range(groups):
            for part in range(2):
                packed = pl.ds((g * 2 + part) * GW, GW)
                wp[:, packed] = nn(w[:, pl.ds((g * 3 + part) * GW, GW)], perm).astype(BF16)
                natural = pl.ds(part * width + (g0 + g) * GW, GW)
                spread = jnp.broadcast_to(bias_ref[:, natural].astype(BF16), (16, GW))
                bp[:, packed] = nn(spread, perm)[:8]

    n1 = n1_ref[...]
    for g in range(groups):
        cosine = cos_ref[:, pl.ds((g0 + g) * HALF, HALF)]
        sine = sin_ref[:, pl.ds((g0 + g) * HALF, HALF)]
        for part, out, scale in ((0, q_ref, HD**-0.5 * LOG2E), (1, k_ref, 1.0)):
            packed = pl.ds((g * 2 + part) * GW, GW)
            mixed = nn(n1, wp[:, packed]) + bp[0:1, packed]
            a, b = mixed[:, :HALF], mixed[:, HALF:]
            first = a * cosine - b * sine
            second = a * sine + b * cosine
            if scale != 1.0:
                first = first * scale
                second = second * scale
            out[:, pl.ds(g * GW, HALF)] = first.astype(BF16)
            out[:, pl.ds(g * GW + HALF, HALF)] = second.astype(BF16)
        bias = bias_ref[:, pl.ds(2 * width + (g0 + g) * GW, GW)]
        v_ref[:, pl.ds(g * GW, GW)] = (nn(n1, w[:, pl.ds((g * 3 + 2) * GW, GW)]) + bias).astype(BF16)


def qkv(g0, groups, rows, table, n1, vec, cosine, sine, pieces, rb=256):
    total, width = n1.shape
    pairs = width // 2
    grid = (total // rb,)
    blk = lambda w: pl.BlockSpec((rb, w), lambda i: (i, 0))
    out = kept((total, groups * GW), BF16)
    copies = piece_count(pieces)
    return pl.pallas_call(
        functools.partial(qkv_kernel, g0, len(pieces), rows),
        grid=grid,
        in_specs=[SMEM, blk(width), whole(vec.shape), blk(pairs), blk(pairs)] + [ANY] * len(pieces),
        out_specs=[blk(groups * GW)] * 3,
        out_shape=[out] * 3,
        scratch_shapes=[
            pltpu.VMEM((width, 3 * groups * GW), BF16),
            pltpu.VMEM((width, 2 * groups * GW), BF16),
            pltpu.VMEM((8, 2 * groups * GW), F32),
            pltpu.SemaphoreType.DMA((copies,)),
        ],
        compiler_params=params(grid, 24),
        cost_estimate=cost(total * width * groups * GW * 6, total * width * 8 + width * groups * GW * 6),
        name="qkv",
    )(table, *far(n1, vec, cosine, sine, *pieces))


def attend_kernel(q_ref, k_ref, v_ref, pos_ref, *rest):
    att_ref, lse_ref, wide_ref, mask = rest[-4:]
    g, r = pl.program_id(0), pl.program_id(1)
    rb, keys = q_ref.shape[0], k_ref.shape[0]
    here = pl.ds(pl.multiple_of(r * rb, rb), rb)

    @pl.when(g == 0)
    def _():
        row = lax.broadcasted_iota(jnp.int32, (rb, keys), 0) + r * rb
        col = lax.broadcasted_iota(jnp.int32, (rb, keys), 1)
        mask[here, :] = jnp.where(row == col, 0.0, jnp.broadcast_to(pos_ref[2:3, :], (rb, keys)))

    q = q_ref[...]
    k = k_ref[...]
    v = v_ref[...]
    total = jnp.zeros((rb, GW), F32)
    lane = lax.broadcasted_iota(jnp.int32, (rb, 128), 1)
    logs = jnp.zeros((rb, 128), F32)
    for h in range(GH):
        qm = jnp.where(packed_head_mask(h), q, jnp.zeros_like(q))
        scores = nt(qm, k) + mask[here, :]
        top = jnp.max(scores, axis=-1, keepdims=True)
        weight = jnp.exp2(scores - top)
        norm = jnp.sum(weight, axis=-1, keepdims=True)
        vm = jnp.where(natural_head_mask(h), v, jnp.zeros_like(v))
        total = total + nn(weight.astype(BF16), vm) * (1.0 / norm)
        logs = jnp.where(lane == h, top + jnp.log2(norm), logs)
    att_ref[...] = total.astype(BF16)
    wide_ref[...] = total
    lse_ref[...] = jnp.transpose(logs)[:8, :]


def attend(g0, full, q, k, v, pos, *att, rb=512):
    total, width = q.shape
    groups = width // GW
    grid = (groups, total // rb)
    return pl.pallas_call(
        attend_kernel,
        grid=grid,
        in_specs=[
            pl.BlockSpec((rb, GW), lambda g, r: (r, g)),
            pl.BlockSpec((total, GW), lambda g, r: (0, g)),
            pl.BlockSpec((total, GW), lambda g, r: (0, g)),
            whole((8, total)),
        ]
        + [ANY] * len(att),
        out_specs=[
            pl.BlockSpec((rb, GW), lambda g, r: (r, g + g0)),
            pl.BlockSpec((None, 8, rb), lambda g, r: (g, 0, r)),
            pl.BlockSpec((rb, GW), lambda g, r: (r, g)),
        ],
        out_shape=[
            kept((total, full), BF16),
            kept((groups, 8, total), F32),
            kept((total, width), F32),
        ],
        input_output_aliases={4: 0} if att else {},
        scratch_shapes=[pltpu.VMEM((total, total), F32)],
        compiler_params=params(grid, 32),
        cost_estimate=cost(total * total * width * 16, total * width * 8, total * total * 12),
        name="attend",
    )(*far(q, k, v, pos, *att))


PHI_SCALE = 0.3989422804014327
TAIL_SCALE = 0.44 * 0.7071067811865476
TAIL = (
    0.12411047596471954,
    0.12443560910041027,
    0.10865662380098591,
    0.10790671631036299,
    -0.010091621907114547,
    0.14834527631989725,
    -0.13897496529649409,
    0.03561197654899638,
)


def gelu_parts(h):
    t = 1.0 / (1.0 + TAIL_SCALE * jnp.abs(h))
    poly = TAIL[-1]
    for coefficient in TAIL[-2::-1]:
        poly = poly * t + coefficient
    bell = jnp.exp(-0.5 * h * h)
    tail = poly * t * bell
    phi = jnp.where(h < 0, tail, 1.0 - tail)
    return h * phi, phi + h * (bell * PHI_SCALE)


def up_kernel(npieces, rows, table, count, att_ref, x_ref, cot_ref, vec_ref, *rest):
    pieces = rest[:npieces]
    mid_ref, n2_ref, act_ref, gp_ref, gd_ref, w, sem = rest[npieces:]
    rb, width = x_ref.shape
    wide = act_ref.shape[1]

    @pl.when(pl.program_id(0) == 0)
    def _():
        copies = load_pieces(table, pieces, w, sem, rows)
        for copy in copies:
            copy.start()
        for copy in copies:
            copy.wait()

    slot = lax.broadcasted_iota(jnp.int32, (rb, 1), 0) + pl.program_id(0) * rb
    valid = jnp.where(slot < count[0], 1.0, 0.0)
    gd_ref[...] = (valid * cot_ref[...]).astype(BF16)
    branch = nn(att_ref[...], w[:, pl.ds(0, width)]) + vec_ref[V_OBIAS : V_OBIAS + 1, :width]
    middle = x_ref[...] + valid * branch
    mid_ref[...] = middle
    xhat, _ = normalize(middle)
    n2 = (xhat * vec_ref[V_MGAIN : V_MGAIN + 1, :width] + vec_ref[V_MSHIFT : V_MSHIFT + 1, :width]).astype(BF16)
    n2_ref[...] = n2
    step = 512
    for c in range(wide // step):
        cut = pl.ds(c * step, step)
        hidden = nn(n2, w[:, pl.ds(width + c * step, step)]) + vec_ref[V_UBIAS : V_UBIAS + 1, cut]
        act, slope = gelu_parts(hidden)
        act_ref[:, cut] = act.astype(BF16)
        gp_ref[:, cut] = slope.astype(BF16)


def up(rows, wide, table, count, att, x, cot, vec, pieces, rb=256):
    total, width = x.shape
    grid = (total // rb,)
    blk = lambda w: pl.BlockSpec((rb, w), lambda i: (i, 0))
    copies = piece_count(pieces)
    return pl.pallas_call(
        functools.partial(up_kernel, len(pieces), rows),
        grid=grid,
        in_specs=[SMEM, SMEM, blk(width), blk(width), blk(width), whole(vec.shape)] + [ANY] * len(pieces),
        out_specs=[blk(width), blk(width), blk(wide), blk(wide), blk(width)],
        out_shape=[
            kept((total, width), F32),
            kept((total, width), BF16),
            kept((total, wide), BF16),
            kept((total, wide), BF16),
            kept((total, width), BF16),
        ],
        scratch_shapes=[
            pltpu.VMEM((width, width + wide), BF16),
            pltpu.SemaphoreType.DMA((copies,)),
        ],
        compiler_params=params(grid, 32),
        cost_estimate=cost(total * width * (width + wide) * 2, total * (width * 12 + wide * 4), total * wide * 2),
        name="up",
    )(table, count, *far(att, x, cot, vec, *pieces))


def down_kernel(nup, ndown, rows, table, count, act_ref, gp_ref, mid_ref, cot_ref, gd_ref, vec_ref, *rest):
    ups = rest[:nup]
    downs = rest[nup : nup + ndown]
    (out_ref, gm_ref, gb_ref, ga_ref, gu_ref, sums_ref, ubsum_ref, w, wd, sem, sem_d) = rest[nup + ndown :]
    i = pl.program_id(0)
    rb, width = mid_ref.shape
    wide = act_ref.shape[1]

    @pl.when(i == 0)
    def _():
        first = load_pieces(table, downs, wd, sem_d, rows * (wide // width))
        second = load_pieces(table, ups, w, sem, rows)
        for copy in first + second:
            copy.start()
        for copy in first + second:
            copy.wait()
        sums_ref[...] = jnp.zeros_like(sums_ref)
        ubsum_ref[...] = jnp.zeros_like(ubsum_ref)

    slot = lax.broadcasted_iota(jnp.int32, (rb, 1), 0) + i * rb
    valid = jnp.where(slot < count[0], 1.0, 0.0)
    middle = mid_ref[...]
    cot = cot_ref[...]
    gd = gd_ref[...]
    lowered = nn(act_ref[...], wd[...]) + vec_ref[V_DBIAS : V_DBIAS + 1, :width]
    out_ref[...] = middle + valid * lowered
    step = 1024
    gn2 = jnp.zeros((rb, width), F32)
    for c in range(wide // step):
        cut = pl.ds(c * step, step)
        g = nt(gd, wd[cut, :]) * gp_ref[:, cut].astype(F32)
        g_low = g.astype(BF16)
        gu_ref[:, cut] = g_low
        ubsum_ref[0:1, cut] += jnp.sum(g_low.astype(F32), axis=0, keepdims=True)
        gn2 = gn2 + nt(g_low, w[:, pl.ds(width + c * step, step)])
    xhat, inverse = normalize(middle)
    sums_ref[0:1, :] += jnp.sum(gn2 * xhat, axis=0, keepdims=True)
    sums_ref[1:2, :] += jnp.sum(gn2, axis=0, keepdims=True)
    e = gn2 * vec_ref[V_MGAIN : V_MGAIN + 1, :width]
    back = (e - jnp.mean(e, axis=-1, keepdims=True) - xhat * jnp.mean(e * xhat, axis=-1, keepdims=True)) * inverse
    gmid = cot + back
    gm_ref[...] = gmid
    gb = (valid * gmid).astype(BF16)
    gb_ref[...] = gb
    sums_ref[2:3, :] += jnp.sum(gb.astype(F32), axis=0, keepdims=True)
    sums_ref[3:4, :] += jnp.sum(gd.astype(F32), axis=0, keepdims=True)
    ga_ref[...] = nt(gb, w[:, pl.ds(0, width)]).astype(BF16)


def down(rows, table, count, act, gp, mid, cot, gd, vec, ups, downs, rb=256):
    total, width = mid.shape
    wide = act.shape[1]
    grid = (total // rb,)
    blk = lambda w: pl.BlockSpec((rb, w), lambda i: (i, 0))
    return pl.pallas_call(
        functools.partial(down_kernel, len(ups), len(downs), rows),
        grid=grid,
        in_specs=[SMEM, SMEM, blk(wide), blk(wide), blk(width), blk(width), blk(width), whole(vec.shape)]
        + [ANY] * (len(ups) + len(downs)),
        out_specs=[blk(width), blk(width), blk(width), blk(width), blk(wide), whole((8, width)), whole((8, wide))],
        out_shape=[
            kept((total, width), F32),
            kept((total, width), F32),
            kept((total, width), BF16),
            kept((total, width), BF16),
            kept((total, wide), BF16),
            kept((8, width), F32),
            kept((8, wide), F32),
        ],
        scratch_shapes=[
            pltpu.VMEM((width, width + wide), BF16),
            pltpu.VMEM((wide, width), BF16),
            pltpu.SemaphoreType.DMA((piece_count(ups),)),
            pltpu.SemaphoreType.DMA((piece_count(downs),)),
        ],
        compiler_params=params(grid, 44),
        cost_estimate=cost(total * width * (width + 3 * wide) * 2, total * (width * 20 + wide * 6)),
        name="down",
    )(table, count, *far(act, gp, mid, cot, gd, vec, *ups, *downs))


def grad_kernel(pairs, mids, reps, rows, core, *rest):
    keep_ref, send_ref = rest[-2:]
    part = core[0]

    def spot(parity, mid, rep):
        return jnp.where(parity == 0, mid, rep), jnp.where(parity == 0, rep, mid)

    each = keep_ref.shape[-1]
    offset = 0
    for at, bt in pairs:
        a, b_ref = rest[at][...], rest[bt]
        begin = 0
        while begin < b_ref.shape[1]:
            column = offset + begin
            step = min(b_ref.shape[1] - begin, each - column % each, 768)
            result = tn(a, b_ref[:, pl.ds(begin, step)])
            rep, cut = column // each, pl.ds(column % each, step)
            for pair in range(a.shape[1] // (2 * rows)):
                low = result[pair * 2 * rows : pair * 2 * rows + rows]
                high = result[pair * 2 * rows + rows : (pair + 1) * 2 * rows]
                zz, mid = pair // mids, pair % mids
                one, two = spot(part, mid, rep)
                keep_ref[one, two, zz, :, cut] = jnp.where(part == 0, low, high).astype(BF16)
                one, two = spot(1 - part, mid, rep)
                send_ref[one, two, zz, :, cut] = jnp.where(part == 0, high, low).astype(BF16)
            begin += step
        offset += b_ref.shape[1]


def operands(pairs):
    arrays, index = [], []
    for pair in pairs:
        spots = []
        for array in pair:
            if not any(array is other for other in arrays):
                arrays.append(array)
            spots.append([array is other for other in arrays].index(True))
        index.append(spots)
    lefts = {one for one, _ in index}
    return arrays, index, lefts


def weight_grad(core, pairs, layout, name):
    slow, mids, reps = layout
    arrays, index, lefts = operands(pairs)
    total, height = pairs[0][0].shape
    width = sum(b.shape[1] for _, b in pairs)
    rows = height // (slow * mids * 2)
    chunk = 384 if 384 % (2 * mids * rows) == 0 else 2 * mids * rows
    slows = chunk // (2 * mids * rows)
    grid = (height // chunk,)
    out = jax.ShapeDtypeStruct((mids, reps, slow, rows, width // reps), BF16)
    spec = pl.BlockSpec((mids, reps, slows, rows, width // reps), lambda i: (0, 0, i, 0, 0))
    return pl.pallas_call(
        functools.partial(grad_kernel, index, mids, reps, rows),
        grid=grid,
        in_specs=[SMEM]
        + [
            pl.BlockSpec((total, chunk), lambda i: (0, i)) if n in lefts else whole(a.shape)
            for n, a in enumerate(arrays)
        ],
        out_specs=[spec, spec],
        out_shape=[out, out],
        compiler_params=params(grid, 40),
        cost_estimate=cost(total * height * width * 2, total * (height + width) * 2 + height * width * 2),
        name=name,
    )(core, *far(*arrays))


def plain_grad_kernel(pairs, *rest):
    out_ref = rest[-1]
    offset = 0
    for at, bt in pairs:
        a, b_ref = rest[at][...], rest[bt]
        step = min(b_ref.shape[1], 768)
        for c in range(b_ref.shape[1] // step):
            out_ref[:, pl.ds(offset + c * step, step)] = tn(a, b_ref[:, pl.ds(c * step, step)])
        offset += b_ref.shape[1]


def plain_grad(pairs, name):
    arrays, index, lefts = operands(pairs)
    total, height = pairs[0][0].shape
    width = sum(b.shape[1] for _, b in pairs)
    chunk = 384
    grid = (height // chunk,)
    return pl.pallas_call(
        functools.partial(plain_grad_kernel, index),
        grid=grid,
        in_specs=[
            pl.BlockSpec((total, chunk), lambda i: (0, i)) if n in lefts else whole(a.shape)
            for n, a in enumerate(arrays)
        ],
        out_specs=pl.BlockSpec((chunk, width), lambda i: (i, 0)),
        out_shape=jax.ShapeDtypeStruct((height, width), F32),
        compiler_params=params(grid, 63),
        cost_estimate=cost(total * height * width * 2, total * (height + width) * 2 + height * width * 4),
        name=name,
    )(*arrays)


def unrotate(grad, cosine, sine):
    first, second = grad[:, :HALF], grad[:, HALF:]
    return first * cosine + second * sine, second * cosine - first * sine


def angle_grad(grad, rotated):
    return grad[:, HALF:] * rotated[:, :HALF] - grad[:, :HALF] * rotated[:, HALF:]


def back_kernel(q_ref, k_ref, v_ref, do_ref, lse_ref, wide_ref, aux_ref, cos_ref, sin_ref,
                g_ref, fsum_ref, bsum_ref, ds_s, p_s, dk_s, dv_s):
    r = pl.program_id(0)
    rb, keys = q_ref.shape[0], k_ref.shape[0]
    here = pl.ds(pl.multiple_of(r * rb, rb), rb)
    q = q_ref[...]
    k = k_ref[...]
    v = v_ref[...]
    do = do_ref[...]
    zero = jnp.zeros_like(q)
    product = do.astype(F32) * wide_ref[...]
    high = product.astype(BF16)
    low = (product - high.astype(F32)).astype(BF16)
    lane = lax.broadcasted_iota(jnp.int32, (16, GW), 1)
    pick_head = jnp.where(lane // HD == lax.broadcasted_iota(jnp.int32, (16, GW), 0), 1.0, 0.0).astype(BF16)
    inner = nt(pick_head, high) + nt(pick_head, low)
    key = lax.broadcasted_iota(jnp.int32, (keys, rb), 0)
    query = lax.broadcasted_iota(jnp.int32, (keys, rb), 1) + r * rb
    mask = jnp.where(key == query, 0.0, jnp.broadcast_to(aux_ref[:, 2:3], (keys, rb)))
    dq = jnp.zeros((rb, GW), F32)
    qms, doms = [], []
    for h in range(GH):
        qm = jnp.where(packed_head_mask(h), q, zero)
        dom = jnp.where(natural_head_mask(h), do, zero)
        qms.append(qm)
        doms.append(dom)
        soft = jnp.exp2(nt(k, qm) + mask - lse_ref[h : h + 1, :])
        ds = (soft * (nt(v, dom) - inner[h : h + 1, :])).astype(BF16)
        cut = pl.ds(h * rb, rb)
        ds_s[:, cut] = ds
        p_s[:, cut] = soft.astype(BF16)
        km = jnp.where(packed_head_mask(h), k, jnp.zeros_like(k))
        dq = dq + tn(ds, km)
    dk = nn(ds_s[...], jnp.concatenate(qms, axis=0)) * (1.0 / LOG2E)
    dv = nn(p_s[...], jnp.concatenate(doms, axis=0))

    perm = group_perm(True)
    cosine, sine = cos_ref[here, :], sin_ref[here, :]
    dq = dq * (HD**-0.5)
    ang = angle_grad(dq, q.astype(F32) * (HD**0.5 / LOG2E))
    first, second = unrotate(dq, cosine, sine)
    gq = nn(jnp.concatenate([first.astype(BF16), second.astype(BF16)], axis=1), perm)
    g_ref[here, pl.ds(0, GW)] = gq.astype(BF16)
    col, row = aux_ref[here, 0:1], aux_ref[here, 1:2]
    fcol = jnp.sum(ang * col, axis=0, keepdims=True)
    frow = jnp.sum(ang * row, axis=0, keepdims=True)
    qsum = jnp.sum(gq, axis=0, keepdims=True)

    @pl.when(r == 0)
    def _():
        dk_s[...] = dk
        dv_s[...] = dv
        fsum_ref[...] = jnp.zeros_like(fsum_ref)
        fsum_ref[0:1, pl.ds(0, HALF)] = fcol
        fsum_ref[1:2, pl.ds(0, HALF)] = frow
        bsum_ref[0:1, pl.ds(0, GW)] = qsum

    @pl.when(r > 0)
    def _():
        dk_s[...] += dk
        dv_s[...] += dv
        fsum_ref[0:1, pl.ds(0, HALF)] += fcol
        fsum_ref[1:2, pl.ds(0, HALF)] += frow
        bsum_ref[0:1, pl.ds(0, GW)] += qsum

    @pl.when(r == pl.num_programs(0) - 1)
    def _():
        dkf = dk_s[...]
        angk = angle_grad(dkf, k.astype(F32))
        fsum_ref[0:1, pl.ds(0, HALF)] += jnp.sum(angk * aux_ref[:, 0:1], axis=0, keepdims=True)
        fsum_ref[1:2, pl.ds(0, HALF)] += jnp.sum(angk * aux_ref[:, 1:2], axis=0, keepdims=True)
        one, two = unrotate(dkf, cos_ref[...], sin_ref[...])
        gk = nn(jnp.concatenate([one.astype(BF16), two.astype(BF16)], axis=1), perm)
        g_ref[:, pl.ds(GW, GW)] = gk.astype(BF16)
        bsum_ref[0:1, pl.ds(GW, GW)] = jnp.sum(gk, axis=0, keepdims=True)
        gv = dv_s[...].astype(BF16)
        g_ref[:, pl.ds(2 * GW, GW)] = gv
        lane = lax.broadcasted_iota(jnp.int32, (HALF, 2 * HALF), 1)
        pair = lax.broadcasted_iota(jnp.int32, (HALF, 2 * HALF), 0)
        sums = fsum_ref[:, pl.ds(0, HALF)]
        spread = [
            jnp.dot(sums, jnp.where(lane == 2 * pair + odd, 1.0, 0.0), precision=lax.Precision.HIGHEST)
            for odd in range(2)
        ]
        fsum_ref[0:1, :] = spread[0][0:1] + spread[1][1:2]
        bsum_ref[0:1, pl.ds(2 * GW, GW)] = jnp.sum(gv.astype(F32), axis=0, keepdims=True)


def attend_back(g0, l0, q, k, v, do, lse, wide, aux, cosine, sine, rb=512):
    total = q.shape[0]
    grid = (total // rb,)
    return pl.pallas_call(
        back_kernel,
        grid=grid,
        in_specs=[
            pl.BlockSpec((rb, GW), lambda r: (r, l0)),
            pl.BlockSpec((total, GW), lambda r: (0, l0)),
            pl.BlockSpec((total, GW), lambda r: (0, l0)),
            pl.BlockSpec((rb, GW), lambda r: (r, g0)),
            pl.BlockSpec((None, 8, rb), lambda r: (l0, 0, r)),
            pl.BlockSpec((rb, GW), lambda r: (r, l0)),
            whole((total, 128)),
            pl.BlockSpec((total, HALF), lambda r: (0, g0)),
            pl.BlockSpec((total, HALF), lambda r: (0, g0)),
        ],
        out_specs=[whole((total, 3 * GW)), whole((8, GW)), whole((8, 3 * GW))],
        out_shape=[
            kept((total, 3 * GW), BF16),
            jax.ShapeDtypeStruct((8, GW), F32),
            jax.ShapeDtypeStruct((8, 3 * GW), F32),
        ],
        scratch_shapes=[
            pltpu.VMEM((total, GH * rb), BF16),
            pltpu.VMEM((total, GH * rb), BF16),
            pltpu.VMEM((total, GW), F32),
            pltpu.VMEM((total, GW), F32),
        ],
        compiler_params=params(grid, 48),
        cost_estimate=cost(total * total * GW * 40, total * GW * 20, total * total * GH),
        name="attend_back",
    )(*far(q, k, v, do, lse, wide, aux, cosine, sine))


def final_kernel(count, counts, rows, table_one, table_two, x_ref, gm_ref, vec_ref, *rest):
    grads, place = rest[:count], count
    pieces = []
    for number in counts:
        pieces.append(rest[place : place + number])
        place += number
    out_ref, sums_ref = rest[place : place + 2]
    weights = rest[place + 2 : place + 2 + len(counts)]
    sems = rest[place + 2 + len(counts) :]

    @pl.when(pl.program_id(0) == 0)
    def _():
        copies = []
        for table, p, w, sem in zip((table_one, table_two), pieces, weights, sems):
            copies += load_pieces(table, p, w, sem, rows)
        for copy in copies:
            copy.start()
        for copy in copies:
            copy.wait()
        sums_ref[...] = jnp.zeros_like(sums_ref)

    e = jnp.zeros(x_ref.shape, F32)
    group = 0
    for w in weights:
        for g in range(w.shape[1] // (3 * GW)):
            e = e + nt(grads[group][...], w[:, pl.ds(g * 3 * GW, 3 * GW)])
            group += 1
    xhat, inverse = normalize(x_ref[...])
    sums_ref[0:1, :] += jnp.sum(e * xhat, axis=0, keepdims=True)
    sums_ref[1:2, :] += jnp.sum(e, axis=0, keepdims=True)
    eg = e * vec_ref[V_GAIN : V_GAIN + 1, : x_ref.shape[1]]
    back = (eg - jnp.mean(eg, axis=-1, keepdims=True) - xhat * jnp.mean(eg * xhat, axis=-1, keepdims=True)) * inverse
    out_ref[...] = gm_ref[...] + back


def final(rows, widths, tables, x, gmid, vec, grads, piece_sets, rb=256):
    total, width = x.shape
    grid = (total // rb,)
    blk = lambda w: pl.BlockSpec((rb, w), lambda i: (i, 0))
    pieces = [p for ps in piece_sets for p in ps]
    return pl.pallas_call(
        functools.partial(final_kernel, len(grads), [len(ps) for ps in piece_sets], rows),
        grid=grid,
        in_specs=[SMEM, SMEM, blk(width), blk(width), whole(vec.shape)]
        + [blk(g.shape[1]) for g in grads]
        + [ANY] * len(pieces),
        out_specs=[blk(width), whole((8, width))],
        out_shape=[kept((total, width), F32), jax.ShapeDtypeStruct((8, width), F32)],
        scratch_shapes=[pltpu.VMEM((width, w), BF16) for w in widths]
        + [pltpu.SemaphoreType.DMA((piece_count(ps),)) for ps in piece_sets],
        compiler_params=params(grid, 32),
        cost_estimate=cost(total * width * width * 6, total * width * 20 + width * width * 6),
        name="final",
    )(*tables, *far(x, gmid, vec), *far(*grads), *far(*pieces))


FOLD = (
    ("bias", 0, 0), ("value", 1, 0), ("freqs", 1, 64), ("gain", 2, 0), ("shift", 2, 64),
    ("obias", 3, 0), ("dbias", 3, 64), ("mgain", 4, 0), ("mshift", 4, 64), ("ubias", 5, 0),
)


def fold_kernel(groups, owners, spot, *refs):
    out_ref = refs[-1]
    fsums, bsums = refs[:groups], refs[groups : 2 * groups]
    mid_ref, wide_ref, first_ref = refs[2 * groups : 2 * groups + 3]
    lines = {
        "bias": [(b, 0, part * GW, GW) for part in range(2) for b in bsums],
        "value": [(b, 0, 2 * GW, GW) for b in bsums],
        "freqs": [(f, 0, 0, GW) for f in fsums],
        "gain": [(first_ref, 0, 0, first_ref.shape[1])],
        "shift": [(first_ref, 1, 0, first_ref.shape[1])],
        "mgain": [(mid_ref, 0, 0, mid_ref.shape[1])],
        "mshift": [(mid_ref, 1, 0, mid_ref.shape[1])],
        "obias": [(mid_ref, 2, 0, mid_ref.shape[1])],
        "dbias": [(mid_ref, 3, 0, mid_ref.shape[1])],
        "ubias": [(wide_ref, 0, 0, wide_ref.shape[1])],
    }
    out_ref[...] = jnp.zeros_like(out_ref)
    for name, row, lane in FOLD:
        total = sum(length for _, _, _, length in lines[name])
        each = total // owners
        for owner in range(owners):
            begin, end = owner * each, (owner + 1) * each
            offset = 0
            for ref, line, start, length in lines[name]:
                low, high = max(begin, offset), min(end, offset + length)
                while low < high:
                    place = row * 128 + lane + low - begin
                    at = start + low - offset
                    lead, last = spot(owner)
                    out_ref[(*lead, slice(last, last + 1), slice(place, place + high - low))] = (
                        ref[line : line + 1, at : at + high - low]
                    )
                    low = high
                offset += length


def fold(owners, cube, fsums, bsums, mid, wide, first):
    arrays = [*fsums, *bsums, mid, wide, first]
    shape, spot = (owners, 1024), lambda owner: ((), owner)
    if cube:
        shape, spot = (2, 2, 4, 1024), lambda owner: ((owner % 2, owner // 2 % 2), owner // 4)
    return pl.pallas_call(
        functools.partial(fold_kernel, len(fsums), owners, spot),
        in_specs=[pl.BlockSpec(memory_space=pltpu.VMEM)] * len(arrays),
        out_specs=pl.BlockSpec(memory_space=pltpu.VMEM),
        out_shape=jax.ShapeDtypeStruct(shape, F32),
        cost_estimate=cost(0, 100000),
        name="fold",
    )(*arrays)


def finish_kernel(groups, rep, *refs):
    halves, (in_ref, out_ref, up_ref, down_ref) = refs[:-4], refs[-4:]
    swap = rep[0] == 1

    def column(pair, place, width):
        mine, other = pair
        each = mine.shape[1]
        cut = pl.ds(place % each, width)
        first = (place // each) == 0
        a, b = (mine, other) if first else (other, mine)
        return jnp.where(swap, b[:, cut], a[:, cut])

    pairs = [halves[2 * n : 2 * n + 2] for n in range(len(halves) // 2)]
    total = in_ref.shape[1] // 3
    step = GW // 2
    group = 0
    for pair, count in zip(pairs, groups):
        for g in range(count):
            for part in range(3):
                for half in range(2):
                    place = (g * 3 + part) * GW + half * step
                    target = part * total + group * GW + half * step
                    in_ref[:, pl.ds(target, step)] = column(pair, place, step)
            group += 1
    outup, downs = pairs[len(groups)], pairs[len(groups) + 1]
    width = out_ref.shape[1]
    for place in range(0, outup[0].shape[1] * 2, step):
        value = column(outup, place, step)
        if place < width:
            out_ref[:, pl.ds(place, step)] = value
        else:
            up_ref[:, pl.ds(place - width, step)] = value
    for place in range(0, down_ref.shape[1], step):
        down_ref[:, pl.ds(place, step)] = column(downs, place, step)


def finish(groups, rep, pairs):
    rows, width = pairs[-2][0].shape[0], pairs[-1][0].shape[1] * 2
    wide = pairs[-2][0].shape[1] * 2 - width
    arrays = [a for pair in pairs for a in pair]
    shapes = [(rows, 3 * width), (rows, width), (rows, wide), (pairs[-1][0].shape[0], width)]
    return pl.pallas_call(
        functools.partial(finish_kernel, groups),
        in_specs=[SMEM] + [pl.BlockSpec(memory_space=pltpu.VMEM)] * len(arrays),
        out_specs=[pl.BlockSpec(memory_space=pltpu.VMEM)] * 4,
        out_shape=[jax.ShapeDtypeStruct(shape, F32) for shape in shapes],
        cost_estimate=cost(0, 4000000),
        name="finish",
    )(rep, *arrays)


def place():
    me = lax.axis_index("fsdp")
    return lax.axis_index("rep"), me // 4, (me // 2) % 2, me % 2


def move(value, step):
    moves = []
    for i in range(32):
        y, z, x, c = step(i // 16, (i // 4) % 4, (i // 2) % 2, i % 2)
        moves.append((i, y * 16 + z * 4 + x * 2 + c))
    return lax.ppermute(value, ("rep", "fsdp"), moves)


def across_core(value):
    return move(value, lambda y, z, x, c: (y, z, x, 1 - c))


def across_x(value):
    return move(value, lambda y, z, x, c: (y, z, 1 - x, c))


def across_rep(value):
    return move(value, lambda y, z, x, c: (1 - y, z, x, c))


def across_near(value):
    return move(value, lambda y, z, x, c: (y, z ^ 1, x, c))


def across_far(value):
    return move(value, lambda y, z, x, c: (y, z ^ 2, x, c))


def across_third(value):
    return move(value, lambda y, z, x, c: (y, z ^ 3, x, c))


def across_both(value):
    return move(value, lambda y, z, x, c: (1 - y, z, 1 - x, c))


def across_one(value):
    return move(value, lambda y, z, x, c: (y, z, 1 - x, c) if c == 0 else (1 - y, z, x, c))


def across_two(value):
    return move(value, lambda y, z, x, c: (1 - y, z, x, c) if c == 0 else (y, z, 1 - x, c))


def pick(array, index):
    return lax.dynamic_index_in_dim(array, index, 0, keepdims=False)


def pick_two(array, index):
    return lax.dynamic_slice_in_dim(array, 2 * index, 2, 0)


def piece_tables():
    y, z, x, c = place()
    slot = jnp.arange(4, dtype=jnp.int32)
    here, swap = (lambda core, a, b: a), (lambda core, a, b: jnp.where(core == 0, a, b))
    tables = []
    for choose in (here, swap):
        owners, halves = [], []
        for core in (c, 1 - c):
            for mid, half in ((x, y), (choose(core, x, 1 - x), choose(core, 1 - y, y)),
                              (choose(core, 1 - x, x), choose(core, y, 1 - y)), (1 - x, 1 - y)):
                owners.append((z ^ slot) * 4 + mid * 2 + core)
                halves.append(jnp.broadcast_to(half, (4,)))
        tables.append(jnp.concatenate(owners + halves).astype(jnp.int32))
    return tables


def first_of_owner(table, n):
    slots = table.shape[0] // 2
    match = table[None, :slots] == jnp.arange(n, dtype=jnp.int32)[:, None]
    return jnp.min(jnp.where(match, jnp.arange(slots, dtype=jnp.int32)[None, :], slots), axis=1)


class Reduce:
    stages = (across_core, across_one, across_two, across_far, across_near, across_rep)

    def __init__(self, keep, send):
        self.keep, self.first, self.got, self.stage = keep, send, [], 0
        self.out = None

    def sends(self):
        return [(self.stages[self.stage], self.send())]

    def takes(self, values):
        self.take(values[0])

    def base(self, count, one, two=None, cut=None):
        step = lambda a, i: a if i is None else pick(a, i)
        total = None
        for source, used in ((self.keep, 0), (self.got[0], 0), *((g, n + 1) for n, g in enumerate(self.got[1:count]))):
            value = source
            if used < 1:
                value = step(value, one)
            if used < 2:
                value = step(value, two)
            if cut is not None:
                value = cut(value)
            value = value.astype(F32)
            total = value if total is None else total + value
        return total

    def level(self, index):
        return self.base(3, self.i1, self.i2, lambda a: pick(a, index)) + pick(self.got[3], index % 2).astype(F32)

    def send(self):
        y, z, x, c = place()
        self.i1, self.i2 = jnp.where(c == 0, x, y), jnp.where(c == 0, y, x)
        if self.stage == 0:
            return self.first
        if self.stage == 1:
            return self.base(1, 1 - self.i1).astype(BF16)
        if self.stage == 2:
            return self.base(2, self.i1, 1 - self.i2).astype(BF16)
        if self.stage == 3:
            return self.base(3, self.i1, self.i2, lambda a: pick_two(a, 1 - z // 2)).astype(BF16)
        if self.stage == 4:
            return self.level(z ^ 1).astype(BF16)
        self.total = self.level(z) + self.got[4].astype(F32)
        return self.total

    def take(self, value):
        self.stage += 1
        if self.stage == 6:
            self.out = (self.total, value)
        else:
            self.got.append(value)


class SmallReduce:
    stages = (across_core, across_x, across_far, across_near, across_rep)

    def __init__(self, cube):
        self.part, self.stage = cube, 0

    sends, takes = Reduce.sends, Reduce.takes

    def send(self):
        y, z, x, c = place()
        if self.stage == 4:
            self.kept = self.part
            return self.part
        cut = pick_two if self.stage == 2 else pick
        index = (c, x, z // 2, z % 2)[self.stage]
        self.kept = cut(self.part, index)
        return cut(self.part, 1 - index)

    def take(self, value):
        self.stage += 1
        self.part = self.kept + value
        self.out = self.part


class QuickGather:
    def __init__(self, half):
        self.part, self.stage = half, 0

    def sends(self):
        if self.stage == 0:
            return [(f, self.part) for f in (across_near, across_far, across_third)]
        if self.stage == 1:
            return [(f, self.part) for f in (across_rep, across_x, across_both, across_core)]
        return [(across_core, part) for part in self.beside]

    def takes(self, values):
        self.stage += 1
        if self.stage == 1:
            self.part = jnp.concatenate([self.part, *values])
        elif self.stage == 2:
            self.beside, self.other = values[:3], values[3]
        else:
            self.out = [self.part, *self.beside, self.other, *values]


class Gather:
    def __init__(self, half, cuts=1):
        self.part, self.stage, self.cuts, self.got = half, 0, cuts, []

    def sends(self):
        if self.stage == 1 and self.cuts > 1:
            each = self.part.shape[2] // self.cuts
            begin = len(self.got) * each
            return [(across_far, self.part[:, :, begin : begin + each])]
        if self.stage < 3:
            return [((across_near, across_far, across_two)[self.stage], self.part)]
        if self.stage == 3:
            return [(across_one, self.part), (across_one, self.two), (across_core, self.part), (across_core, self.two)]
        return [(across_core, part) for part in self.one]

    def takes(self, values):
        if self.stage == 1:
            self.got += values
            if len(self.got) < self.cuts:
                return
            values = [jnp.concatenate(self.got, axis=2)] if self.cuts > 1 else values
        self.stage += 1
        if self.stage < 3:
            self.part = jnp.concatenate([self.part, values[0]])
        elif self.stage == 3:
            self.two = values[0]
        elif self.stage == 4:
            self.one, self.other = values[:2], values[2:]
        else:
            self.out = [self.part, self.two, *self.one, *self.other, *values]


def step(movers, kernel=None, *inputs):
    sends = [m.sends() for m in movers]
    inputs, arrays = lax.optimization_barrier((inputs, [[a for _, a in s] for s in sends]))
    got = [[f(a) for (f, _), a in zip(s, each)] for s, each in zip(sends, arrays)]
    outs = kernel(*inputs) if kernel is not None else ()
    outs, got = lax.optimization_barrier((outs, got))
    for m, g in zip(movers, got):
        m.takes(g)
    return outs


def group_columns(weight, g0, ng, width):
    cuts = []
    for g in range(g0, g0 + ng):
        cuts += [weight[:, part * width + g * GW : part * width + (g + 1) * GW] for part in range(3)]
    return jnp.concatenate(cuts, axis=1)


def small_block(smalls, lanes):
    total = None
    for row, vector in enumerate(smalls):
        block = jnp.pad(vector[None, :], ((row, SMALL_ROWS - 1 - row), (0, lanes - vector.shape[0])))
        total = block if total is None else total + block
    return total


class Done:
    def __init__(self, out):
        self.out = out


def local(tuned, n, tokens, pre_gain, pre_shift, inward_weight, inward_bias, rotary_freqs, outward_weight,
          outward_bias, mlp_gain, mlp_shift, up_weight, up_bias, down_weight, down_bias, keep_mask, kept_counts,
          patch_rows, patch_cols, cotangent):
    total, width = tokens.shape
    groups = width // GW
    wide = up_weight.shape[1]
    rows = width // n
    smalls = [pre_gain, pre_shift, inward_bias, rotary_freqs, outward_bias, mlp_gain, mlp_shift, up_bias, down_bias]
    lengths = [s.shape[0] for s in smalls]
    small = small_block(smalls, 3 * GW // 2)
    slot = jnp.arange(total, dtype=jnp.int32)
    count = kept_counts
    key_bias = jnp.where((slot < count[0]) & (keep_mask[0] == 1), 0.0, NEG).astype(F32)
    lines = [patch_cols[0].astype(F32), patch_rows[0].astype(F32), key_bias]
    pos = jnp.stack(lines + [jnp.zeros_like(key_bias)] * 5)
    core = (lax.axis_index("fsdp") % 2).astype(jnp.int32)[None]
    rep = lax.axis_index("rep").astype(jnp.int32)[None]

    if tuned:
        shards = pack(rep, inward_weight, outward_weight, up_weight, down_weight, small)
        first, second, outup, downs = QuickGather(shards[0]), Gather(shards[1]), Gather(shards[2], 2), Gather(shards[3])
        quick, table = piece_tables()
        order = first_of_owner(quick, n)
        step([first])
        step([first, second])
        step([first])
        load = skip = rows
        small_pieces = first.out
    else:
        gather = lambda a: lax.all_gather(a, "fsdp", axis=0, tiled=True)
        quick = table = jnp.zeros((2,), jnp.int32)
        order = jnp.arange(n, dtype=jnp.int32)
        load, skip = width, SMALL_ROWS
        small_pieces = [jnp.pad(gather(small[None]), ((0, 0), (skip, 0), (0, 0)))]
        weights = [group_columns(inward_weight, 0, 1, width), group_columns(inward_weight, 1, groups - 1, width),
                   jnp.concatenate([outward_weight, up_weight], axis=1), down_weight]
        first, second, outup, downs = [Done([gather(w)[None]]) for w in weights]

    def run(movers, kernel, *inputs):
        return step(movers, kernel, *inputs) if tuned else kernel(*inputs)

    part = functools.partial
    n1, cosine, sine, vec, aux = run([second, outup], part(prologue, lengths, n, skip), order, tokens, pos, small_pieces)

    q0, k0, v0 = run([second, outup], part(qkv, 0, 1, load), quick, n1, vec, cosine, sine, first.out)
    att, lse0, wide0 = run([second, outup], part(attend, 0, width), q0, k0, v0, pos)
    if tuned:
        step([second])
    q1, k1, v1 = run([outup, downs], part(qkv, 1, groups - 1, load), table, n1, vec, cosine, sine, second.out)
    att, lse1, wide1 = run([outup, downs], part(attend, 1, width), q1, k1, v1, pos, att)
    if tuned:
        step([outup])
    middle, n2, act, slope, gd = run([downs], part(up, load, wide), table, count, att, tokens, cotangent, vec, outup.out)

    layout = (n // 4, 2, 2)

    def gradient(name, pairs):
        if tuned:
            return weight_grad(core, pairs, layout, name)
        return lax.psum(lax.psum_scatter(plain_grad(pairs, name), "fsdp", scatter_dimension=0, tiled=True), "rep")

    def reduction(movers, name, pairs):
        out = run(movers, part(gradient, name), pairs)
        return Reduce(*out) if tuned else Done(out)

    r_down = reduction([downs], "down_grad", [(act, gd)])
    if tuned:
        step([downs])
    outputs, gmid, gb, ga, gu, sums, ubsum = run(
        [r_down], part(down, load), table, count, act, slope, middle, cotangent, gd, vec, outup.out, downs.out
    )
    r_up = reduction([r_down], "up_grad", [(att, gb), (n2, gu)])
    backs = []
    heads = ((0, 0, q0, k0, v0, lse0, wide0), (1, 0, q1, k1, v1, lse1, wide1), (2, 1, q1, k1, v1, lse1, wide1))

    def back(movers, which):
        g0, l0, q, k, v, lse, att_wide = heads[which]
        backs.append(run(movers, part(attend_back, g0, l0), q, k, v, ga, lse, att_wide, aux, cosine, sine))

    def in_gradient(movers, name, which):
        return reduction(movers, name, [(n1, backs[g][0]) for g in which])

    back([r_down, r_up], 0)
    back([r_down, r_up], 1)
    r_in0 = in_gradient([r_down, r_up], "in_grad0", (0, 1))
    if tuned:
        step([r_in0])
    back([r_down, r_up, r_in0], 2)
    r_in1 = in_gradient([r_up, r_in0], "in_grad1", (2,))
    grad_tokens, first_sums = run(
        [r_up, r_in0, r_in1], part(final, load, [3 * GW, 3 * GW * (groups - 1)]),
        (quick, table), tokens, gmid, vec, [b[0] for b in backs], [first.out, second.out]
    )
    small_sums = fold(n, tuned, [b[1] for b in backs], [b[2] for b in backs], sums, ubsum, first_sums)
    if tuned:
        r_small = SmallReduce(small_sums)
        step([r_small, r_in0, r_in1])
        step([r_small, r_in0, r_in1])
        step([r_small, r_in1])
        step([r_small, r_in1])
        step([r_small, r_in1])
        mine = r_small.out
        d_inward, d_out, d_up, d_down = finish((2, 1), rep, [r.out for r in (r_in0, r_in1, r_up, r_down)])
    else:
        mine = lax.psum(lax.psum_scatter(small_sums, "fsdp", scatter_dimension=0, tiled=True), "rep")[0]
        blocks = [r.out[:, 3 * g * GW : 3 * (g + 1) * GW] for r, ng in ((r_in0, 2), (r_in1, 1)) for g in range(ng)]
        d_inward = jnp.concatenate([b[:, p * GW : (p + 1) * GW] for p in range(3) for b in blocks], axis=1)
        d_out, d_up, d_down = r_up.out[:, :width], r_up.out[:, width:], r_down.out
    each = width // n
    line = {name: mine[row * 128 + lane :] for name, row, lane in FOLD}
    o_bias, o_ubias = line["bias"][: 2 * each], line["ubias"][: wide // n]
    o_vbias, o_freqs, o_gain, o_shift, o_obias, o_mgain, o_mshift, o_dbias = [
        line[name][:each] for name in ("value", "freqs", "gain", "shift", "obias", "mgain", "mshift", "dbias")
    ]
    return (outputs, grad_tokens, o_gain, o_shift, d_inward, o_bias, o_vbias, o_freqs, d_out, o_obias,
            o_mgain, o_mshift, d_up, o_ubias, d_down, o_dbias)


def solution(mesh):
    n = mesh.shape["fsdp"]
    tuned = mesh.shape["rep"] == 2 and n == 16
    row = P(("rep", "fsdp"), None)
    vec, mat = P("fsdp"), P("fsdp", None)
    return jax.shard_map(
        functools.partial(local, tuned, n),
        mesh=mesh,
        in_specs=(row, vec, vec, mat, vec, vec, mat, vec, vec, vec, mat, vec, mat, vec, row,
                  P(("rep", "fsdp")), row, row, row),
        out_specs=(row, row, vec, vec, mat, vec, vec, vec, mat, vec, vec, vec, mat, vec, mat, vec),
        check_vma=False,
    )
```

```python
import functools
import math

import jax
import jax.numpy as jnp
from jax import lax
from jax.experimental import pallas as pl
from jax.experimental.pallas import tpu as pltpu
from jax.sharding import PartitionSpec as P

HD = 64
LOG2E = 1.4426950408889634
EPS = 1e-06
NEG = -1e30
F32 = jnp.float32
BF16 = jnp.bfloat16
GH = 4
GW = GH * HD
HALF = GW // 2


def dims(lhs, rhs, lhs_axis, rhs_axis):
    return lax.dot_general(
        lhs, rhs, (((lhs_axis,), (rhs_axis,)), ((), ())), preferred_element_type=F32
    )


def nn(lhs, rhs):
    return dims(lhs, rhs, 1, 0)


def nt(lhs, rhs):
    return dims(lhs, rhs, 1, 1)


def tn(lhs, rhs):
    return dims(lhs, rhs, 0, 0)


def params(grid, mib):
    return pltpu.CompilerParams(
        dimension_semantics=("arbitrary",) * len(grid), vmem_limit_bytes=mib * 2**20
    )


def whole(shape):
    return pl.BlockSpec(shape, lambda *idx: (0,) * len(shape))


ANY = pl.BlockSpec(memory_space=pl.ANY)
SMEM = pl.BlockSpec(memory_space=pltpu.SMEM)
NEAR = pl.BlockSpec(memory_space=pltpu.VMEM)


def kept(shape, dtype):
    return pltpu.HBM(shape, dtype)


def far(*arrays):
    return [pltpu.with_memory_space_constraint(a, pltpu.HBM) for a in arrays]


def cost(flops, bytes_moved, transcendental=0):
    return pl.CostEstimate(
        flops=int(flops), bytes_accessed=int(bytes_moved), transcendentals=int(transcendental)
    )


def group_perm(transposed):
    row = lax.broadcasted_iota(jnp.int32, (GW, GW), 0)
    col = lax.broadcasted_iota(jnp.int32, (GW, GW), 1)
    packed, natural = (row, col) if transposed else (col, row)
    half = packed // HALF
    head = (packed % HALF) // (HD // 2)
    source = head * HD + half * (HD // 2) + packed % (HD // 2)
    return jnp.where(source == natural, 1.0, 0.0).astype(BF16)


def packed_head_mask(head):
    lane = lax.broadcasted_iota(jnp.int32, (1, GW), 1)
    return (lane % HALF) // (HD // 2) == head


def natural_head_mask(head):
    lane = lax.broadcasted_iota(jnp.int32, (1, GW), 1)
    return lane // HD == head


def normalize(values):
    center = values - jnp.mean(values, axis=-1, keepdims=True)
    spread = jnp.mean(center * center, axis=-1, keepdims=True)
    inverse = lax.rsqrt(spread + EPS)
    return center * inverse, inverse


def load_pieces(table, sources, target, sem, rows, column=True):
    copies = []
    slots = table.shape[0] // 2
    for source in sources:
        width = source.shape[2]
        for slot in range(source.shape[0]):
            number = len(copies)
            row = pl.multiple_of(table[number] * rows, rows)
            col = pl.multiple_of(table[slots + number] * width, width) if column else 0
            copies.append(
                pltpu.make_async_copy(
                    source.at[slot, pl.ds(0, rows)], target.at[pl.ds(row, rows), pl.ds(col, width)], sem.at[number]
                )
            )
    return copies


def piece_count(sources):
    return sum(s.shape[0] for s in sources)


SMALL_ROWS = 16


def pack_kernel(rep, in_ref, out_ref, up_ref, down_ref, small_ref, one_ref, two_ref, three_ref, four_ref):
    def write(y):
        rows, third = in_ref.shape[0], in_ref.shape[1] // 3
        groups = third // GW
        cuts = [in_ref[:, pl.ds(part * third + g * GW, GW)] for g in range(groups) for part in range(3)]
        first = jnp.concatenate(cuts[:3], axis=1)
        half = first.shape[1] // 2
        one_ref[0, pl.ds(0, rows), :] = first[:, y * half : (y + 1) * half]
        one_ref[0, pl.ds(rows, SMALL_ROWS), :] = small_ref[...]
        rest = jnp.concatenate(cuts[3:], axis=1)
        half = rest.shape[1] // 2
        two_ref[0] = rest[:, y * half : (y + 1) * half]
        both = jnp.concatenate([out_ref[...], up_ref[...]], axis=1)
        half = both.shape[1] // 2
        three_ref[0] = both[:, y * half : (y + 1) * half]
        half = down_ref.shape[1] // 2
        four_ref[0] = down_ref[:, pl.ds(y * half, half)]

    @pl.when(rep[0] == 0)
    def _():
        write(0)

    @pl.when(rep[0] == 1)
    def _():
        write(1)


def pack(rep, inward, outward, upward, downward, small):
    rows, wide = inward.shape
    width = wide // 3
    shapes = [
        (1, rows + SMALL_ROWS, 3 * GW // 2),
        (1, rows, (wide - 3 * GW) // 2),
        (1, rows, (width + upward.shape[1]) // 2),
        (1, downward.shape[0], width // 2),
    ]
    return pl.pallas_call(
        pack_kernel,
        in_specs=[SMEM] + [pl.BlockSpec(memory_space=pltpu.VMEM)] * 5,
        out_specs=[pl.BlockSpec(memory_space=pltpu.VMEM)] * 4,
        out_shape=[jax.ShapeDtypeStruct(shape, BF16) for shape in shapes],
        cost_estimate=cost(0, 2 * rows * width * 24),
        name="pack",
    )(rep, inward, outward, upward, downward, small)


V_GAIN, V_SHIFT, V_BIAS, V_FREQ, V_OBIAS, V_MGAIN, V_MSHIFT, V_UBIAS, V_DBIAS = range(9)


def prologue_kernel(lengths, owners, rows, npieces, order, x_ref, pos_ref, *rest):
    pieces = rest[:npieces]
    n1_ref, cos_ref, sin_ref, vec_ref, aux_ref, got, fc, fr, sem = rest[npieces:]
    width = x_ref.shape[1]

    @pl.when(pl.program_id(0) == 0)
    def _():
        copies = []
        for number, piece in enumerate(pieces):
            slots = piece.shape[0]
            copies.append(
                pltpu.make_async_copy(
                    piece.at[:, pl.ds(rows, SMALL_ROWS)], got.at[pl.ds(number * slots, slots)], sem.at[number]
                )
            )
        for copy in copies:
            copy.start()
        for copy in copies:
            copy.wait()
        vec_ref[...] = jnp.zeros_like(vec_ref)
        for owner in range(owners):
            tile = got[order[owner]].astype(F32)
            for row, length in enumerate(lengths):
                vec_ref[row : row + 1, owner * length : (owner + 1) * length] = tile[row : row + 1, :length]
        freq = jnp.broadcast_to(vec_ref[V_FREQ : V_FREQ + 1, :width], (16, width)).astype(BF16)
        source = lax.broadcasted_iota(jnp.int32, (width, width // 2), 0)
        target = lax.broadcasted_iota(jnp.int32, (width, width // 2), 1)
        fc[...] = nn(freq, jnp.where(source == 2 * target, 1.0, 0.0).astype(BF16))[:8]
        fr[...] = nn(freq, jnp.where(source == 2 * target + 1, 1.0, 0.0).astype(BF16))[:8]

    xhat, _ = normalize(x_ref[...])
    n1_ref[...] = (xhat * vec_ref[V_GAIN : V_GAIN + 1, :width] + vec_ref[V_SHIFT : V_SHIFT + 1, :width]).astype(BF16)
    pos = pos_ref[...]
    aux = jnp.transpose(jnp.concatenate([pos, jnp.zeros((120, pos.shape[1]), F32)], axis=0))
    aux_ref[...] = aux
    angle = aux[:, 0:1] * fc[0:1, :] + aux[:, 1:2] * fr[0:1, :]
    cosine, sine = cos_sin(angle)
    cos_ref[...] = cosine
    sin_ref[...] = sine


def prologue(lengths, owners, rows, order, x, pos, pieces, rb=256):
    total, width = x.shape
    pairs = width // 2
    grid = (total // rb,)
    blk = lambda w: pl.BlockSpec((rb, w), lambda i: (i, 0))
    wide = max(lengths) * owners
    return pl.pallas_call(
        functools.partial(prologue_kernel, lengths, owners, rows, len(pieces)),
        grid=grid,
        in_specs=[SMEM, blk(width), pl.BlockSpec((8, rb), lambda i: (0, i))] + [ANY] * len(pieces),
        out_specs=[blk(width), blk(pairs), blk(pairs), whole((16, wide)), blk(128)],
        out_shape=[
            kept((total, width), BF16),
            kept((total, pairs), F32),
            kept((total, pairs), F32),
            kept((16, wide), F32),
            kept((total, 128), F32),
        ],
        scratch_shapes=[
            pltpu.VMEM((piece_count(pieces), SMALL_ROWS, pieces[0].shape[2]), BF16),
            pltpu.VMEM((8, pairs), F32),
            pltpu.VMEM((8, pairs), F32),
            pltpu.SemaphoreType.DMA((len(pieces),)),
        ],
        compiler_params=params(grid, 24),
        cost_estimate=cost(total * width * 40, total * width * 10),
        name="prologue",
    )(order, *far(x), pos, *far(*pieces))


QUARTER = (1.5703125, 4.837512969970703125e-4, 7.549789948768648e-8)


def cos_sin(angle):
    turns = jnp.floor(angle * 0.6366197723675814 + 0.5)
    r = ((angle - turns * QUARTER[0]) - turns * QUARTER[1]) - turns * QUARTER[2]
    r2 = r * r
    s = r + r * r2 * (-1.6666654611e-1 + r2 * (8.3321608736e-3 - 1.9515295891e-4 * r2))
    c = 1.0 - 0.5 * r2 + r2 * r2 * (4.166664568298827e-2 + r2 * (-1.388731625493765e-3 + 2.443315711809948e-5 * r2))
    quad = turns.astype(jnp.int32)
    odd = (quad & 1) == 1
    cosine = jnp.where(odd, s, c)
    sine = jnp.where(odd, c, s)
    cosine = jnp.where(((quad + 1) & 2) == 2, -cosine, cosine)
    sine = jnp.where((quad & 2) == 2, -sine, sine)
    return cosine, sine


def qkv_kernel(g0, npieces, rows, table, n1_ref, vec_ref, cos_ref, sin_ref, *rest):
    pieces = rest[:npieces]
    q_ref, k_ref, v_ref, w, wp, bp, sem = rest[npieces:]
    width = n1_ref.shape[1]
    groups = w.shape[1] // (3 * GW)
    bias_ref = vec_ref.at[V_BIAS : V_BIAS + 1, :]

    @pl.when(pl.program_id(0) == 0)
    def _():
        copies = load_pieces(table, pieces, w, sem, rows)
        for copy in copies:
            copy.start()
        perm = group_perm(False)
        for copy in copies:
            copy.wait()
        for g in range(groups):
            for part in range(2):
                packed = pl.ds((g * 2 + part) * GW, GW)
                wp[:, packed] = nn(w[:, pl.ds((g * 3 + part) * GW, GW)], perm).astype(BF16)
                natural = pl.ds(part * width + (g0 + g) * GW, GW)
                spread = jnp.broadcast_to(bias_ref[:, natural].astype(BF16), (16, GW))
                bp[:, packed] = nn(spread, perm)[:8]

    n1 = n1_ref[...]
    for g in range(groups):
        cosine = cos_ref[:, pl.ds((g0 + g) * HALF, HALF)]
        sine = sin_ref[:, pl.ds((g0 + g) * HALF, HALF)]
        for part, out, scale in ((0, q_ref, HD**-0.5 * LOG2E), (1, k_ref, 1.0)):
            packed = pl.ds((g * 2 + part) * GW, GW)
            mixed = nn(n1, wp[:, packed]) + bp[0:1, packed]
            a, b = mixed[:, :HALF], mixed[:, HALF:]
            first = a * cosine - b * sine
            second = a * sine + b * cosine
            if scale != 1.0:
                first = first * scale
                second = second * scale
            out[:, pl.ds(g * GW, HALF)] = first.astype(BF16)
            out[:, pl.ds(g * GW + HALF, HALF)] = second.astype(BF16)
        bias = bias_ref[:, pl.ds(2 * width + (g0 + g) * GW, GW)]
        v_ref[:, pl.ds(g * GW, GW)] = (nn(n1, w[:, pl.ds((g * 3 + 2) * GW, GW)]) + bias).astype(BF16)


def qkv(g0, groups, rows, table, n1, vec, cosine, sine, pieces):
    total, width = n1.shape
    rb = 512
    pairs = width // 2
    grid = (total // rb,)
    blk = lambda w: pl.BlockSpec((rb, w), lambda i: (i, 0))
    out = kept((total, groups * GW), BF16)
    copies = piece_count(pieces)
    return pl.pallas_call(
        functools.partial(qkv_kernel, g0, len(pieces), rows),
        grid=grid,
        in_specs=[SMEM, blk(width), whole(vec.shape), blk(pairs), blk(pairs)] + [ANY] * len(pieces),
        out_specs=[blk(groups * GW)] * 3,
        out_shape=[out] * 3,
        scratch_shapes=[
            pltpu.VMEM((width, 3 * groups * GW), BF16),
            pltpu.VMEM((width, 2 * groups * GW), BF16),
            pltpu.VMEM((8, 2 * groups * GW), F32),
            pltpu.SemaphoreType.DMA((copies,)),
        ],
        compiler_params=params(grid, 24),
        cost_estimate=cost(total * width * groups * GW * 6, total * width * 8 + width * groups * GW * 6),
        name="qkv",
    )(table, *far(n1, vec, cosine, sine, *pieces))


def attend_kernel(q_ref, k_ref, v_ref, pos_ref, *rest):
    att_ref, lse_ref, wide_ref, mask = rest[-4:]
    g, r = pl.program_id(0), pl.program_id(1)
    rb, keys = q_ref.shape[0], k_ref.shape[0]
    here = pl.ds(pl.multiple_of(r * rb, rb), rb)

    @pl.when(g == 0)
    def _():
        row = lax.broadcasted_iota(jnp.int32, (rb, keys), 0) + r * rb
        col = lax.broadcasted_iota(jnp.int32, (rb, keys), 1)
        mask[here, :] = jnp.where(row == col, 0.0, jnp.broadcast_to(pos_ref[2:3, :], (rb, keys)))

    q = q_ref[...]
    k = k_ref[...]
    v = v_ref[...]
    total = jnp.zeros((rb, GW), F32)
    lane = lax.broadcasted_iota(jnp.int32, (rb, 128), 1)
    logs = jnp.zeros((rb, 128), F32)
    for h in range(GH):
        qm = jnp.where(packed_head_mask(h), q, jnp.zeros_like(q))
        scores = nt(qm, k) + mask[here, :]
        top = jnp.max(scores, axis=-1, keepdims=True)
        weight = jnp.exp2(scores - top)
        norm = jnp.sum(weight, axis=-1, keepdims=True)
        vm = jnp.where(natural_head_mask(h), v, jnp.zeros_like(v))
        total = total + nn(weight.astype(BF16), vm) * (1.0 / norm)
        logs = jnp.where(lane == h, top + jnp.log2(norm), logs)
    att_ref[...] = total.astype(BF16)
    wide_ref[...] = total
    lse_ref[...] = jnp.transpose(logs)[:8, :]


def attend(g0, full, q, k, v, pos, *att, rb=512):
    total, width = q.shape
    groups = width // GW
    grid = (groups, total // rb)
    return pl.pallas_call(
        attend_kernel,
        grid=grid,
        in_specs=[
            pl.BlockSpec((rb, GW), lambda g, r: (r, g)),
            pl.BlockSpec((total, GW), lambda g, r: (0, g)),
            pl.BlockSpec((total, GW), lambda g, r: (0, g)),
            whole((8, total)),
        ]
        + [ANY] * len(att),
        out_specs=[
            pl.BlockSpec((rb, GW), lambda g, r: (r, g + g0)),
            pl.BlockSpec((None, 8, rb), lambda g, r: (g, 0, r)),
            pl.BlockSpec((rb, GW), lambda g, r: (r, g)),
        ],
        out_shape=[
            kept((total, full), BF16),
            kept((groups, 8, total), F32),
            kept((total, width), F32),
        ],
        input_output_aliases={4: 0} if att else {},
        scratch_shapes=[pltpu.VMEM((total, total), F32)],
        compiler_params=params(grid, 32),
        cost_estimate=cost(total * total * width * 16, total * width * 8, total * total * 12),
        name="attend",
    )(*far(q, k, v, pos, *att))


PHI_SCALE = 0.3989422804014327
TAIL_SCALE = 0.44 * 0.7071067811865476
TAIL = (
    0.12411047596471954,
    0.12443560910041027,
    0.10865662380098591,
    0.10790671631036299,
    -0.010091621907114547,
    0.14834527631989725,
    -0.13897496529649409,
    0.03561197654899638,
)


def gelu_parts(h):
    t = 1.0 / (1.0 + TAIL_SCALE * jnp.abs(h))
    poly = TAIL[-1]
    for coefficient in TAIL[-2::-1]:
        poly = poly * t + coefficient
    bell = jnp.exp2((-0.5 * LOG2E) * (h * h))
    tail = poly * t * bell
    phi = jnp.where(h < 0, tail, 1.0 - tail)
    return h * phi, phi + h * (bell * PHI_SCALE)


def up_kernel(half, npieces, rows, table, count, *refs):
    if half == 0:
        att_ref, x_ref, cot_ref, vec_ref = refs[:4]
        pieces = refs[4 : 4 + npieces]
        mid_ref, n2_ref, gd_ref, act_ref, gp_ref, w, sem = refs[4 + npieces :]
    else:
        n2_ref, vec_ref = refs[:2]
        pieces = refs[2 : 2 + npieces]
        act_ref, gp_ref, w, sem = refs[-4:]
    rb, width = n2_ref.shape

    @pl.when(pl.program_id(0) == 0)
    def _():
        slots = table.shape[0] // 2
        copies = load_pieces(table, pieces, w, sem, rows, column=False)
        for start in (True, False):
            for number, copy in enumerate(copies):

                @pl.when(table[slots + number] == half)
                def _():
                    if start:
                        copy.start()
                    else:
                        copy.wait()

    if half == 0:
        slot = lax.broadcasted_iota(jnp.int32, (rb, 1), 0) + pl.program_id(0) * rb
        valid = jnp.where(slot < count[0], 1.0, 0.0)
        gd_ref[...] = (valid * cot_ref[...]).astype(BF16)
        branch = nn(att_ref[...], w[:, pl.ds(0, width)]) + vec_ref[V_OBIAS : V_OBIAS + 1, :width]
        middle = x_ref[...] + valid * branch
        mid_ref[...] = middle
        xhat, _ = normalize(middle)
        n2 = (xhat * vec_ref[V_MGAIN : V_MGAIN + 1, :width] + vec_ref[V_MSHIFT : V_MSHIFT + 1, :width]).astype(BF16)
        n2_ref[...] = n2
        place = width
    else:
        n2 = n2_ref[...]
        place = 0
    first = half * (w.shape[1] - width)
    step = 384
    for c in range(act_ref.shape[1] // step):
        cut = pl.ds(c * step, step)
        hidden = nn(n2, w[:, pl.ds(place + c * step, step)]) + vec_ref[V_UBIAS : V_UBIAS + 1, pl.ds(first + c * step, step)]
        act, slope = gelu_parts(hidden)
        act_ref[:, cut] = act.astype(BF16)
        gp_ref[:, cut] = slope.astype(BF16)


def up_first(rows, wide, table, count, att, x, cot, vec, pieces, rb=256):
    total, width = x.shape
    part = (width + wide) // 2
    grid = (total // rb,)
    blk = lambda w: pl.BlockSpec((rb, w), lambda i: (i, 0))
    return pl.pallas_call(
        functools.partial(up_kernel, 0, len(pieces), rows),
        grid=grid,
        in_specs=[SMEM, SMEM, blk(width), blk(width), blk(width), whole(vec.shape)] + [ANY] * len(pieces),
        out_specs=[blk(width), blk(width), blk(width), blk(part - width), blk(part - width)],
        out_shape=[
            kept((total, width), F32),
            kept((total, width), BF16),
            kept((total, width), BF16),
            kept((total, wide), BF16),
            kept((total, wide), BF16),
        ],
        scratch_shapes=[pltpu.VMEM((width, part), BF16), pltpu.SemaphoreType.DMA((piece_count(pieces),))],
        compiler_params=params(grid, 32),
        cost_estimate=cost(total * width * part * 2, total * width * 20, total * wide),
        name="up_first",
    )(table, count, *far(att, x, cot, vec, *pieces))


def up_second(rows, table, count, n2, act, slope, vec, pieces, rb=256):
    total, width = n2.shape
    wide = act.shape[1]
    part = (width + wide) // 2
    grid = (total // rb,)
    cols = pl.BlockSpec((pl.Element(rb), pl.Element(part)), lambda i: (i * rb, part - width))
    return pl.pallas_call(
        functools.partial(up_kernel, 1, len(pieces), rows),
        grid=grid,
        in_specs=[SMEM, SMEM, pl.BlockSpec((rb, width), lambda i: (i, 0)), whole(vec.shape)]
        + [ANY] * (len(pieces) + 2),
        out_specs=[cols, cols],
        out_shape=[kept((total, wide), BF16)] * 2,
        input_output_aliases={4 + len(pieces): 0, 5 + len(pieces): 1},
        scratch_shapes=[pltpu.VMEM((width, part), BF16), pltpu.SemaphoreType.DMA((piece_count(pieces),))],
        compiler_params=params(grid, 32),
        cost_estimate=cost(total * width * part * 2, total * width * 20, total * wide),
        name="up_second",
    )(table, count, *far(n2, vec, *pieces, act, slope))


def down_kernel(nup, ndown, rows, table, count, act_ref, gp_ref, mid_ref, cot_ref, gd_ref, vec_ref, *rest):
    ups = rest[:nup]
    downs = rest[nup : nup + ndown]
    (out_ref, gm_ref, gb_ref, ga_ref, gu_ref, sums_ref, ubsum_ref, w, wd, sem, sem_d) = rest[nup + ndown :]
    i = pl.program_id(0)
    rb, width = mid_ref.shape
    wide = act_ref.shape[1]

    @pl.when(i == 0)
    def _():
        first = load_pieces(table, downs, wd, sem_d, rows * (wide // width))
        second = load_pieces(table, ups, w, sem, rows)
        for copy in first + second:
            copy.start()
        for copy in first + second:
            copy.wait()
        sums_ref[...] = jnp.zeros_like(sums_ref)
        ubsum_ref[...] = jnp.zeros_like(ubsum_ref)

    slot = lax.broadcasted_iota(jnp.int32, (rb, 1), 0) + i * rb
    valid = jnp.where(slot < count[0], 1.0, 0.0)
    middle = mid_ref[...]
    cot = cot_ref[...]
    gd = gd_ref[...]
    lowered = nn(act_ref[...], wd[...]) + vec_ref[V_DBIAS : V_DBIAS + 1, :width]
    out_ref[...] = middle + valid * lowered
    step = 1024
    gn2 = jnp.zeros((rb, width), F32)
    for c in range(wide // step):
        cut = pl.ds(c * step, step)
        g = nt(gd, wd[cut, :]) * gp_ref[:, cut].astype(F32)
        g_low = g.astype(BF16)
        gu_ref[:, cut] = g_low
        ubsum_ref[0:1, cut] += jnp.sum(g_low.astype(F32), axis=0, keepdims=True)
        gn2 = gn2 + nt(g_low, w[:, pl.ds(width + c * step, step)])
    xhat, inverse = normalize(middle)
    sums_ref[0:1, :] += jnp.sum(gn2 * xhat, axis=0, keepdims=True)
    sums_ref[1:2, :] += jnp.sum(gn2, axis=0, keepdims=True)
    e = gn2 * vec_ref[V_MGAIN : V_MGAIN + 1, :width]
    back = (e - jnp.mean(e, axis=-1, keepdims=True) - xhat * jnp.mean(e * xhat, axis=-1, keepdims=True)) * inverse
    gmid = cot + back
    gm_ref[...] = gmid
    gb = (valid * gmid).astype(BF16)
    gb_ref[...] = gb
    sums_ref[2:3, :] += jnp.sum(gb.astype(F32), axis=0, keepdims=True)
    sums_ref[3:4, :] += jnp.sum(gd.astype(F32), axis=0, keepdims=True)
    ga_ref[...] = nt(gb, w[:, pl.ds(0, width)]).astype(BF16)


def down(rows, table, count, act, gp, mid, cot, gd, vec, ups, downs, rb=256):
    total, width = mid.shape
    wide = act.shape[1]
    grid = (total // rb,)
    blk = lambda w: pl.BlockSpec((rb, w), lambda i: (i, 0))
    return pl.pallas_call(
        functools.partial(down_kernel, len(ups), len(downs), rows),
        grid=grid,
        in_specs=[SMEM, SMEM, blk(wide), blk(wide), blk(width), blk(width), blk(width), whole(vec.shape)]
        + [ANY] * (len(ups) + len(downs)),
        out_specs=[blk(width), blk(width), blk(width), blk(width), blk(wide), whole((8, width)), whole((8, wide))],
        out_shape=[
            kept((total, width), F32),
            kept((total, width), F32),
            kept((total, width), BF16),
            kept((total, width), BF16),
            kept((total, wide), BF16),
            kept((8, width), F32),
            kept((8, wide), F32),
        ],
        scratch_shapes=[
            pltpu.VMEM((width, width + wide), BF16),
            pltpu.VMEM((wide, width), BF16),
            pltpu.SemaphoreType.DMA((piece_count(ups),)),
            pltpu.SemaphoreType.DMA((piece_count(downs),)),
        ],
        compiler_params=params(grid, 44),
        cost_estimate=cost(total * width * (width + 3 * wide) * 2, total * (width * 20 + wide * 6)),
        name="down",
    )(table, count, *far(act, gp, mid, cot, gd, vec, *ups, *downs))


def grad_kernel(pairs, mids, reps, rows, core, *rest):
    keep_ref, send_ref = rest[-2:]
    part = core[0]

    def spot(parity, mid, rep):
        return jnp.where(parity == 0, mid, rep), jnp.where(parity == 0, rep, mid)

    each = keep_ref.shape[-1]
    offset = 0
    for at, bt in pairs:
        a, b_ref = rest[at][...], rest[bt]
        begin = 0
        while begin < b_ref.shape[1]:
            column = offset + begin
            step = min(b_ref.shape[1] - begin, each - column % each, 768)
            result = tn(a, b_ref[:, pl.ds(begin, step)])
            rep, cut = column // each, pl.ds(column % each, step)
            for pair in range(a.shape[1] // (2 * rows)):
                low = result[pair * 2 * rows : pair * 2 * rows + rows]
                high = result[pair * 2 * rows + rows : (pair + 1) * 2 * rows]
                zz, mid = pair // mids, pair % mids
                one, two = spot(part, mid, rep)
                keep_ref[one, two, zz, :, cut] = jnp.where(part == 0, low, high).astype(BF16)
                one, two = spot(1 - part, mid, rep)
                send_ref[one, two, zz, :, cut] = jnp.where(part == 0, high, low).astype(BF16)
            begin += step
        offset += b_ref.shape[1]


def operands(pairs):
    arrays, index = [], []
    for pair in pairs:
        spots = []
        for array in pair:
            if not any(array is other for other in arrays):
                arrays.append(array)
            spots.append([array is other for other in arrays].index(True))
        index.append(spots)
    lefts = {one for one, _ in index}
    return arrays, index, lefts


def weight_grad(core, pairs, layout, name):
    slow, mids, reps = layout
    arrays, index, lefts = operands(pairs)
    total, height = pairs[0][0].shape
    width = sum(b.shape[1] for _, b in pairs)
    rows = height // (slow * mids * 2)
    chunk = 384 if 384 % (2 * mids * rows) == 0 else 2 * mids * rows
    slows = chunk // (2 * mids * rows)
    grid = (height // chunk,)
    out = jax.ShapeDtypeStruct((mids, reps, slow, rows, width // reps), BF16)
    spec = pl.BlockSpec((mids, reps, slows, rows, width // reps), lambda i: (0, 0, i, 0, 0))
    return pl.pallas_call(
        functools.partial(grad_kernel, index, mids, reps, rows),
        grid=grid,
        in_specs=[SMEM]
        + [
            pl.BlockSpec((total, chunk), lambda i: (0, i)) if n in lefts else whole(a.shape)
            for n, a in enumerate(arrays)
        ],
        out_specs=[spec, spec],
        out_shape=[out, out],
        compiler_params=params(grid, 40),
        cost_estimate=cost(total * height * width * 2, total * (height + width) * 2 + height * width * 2),
        name=name,
    )(core, *far(*arrays))


def plain_grad_kernel(pairs, *rest):
    out_ref = rest[-1]
    offset = 0
    for at, bt in pairs:
        a, b_ref = rest[at][...], rest[bt]
        step = min(b_ref.shape[1], 768)
        for c in range(b_ref.shape[1] // step):
            out_ref[:, pl.ds(offset + c * step, step)] = tn(a, b_ref[:, pl.ds(c * step, step)])
        offset += b_ref.shape[1]


def plain_grad(pairs, name):
    arrays, index, lefts = operands(pairs)
    total, height = pairs[0][0].shape
    width = sum(b.shape[1] for _, b in pairs)
    chunk = 384
    grid = (height // chunk,)
    return pl.pallas_call(
        functools.partial(plain_grad_kernel, index),
        grid=grid,
        in_specs=[
            pl.BlockSpec((total, chunk), lambda i: (0, i)) if n in lefts else whole(a.shape)
            for n, a in enumerate(arrays)
        ],
        out_specs=pl.BlockSpec((chunk, width), lambda i: (i, 0)),
        out_shape=jax.ShapeDtypeStruct((height, width), F32),
        compiler_params=params(grid, 63),
        cost_estimate=cost(total * height * width * 2, total * (height + width) * 2 + height * width * 4),
        name=name,
    )(*arrays)


def unrotate(grad, cosine, sine):
    first, second = grad[:, :HALF], grad[:, HALF:]
    return first * cosine + second * sine, second * cosine - first * sine


def angle_grad(grad, rotated):
    return grad[:, HALF:] * rotated[:, :HALF] - grad[:, :HALF] * rotated[:, HALF:]


def back_kernel(q_ref, k_ref, v_ref, do_ref, lse_ref, wide_ref, aux_ref, cos_ref, sin_ref,
                g_ref, fsum_ref, bsum_ref, ds_s, p_s, dk_s, dv_s):
    r = pl.program_id(0)
    rb, keys = q_ref.shape[0], k_ref.shape[0]
    here = pl.ds(pl.multiple_of(r * rb, rb), rb)
    q = q_ref[...]
    k = k_ref[...]
    v = v_ref[...]
    do = do_ref[...]
    zero = jnp.zeros_like(q)
    product = do.astype(F32) * wide_ref[...]
    high = product.astype(BF16)
    low = (product - high.astype(F32)).astype(BF16)
    lane = lax.broadcasted_iota(jnp.int32, (16, GW), 1)
    pick_head = jnp.where(lane // HD == lax.broadcasted_iota(jnp.int32, (16, GW), 0), 1.0, 0.0).astype(BF16)
    inner = nt(pick_head, high) + nt(pick_head, low)
    key = lax.broadcasted_iota(jnp.int32, (keys, rb), 0)
    query = lax.broadcasted_iota(jnp.int32, (keys, rb), 1) + r * rb
    mask = jnp.where(key == query, 0.0, jnp.broadcast_to(aux_ref[:, 2:3], (keys, rb)))
    dq = jnp.zeros((rb, GW), F32)
    qms, doms = [], []
    for h in range(GH):
        qm = jnp.where(packed_head_mask(h), q, zero)
        dom = jnp.where(natural_head_mask(h), do, zero)
        qms.append(qm)
        doms.append(dom)
        soft = jnp.exp2(nt(k, qm) + mask - lse_ref[h : h + 1, :])
        ds = (soft * (nt(v, dom) - inner[h : h + 1, :])).astype(BF16)
        cut = pl.ds(h * rb, rb)
        ds_s[:, cut] = ds
        p_s[:, cut] = soft.astype(BF16)
        km = jnp.where(packed_head_mask(h), k, jnp.zeros_like(k))
        dq = dq + tn(ds, km)
    dk = nn(ds_s[...], jnp.concatenate(qms, axis=0)) * (1.0 / LOG2E)
    dv = nn(p_s[...], jnp.concatenate(doms, axis=0))

    perm = group_perm(True)
    cosine, sine = cos_ref[here, :], sin_ref[here, :]
    dq = dq * (HD**-0.5)
    ang = angle_grad(dq, q.astype(F32) * (HD**0.5 / LOG2E))
    first, second = unrotate(dq, cosine, sine)
    gq = nn(jnp.concatenate([first.astype(BF16), second.astype(BF16)], axis=1), perm)
    g_ref[here, pl.ds(0, GW)] = gq.astype(BF16)
    col, row = aux_ref[here, 0:1], aux_ref[here, 1:2]
    fcol = jnp.sum(ang * col, axis=0, keepdims=True)
    frow = jnp.sum(ang * row, axis=0, keepdims=True)
    qsum = jnp.sum(gq, axis=0, keepdims=True)

    @pl.when(r == 0)
    def _():
        dk_s[...] = dk
        dv_s[...] = dv
        fsum_ref[...] = jnp.zeros_like(fsum_ref)
        fsum_ref[0:1, pl.ds(0, HALF)] = fcol
        fsum_ref[1:2, pl.ds(0, HALF)] = frow
        bsum_ref[0:1, pl.ds(0, GW)] = qsum

    @pl.when(r > 0)
    def _():
        dk_s[...] += dk
        dv_s[...] += dv
        fsum_ref[0:1, pl.ds(0, HALF)] += fcol
        fsum_ref[1:2, pl.ds(0, HALF)] += frow
        bsum_ref[0:1, pl.ds(0, GW)] += qsum

    @pl.when(r == pl.num_programs(0) - 1)
    def _():
        dkf = dk_s[...]
        angk = angle_grad(dkf, k.astype(F32))
        fsum_ref[0:1, pl.ds(0, HALF)] += jnp.sum(angk * aux_ref[:, 0:1], axis=0, keepdims=True)
        fsum_ref[1:2, pl.ds(0, HALF)] += jnp.sum(angk * aux_ref[:, 1:2], axis=0, keepdims=True)
        one, two = unrotate(dkf, cos_ref[...], sin_ref[...])
        gk = nn(jnp.concatenate([one.astype(BF16), two.astype(BF16)], axis=1), perm)
        g_ref[:, pl.ds(GW, GW)] = gk.astype(BF16)
        bsum_ref[0:1, pl.ds(GW, GW)] = jnp.sum(gk, axis=0, keepdims=True)
        gv = dv_s[...].astype(BF16)
        g_ref[:, pl.ds(2 * GW, GW)] = gv
        lane = lax.broadcasted_iota(jnp.int32, (HALF, 2 * HALF), 1)
        pair = lax.broadcasted_iota(jnp.int32, (HALF, 2 * HALF), 0)
        sums = fsum_ref[:, pl.ds(0, HALF)]
        spread = [
            jnp.dot(sums, jnp.where(lane == 2 * pair + odd, 1.0, 0.0), precision=lax.Precision.HIGHEST)
            for odd in range(2)
        ]
        fsum_ref[0:1, :] = spread[0][0:1] + spread[1][1:2]
        bsum_ref[0:1, pl.ds(2 * GW, GW)] = jnp.sum(gv.astype(F32), axis=0, keepdims=True)


def attend_back(g0, l0, q, k, v, do, lse, wide, aux, cosine, sine, rb=512):
    total = q.shape[0]
    grid = (total // rb,)
    return pl.pallas_call(
        back_kernel,
        grid=grid,
        in_specs=[
            pl.BlockSpec((rb, GW), lambda r: (r, l0)),
            pl.BlockSpec((total, GW), lambda r: (0, l0)),
            pl.BlockSpec((total, GW), lambda r: (0, l0)),
            pl.BlockSpec((rb, GW), lambda r: (r, g0)),
            pl.BlockSpec((None, 8, rb), lambda r: (l0, 0, r)),
            pl.BlockSpec((rb, GW), lambda r: (r, l0)),
            whole((total, 128)),
            pl.BlockSpec((total, HALF), lambda r: (0, g0)),
            pl.BlockSpec((total, HALF), lambda r: (0, g0)),
        ],
        out_specs=[whole((total, 3 * GW)), whole((8, GW)), whole((8, 3 * GW))],
        out_shape=[
            kept((total, 3 * GW), BF16),
            jax.ShapeDtypeStruct((8, GW), F32),
            jax.ShapeDtypeStruct((8, 3 * GW), F32),
        ],
        scratch_shapes=[
            pltpu.VMEM((total, GH * rb), BF16),
            pltpu.VMEM((total, GH * rb), BF16),
            pltpu.VMEM((total, GW), F32),
            pltpu.VMEM((total, GW), F32),
        ],
        compiler_params=params(grid, 48),
        cost_estimate=cost(total * total * GW * 40, total * GW * 20, total * total * GH),
        name="attend_back",
    )(*far(q, k, v, do, lse, wide, aux, cosine, sine))


def final_kernel(count, counts, rows, table_one, table_two, x_ref, gm_ref, vec_ref, *rest):
    grads, place = rest[:count], count
    pieces = []
    for number in counts:
        pieces.append(rest[place : place + number])
        place += number
    out_ref, sums_ref = rest[place : place + 2]
    weights = rest[place + 2 : place + 2 + len(counts)]
    sems = rest[place + 2 + len(counts) :]

    @pl.when(pl.program_id(0) == 0)
    def _():
        copies = []
        for table, p, w, sem in zip((table_one, table_two), pieces, weights, sems):
            copies += load_pieces(table, p, w, sem, rows)
        for copy in copies:
            copy.start()
        for copy in copies:
            copy.wait()
        sums_ref[...] = jnp.zeros_like(sums_ref)

    e = jnp.zeros(x_ref.shape, F32)
    group = 0
    for w in weights:
        for g in range(w.shape[1] // (3 * GW)):
            e = e + nt(grads[group][...], w[:, pl.ds(g * 3 * GW, 3 * GW)])
            group += 1
    xhat, inverse = normalize(x_ref[...])
    sums_ref[0:1, :] += jnp.sum(e * xhat, axis=0, keepdims=True)
    sums_ref[1:2, :] += jnp.sum(e, axis=0, keepdims=True)
    eg = e * vec_ref[V_GAIN : V_GAIN + 1, : x_ref.shape[1]]
    back = (eg - jnp.mean(eg, axis=-1, keepdims=True) - xhat * jnp.mean(eg * xhat, axis=-1, keepdims=True)) * inverse
    out_ref[...] = gm_ref[...] + back


def final(rows, widths, tables, x, gmid, vec, grads, piece_sets, rb=256):
    total, width = x.shape
    grid = (total // rb,)
    blk = lambda w: pl.BlockSpec((rb, w), lambda i: (i, 0))
    pieces = [p for ps in piece_sets for p in ps]
    return pl.pallas_call(
        functools.partial(final_kernel, len(grads), [len(ps) for ps in piece_sets], rows),
        grid=grid,
        in_specs=[SMEM, SMEM, blk(width), blk(width), whole(vec.shape)]
        + [blk(g.shape[1]) for g in grads]
        + [ANY] * len(pieces),
        out_specs=[blk(width), whole((8, width))],
        out_shape=[kept((total, width), F32), jax.ShapeDtypeStruct((8, width), F32)],
        scratch_shapes=[pltpu.VMEM((width, w), BF16) for w in widths]
        + [pltpu.SemaphoreType.DMA((piece_count(ps),)) for ps in piece_sets],
        compiler_params=params(grid, 32),
        cost_estimate=cost(total * width * width * 6, total * width * 20 + width * width * 6),
        name="final",
    )(*tables, *far(x, gmid, vec), *far(*grads), *far(*pieces))


FOLD = (
    ("bias", 0, 0), ("value", 1, 0), ("freqs", 1, 64), ("gain", 2, 0), ("shift", 2, 64),
    ("obias", 3, 0), ("dbias", 3, 64), ("mgain", 4, 0), ("mshift", 4, 64), ("ubias", 5, 0),
)


def fold_kernel(groups, owners, spot, *refs):
    out_ref = refs[-1]
    fsums, bsums = refs[:groups], refs[groups : 2 * groups]
    mid_ref, wide_ref, first_ref = refs[2 * groups : 2 * groups + 3]
    lines = {
        "bias": [(b, 0, part * GW, GW) for part in range(2) for b in bsums],
        "value": [(b, 0, 2 * GW, GW) for b in bsums],
        "freqs": [(f, 0, 0, GW) for f in fsums],
        "gain": [(first_ref, 0, 0, first_ref.shape[1])],
        "shift": [(first_ref, 1, 0, first_ref.shape[1])],
        "mgain": [(mid_ref, 0, 0, mid_ref.shape[1])],
        "mshift": [(mid_ref, 1, 0, mid_ref.shape[1])],
        "obias": [(mid_ref, 2, 0, mid_ref.shape[1])],
        "dbias": [(mid_ref, 3, 0, mid_ref.shape[1])],
        "ubias": [(wide_ref, 0, 0, wide_ref.shape[1])],
    }
    out_ref[...] = jnp.zeros_like(out_ref)
    for name, row, lane in FOLD:
        total = sum(length for _, _, _, length in lines[name])
        each = total // owners
        for owner in range(owners):
            begin, end = owner * each, (owner + 1) * each
            offset = 0
            for ref, line, start, length in lines[name]:
                low, high = max(begin, offset), min(end, offset + length)
                while low < high:
                    place = row * 128 + lane + low - begin
                    at = start + low - offset
                    lead, last = spot(owner)
                    out_ref[(*lead, slice(last, last + 1), slice(place, place + high - low))] = (
                        ref[line : line + 1, at : at + high - low]
                    )
                    low = high
                offset += length


def fold(owners, cube, fsums, bsums, mid, wide, first):
    arrays = [*fsums, *bsums, mid, wide, first]
    shape, spot = (owners, 1024), lambda owner: ((), owner)
    if cube:
        shape, spot = (2, 2, 4, 1024), lambda owner: ((owner % 2, owner // 2 % 2), owner // 4)
    return pl.pallas_call(
        functools.partial(fold_kernel, len(fsums), owners, spot),
        in_specs=[pl.BlockSpec(memory_space=pltpu.VMEM)] * len(arrays),
        out_specs=pl.BlockSpec(memory_space=pltpu.VMEM),
        out_shape=jax.ShapeDtypeStruct(shape, F32),
        cost_estimate=cost(0, 100000),
        name="fold",
    )(*arrays)


def half_column(pair, swap, place, width):
    mine, other = pair
    each = mine.shape[1]
    cut = pl.ds(place % each, width)
    a, b = (mine, other) if place < each else (other, mine)
    return jnp.where(swap, b[:, cut], a[:, cut])


def finish_kernel(rep, *refs):
    outup, downs, (out_ref, up_ref, down_ref) = refs[:2], refs[2:4], refs[4:]
    swap, step, width = rep[0] == 1, GW // 2, out_ref.shape[1]
    for place in range(0, outup[0].shape[1] * 2, step):
        value = half_column(outup, swap, place, step)
        if place < width:
            out_ref[:, pl.ds(place, step)] = value
        else:
            up_ref[:, pl.ds(place - width, step)] = value
    for place in range(0, down_ref.shape[1], step):
        down_ref[:, pl.ds(place, step)] = half_column(downs, swap, place, step)


def finish(rep, outup, downs):
    width = downs[0].shape[1] * 2
    rows = outup[0].shape[0]
    shapes = [(rows, width), (rows, outup[0].shape[1] * 2 - width), (downs[0].shape[0], width)]
    return pl.pallas_call(
        finish_kernel,
        in_specs=[SMEM] + [NEAR] * 4,
        out_specs=[NEAR] * 3,
        out_shape=[jax.ShapeDtypeStruct(shape, F32) for shape in shapes],
        cost_estimate=cost(0, 4000000),
        name="finish",
    )(rep, *outup, *downs)


def finish_inward_kernel(groups, rep, *refs):
    halves, in_ref = refs[:-1], refs[-1]
    swap, step, group, total = rep[0] == 1, GW // 2, 0, in_ref.shape[1] // 3
    for n, count in enumerate(groups):
        for g in range(count):
            for part in range(3):
                for half in range(2):
                    value = half_column(halves[2 * n : 2 * n + 2], swap, (g * 3 + part) * GW + half * step, step)
                    in_ref[:, pl.ds(part * total + group * GW + half * step, step)] = value
            group += 1


def finish_inward(groups, rep, pairs):
    arrays = [a for pair in pairs for a in pair]
    return pl.pallas_call(
        functools.partial(finish_inward_kernel, groups),
        in_specs=[SMEM] + [NEAR] * len(arrays),
        out_specs=NEAR,
        out_shape=jax.ShapeDtypeStruct((arrays[0].shape[0], 3 * GW * sum(groups)), F32),
        cost_estimate=cost(0, 1000000),
        name="finish_inward",
    )(rep, *arrays)


def place():
    me = lax.axis_index("fsdp")
    return lax.axis_index("rep"), me // 4, (me // 2) % 2, me % 2


def move(value, step):
    moves = []
    for i in range(32):
        y, z, x, c = step(i // 16, (i // 4) % 4, (i // 2) % 2, i % 2)
        moves.append((i, y * 16 + z * 4 + x * 2 + c))
    return lax.ppermute(value, ("rep", "fsdp"), moves)


def across_core(value):
    return move(value, lambda y, z, x, c: (y, z, x, 1 - c))


def across_x(value):
    return move(value, lambda y, z, x, c: (y, z, 1 - x, c))


def across_rep(value):
    return move(value, lambda y, z, x, c: (1 - y, z, x, c))


def across_near(value):
    return move(value, lambda y, z, x, c: (y, z ^ 1, x, c))


def across_far(value):
    return move(value, lambda y, z, x, c: (y, z ^ 2, x, c))


def across_third(value):
    return move(value, lambda y, z, x, c: (y, z ^ 3, x, c))


def across_both(value):
    return move(value, lambda y, z, x, c: (1 - y, z, 1 - x, c))


def across_one(value):
    return move(value, lambda y, z, x, c: (y, z, 1 - x, c) if c == 0 else (1 - y, z, x, c))


def across_two(value):
    return move(value, lambda y, z, x, c: (1 - y, z, x, c) if c == 0 else (y, z, 1 - x, c))


def pick(array, index):
    return lax.dynamic_index_in_dim(array, index, 0, keepdims=False)


def pick_two(array, index):
    return lax.dynamic_slice_in_dim(array, 2 * index, 2, 0)


def piece_tables():
    y, z, x, c = place()
    slot = jnp.arange(4, dtype=jnp.int32)
    here, swap = (lambda core, a, b: a), (lambda core, a, b: jnp.where(core == 0, a, b))
    tables = []
    for choose in (here, swap):
        owners, halves = [], []
        for core in (c, 1 - c):
            for mid, half in ((x, y), (choose(core, x, 1 - x), choose(core, 1 - y, y)),
                              (choose(core, 1 - x, x), choose(core, y, 1 - y)), (1 - x, 1 - y)):
                owners.append((z ^ slot) * 4 + mid * 2 + core)
                halves.append(jnp.broadcast_to(half, (4,)))
        tables.append(jnp.concatenate(owners + halves).astype(jnp.int32))
    return tables


def first_of_owner(table, n):
    slots = table.shape[0] // 2
    match = table[None, :slots] == jnp.arange(n, dtype=jnp.int32)[:, None]
    return jnp.min(jnp.where(match, jnp.arange(slots, dtype=jnp.int32)[None, :], slots), axis=1)


class Reduce:
    stages = (across_core, across_one, across_two, across_far, across_near, across_rep)

    def __init__(self, keep, send):
        self.keep, self.first, self.got, self.stage = keep, send, [], 0
        self.out = None

    def sends(self):
        return [(self.stages[self.stage], self.send())]

    def takes(self, values):
        self.take(values[0])

    def base(self, count, one, two=None, cut=None):
        step = lambda a, i: a if i is None else pick(a, i)
        total = None
        for source, used in ((self.keep, 0), (self.got[0], 0), *((g, n + 1) for n, g in enumerate(self.got[1:count]))):
            value = source
            if used < 1:
                value = step(value, one)
            if used < 2:
                value = step(value, two)
            if cut is not None:
                value = cut(value)
            value = value.astype(F32)
            total = value if total is None else total + value
        return total

    def level(self, index):
        return self.base(3, self.i1, self.i2, lambda a: pick(a, index)) + pick(self.got[3], index % 2).astype(F32)

    def send(self):
        y, z, x, c = place()
        self.i1, self.i2 = jnp.where(c == 0, x, y), jnp.where(c == 0, y, x)
        if self.stage == 0:
            return self.first
        if self.stage == 1:
            return self.base(1, 1 - self.i1).astype(BF16)
        if self.stage == 2:
            return self.base(2, self.i1, 1 - self.i2).astype(BF16)
        if self.stage == 3:
            return self.base(3, self.i1, self.i2, lambda a: pick_two(a, 1 - z // 2)).astype(BF16)
        if self.stage == 4:
            return self.level(z ^ 1).astype(BF16)
        self.total = self.level(z) + self.got[4].astype(F32)
        return self.total

    def take(self, value):
        self.stage += 1
        if self.stage == 6:
            self.out = (self.total, value)
        else:
            self.got.append(value)


class SmallReduce:
    stages = (across_core, across_x, across_far, across_near, across_rep)

    def __init__(self, cube):
        self.part, self.stage = cube, 0

    sends, takes = Reduce.sends, Reduce.takes

    def send(self):
        y, z, x, c = place()
        if self.stage == 4:
            self.kept = self.part
            return self.part
        cut = pick_two if self.stage == 2 else pick
        index = (c, x, z // 2, z % 2)[self.stage]
        self.kept = cut(self.part, index)
        return cut(self.part, 1 - index)

    def take(self, value):
        self.stage += 1
        self.part = self.kept + value
        self.out = self.part


class QuickGather:
    def __init__(self, half):
        self.part, self.stage = half, 0

    def sends(self):
        if self.stage == 0:
            return [(f, self.part) for f in (across_near, across_far, across_third)]
        if self.stage == 1:
            return [(f, self.part) for f in (across_rep, across_x, across_both, across_core)]
        return [(across_core, part) for part in self.beside]

    def takes(self, values):
        self.stage += 1
        if self.stage == 1:
            self.part = jnp.concatenate([self.part, *values])
        elif self.stage == 2:
            self.beside, self.other = values[:3], values[3]
        else:
            self.out = [self.part, *self.beside, self.other, *values]


class Gather:
    def __init__(self, half, cuts=1):
        self.part, self.stage, self.cuts, self.got = half, 0, cuts, []

    def sends(self):
        if self.stage == 1 and self.cuts > 1:
            each = self.part.shape[2] // self.cuts
            begin = len(self.got) * each
            return [(across_far, self.part[:, :, begin : begin + each])]
        if self.stage < 3:
            return [((across_near, across_far, across_two)[self.stage], self.part)]
        if self.stage == 3:
            return [(across_one, self.part), (across_one, self.two), (across_core, self.part), (across_core, self.two)]
        return [(across_core, part) for part in self.one]

    def takes(self, values):
        if self.stage == 1:
            self.got += values
            if len(self.got) < self.cuts:
                return
            values = [jnp.concatenate(self.got, axis=2)] if self.cuts > 1 else values
        self.stage += 1
        if self.stage < 3:
            self.part = jnp.concatenate([self.part, values[0]])
        elif self.stage == 3:
            self.two = values[0]
        elif self.stage == 4:
            self.one, self.other = values[:2], values[2:]
        else:
            self.out = [self.part, self.two, *self.one, *self.other, *values]


def step(movers, kernel=None, *inputs):
    sends = [m.sends() for m in movers]
    inputs, arrays = lax.optimization_barrier((inputs, [[a for _, a in s] for s in sends]))
    got = [[f(a) for (f, _), a in zip(s, each)] for s, each in zip(sends, arrays)]
    outs = kernel(*inputs) if kernel is not None else ()
    outs, got = lax.optimization_barrier((outs, got))
    for m, g in zip(movers, got):
        m.takes(g)
    return outs


def group_columns(weight, g0, ng, width):
    cuts = []
    for g in range(g0, g0 + ng):
        cuts += [weight[:, part * width + g * GW : part * width + (g + 1) * GW] for part in range(3)]
    return jnp.concatenate(cuts, axis=1)


def small_block(smalls, lanes):
    total = None
    for row, vector in enumerate(smalls):
        block = jnp.pad(vector[None, :], ((row, SMALL_ROWS - 1 - row), (0, lanes - vector.shape[0])))
        total = block if total is None else total + block
    return total


class Done:
    def __init__(self, out):
        self.out = out


def local(tuned, n, tokens, pre_gain, pre_shift, inward_weight, inward_bias, rotary_freqs, outward_weight,
          outward_bias, mlp_gain, mlp_shift, up_weight, up_bias, down_weight, down_bias, keep_mask, kept_counts,
          patch_rows, patch_cols, cotangent):
    total, width = tokens.shape
    groups = width // GW
    wide = up_weight.shape[1]
    rows = width // n
    smalls = [pre_gain, pre_shift, inward_bias, rotary_freqs, outward_bias, mlp_gain, mlp_shift, up_bias, down_bias]
    lengths = [s.shape[0] for s in smalls]
    small = small_block(smalls, 3 * GW // 2)
    slot = jnp.arange(total, dtype=jnp.int32)
    count = kept_counts
    key_bias = jnp.where((slot < count[0]) & (keep_mask[0] == 1), 0.0, NEG).astype(F32)
    lines = [patch_cols[0].astype(F32), patch_rows[0].astype(F32), key_bias]
    pos = jnp.stack(lines + [jnp.zeros_like(key_bias)] * 5)
    core = (lax.axis_index("fsdp") % 2).astype(jnp.int32)[None]
    rep = lax.axis_index("rep").astype(jnp.int32)[None]

    if tuned:
        shards = pack(rep, inward_weight, outward_weight, up_weight, down_weight, small)
        first, second, outup, downs = QuickGather(shards[0]), Gather(shards[1]), Gather(shards[2], 2), Gather(shards[3])
        quick, table = piece_tables()
        order = first_of_owner(quick, n)
        step([first])
        step([first, second])
        step([first])
        load = skip = rows
        small_pieces = first.out
    else:
        gather = lambda a: lax.all_gather(a, "fsdp", axis=0, tiled=True)
        quick = table = jnp.array([0, 0, 0, 1], jnp.int32)
        order = jnp.arange(n, dtype=jnp.int32)
        load, skip = width, SMALL_ROWS
        small_pieces = [jnp.pad(gather(small[None]), ((0, 0), (skip, 0), (0, 0)))]
        weights = [group_columns(inward_weight, 0, 1, width), group_columns(inward_weight, 1, groups - 1, width),
                   jnp.concatenate([outward_weight, up_weight], axis=1), down_weight]
        first, second, outup, downs = [Done([gather(w)[None]]) for w in weights]
        outup = Done([half[None] for half in jnp.split(outup.out[0][0], 2, axis=1)])

    def run(movers, kernel, *inputs):
        return step(movers, kernel, *inputs) if tuned else kernel(*inputs)

    part = functools.partial
    n1, cosine, sine, vec, aux = run([second, outup], part(prologue, lengths, n, skip), order, tokens, pos, small_pieces)

    q0, k0, v0 = run([second, outup], part(qkv, 0, 1, load), quick, n1, vec, cosine, sine, first.out)
    att, lse0, wide0 = run([second, outup], part(attend, 0, width), q0, k0, v0, pos)
    if tuned:
        step([second])
    q1, k1, v1 = run([outup, downs], part(qkv, 1, groups - 1, load), table, n1, vec, cosine, sine, second.out)
    att, lse1, wide1 = run([outup, downs], part(attend, 1, width), q1, k1, v1, pos, att)
    if tuned:
        step([outup])
    middle, n2, gd, act, slope = run(
        [downs], part(up_first, load, wide), table, count, att, tokens, cotangent, vec, outup.out
    )
    act, slope = run([downs], part(up_second, load), table, count, n2, act, slope, vec, outup.out)

    layout = (n // 4, 2, 2)

    def gradient(name, pairs):
        if tuned:
            return weight_grad(core, pairs, layout, name)
        return lax.psum(lax.psum_scatter(plain_grad(pairs, name), "fsdp", scatter_dimension=0, tiled=True), "rep")

    def reduction(movers, name, pairs):
        out = run(movers, part(gradient, name), pairs)
        return Reduce(*out) if tuned else Done(out)

    r_down = reduction([downs], "down_grad", [(act, gd)])
    outputs, gmid, gb, ga, gu, sums, ubsum = run(
        [r_down], part(down, load), table, count, act, slope, middle, cotangent, gd, vec, outup.out, downs.out
    )
    r_up = reduction([r_down], "up_grad", [(att, gb), (n2, gu)])
    backs = []
    heads = ((0, 0, q0, k0, v0, lse0, wide0), (1, 0, q1, k1, v1, lse1, wide1), (2, 1, q1, k1, v1, lse1, wide1))

    def back(movers, which):
        g0, l0, q, k, v, lse, att_wide = heads[which]
        backs.append(run(movers, part(attend_back, g0, l0), q, k, v, ga, lse, att_wide, aux, cosine, sine))

    def in_gradient(movers, name, which):
        return reduction(movers, name, [(n1, backs[g][0]) for g in which])

    back([r_down, r_up], 0)
    back([r_down, r_up], 1)
    r_in0 = in_gradient([r_down, r_up], "in_grad0", (0, 1))
    if tuned:
        step([r_in0])
    back([r_down, r_up, r_in0], 2)
    r_in1 = in_gradient([r_up, r_in0], "in_grad1", (2,))
    grad_tokens, first_sums = run(
        [r_up, r_in0, r_in1], part(final, load, [3 * GW, 3 * GW * (groups - 1)]),
        (quick, table), tokens, gmid, vec, [b[0] for b in backs], [first.out, second.out]
    )
    small_sums = fold(n, tuned, [b[1] for b in backs], [b[2] for b in backs], sums, ubsum, first_sums)
    if tuned:
        r_small = SmallReduce(small_sums)
        step([r_small, r_in0, r_in1])
        step([r_small, r_in0, r_in1])
        step([r_small, r_in1])
        step([r_small, r_in1])
        d_out, d_up, d_down = step([r_small, r_in1], finish, rep, r_up.out, r_down.out)
        mine = r_small.out
        d_inward = finish_inward((2, 1), rep, [r_in0.out, r_in1.out])
    else:
        mine = lax.psum(lax.psum_scatter(small_sums, "fsdp", scatter_dimension=0, tiled=True), "rep")[0]
        blocks = [r.out[:, 3 * g * GW : 3 * (g + 1) * GW] for r, ng in ((r_in0, 2), (r_in1, 1)) for g in range(ng)]
        d_inward = jnp.concatenate([b[:, p * GW : (p + 1) * GW] for p in range(3) for b in blocks], axis=1)
        d_out, d_up, d_down = r_up.out[:, :width], r_up.out[:, width:], r_down.out
    each = width // n
    line = {name: mine[row * 128 + lane :] for name, row, lane in FOLD}
    o_bias, o_ubias = line["bias"][: 2 * each], line["ubias"][: wide // n]
    o_vbias, o_freqs, o_gain, o_shift, o_obias, o_mgain, o_mshift, o_dbias = [
        line[name][:each] for name in ("value", "freqs", "gain", "shift", "obias", "mgain", "mshift", "dbias")
    ]
    return (outputs, grad_tokens, o_gain, o_shift, d_inward, o_bias, o_vbias, o_freqs, d_out, o_obias,
            o_mgain, o_mshift, d_up, o_ubias, d_down, o_dbias)


def solution(mesh):
    n = mesh.shape["fsdp"]
    tuned = mesh.shape["rep"] == 2 and n == 16
    row = P(("rep", "fsdp"), None)
    vec, mat = P("fsdp"), P("fsdp", None)
    return jax.shard_map(
        functools.partial(local, tuned, n),
        mesh=mesh,
        in_specs=(row, vec, vec, mat, vec, vec, mat, vec, vec, vec, mat, vec, mat, vec, row,
                  P(("rep", "fsdp")), row, row, row),
        out_specs=(row, row, vec, vec, mat, vec, vec, vec, mat, vec, vec, vec, mat, vec, mat, vec),
        check_vma=False,
    )
```

```python
import functools
import math

import jax
import jax.numpy as jnp
from jax import lax
from jax.experimental import pallas as pl
from jax.experimental.pallas import tpu as pltpu
from jax.sharding import PartitionSpec as P

HD = 64
LOG2E = 1.4426950408889634
EPS = 1e-06
NEG = -1e30
F32 = jnp.float32
BF16 = jnp.bfloat16
GH = 4
GW = GH * HD
HALF = GW // 2


def dims(lhs, rhs, lhs_axis, rhs_axis):
    return lax.dot_general(
        lhs, rhs, (((lhs_axis,), (rhs_axis,)), ((), ())), preferred_element_type=F32
    )


def nn(lhs, rhs):
    return dims(lhs, rhs, 1, 0)


def nt(lhs, rhs):
    return dims(lhs, rhs, 1, 1)


def tn(lhs, rhs):
    return dims(lhs, rhs, 0, 0)


def params(grid, mib):
    return pltpu.CompilerParams(
        dimension_semantics=("arbitrary",) * len(grid), vmem_limit_bytes=mib * 2**20
    )


def whole(shape):
    return pl.BlockSpec(shape, lambda *idx: (0,) * len(shape))


ANY = pl.BlockSpec(memory_space=pl.ANY)
SMEM = pl.BlockSpec(memory_space=pltpu.SMEM)
NEAR = pl.BlockSpec(memory_space=pltpu.VMEM)


def kept(shape, dtype):
    return pltpu.HBM(shape, dtype)


def far(*arrays):
    return [pltpu.with_memory_space_constraint(a, pltpu.HBM) for a in arrays]


def cost(flops, bytes_moved, transcendental=0):
    return pl.CostEstimate(
        flops=int(flops), bytes_accessed=int(bytes_moved), transcendentals=int(transcendental)
    )


def group_perm(transposed):
    row = lax.broadcasted_iota(jnp.int32, (GW, GW), 0)
    col = lax.broadcasted_iota(jnp.int32, (GW, GW), 1)
    packed, natural = (row, col) if transposed else (col, row)
    half = packed // HALF
    head = (packed % HALF) // (HD // 2)
    source = head * HD + half * (HD // 2) + packed % (HD // 2)
    return jnp.where(source == natural, 1.0, 0.0).astype(BF16)


def packed_head_mask(head):
    lane = lax.broadcasted_iota(jnp.int32, (1, GW), 1)
    return (lane % HALF) // (HD // 2) == head


def natural_head_mask(head):
    lane = lax.broadcasted_iota(jnp.int32, (1, GW), 1)
    return lane // HD == head


def normalize(values):
    center = values - jnp.mean(values, axis=-1, keepdims=True)
    spread = jnp.mean(center * center, axis=-1, keepdims=True)
    inverse = lax.rsqrt(spread + EPS)
    return center * inverse, inverse


def load_pieces(table, sources, target, sem, rows, column=True):
    copies = []
    slots = table.shape[0] // 2
    for source in sources:
        width = source.shape[2]
        for slot in range(source.shape[0]):
            number = len(copies)
            row = pl.multiple_of(table[number] * rows, rows)
            col = pl.multiple_of(table[slots + number] * width, width) if column else 0
            copies.append(
                pltpu.make_async_copy(
                    source.at[slot, pl.ds(0, rows)], target.at[pl.ds(row, rows), pl.ds(col, width)], sem.at[number]
                )
            )
    return copies


def piece_count(sources):
    return sum(s.shape[0] for s in sources)


SMALL_ROWS = 16


def pack_kernel(rep, in_ref, out_ref, up_ref, down_ref, *rest):
    vectors, (one_ref, two_ref, three_ref, four_ref, small_ref) = rest[:-5], rest[-5:]
    small_ref[...] = jnp.zeros_like(small_ref)
    for row, vector in enumerate(vectors):
        length = vector.shape[0]
        small_ref[row : row + 1, :length] = vector[...].astype(F32).reshape(1, length)

    def write(y):
        rows, third = in_ref.shape[0], in_ref.shape[1] // 3
        groups = third // GW
        cuts = [in_ref[:, pl.ds(part * third + g * GW, GW)] for g in range(groups) for part in range(3)]
        first = jnp.concatenate(cuts[:3], axis=1)
        half = first.shape[1] // 2
        one_ref[0, pl.ds(0, rows), :] = first[:, y * half : (y + 1) * half]
        one_ref[0, pl.ds(rows, SMALL_ROWS), :] = small_ref[...].astype(BF16)
        rest = jnp.concatenate(cuts[3:], axis=1)
        half = rest.shape[1] // 2
        two_ref[0] = rest[:, y * half : (y + 1) * half]
        both = jnp.concatenate([out_ref[...], up_ref[...]], axis=1)
        half = both.shape[1] // 2
        three_ref[0] = both[:, y * half : (y + 1) * half]
        half = down_ref.shape[1] // 2
        four_ref[0] = down_ref[:, pl.ds(y * half, half)]

    @pl.when(rep[0] == 0)
    def _():
        write(0)

    @pl.when(rep[0] == 1)
    def _():
        write(1)


def pack(rep, inward, outward, upward, downward, smalls):
    rows, wide = inward.shape
    width = wide // 3
    shapes = [
        (1, rows + SMALL_ROWS, 3 * GW // 2),
        (1, rows, (wide - 3 * GW) // 2),
        (1, rows, (width + upward.shape[1]) // 2),
        (1, downward.shape[0], width // 2),
    ]
    return pl.pallas_call(
        pack_kernel,
        in_specs=[SMEM] + [pl.BlockSpec(memory_space=pltpu.VMEM)] * (4 + len(smalls)),
        out_specs=[pl.BlockSpec(memory_space=pltpu.VMEM)] * 4,
        out_shape=[jax.ShapeDtypeStruct(shape, BF16) for shape in shapes],
        scratch_shapes=[pltpu.VMEM((SMALL_ROWS, 3 * GW // 2), F32)],
        cost_estimate=cost(0, 2 * rows * width * 24),
        name="pack",
    )(rep, inward, outward, upward, downward, *smalls)


V_GAIN, V_SHIFT, V_BIAS, V_FREQ, V_OBIAS, V_MGAIN, V_MSHIFT, V_UBIAS, V_DBIAS = range(9)


def prologue_kernel(lengths, owners, rows, npieces, order, x_ref, pos_ref, *rest):
    pieces = rest[:npieces]
    n1_ref, cos_ref, sin_ref, vec_ref, aux_ref, got, fc, fr, sem = rest[npieces:]
    width = x_ref.shape[1]

    @pl.when(pl.program_id(0) == 0)
    def _():
        copies = []
        for number, piece in enumerate(pieces):
            slots = piece.shape[0]
            copies.append(
                pltpu.make_async_copy(
                    piece.at[:, pl.ds(rows, SMALL_ROWS)], got.at[pl.ds(number * slots, slots)], sem.at[number]
                )
            )
        for copy in copies:
            copy.start()
        for copy in copies:
            copy.wait()
        vec_ref[...] = jnp.zeros_like(vec_ref)
        for owner in range(owners):
            tile = got[order[owner]].astype(F32)
            for row, length in enumerate(lengths):
                vec_ref[row : row + 1, owner * length : (owner + 1) * length] = tile[row : row + 1, :length]
        freq = jnp.broadcast_to(vec_ref[V_FREQ : V_FREQ + 1, :width], (16, width)).astype(BF16)
        source = lax.broadcasted_iota(jnp.int32, (width, width // 2), 0)
        target = lax.broadcasted_iota(jnp.int32, (width, width // 2), 1)
        fc[...] = nn(freq, jnp.where(source == 2 * target, 1.0, 0.0).astype(BF16))[:8]
        fr[...] = nn(freq, jnp.where(source == 2 * target + 1, 1.0, 0.0).astype(BF16))[:8]

    xhat, _ = normalize(x_ref[...])
    n1_ref[...] = (xhat * vec_ref[V_GAIN : V_GAIN + 1, :width] + vec_ref[V_SHIFT : V_SHIFT + 1, :width]).astype(BF16)
    pos = pos_ref[...]
    aux = jnp.transpose(jnp.concatenate([pos, jnp.zeros((120, pos.shape[1]), F32)], axis=0))
    aux_ref[...] = aux
    angle = aux[:, 0:1] * fc[0:1, :] + aux[:, 1:2] * fr[0:1, :]
    cosine, sine = cos_sin(angle)
    cos_ref[...] = cosine
    sin_ref[...] = sine


def prologue(lengths, owners, rows, order, x, pos, pieces, rb=256):
    total, width = x.shape
    pairs = width // 2
    grid = (total // rb,)
    blk = lambda w: pl.BlockSpec((rb, w), lambda i: (i, 0))
    wide = max(lengths) * owners
    return pl.pallas_call(
        functools.partial(prologue_kernel, lengths, owners, rows, len(pieces)),
        grid=grid,
        in_specs=[SMEM, blk(width), pl.BlockSpec((8, rb), lambda i: (0, i))] + [ANY] * len(pieces),
        out_specs=[blk(width), blk(pairs), blk(pairs), whole((16, wide)), blk(128)],
        out_shape=[
            kept((total, width), BF16),
            kept((total, pairs), F32),
            kept((total, pairs), F32),
            kept((16, wide), F32),
            kept((total, 128), F32),
        ],
        scratch_shapes=[
            pltpu.VMEM((piece_count(pieces), SMALL_ROWS, pieces[0].shape[2]), BF16),
            pltpu.VMEM((8, pairs), F32),
            pltpu.VMEM((8, pairs), F32),
            pltpu.SemaphoreType.DMA((len(pieces),)),
        ],
        compiler_params=params(grid, 24),
        cost_estimate=cost(total * width * 40, total * width * 10),
        name="prologue",
    )(order, *far(x), pos, *far(*pieces))


QUARTER = (1.5703125, 4.837512969970703125e-4, 7.549789948768648e-8)


def cos_sin(angle):
    turns = jnp.floor(angle * 0.6366197723675814 + 0.5)
    r = ((angle - turns * QUARTER[0]) - turns * QUARTER[1]) - turns * QUARTER[2]
    r2 = r * r
    s = r + r * r2 * (-1.6666654611e-1 + r2 * (8.3321608736e-3 - 1.9515295891e-4 * r2))
    c = 1.0 - 0.5 * r2 + r2 * r2 * (4.166664568298827e-2 + r2 * (-1.388731625493765e-3 + 2.443315711809948e-5 * r2))
    quad = turns.astype(jnp.int32)
    odd = (quad & 1) == 1
    cosine = jnp.where(odd, s, c)
    sine = jnp.where(odd, c, s)
    cosine = jnp.where(((quad + 1) & 2) == 2, -cosine, cosine)
    sine = jnp.where((quad & 2) == 2, -sine, sine)
    return cosine, sine


def qkv_kernel(g0, npieces, rows, table, n1_ref, vec_ref, cos_ref, sin_ref, *rest):
    pieces = rest[:npieces]
    q_ref, k_ref, v_ref, w, wp, bp, sem = rest[npieces:]
    width = n1_ref.shape[1]
    groups = w.shape[1] // (3 * GW)
    bias_ref = vec_ref.at[V_BIAS : V_BIAS + 1, :]

    @pl.when(pl.program_id(0) == 0)
    def _():
        copies = load_pieces(table, pieces, w, sem, rows)
        for copy in copies:
            copy.start()
        perm = group_perm(False)
        for copy in copies:
            copy.wait()
        for g in range(groups):
            for part in range(2):
                packed = pl.ds((g * 2 + part) * GW, GW)
                wp[:, packed] = nn(w[:, pl.ds((g * 3 + part) * GW, GW)], perm).astype(BF16)
                natural = pl.ds(part * width + (g0 + g) * GW, GW)
                spread = jnp.broadcast_to(bias_ref[:, natural].astype(BF16), (16, GW))
                bp[:, packed] = nn(spread, perm)[:8]

    n1 = n1_ref[...]
    for g in range(groups):
        cosine = cos_ref[:, pl.ds((g0 + g) * HALF, HALF)]
        sine = sin_ref[:, pl.ds((g0 + g) * HALF, HALF)]
        for part, out, scale in ((0, q_ref, HD**-0.5 * LOG2E), (1, k_ref, 1.0)):
            packed = pl.ds((g * 2 + part) * GW, GW)
            mixed = nn(n1, wp[:, packed]) + bp[0:1, packed]
            a, b = mixed[:, :HALF], mixed[:, HALF:]
            first = a * cosine - b * sine
            second = a * sine + b * cosine
            if scale != 1.0:
                first = first * scale
                second = second * scale
            out[:, pl.ds(g * GW, HALF)] = first.astype(BF16)
            out[:, pl.ds(g * GW + HALF, HALF)] = second.astype(BF16)
        bias = bias_ref[:, pl.ds(2 * width + (g0 + g) * GW, GW)]
        v_ref[:, pl.ds(g * GW, GW)] = (nn(n1, w[:, pl.ds((g * 3 + 2) * GW, GW)]) + bias).astype(BF16)


def qkv(g0, groups, rows, table, n1, vec, cosine, sine, pieces):
    total, width = n1.shape
    rb = 512
    pairs = width // 2
    grid = (total // rb,)
    blk = lambda w: pl.BlockSpec((rb, w), lambda i: (i, 0))
    out = kept((total, groups * GW), BF16)
    copies = piece_count(pieces)
    return pl.pallas_call(
        functools.partial(qkv_kernel, g0, len(pieces), rows),
        grid=grid,
        in_specs=[SMEM, blk(width), whole(vec.shape), blk(pairs), blk(pairs)] + [ANY] * len(pieces),
        out_specs=[blk(groups * GW)] * 3,
        out_shape=[out] * 3,
        scratch_shapes=[
            pltpu.VMEM((width, 3 * groups * GW), BF16),
            pltpu.VMEM((width, 2 * groups * GW), BF16),
            pltpu.VMEM((8, 2 * groups * GW), F32),
            pltpu.SemaphoreType.DMA((copies,)),
        ],
        compiler_params=params(grid, 24),
        cost_estimate=cost(total * width * groups * GW * 6, total * width * 8 + width * groups * GW * 6),
        name="qkv",
    )(table, *far(n1, vec, cosine, sine, *pieces))


def attend_kernel(q_ref, k_ref, v_ref, pos_ref, *rest):
    att_ref, lse_ref, wide_ref, mask = rest[-4:]
    g, r = pl.program_id(0), pl.program_id(1)
    rb, keys = q_ref.shape[0], k_ref.shape[0]
    here = pl.ds(pl.multiple_of(r * rb, rb), rb)

    @pl.when(g == 0)
    def _():
        row = lax.broadcasted_iota(jnp.int32, (rb, keys), 0) + r * rb
        col = lax.broadcasted_iota(jnp.int32, (rb, keys), 1)
        mask[here, :] = jnp.where(row == col, 0.0, jnp.broadcast_to(pos_ref[2:3, :], (rb, keys)))

    q = q_ref[...]
    k = k_ref[...]
    v = v_ref[...]
    total = jnp.zeros((rb, GW), F32)
    lane = lax.broadcasted_iota(jnp.int32, (rb, 128), 1)
    logs = jnp.zeros((rb, 128), F32)
    for h in range(GH):
        qm = jnp.where(packed_head_mask(h), q, jnp.zeros_like(q))
        scores = nt(qm, k) + mask[here, :]
        top = jnp.max(scores, axis=-1, keepdims=True)
        weight = jnp.exp2(scores - top)
        norm = jnp.sum(weight, axis=-1, keepdims=True)
        vm = jnp.where(natural_head_mask(h), v, jnp.zeros_like(v))
        total = total + nn(weight.astype(BF16), vm) * (1.0 / norm)
        logs = jnp.where(lane == h, top + jnp.log2(norm), logs)
    att_ref[...] = total.astype(BF16)
    wide_ref[...] = total
    lse_ref[...] = jnp.transpose(logs)[:8, :]


def attend(g0, full, q, k, v, pos, *att, rb=512):
    total, width = q.shape
    groups = width // GW
    grid = (groups, total // rb)
    return pl.pallas_call(
        attend_kernel,
        grid=grid,
        in_specs=[
            pl.BlockSpec((rb, GW), lambda g, r: (r, g)),
            pl.BlockSpec((total, GW), lambda g, r: (0, g)),
            pl.BlockSpec((total, GW), lambda g, r: (0, g)),
            whole((8, total)),
        ]
        + [ANY] * len(att),
        out_specs=[
            pl.BlockSpec((rb, GW), lambda g, r: (r, g + g0)),
            pl.BlockSpec((None, 8, rb), lambda g, r: (g, 0, r)),
            pl.BlockSpec((rb, GW), lambda g, r: (r, g)),
        ],
        out_shape=[
            kept((total, full), BF16),
            kept((groups, 8, total), F32),
            kept((total, width), F32),
        ],
        input_output_aliases={4: 0} if att else {},
        scratch_shapes=[pltpu.VMEM((total, total), F32)],
        compiler_params=params(grid, 32),
        cost_estimate=cost(total * total * width * 16, total * width * 8, total * total * 12),
        name="attend",
    )(*far(q, k, v, pos, *att))


PHI_SCALE = 0.3989422804014327
TAIL_SCALE = 0.44 * 0.7071067811865476
TAIL = (
    0.12411047596471954,
    0.12443560910041027,
    0.10865662380098591,
    0.10790671631036299,
    -0.010091621907114547,
    0.14834527631989725,
    -0.13897496529649409,
    0.03561197654899638,
)


def gelu_parts(h):
    t = 1.0 / (1.0 + TAIL_SCALE * jnp.abs(h))
    poly = TAIL[-1]
    for coefficient in TAIL[-2::-1]:
        poly = poly * t + coefficient
    bell = jnp.exp2((-0.5 * LOG2E) * (h * h))
    tail = poly * t * bell
    phi = jnp.where(h < 0, tail, 1.0 - tail)
    return h * phi, phi + h * (bell * PHI_SCALE)


def up_kernel(half, npieces, rows, table, count, *refs):
    if half == 0:
        att_ref, x_ref, cot_ref, vec_ref = refs[:4]
        pieces = refs[4 : 4 + npieces]
        mid_ref, n2_ref, gd_ref, act_ref, gp_ref, w, sem = refs[4 + npieces :]
    else:
        n2_ref, vec_ref = refs[:2]
        pieces = refs[2 : 2 + npieces]
        act_ref, gp_ref, w, sem = refs[-4:]
    rb, width = n2_ref.shape

    @pl.when(pl.program_id(0) == 0)
    def _():
        slots = table.shape[0] // 2
        copies = load_pieces(table, pieces, w, sem, rows, column=False)
        for start in (True, False):
            for number, copy in enumerate(copies):

                @pl.when(table[slots + number] == half)
                def _():
                    if start:
                        copy.start()
                    else:
                        copy.wait()

    if half == 0:
        slot = lax.broadcasted_iota(jnp.int32, (rb, 1), 0) + pl.program_id(0) * rb
        valid = jnp.where(slot < count[0], 1.0, 0.0)
        gd_ref[...] = (valid * cot_ref[...]).astype(BF16)
        branch = nn(att_ref[...], w[:, pl.ds(0, width)]) + vec_ref[V_OBIAS : V_OBIAS + 1, :width]
        middle = x_ref[...] + valid * branch
        mid_ref[...] = middle
        xhat, _ = normalize(middle)
        n2 = (xhat * vec_ref[V_MGAIN : V_MGAIN + 1, :width] + vec_ref[V_MSHIFT : V_MSHIFT + 1, :width]).astype(BF16)
        n2_ref[...] = n2
        place = width
    else:
        n2 = n2_ref[...]
        place = 0
    first = half * (w.shape[1] - width)
    step = 384
    for c in range(act_ref.shape[1] // step):
        cut = pl.ds(c * step, step)
        hidden = nn(n2, w[:, pl.ds(place + c * step, step)]) + vec_ref[V_UBIAS : V_UBIAS + 1, pl.ds(first + c * step, step)]
        act, slope = gelu_parts(hidden)
        act_ref[:, cut] = act.astype(BF16)
        gp_ref[:, cut] = slope.astype(BF16)


def up_first(rows, wide, table, count, att, x, cot, vec, pieces, rb=256):
    total, width = x.shape
    part = (width + wide) // 2
    grid = (total // rb,)
    blk = lambda w: pl.BlockSpec((rb, w), lambda i: (i, 0))
    return pl.pallas_call(
        functools.partial(up_kernel, 0, len(pieces), rows),
        grid=grid,
        in_specs=[SMEM, SMEM, blk(width), blk(width), blk(width), whole(vec.shape)] + [ANY] * len(pieces),
        out_specs=[blk(width), blk(width), blk(width), blk(part - width), blk(part - width)],
        out_shape=[
            kept((total, width), F32),
            kept((total, width), BF16),
            kept((total, width), BF16),
            kept((total, wide), BF16),
            kept((total, wide), BF16),
        ],
        scratch_shapes=[pltpu.VMEM((width, part), BF16), pltpu.SemaphoreType.DMA((piece_count(pieces),))],
        compiler_params=params(grid, 32),
        cost_estimate=cost(total * width * part * 2, total * width * 20, total * wide),
        name="up_first",
    )(table, count, *far(att, x, cot, vec, *pieces))


def up_second(rows, table, count, n2, act, slope, vec, pieces, rb=256):
    total, width = n2.shape
    wide = act.shape[1]
    part = (width + wide) // 2
    grid = (total // rb,)
    cols = pl.BlockSpec((pl.Element(rb), pl.Element(part)), lambda i: (i * rb, part - width))
    return pl.pallas_call(
        functools.partial(up_kernel, 1, len(pieces), rows),
        grid=grid,
        in_specs=[SMEM, SMEM, pl.BlockSpec((rb, width), lambda i: (i, 0)), whole(vec.shape)]
        + [ANY] * (len(pieces) + 2),
        out_specs=[cols, cols],
        out_shape=[kept((total, wide), BF16)] * 2,
        input_output_aliases={4 + len(pieces): 0, 5 + len(pieces): 1},
        scratch_shapes=[pltpu.VMEM((width, part), BF16), pltpu.SemaphoreType.DMA((piece_count(pieces),))],
        compiler_params=params(grid, 32),
        cost_estimate=cost(total * width * part * 2, total * width * 20, total * wide),
        name="up_second",
    )(table, count, *far(n2, vec, *pieces, act, slope))


def down_kernel(nup, ndown, rows, table, count, act_ref, gp_ref, mid_ref, cot_ref, gd_ref, vec_ref, *rest):
    ups = rest[:nup]
    downs = rest[nup : nup + ndown]
    (out_ref, gm_ref, gb_ref, ga_ref, gu_ref, sums_ref, ubsum_ref, w, wd, sem, sem_d) = rest[nup + ndown :]
    i = pl.program_id(0)
    rb, width = mid_ref.shape
    wide = act_ref.shape[1]

    @pl.when(i == 0)
    def _():
        first = load_pieces(table, downs, wd, sem_d, rows * (wide // width))
        second = load_pieces(table, ups, w, sem, rows)
        for copy in first + second:
            copy.start()
        for copy in first + second:
            copy.wait()
        sums_ref[...] = jnp.zeros_like(sums_ref)
        ubsum_ref[...] = jnp.zeros_like(ubsum_ref)

    slot = lax.broadcasted_iota(jnp.int32, (rb, 1), 0) + i * rb
    valid = jnp.where(slot < count[0], 1.0, 0.0)
    middle = mid_ref[...]
    cot = cot_ref[...]
    gd = gd_ref[...]
    lowered = nn(act_ref[...], wd[...]) + vec_ref[V_DBIAS : V_DBIAS + 1, :width]
    out_ref[...] = middle + valid * lowered
    step = 1024
    gn2 = jnp.zeros((rb, width), F32)
    for c in range(wide // step):
        cut = pl.ds(c * step, step)
        g = nt(gd, wd[cut, :]) * gp_ref[:, cut].astype(F32)
        g_low = g.astype(BF16)
        gu_ref[:, cut] = g_low
        ubsum_ref[0:1, cut] += jnp.sum(g_low.astype(F32), axis=0, keepdims=True)
        gn2 = gn2 + nt(g_low, w[:, pl.ds(width + c * step, step)])
    xhat, inverse = normalize(middle)
    sums_ref[0:1, :] += jnp.sum(gn2 * xhat, axis=0, keepdims=True)
    sums_ref[1:2, :] += jnp.sum(gn2, axis=0, keepdims=True)
    e = gn2 * vec_ref[V_MGAIN : V_MGAIN + 1, :width]
    back = (e - jnp.mean(e, axis=-1, keepdims=True) - xhat * jnp.mean(e * xhat, axis=-1, keepdims=True)) * inverse
    gmid = cot + back
    gm_ref[...] = gmid
    gb = (valid * gmid).astype(BF16)
    gb_ref[...] = gb
    sums_ref[2:3, :] += jnp.sum(gb.astype(F32), axis=0, keepdims=True)
    sums_ref[3:4, :] += jnp.sum(gd.astype(F32), axis=0, keepdims=True)
    ga_ref[...] = nt(gb, w[:, pl.ds(0, width)]).astype(BF16)


def down(rows, table, count, act, gp, mid, cot, gd, vec, ups, downs, rb=256):
    total, width = mid.shape
    wide = act.shape[1]
    grid = (total // rb,)
    blk = lambda w: pl.BlockSpec((rb, w), lambda i: (i, 0))
    return pl.pallas_call(
        functools.partial(down_kernel, len(ups), len(downs), rows),
        grid=grid,
        in_specs=[SMEM, SMEM, blk(wide), blk(wide), blk(width), blk(width), blk(width), whole(vec.shape)]
        + [ANY] * (len(ups) + len(downs)),
        out_specs=[blk(width), blk(width), blk(width), blk(width), blk(wide), whole((8, width)), whole((8, wide))],
        out_shape=[
            kept((total, width), F32),
            kept((total, width), F32),
            kept((total, width), BF16),
            kept((total, width), BF16),
            kept((total, wide), BF16),
            kept((8, width), F32),
            kept((8, wide), F32),
        ],
        scratch_shapes=[
            pltpu.VMEM((width, width + wide), BF16),
            pltpu.VMEM((wide, width), BF16),
            pltpu.SemaphoreType.DMA((piece_count(ups),)),
            pltpu.SemaphoreType.DMA((piece_count(downs),)),
        ],
        compiler_params=params(grid, 44),
        cost_estimate=cost(total * width * (width + 3 * wide) * 2, total * (width * 20 + wide * 6)),
        name="down",
    )(table, count, *far(act, gp, mid, cot, gd, vec, *ups, *downs))


def grad_kernel(pairs, mids, reps, rows, core, *rest):
    keep_ref, send_ref = rest[-2:]
    part = core[0]

    def spot(parity, mid, rep):
        return jnp.where(parity == 0, mid, rep), jnp.where(parity == 0, rep, mid)

    each = keep_ref.shape[-1]
    offset = 0
    for at, bt in pairs:
        a, b_ref = rest[at][...], rest[bt]
        begin = 0
        while begin < b_ref.shape[1]:
            column = offset + begin
            step = min(b_ref.shape[1] - begin, each - column % each, 768)
            result = tn(a, b_ref[:, pl.ds(begin, step)])
            rep, cut = column // each, pl.ds(column % each, step)
            for pair in range(a.shape[1] // (2 * rows)):
                low = result[pair * 2 * rows : pair * 2 * rows + rows]
                high = result[pair * 2 * rows + rows : (pair + 1) * 2 * rows]
                zz, mid = pair // mids, pair % mids
                one, two = spot(part, mid, rep)
                keep_ref[one, two, zz, :, cut] = jnp.where(part == 0, low, high).astype(BF16)
                one, two = spot(1 - part, mid, rep)
                send_ref[one, two, zz, :, cut] = jnp.where(part == 0, high, low).astype(BF16)
            begin += step
        offset += b_ref.shape[1]


def operands(pairs):
    arrays, index = [], []
    for pair in pairs:
        spots = []
        for array in pair:
            if not any(array is other for other in arrays):
                arrays.append(array)
            spots.append([array is other for other in arrays].index(True))
        index.append(spots)
    lefts = {one for one, _ in index}
    return arrays, index, lefts


def weight_grad(core, pairs, layout, name, lasting=False):
    slow, mids, reps = layout
    arrays, index, lefts = operands(pairs)
    total, height = pairs[0][0].shape
    width = sum(b.shape[1] for _, b in pairs)
    rows = height // (slow * mids * 2)
    chunk = 384 if 384 % (2 * mids * rows) == 0 else 2 * mids * rows
    slows = chunk // (2 * mids * rows)
    grid = (height // chunk,)
    shape = (mids, reps, slow, rows, width // reps)
    out = jax.ShapeDtypeStruct(shape, BF16)
    spec = pl.BlockSpec((mids, reps, slows, rows, width // reps), lambda i: (0, 0, i, 0, 0))
    return pl.pallas_call(
        functools.partial(grad_kernel, index, mids, reps, rows),
        grid=grid,
        in_specs=[SMEM]
        + [
            pl.BlockSpec((total, chunk), lambda i: (0, i)) if n in lefts else whole(a.shape)
            for n, a in enumerate(arrays)
        ],
        out_specs=[spec, spec],
        out_shape=[kept(shape, BF16) if lasting else out, out],
        compiler_params=params(grid, 40),
        cost_estimate=cost(total * height * width * 2, total * (height + width) * 2 + height * width * 2),
        name=name,
    )(core, *far(*arrays))


def plain_grad_kernel(pairs, *rest):
    out_ref = rest[-1]
    offset = 0
    for at, bt in pairs:
        a, b_ref = rest[at][...], rest[bt]
        step = min(b_ref.shape[1], 768)
        for c in range(b_ref.shape[1] // step):
            out_ref[:, pl.ds(offset + c * step, step)] = tn(a, b_ref[:, pl.ds(c * step, step)])
        offset += b_ref.shape[1]


def plain_grad(pairs, name):
    arrays, index, lefts = operands(pairs)
    total, height = pairs[0][0].shape
    width = sum(b.shape[1] for _, b in pairs)
    chunk = 384
    grid = (height // chunk,)
    return pl.pallas_call(
        functools.partial(plain_grad_kernel, index),
        grid=grid,
        in_specs=[
            pl.BlockSpec((total, chunk), lambda i: (0, i)) if n in lefts else whole(a.shape)
            for n, a in enumerate(arrays)
        ],
        out_specs=pl.BlockSpec((chunk, width), lambda i: (i, 0)),
        out_shape=jax.ShapeDtypeStruct((height, width), F32),
        compiler_params=params(grid, 63),
        cost_estimate=cost(total * height * width * 2, total * (height + width) * 2 + height * width * 4),
        name=name,
    )(*arrays)


def unrotate(grad, cosine, sine):
    first, second = grad[:, :HALF], grad[:, HALF:]
    return first * cosine + second * sine, second * cosine - first * sine


def angle_grad(grad, rotated):
    return grad[:, HALF:] * rotated[:, :HALF] - grad[:, :HALF] * rotated[:, HALF:]


def back_kernel(q_ref, k_ref, v_ref, do_ref, lse_ref, wide_ref, aux_ref, cos_ref, sin_ref,
                g_ref, fsum_ref, bsum_ref, ds_s, p_s, dk_s, dv_s):
    r = pl.program_id(0)
    rb, keys = q_ref.shape[0], k_ref.shape[0]
    here = pl.ds(pl.multiple_of(r * rb, rb), rb)
    q = q_ref[...]
    k = k_ref[...]
    v = v_ref[...]
    do = do_ref[...]
    zero = jnp.zeros_like(q)
    product = do.astype(F32) * wide_ref[...]
    high = product.astype(BF16)
    low = (product - high.astype(F32)).astype(BF16)
    lane = lax.broadcasted_iota(jnp.int32, (16, GW), 1)
    pick_head = jnp.where(lane // HD == lax.broadcasted_iota(jnp.int32, (16, GW), 0), 1.0, 0.0).astype(BF16)
    inner = nt(pick_head, high) + nt(pick_head, low)
    key = lax.broadcasted_iota(jnp.int32, (keys, rb), 0)
    query = lax.broadcasted_iota(jnp.int32, (keys, rb), 1) + r * rb
    mask = jnp.where(key == query, 0.0, jnp.broadcast_to(aux_ref[:, 2:3], (keys, rb)))
    dq = jnp.zeros((rb, GW), F32)
    qms, doms = [], []
    for h in range(GH):
        qm = jnp.where(packed_head_mask(h), q, zero)
        dom = jnp.where(natural_head_mask(h), do, zero)
        qms.append(qm)
        doms.append(dom)
        soft = jnp.exp2(nt(k, qm) + mask - lse_ref[h : h + 1, :])
        ds = (soft * (nt(v, dom) - inner[h : h + 1, :])).astype(BF16)
        cut = pl.ds(h * rb, rb)
        ds_s[:, cut] = ds
        p_s[:, cut] = soft.astype(BF16)
        km = jnp.where(packed_head_mask(h), k, jnp.zeros_like(k))
        dq = dq + tn(ds, km)
    dk = nn(ds_s[...], jnp.concatenate(qms, axis=0)) * (1.0 / LOG2E)
    dv = nn(p_s[...], jnp.concatenate(doms, axis=0))

    perm = group_perm(True)
    cosine, sine = cos_ref[here, :], sin_ref[here, :]
    dq = dq * (HD**-0.5)
    ang = angle_grad(dq, q.astype(F32) * (HD**0.5 / LOG2E))
    first, second = unrotate(dq, cosine, sine)
    gq = nn(jnp.concatenate([first.astype(BF16), second.astype(BF16)], axis=1), perm)
    g_ref[here, pl.ds(0, GW)] = gq.astype(BF16)
    col, row = aux_ref[here, 0:1], aux_ref[here, 1:2]
    fcol = jnp.sum(ang * col, axis=0, keepdims=True)
    frow = jnp.sum(ang * row, axis=0, keepdims=True)
    qsum = jnp.sum(gq, axis=0, keepdims=True)

    @pl.when(r == 0)
    def _():
        dk_s[...] = dk
        dv_s[...] = dv
        fsum_ref[...] = jnp.zeros_like(fsum_ref)
        fsum_ref[0:1, pl.ds(0, HALF)] = fcol
        fsum_ref[1:2, pl.ds(0, HALF)] = frow
        bsum_ref[0:1, pl.ds(0, GW)] = qsum

    @pl.when(r > 0)
    def _():
        dk_s[...] += dk
        dv_s[...] += dv
        fsum_ref[0:1, pl.ds(0, HALF)] += fcol
        fsum_ref[1:2, pl.ds(0, HALF)] += frow
        bsum_ref[0:1, pl.ds(0, GW)] += qsum

    @pl.when(r == pl.num_programs(0) - 1)
    def _():
        dkf = dk_s[...]
        angk = angle_grad(dkf, k.astype(F32))
        fsum_ref[0:1, pl.ds(0, HALF)] += jnp.sum(angk * aux_ref[:, 0:1], axis=0, keepdims=True)
        fsum_ref[1:2, pl.ds(0, HALF)] += jnp.sum(angk * aux_ref[:, 1:2], axis=0, keepdims=True)
        one, two = unrotate(dkf, cos_ref[...], sin_ref[...])
        gk = nn(jnp.concatenate([one.astype(BF16), two.astype(BF16)], axis=1), perm)
        g_ref[:, pl.ds(GW, GW)] = gk.astype(BF16)
        bsum_ref[0:1, pl.ds(GW, GW)] = jnp.sum(gk, axis=0, keepdims=True)
        gv = dv_s[...].astype(BF16)
        g_ref[:, pl.ds(2 * GW, GW)] = gv
        lane = lax.broadcasted_iota(jnp.int32, (HALF, 2 * HALF), 1)
        pair = lax.broadcasted_iota(jnp.int32, (HALF, 2 * HALF), 0)
        sums = fsum_ref[:, pl.ds(0, HALF)]
        spread = [
            jnp.dot(sums, jnp.where(lane == 2 * pair + odd, 1.0, 0.0), precision=lax.Precision.HIGHEST)
            for odd in range(2)
        ]
        fsum_ref[0:1, :] = spread[0][0:1] + spread[1][1:2]
        bsum_ref[0:1, pl.ds(2 * GW, GW)] = jnp.sum(gv.astype(F32), axis=0, keepdims=True)


def attend_back(g0, l0, q, k, v, do, lse, wide, aux, cosine, sine, rb=512):
    total = q.shape[0]
    grid = (total // rb,)
    return pl.pallas_call(
        back_kernel,
        grid=grid,
        in_specs=[
            pl.BlockSpec((rb, GW), lambda r: (r, l0)),
            pl.BlockSpec((total, GW), lambda r: (0, l0)),
            pl.BlockSpec((total, GW), lambda r: (0, l0)),
            pl.BlockSpec((rb, GW), lambda r: (r, g0)),
            pl.BlockSpec((None, 8, rb), lambda r: (l0, 0, r)),
            pl.BlockSpec((rb, GW), lambda r: (r, l0)),
            whole((total, 128)),
            pl.BlockSpec((total, HALF), lambda r: (0, g0)),
            pl.BlockSpec((total, HALF), lambda r: (0, g0)),
        ],
        out_specs=[whole((total, 3 * GW)), whole((8, GW)), whole((8, 3 * GW))],
        out_shape=[
            kept((total, 3 * GW), BF16),
            jax.ShapeDtypeStruct((8, GW), F32),
            jax.ShapeDtypeStruct((8, 3 * GW), F32),
        ],
        scratch_shapes=[
            pltpu.VMEM((total, GH * rb), BF16),
            pltpu.VMEM((total, GH * rb), BF16),
            pltpu.VMEM((total, GW), F32),
            pltpu.VMEM((total, GW), F32),
        ],
        compiler_params=params(grid, 48),
        cost_estimate=cost(total * total * GW * 40, total * GW * 20, total * total * GH),
        name="attend_back",
    )(*far(q, k, v, do, lse, wide, aux, cosine, sine))


def final_kernel(count, counts, rows, table_one, table_two, x_ref, gm_ref, vec_ref, *rest):
    grads, place = rest[:count], count
    pieces = []
    for number in counts:
        pieces.append(rest[place : place + number])
        place += number
    out_ref, sums_ref = rest[place : place + 2]
    weights = rest[place + 2 : place + 2 + len(counts)]
    sems = rest[place + 2 + len(counts) :]

    @pl.when(pl.program_id(0) == 0)
    def _():
        copies = []
        for table, p, w, sem in zip((table_one, table_two), pieces, weights, sems):
            copies += load_pieces(table, p, w, sem, rows)
        for copy in copies:
            copy.start()
        for copy in copies:
            copy.wait()
        sums_ref[...] = jnp.zeros_like(sums_ref)

    e = jnp.zeros(x_ref.shape, F32)
    group = 0
    for w in weights:
        for g in range(w.shape[1] // (3 * GW)):
            e = e + nt(grads[group][...], w[:, pl.ds(g * 3 * GW, 3 * GW)])
            group += 1
    xhat, inverse = normalize(x_ref[...])
    sums_ref[0:1, :] += jnp.sum(e * xhat, axis=0, keepdims=True)
    sums_ref[1:2, :] += jnp.sum(e, axis=0, keepdims=True)
    eg = e * vec_ref[V_GAIN : V_GAIN + 1, : x_ref.shape[1]]
    back = (eg - jnp.mean(eg, axis=-1, keepdims=True) - xhat * jnp.mean(eg * xhat, axis=-1, keepdims=True)) * inverse
    out_ref[...] = gm_ref[...] + back


def final(rows, widths, tables, x, gmid, vec, grads, piece_sets, rb=256):
    total, width = x.shape
    grid = (total // rb,)
    blk = lambda w: pl.BlockSpec((rb, w), lambda i: (i, 0))
    pieces = [p for ps in piece_sets for p in ps]
    return pl.pallas_call(
        functools.partial(final_kernel, len(grads), [len(ps) for ps in piece_sets], rows),
        grid=grid,
        in_specs=[SMEM, SMEM, blk(width), blk(width), whole(vec.shape)]
        + [blk(g.shape[1]) for g in grads]
        + [ANY] * len(pieces),
        out_specs=[blk(width), whole((8, width))],
        out_shape=[kept((total, width), F32), jax.ShapeDtypeStruct((8, width), F32)],
        scratch_shapes=[pltpu.VMEM((width, w), BF16) for w in widths]
        + [pltpu.SemaphoreType.DMA((piece_count(ps),)) for ps in piece_sets],
        compiler_params=params(grid, 32),
        cost_estimate=cost(total * width * width * 6, total * width * 20 + width * width * 6),
        name="final",
    )(*tables, *far(x, gmid, vec), *far(*grads), *far(*pieces))


FOLD = (
    ("bias", 0, 0), ("value", 1, 0), ("freqs", 1, 64), ("gain", 2, 0), ("shift", 2, 64),
    ("obias", 3, 0), ("dbias", 3, 64), ("mgain", 4, 0), ("mshift", 4, 64), ("ubias", 5, 0),
)


def fold_kernel(groups, owners, spot, *refs):
    out_ref = refs[-1]
    fsums, bsums = refs[:groups], refs[groups : 2 * groups]
    mid_ref, wide_ref, first_ref = refs[2 * groups : 2 * groups + 3]
    lines = {
        "bias": [(b, 0, part * GW, GW) for part in range(2) for b in bsums],
        "value": [(b, 0, 2 * GW, GW) for b in bsums],
        "freqs": [(f, 0, 0, GW) for f in fsums],
        "gain": [(first_ref, 0, 0, first_ref.shape[1])],
        "shift": [(first_ref, 1, 0, first_ref.shape[1])],
        "mgain": [(mid_ref, 0, 0, mid_ref.shape[1])],
        "mshift": [(mid_ref, 1, 0, mid_ref.shape[1])],
        "obias": [(mid_ref, 2, 0, mid_ref.shape[1])],
        "dbias": [(mid_ref, 3, 0, mid_ref.shape[1])],
        "ubias": [(wide_ref, 0, 0, wide_ref.shape[1])],
    }
    out_ref[...] = jnp.zeros_like(out_ref)
    for name, row, lane in FOLD:
        total = sum(length for _, _, _, length in lines[name])
        each = total // owners
        for owner in range(owners):
            begin, end = owner * each, (owner + 1) * each
            offset = 0
            for ref, line, start, length in lines[name]:
                low, high = max(begin, offset), min(end, offset + length)
                while low < high:
                    place = row * 128 + lane + low - begin
                    at = start + low - offset
                    lead, last = spot(owner)
                    out_ref[(*lead, slice(last, last + 1), slice(place, place + high - low))] = (
                        ref[line : line + 1, at : at + high - low]
                    )
                    low = high
                offset += length


def fold(owners, cube, fsums, bsums, mid, wide, first):
    arrays = [*fsums, *bsums, mid, wide, first]
    shape, spot = (owners, 1024), lambda owner: ((), owner)
    if cube:
        shape, spot = (2, 2, 4, 1024), lambda owner: ((owner % 2, owner // 2 % 2), owner // 4)
    return pl.pallas_call(
        functools.partial(fold_kernel, len(fsums), owners, spot),
        in_specs=[pl.BlockSpec(memory_space=pltpu.VMEM)] * len(arrays),
        out_specs=pl.BlockSpec(memory_space=pltpu.VMEM),
        out_shape=jax.ShapeDtypeStruct(shape, F32),
        cost_estimate=cost(0, 100000),
        name="fold",
    )(*arrays)


def half_column(pair, swap, place, width):
    mine, other = pair
    each = mine.shape[1]
    cut = pl.ds(place % each, width)
    a, b = (mine, other) if place < each else (other, mine)
    return jnp.where(swap, b[:, cut], a[:, cut])


def finish_kernel(rep, *refs):
    outup, downs, (out_ref, up_ref, down_ref) = refs[:2], refs[2:4], refs[4:]
    swap, step, width = rep[0] == 1, GW // 2, out_ref.shape[1]
    for place in range(0, outup[0].shape[1] * 2, step):
        value = half_column(outup, swap, place, step)
        if place < width:
            out_ref[:, pl.ds(place, step)] = value
        else:
            up_ref[:, pl.ds(place - width, step)] = value
    for place in range(0, down_ref.shape[1], step):
        down_ref[:, pl.ds(place, step)] = half_column(downs, swap, place, step)


def finish(rep, outup, downs):
    width = downs[0].shape[1] * 2
    rows = outup[0].shape[0]
    shapes = [(rows, width), (rows, outup[0].shape[1] * 2 - width), (downs[0].shape[0], width)]
    return pl.pallas_call(
        finish_kernel,
        in_specs=[SMEM] + [NEAR] * 4,
        out_specs=[NEAR] * 3,
        out_shape=[jax.ShapeDtypeStruct(shape, F32) for shape in shapes],
        cost_estimate=cost(0, 4000000),
        name="finish",
    )(rep, *outup, *downs)


def finish_inward_kernel(groups, rep, *refs):
    halves, in_ref = refs[:-1], refs[-1]
    swap, step, group, total = rep[0] == 1, GW // 2, 0, in_ref.shape[1] // 3
    for n, count in enumerate(groups):
        for g in range(count):
            for part in range(3):
                for half in range(2):
                    value = half_column(halves[2 * n : 2 * n + 2], swap, (g * 3 + part) * GW + half * step, step)
                    in_ref[:, pl.ds(part * total + group * GW + half * step, step)] = value
            group += 1


def finish_inward(groups, rep, pairs):
    arrays = [a for pair in pairs for a in pair]
    return pl.pallas_call(
        functools.partial(finish_inward_kernel, groups),
        in_specs=[SMEM] + [NEAR] * len(arrays),
        out_specs=NEAR,
        out_shape=jax.ShapeDtypeStruct((arrays[0].shape[0], 3 * GW * sum(groups)), F32),
        cost_estimate=cost(0, 1000000),
        name="finish_inward",
    )(rep, *arrays)


def place():
    me = lax.axis_index("fsdp")
    return lax.axis_index("rep"), me // 4, (me // 2) % 2, me % 2


def move(value, step):
    moves = []
    for i in range(32):
        y, z, x, c = step(i // 16, (i // 4) % 4, (i // 2) % 2, i % 2)
        moves.append((i, y * 16 + z * 4 + x * 2 + c))
    return lax.ppermute(value, ("rep", "fsdp"), moves)


def across_core(value):
    return move(value, lambda y, z, x, c: (y, z, x, 1 - c))


def across_x(value):
    return move(value, lambda y, z, x, c: (y, z, 1 - x, c))


def across_rep(value):
    return move(value, lambda y, z, x, c: (1 - y, z, x, c))


def across_near(value):
    return move(value, lambda y, z, x, c: (y, z ^ 1, x, c))


def across_far(value):
    return move(value, lambda y, z, x, c: (y, z ^ 2, x, c))


def across_third(value):
    return move(value, lambda y, z, x, c: (y, z ^ 3, x, c))


def across_both(value):
    return move(value, lambda y, z, x, c: (1 - y, z, 1 - x, c))


def across_one(value):
    return move(value, lambda y, z, x, c: (y, z, 1 - x, c) if c == 0 else (1 - y, z, x, c))


def across_two(value):
    return move(value, lambda y, z, x, c: (1 - y, z, x, c) if c == 0 else (y, z, 1 - x, c))


def pick(array, index):
    return lax.dynamic_index_in_dim(array, index, 0, keepdims=False)


def pick_two(array, index):
    return lax.dynamic_slice_in_dim(array, 2 * index, 2, 0)


def piece_tables():
    y, z, x, c = place()
    slot = jnp.arange(4, dtype=jnp.int32)
    here, swap = (lambda core, a, b: a), (lambda core, a, b: jnp.where(core == 0, a, b))
    tables = []
    for choose in (here, swap):
        owners, halves = [], []
        for core in (c, 1 - c):
            for mid, half in ((x, y), (choose(core, x, 1 - x), choose(core, 1 - y, y)),
                              (choose(core, 1 - x, x), choose(core, y, 1 - y)), (1 - x, 1 - y)):
                owners.append((z ^ slot) * 4 + mid * 2 + core)
                halves.append(jnp.broadcast_to(half, (4,)))
        tables.append(jnp.concatenate(owners + halves).astype(jnp.int32))
    return tables


def first_of_owner(table, n):
    slots = table.shape[0] // 2
    match = table[None, :slots] == jnp.arange(n, dtype=jnp.int32)[:, None]
    return jnp.min(jnp.where(match, jnp.arange(slots, dtype=jnp.int32)[None, :], slots), axis=1)


class Reduce:
    stages = (across_core, across_one, across_two, across_far, across_near, across_rep)

    def __init__(self, keep, send):
        self.keep, self.first, self.got, self.stage = keep, send, [], 0
        self.out = None

    def sends(self):
        return [(self.stages[self.stage], self.send())]

    def takes(self, values):
        self.take(values[0])

    def base(self, count, one, two=None, cut=None):
        step = lambda a, i: a if i is None else pick(a, i)
        total = None
        for source, used in ((self.keep, 0), (self.got[0], 0), *((g, n + 1) for n, g in enumerate(self.got[1:count]))):
            value = source
            if used < 1:
                value = step(value, one)
            if used < 2:
                value = step(value, two)
            if cut is not None:
                value = cut(value)
            value = value.astype(F32)
            total = value if total is None else total + value
        return total

    def level(self, index):
        return self.base(3, self.i1, self.i2, lambda a: pick(a, index)) + pick(self.got[3], index % 2).astype(F32)

    def send(self):
        y, z, x, c = place()
        self.i1, self.i2 = jnp.where(c == 0, x, y), jnp.where(c == 0, y, x)
        if self.stage == 0:
            return self.first
        if self.stage == 1:
            return self.base(1, 1 - self.i1).astype(BF16)
        if self.stage == 2:
            return self.base(2, self.i1, 1 - self.i2).astype(BF16)
        if self.stage == 3:
            return self.base(3, self.i1, self.i2, lambda a: pick_two(a, 1 - z // 2)).astype(BF16)
        if self.stage == 4:
            return self.level(z ^ 1).astype(BF16)
        self.total = self.level(z) + self.got[4].astype(F32)
        return self.total

    def take(self, value):
        self.stage += 1
        if self.stage == 6:
            self.out = (self.total, value)
        else:
            self.got.append(value)


class SmallReduce:
    stages = (across_core, across_x, across_far, across_near, across_rep)

    def __init__(self, cube):
        self.part, self.stage = cube, 0

    sends, takes = Reduce.sends, Reduce.takes

    def send(self):
        y, z, x, c = place()
        if self.stage == 4:
            self.kept = self.part
            return self.part
        cut = pick_two if self.stage == 2 else pick
        index = (c, x, z // 2, z % 2)[self.stage]
        self.kept = cut(self.part, index)
        return cut(self.part, 1 - index)

    def take(self, value):
        self.stage += 1
        self.part = self.kept + value
        self.out = self.part


class QuickGather:
    def __init__(self, half):
        self.part, self.stage = half, 0

    def sends(self):
        if self.stage == 0:
            return [(f, self.part) for f in (across_near, across_far, across_third)]
        if self.stage == 1:
            return [(f, self.part) for f in (across_rep, across_x, across_both, across_core)]
        return [(across_core, part) for part in self.beside]

    def takes(self, values):
        self.stage += 1
        if self.stage == 1:
            self.part = jnp.concatenate([self.part, *values])
        elif self.stage == 2:
            self.beside, self.other = values[:3], values[3]
        else:
            self.out = [self.part, *self.beside, self.other, *values]


class Gather:
    def __init__(self, half, cuts=()):
        self.part, self.stage, self.cuts, self.got = half, 0, cuts, []

    def sends(self):
        if self.stage == 1 and self.cuts:
            bounds = (0, *self.cuts, self.part.shape[2])
            return [(across_far, self.part[:, :, bounds[len(self.got)] : bounds[len(self.got) + 1]])]
        if self.stage < 3:
            return [((across_near, across_far, across_two)[self.stage], self.part)]
        if self.stage == 3:
            return [(across_one, self.part), (across_one, self.two), (across_core, self.part), (across_core, self.two)]
        return [(across_core, part) for part in self.one]

    def takes(self, values):
        if self.stage == 1:
            self.got += values
            if len(self.got) <= len(self.cuts):
                return
            values = [jnp.concatenate(self.got, axis=2)] if self.cuts else values
        self.stage += 1
        if self.stage < 3:
            self.part = jnp.concatenate([self.part, values[0]])
        elif self.stage == 3:
            self.two = values[0]
        elif self.stage == 4:
            self.one, self.other = values[:2], values[2:]
        else:
            self.out = [self.part, self.two, *self.one, *self.other, *values]


def step(movers, kernel=None, *inputs):
    sends = [m.sends() for m in movers]
    inputs, arrays = lax.optimization_barrier((inputs, [[a for _, a in s] for s in sends]))
    got = [[f(a) for (f, _), a in zip(s, each)] for s, each in zip(sends, arrays)]
    outs = kernel(*inputs) if kernel is not None else ()
    outs, got = lax.optimization_barrier((outs, got))
    for m, g in zip(movers, got):
        m.takes(g)
    return outs


def group_columns(weight, g0, ng, width):
    cuts = []
    for g in range(g0, g0 + ng):
        cuts += [weight[:, part * width + g * GW : part * width + (g + 1) * GW] for part in range(3)]
    return jnp.concatenate(cuts, axis=1)


def small_block(smalls, lanes):
    total = None
    for row, vector in enumerate(smalls):
        block = jnp.pad(vector[None, :], ((row, SMALL_ROWS - 1 - row), (0, lanes - vector.shape[0])))
        total = block if total is None else total + block
    return total


class Done:
    def __init__(self, out):
        self.out = out


def local(tuned, n, tokens, pre_gain, pre_shift, inward_weight, inward_bias, rotary_freqs, outward_weight,
          outward_bias, mlp_gain, mlp_shift, up_weight, up_bias, down_weight, down_bias, keep_mask, kept_counts,
          patch_rows, patch_cols, cotangent):
    total, width = tokens.shape
    groups = width // GW
    wide = up_weight.shape[1]
    rows = width // n
    smalls = [pre_gain, pre_shift, inward_bias, rotary_freqs, outward_bias, mlp_gain, mlp_shift, up_bias, down_bias]
    lengths = [s.shape[0] for s in smalls]
    slot = jnp.arange(total, dtype=jnp.int32)
    count = kept_counts
    key_bias = jnp.where((slot < count[0]) & (keep_mask[0] == 1), 0.0, NEG).astype(F32)
    lines = [patch_cols[0].astype(F32), patch_rows[0].astype(F32), key_bias]
    pos = jnp.stack(lines + [jnp.zeros_like(key_bias)] * 5)
    core = (lax.axis_index("fsdp") % 2).astype(jnp.int32)[None]
    rep = lax.axis_index("rep").astype(jnp.int32)[None]

    if tuned:
        shards = pack(rep, inward_weight, outward_weight, up_weight, down_weight, smalls)
        first, second, outup, downs = QuickGather(shards[0]), Gather(shards[1]), Gather(shards[2], (640,)), Gather(shards[3])
        quick, table = piece_tables()
        order = first_of_owner(quick, n)
        step([first])
        step([first, second])
        step([first])
        load = skip = rows
        small_pieces = first.out
    else:
        gather = lambda a: lax.all_gather(a, "fsdp", axis=0, tiled=True)
        small = small_block(smalls, 3 * GW // 2)
        quick = table = jnp.array([0, 0, 0, 1], jnp.int32)
        order = jnp.arange(n, dtype=jnp.int32)
        load, skip = width, SMALL_ROWS
        small_pieces = [jnp.pad(gather(small[None]), ((0, 0), (skip, 0), (0, 0)))]
        weights = [group_columns(inward_weight, 0, 1, width), group_columns(inward_weight, 1, groups - 1, width),
                   jnp.concatenate([outward_weight, up_weight], axis=1), down_weight]
        first, second, outup, downs = [Done([gather(w)[None]]) for w in weights]
        outup = Done([half[None] for half in jnp.split(outup.out[0][0], 2, axis=1)])

    def run(movers, kernel, *inputs):
        return step(movers, kernel, *inputs) if tuned else kernel(*inputs)

    part = functools.partial
    n1, cosine, sine, vec, aux = run([second, outup], part(prologue, lengths, n, skip), order, tokens, pos, small_pieces)

    q0, k0, v0 = run([second, outup], part(qkv, 0, 1, load), quick, n1, vec, cosine, sine, first.out)
    att, lse0, wide0 = run([second, outup], part(attend, 0, width), q0, k0, v0, pos)
    if tuned:
        step([second])
    q1, k1, v1 = run([outup, downs], part(qkv, 1, groups - 1, load), table, n1, vec, cosine, sine, second.out)
    att, lse1, wide1 = run([outup, downs], part(attend, 1, width), q1, k1, v1, pos, att)
    if tuned:
        step([outup])
    middle, n2, gd, act, slope = run(
        [downs], part(up_first, load, wide), table, count, att, tokens, cotangent, vec, outup.out
    )
    act, slope = run([downs], part(up_second, load), table, count, n2, act, slope, vec, outup.out)

    layout = (n // 4, 2, 2)

    def gradient(name, pairs):
        if tuned:
            return weight_grad(core, pairs, layout, name, name == "in_grad0")
        return lax.psum(lax.psum_scatter(plain_grad(pairs, name), "fsdp", scatter_dimension=0, tiled=True), "rep")

    def reduction(movers, name, pairs):
        out = run(movers, part(gradient, name), pairs)
        return Reduce(*out) if tuned else Done(out)

    r_down = reduction([downs], "down_grad", [(act, gd)])
    outputs, gmid, gb, ga, gu, sums, ubsum = run(
        [r_down], part(down, load), table, count, act, slope, middle, cotangent, gd, vec, outup.out, downs.out
    )
    r_up = reduction([r_down], "up_grad", [(att, gb), (n2, gu)])
    backs = []
    heads = ((0, 0, q0, k0, v0, lse0, wide0), (1, 0, q1, k1, v1, lse1, wide1), (2, 1, q1, k1, v1, lse1, wide1))

    def back(movers, which):
        g0, l0, q, k, v, lse, att_wide = heads[which]
        backs.append(run(movers, part(attend_back, g0, l0), q, k, v, ga, lse, att_wide, aux, cosine, sine))

    def in_gradient(movers, name, which):
        return reduction(movers, name, [(n1, backs[g][0]) for g in which])

    back([r_down, r_up], 0)
    back([r_down, r_up], 1)
    r_in0 = in_gradient([r_down, r_up], "in_grad0", (0, 1))
    if tuned:
        step([r_in0])
    back([r_down, r_up, r_in0], 2)
    r_in1 = in_gradient([r_up, r_in0], "in_grad1", (2,))
    grad_tokens, first_sums = run(
        [r_up, r_in0, r_in1], part(final, load, [3 * GW, 3 * GW * (groups - 1)]),
        (quick, table), tokens, gmid, vec, [b[0] for b in backs], [first.out, second.out]
    )
    small_sums = fold(n, tuned, [b[1] for b in backs], [b[2] for b in backs], sums, ubsum, first_sums)
    if tuned:
        r_small = SmallReduce(small_sums)
        step([r_small, r_in0, r_in1])
        step([r_small, r_in0, r_in1])
        step([r_small, r_in1])
        step([r_small, r_in1])
        d_out, d_up, d_down = step([r_small, r_in1], finish, rep, r_up.out, r_down.out)
        mine = r_small.out
        d_inward = finish_inward((2, 1), rep, [r_in0.out, r_in1.out])
    else:
        mine = lax.psum(lax.psum_scatter(small_sums, "fsdp", scatter_dimension=0, tiled=True), "rep")[0]
        blocks = [r.out[:, 3 * g * GW : 3 * (g + 1) * GW] for r, ng in ((r_in0, 2), (r_in1, 1)) for g in range(ng)]
        d_inward = jnp.concatenate([b[:, p * GW : (p + 1) * GW] for p in range(3) for b in blocks], axis=1)
        d_out, d_up, d_down = r_up.out[:, :width], r_up.out[:, width:], r_down.out
    each = width // n
    line = {name: mine[row * 128 + lane :] for name, row, lane in FOLD}
    o_bias, o_ubias = line["bias"][: 2 * each], line["ubias"][: wide // n]
    o_vbias, o_freqs, o_gain, o_shift, o_obias, o_mgain, o_mshift, o_dbias = [
        line[name][:each] for name in ("value", "freqs", "gain", "shift", "obias", "mgain", "mshift", "dbias")
    ]
    return (outputs, grad_tokens, o_gain, o_shift, d_inward, o_bias, o_vbias, o_freqs, d_out, o_obias,
            o_mgain, o_mshift, d_up, o_ubias, d_down, o_dbias)


def solution(mesh):
    n = mesh.shape["fsdp"]
    tuned = mesh.shape["rep"] == 2 and n == 16
    row = P(("rep", "fsdp"), None)
    vec, mat = P("fsdp"), P("fsdp", None)
    return jax.shard_map(
        functools.partial(local, tuned, n),
        mesh=mesh,
        in_specs=(row, vec, vec, mat, vec, vec, mat, vec, vec, vec, mat, vec, mat, vec, row,
                  P(("rep", "fsdp")), row, row, row),
        out_specs=(row, row, vec, vec, mat, vec, vec, vec, mat, vec, vec, vec, mat, vec, mat, vec),
        check_vma=False,
    )
```

```python
import functools
import math

import jax
import jax.numpy as jnp
from jax import lax
from jax.experimental import pallas as pl
from jax.experimental.pallas import tpu as pltpu
from jax.sharding import PartitionSpec as P

HD = 64
LOG2E = 1.4426950408889634
EPS = 1e-06
NEG = -1e30
F32 = jnp.float32
BF16 = jnp.bfloat16
GH = 4
GW = GH * HD
HALF = GW // 2


def dims(lhs, rhs, lhs_axis, rhs_axis):
    return lax.dot_general(
        lhs, rhs, (((lhs_axis,), (rhs_axis,)), ((), ())), preferred_element_type=F32
    )


def nn(lhs, rhs):
    return dims(lhs, rhs, 1, 0)


def nt(lhs, rhs):
    return dims(lhs, rhs, 1, 1)


def tn(lhs, rhs):
    return dims(lhs, rhs, 0, 0)


def params(grid, mib):
    return pltpu.CompilerParams(
        dimension_semantics=("arbitrary",) * len(grid), vmem_limit_bytes=mib * 2**20
    )


def whole(shape):
    return pl.BlockSpec(shape, lambda *idx: (0,) * len(shape))


ANY = pl.BlockSpec(memory_space=pl.ANY)
SMEM = pl.BlockSpec(memory_space=pltpu.SMEM)
NEAR = pl.BlockSpec(memory_space=pltpu.VMEM)


def kept(shape, dtype):
    return pltpu.HBM(shape, dtype)


def far(*arrays):
    return [pltpu.with_memory_space_constraint(a, pltpu.HBM) for a in arrays]


def cost(flops, bytes_moved, transcendental=0):
    return pl.CostEstimate(
        flops=int(flops), bytes_accessed=int(bytes_moved), transcendentals=int(transcendental)
    )


def group_perm(transposed):
    row = lax.broadcasted_iota(jnp.int32, (GW, GW), 0)
    col = lax.broadcasted_iota(jnp.int32, (GW, GW), 1)
    packed, natural = (row, col) if transposed else (col, row)
    half = packed // HALF
    head = (packed % HALF) // (HD // 2)
    source = head * HD + half * (HD // 2) + packed % (HD // 2)
    return jnp.where(source == natural, 1.0, 0.0).astype(BF16)


def packed_head_mask(head):
    lane = lax.broadcasted_iota(jnp.int32, (1, GW), 1)
    return (lane % HALF) // (HD // 2) == head


def natural_head_mask(head):
    lane = lax.broadcasted_iota(jnp.int32, (1, GW), 1)
    return lane // HD == head


def normalize(values):
    center = values - jnp.mean(values, axis=-1, keepdims=True)
    spread = jnp.mean(center * center, axis=-1, keepdims=True)
    inverse = lax.rsqrt(spread + EPS)
    return center * inverse, inverse


def load_pieces(table, sources, target, sem, rows, column=True):
    copies = []
    slots = table.shape[0] // 2
    for source in sources:
        width = source.shape[2]
        for slot in range(source.shape[0]):
            number = len(copies)
            row = pl.multiple_of(table[number] * rows, rows)
            col = pl.multiple_of(table[slots + number] * width, width) if column else 0
            copies.append(
                pltpu.make_async_copy(
                    source.at[slot, pl.ds(0, rows)], target.at[pl.ds(row, rows), pl.ds(col, width)], sem.at[number]
                )
            )
    return copies


def piece_count(sources):
    return sum(s.shape[0] for s in sources)


SMALL_ROWS = 16


def pack_kernel(rep, in_ref, out_ref, up_ref, down_ref, *rest):
    vectors, (one_ref, two_ref, three_ref, four_ref, small_ref) = rest[:-5], rest[-5:]
    small_ref[...] = jnp.zeros_like(small_ref)
    for row, vector in enumerate(vectors):
        length = vector.shape[0]
        small_ref[row : row + 1, :length] = vector[...].astype(F32).reshape(1, length)

    def write(y):
        rows, third = in_ref.shape[0], in_ref.shape[1] // 3
        groups = third // GW
        cuts = [in_ref[:, pl.ds(part * third + g * GW, GW)] for g in range(groups) for part in range(3)]
        first = jnp.concatenate(cuts[:3], axis=1)
        half = first.shape[1] // 2
        one_ref[0, pl.ds(0, rows), :] = first[:, y * half : (y + 1) * half]
        one_ref[0, pl.ds(rows, SMALL_ROWS), :] = small_ref[...].astype(BF16)
        rest = jnp.concatenate(cuts[3:], axis=1)
        half = rest.shape[1] // 2
        two_ref[0] = rest[:, y * half : (y + 1) * half]
        both = jnp.concatenate([out_ref[...], up_ref[...]], axis=1)
        half = both.shape[1] // 2
        three_ref[0] = both[:, y * half : (y + 1) * half]
        half = down_ref.shape[1] // 2
        four_ref[0] = down_ref[:, pl.ds(y * half, half)]

    @pl.when(rep[0] == 0)
    def _():
        write(0)

    @pl.when(rep[0] == 1)
    def _():
        write(1)


def pack(rep, inward, outward, upward, downward, smalls):
    rows, wide = inward.shape
    width = wide // 3
    shapes = [
        (1, rows + SMALL_ROWS, 3 * GW // 2),
        (1, rows, (wide - 3 * GW) // 2),
        (1, rows, (width + upward.shape[1]) // 2),
        (1, downward.shape[0], width // 2),
    ]
    return pl.pallas_call(
        pack_kernel,
        in_specs=[SMEM] + [pl.BlockSpec(memory_space=pltpu.VMEM)] * (4 + len(smalls)),
        out_specs=[pl.BlockSpec(memory_space=pltpu.VMEM)] * 4,
        out_shape=[jax.ShapeDtypeStruct(shape, BF16) for shape in shapes],
        scratch_shapes=[pltpu.VMEM((SMALL_ROWS, 3 * GW // 2), F32)],
        cost_estimate=cost(0, 2 * rows * width * 24),
        name="pack",
    )(rep, inward, outward, upward, downward, *smalls)


V_GAIN, V_SHIFT, V_BIAS, V_FREQ, V_OBIAS, V_MGAIN, V_MSHIFT, V_UBIAS, V_DBIAS = range(9)


def prologue_kernel(lengths, owners, rows, npieces, order, x_ref, pos_ref, *rest):
    pieces = rest[:npieces]
    n1_ref, cos_ref, sin_ref, vec_ref, aux_ref, got, fc, fr, sem = rest[npieces:]
    width = x_ref.shape[1]

    @pl.when(pl.program_id(0) == 0)
    def _():
        copies = []
        for number, piece in enumerate(pieces):
            slots = piece.shape[0]
            copies.append(
                pltpu.make_async_copy(
                    piece.at[:, pl.ds(rows, SMALL_ROWS)], got.at[pl.ds(number * slots, slots)], sem.at[number]
                )
            )
        for copy in copies:
            copy.start()
        for copy in copies:
            copy.wait()
        vec_ref[...] = jnp.zeros_like(vec_ref)
        for owner in range(owners):
            tile = got[order[owner]].astype(F32)
            for row, length in enumerate(lengths):
                vec_ref[row : row + 1, owner * length : (owner + 1) * length] = tile[row : row + 1, :length]
        freq = jnp.broadcast_to(vec_ref[V_FREQ : V_FREQ + 1, :width], (16, width)).astype(BF16)
        source = lax.broadcasted_iota(jnp.int32, (width, width // 2), 0)
        target = lax.broadcasted_iota(jnp.int32, (width, width // 2), 1)
        fc[...] = nn(freq, jnp.where(source == 2 * target, 1.0, 0.0).astype(BF16))[:8]
        fr[...] = nn(freq, jnp.where(source == 2 * target + 1, 1.0, 0.0).astype(BF16))[:8]

    xhat, _ = normalize(x_ref[...])
    n1_ref[...] = (xhat * vec_ref[V_GAIN : V_GAIN + 1, :width] + vec_ref[V_SHIFT : V_SHIFT + 1, :width]).astype(BF16)
    pos = pos_ref[...]
    aux = jnp.transpose(jnp.concatenate([pos, jnp.zeros((120, pos.shape[1]), F32)], axis=0))
    aux_ref[...] = aux
    angle = aux[:, 0:1] * fc[0:1, :] + aux[:, 1:2] * fr[0:1, :]
    cosine, sine = cos_sin(angle)
    cos_ref[...] = cosine
    sin_ref[...] = sine


def prologue(lengths, owners, rows, order, x, pos, pieces, rb=256):
    total, width = x.shape
    pairs = width // 2
    grid = (total // rb,)
    blk = lambda w: pl.BlockSpec((rb, w), lambda i: (i, 0))
    wide = max(lengths) * owners
    return pl.pallas_call(
        functools.partial(prologue_kernel, lengths, owners, rows, len(pieces)),
        grid=grid,
        in_specs=[SMEM, blk(width), pl.BlockSpec((8, rb), lambda i: (0, i))] + [ANY] * len(pieces),
        out_specs=[blk(width), blk(pairs), blk(pairs), whole((16, wide)), blk(128)],
        out_shape=[
            kept((total, width), BF16),
            kept((total, pairs), F32),
            kept((total, pairs), F32),
            kept((16, wide), F32),
            kept((total, 128), F32),
        ],
        scratch_shapes=[
            pltpu.VMEM((piece_count(pieces), SMALL_ROWS, pieces[0].shape[2]), BF16),
            pltpu.VMEM((8, pairs), F32),
            pltpu.VMEM((8, pairs), F32),
            pltpu.SemaphoreType.DMA((len(pieces),)),
        ],
        compiler_params=params(grid, 24),
        cost_estimate=cost(total * width * 40, total * width * 10),
        name="prologue",
    )(order, *far(x), pos, *far(*pieces))


QUARTER = (1.5703125, 4.837512969970703125e-4, 7.549789948768648e-8)


def cos_sin(angle):
    turns = jnp.floor(angle * 0.6366197723675814 + 0.5)
    r = ((angle - turns * QUARTER[0]) - turns * QUARTER[1]) - turns * QUARTER[2]
    r2 = r * r
    s = r + r * r2 * (-1.6666654611e-1 + r2 * (8.3321608736e-3 - 1.9515295891e-4 * r2))
    c = 1.0 - 0.5 * r2 + r2 * r2 * (4.166664568298827e-2 + r2 * (-1.388731625493765e-3 + 2.443315711809948e-5 * r2))
    quad = turns.astype(jnp.int32)
    odd = (quad & 1) == 1
    cosine = jnp.where(odd, s, c)
    sine = jnp.where(odd, c, s)
    cosine = jnp.where(((quad + 1) & 2) == 2, -cosine, cosine)
    sine = jnp.where((quad & 2) == 2, -sine, sine)
    return cosine, sine


def qkv_kernel(g0, npieces, rows, table, n1_ref, vec_ref, cos_ref, sin_ref, *rest):
    pieces = rest[:npieces]
    q_ref, k_ref, v_ref, w, wp, bp, sem = rest[npieces:]
    width = n1_ref.shape[1]
    groups = w.shape[1] // (3 * GW)
    bias_ref = vec_ref.at[V_BIAS : V_BIAS + 1, :]

    @pl.when(pl.program_id(0) == 0)
    def _():
        copies = load_pieces(table, pieces, w, sem, rows)
        for copy in copies:
            copy.start()
        perm = group_perm(False)
        for copy in copies:
            copy.wait()
        for g in range(groups):
            for part in range(2):
                packed = pl.ds((g * 2 + part) * GW, GW)
                wp[:, packed] = nn(w[:, pl.ds((g * 3 + part) * GW, GW)], perm).astype(BF16)
                natural = pl.ds(part * width + (g0 + g) * GW, GW)
                spread = jnp.broadcast_to(bias_ref[:, natural].astype(BF16), (16, GW))
                bp[:, packed] = nn(spread, perm)[:8]

    n1 = n1_ref[...]
    for g in range(groups):
        cosine = cos_ref[:, pl.ds((g0 + g) * HALF, HALF)]
        sine = sin_ref[:, pl.ds((g0 + g) * HALF, HALF)]
        for part, out, scale in ((0, q_ref, HD**-0.5 * LOG2E), (1, k_ref, 1.0)):
            packed = pl.ds((g * 2 + part) * GW, GW)
            mixed = nn(n1, wp[:, packed]) + bp[0:1, packed]
            a, b = mixed[:, :HALF], mixed[:, HALF:]
            first = a * cosine - b * sine
            second = a * sine + b * cosine
            if scale != 1.0:
                first = first * scale
                second = second * scale
            out[:, pl.ds(g * GW, HALF)] = first.astype(BF16)
            out[:, pl.ds(g * GW + HALF, HALF)] = second.astype(BF16)
        bias = bias_ref[:, pl.ds(2 * width + (g0 + g) * GW, GW)]
        v_ref[:, pl.ds(g * GW, GW)] = (nn(n1, w[:, pl.ds((g * 3 + 2) * GW, GW)]) + bias).astype(BF16)


def qkv(g0, groups, rows, table, n1, vec, cosine, sine, pieces):
    total, width = n1.shape
    rb = 512
    pairs = width // 2
    grid = (total // rb,)
    blk = lambda w: pl.BlockSpec((rb, w), lambda i: (i, 0))
    out = kept((total, groups * GW), BF16)
    copies = piece_count(pieces)
    return pl.pallas_call(
        functools.partial(qkv_kernel, g0, len(pieces), rows),
        grid=grid,
        in_specs=[SMEM, blk(width), whole(vec.shape), blk(pairs), blk(pairs)] + [ANY] * len(pieces),
        out_specs=[blk(groups * GW)] * 3,
        out_shape=[out] * 3,
        scratch_shapes=[
            pltpu.VMEM((width, 3 * groups * GW), BF16),
            pltpu.VMEM((width, 2 * groups * GW), BF16),
            pltpu.VMEM((8, 2 * groups * GW), F32),
            pltpu.SemaphoreType.DMA((copies,)),
        ],
        compiler_params=params(grid, 24),
        cost_estimate=cost(total * width * groups * GW * 6, total * width * 8 + width * groups * GW * 6),
        name="qkv",
    )(table, *far(n1, vec, cosine, sine, *pieces))


def attend_kernel(q_ref, k_ref, v_ref, pos_ref, *rest):
    att_ref, lse_ref, wide_ref, mask = rest[-4:]
    g, r = pl.program_id(0), pl.program_id(1)
    rb, keys = q_ref.shape[0], k_ref.shape[0]
    here = pl.ds(pl.multiple_of(r * rb, rb), rb)

    @pl.when(g == 0)
    def _():
        row = lax.broadcasted_iota(jnp.int32, (rb, keys), 0) + r * rb
        col = lax.broadcasted_iota(jnp.int32, (rb, keys), 1)
        mask[here, :] = jnp.where(row == col, 0.0, jnp.broadcast_to(pos_ref[2:3, :], (rb, keys)))

    q = q_ref[...]
    k = k_ref[...]
    v = v_ref[...]
    total = jnp.zeros((rb, GW), F32)
    lane = lax.broadcasted_iota(jnp.int32, (rb, 128), 1)
    logs = jnp.zeros((rb, 128), F32)
    for h in range(GH):
        qm = jnp.where(packed_head_mask(h), q, jnp.zeros_like(q))
        scores = nt(qm, k) + mask[here, :]
        top = jnp.max(scores, axis=-1, keepdims=True)
        weight = jnp.exp2(scores - top)
        norm = jnp.sum(weight, axis=-1, keepdims=True)
        vm = jnp.where(natural_head_mask(h), v, jnp.zeros_like(v))
        total = total + nn(weight.astype(BF16), vm) * (1.0 / norm)
        logs = jnp.where(lane == h, top + jnp.log2(norm), logs)
    att_ref[...] = total.astype(BF16)
    wide_ref[...] = total
    lse_ref[...] = jnp.transpose(logs)[:8, :]


def attend(g0, full, q, k, v, pos, *att, rb=512):
    total, width = q.shape
    groups = width // GW
    grid = (groups, total // rb)
    return pl.pallas_call(
        attend_kernel,
        grid=grid,
        in_specs=[
            pl.BlockSpec((rb, GW), lambda g, r: (r, g)),
            pl.BlockSpec((total, GW), lambda g, r: (0, g)),
            pl.BlockSpec((total, GW), lambda g, r: (0, g)),
            whole((8, total)),
        ]
        + [ANY] * len(att),
        out_specs=[
            pl.BlockSpec((rb, GW), lambda g, r: (r, g + g0)),
            pl.BlockSpec((None, 8, rb), lambda g, r: (g, 0, r)),
            pl.BlockSpec((rb, GW), lambda g, r: (r, g)),
        ],
        out_shape=[
            kept((total, full), BF16),
            kept((groups, 8, total), F32),
            kept((total, width), F32),
        ],
        input_output_aliases={4: 0} if att else {},
        scratch_shapes=[pltpu.VMEM((total, total), F32)],
        compiler_params=params(grid, 32),
        cost_estimate=cost(total * total * width * 16, total * width * 8, total * total * 12),
        name="attend",
    )(*far(q, k, v, pos, *att))


PHI_SCALE = 0.3989422804014327
TAIL_SCALE = 0.44 * 0.7071067811865476
TAIL = (
    0.12411047596471954,
    0.12443560910041027,
    0.10865662380098591,
    0.10790671631036299,
    -0.010091621907114547,
    0.14834527631989725,
    -0.13897496529649409,
    0.03561197654899638,
)


def gelu_parts(h):
    t = 1.0 / (1.0 + TAIL_SCALE * jnp.abs(h))
    poly = TAIL[-1]
    for coefficient in TAIL[-2::-1]:
        poly = poly * t + coefficient
    bell = jnp.exp2((-0.5 * LOG2E) * (h * h))
    tail = poly * t * bell
    phi = jnp.where(h < 0, tail, 1.0 - tail)
    return h * phi, phi + h * (bell * PHI_SCALE)


def up_kernel(half, npieces, rows, table, count, *refs):
    if half == 0:
        att_ref, x_ref, cot_ref, vec_ref = refs[:4]
        pieces = refs[4 : 4 + npieces]
        mid_ref, n2_ref, gd_ref, act_ref, gp_ref, w, sem = refs[4 + npieces :]
    else:
        n2_ref, vec_ref = refs[:2]
        pieces = refs[2 : 2 + npieces]
        act_ref, gp_ref, w, sem = refs[-4:]
    rb, width = n2_ref.shape

    @pl.when(pl.program_id(0) == 0)
    def _():
        slots = table.shape[0] // 2
        copies = load_pieces(table, pieces, w, sem, rows, column=False)
        for start in (True, False):
            for number, copy in enumerate(copies):

                @pl.when(table[slots + number] == half)
                def _():
                    if start:
                        copy.start()
                    else:
                        copy.wait()

    if half == 0:
        slot = lax.broadcasted_iota(jnp.int32, (rb, 1), 0) + pl.program_id(0) * rb
        valid = jnp.where(slot < count[0], 1.0, 0.0)
        gd_ref[...] = (valid * cot_ref[...]).astype(BF16)
        branch = nn(att_ref[...], w[:, pl.ds(0, width)]) + vec_ref[V_OBIAS : V_OBIAS + 1, :width]
        middle = x_ref[...] + valid * branch
        mid_ref[...] = middle
        xhat, _ = normalize(middle)
        n2 = (xhat * vec_ref[V_MGAIN : V_MGAIN + 1, :width] + vec_ref[V_MSHIFT : V_MSHIFT + 1, :width]).astype(BF16)
        n2_ref[...] = n2
        place = width
    else:
        n2 = n2_ref[...]
        place = 0
    first = half * (w.shape[1] - width)
    step = 384
    for c in range(act_ref.shape[1] // step):
        cut = pl.ds(c * step, step)
        hidden = nn(n2, w[:, pl.ds(place + c * step, step)]) + vec_ref[V_UBIAS : V_UBIAS + 1, pl.ds(first + c * step, step)]
        act, slope = gelu_parts(hidden)
        act_ref[:, cut] = act.astype(BF16)
        gp_ref[:, cut] = slope.astype(BF16)


def up_first(rows, wide, table, count, att, x, cot, vec, pieces, rb=256):
    total, width = x.shape
    part = (width + wide) // 2
    grid = (total // rb,)
    blk = lambda w: pl.BlockSpec((rb, w), lambda i: (i, 0))
    return pl.pallas_call(
        functools.partial(up_kernel, 0, len(pieces), rows),
        grid=grid,
        in_specs=[SMEM, SMEM, blk(width), blk(width), blk(width), whole(vec.shape)] + [ANY] * len(pieces),
        out_specs=[blk(width), blk(width), blk(width), blk(part - width), blk(part - width)],
        out_shape=[
            kept((total, width), F32),
            kept((total, width), BF16),
            kept((total, width), BF16),
            kept((total, wide), BF16),
            kept((total, wide), BF16),
        ],
        scratch_shapes=[pltpu.VMEM((width, part), BF16), pltpu.SemaphoreType.DMA((piece_count(pieces),))],
        compiler_params=params(grid, 32),
        cost_estimate=cost(total * width * part * 2, total * width * 20, total * wide),
        name="up_first",
    )(table, count, *far(att, x, cot, vec, *pieces))


def up_second(rows, table, count, n2, act, slope, vec, pieces, rb=128):
    total, width = n2.shape
    wide = act.shape[1]
    part = (width + wide) // 2
    grid = (total // rb,)
    cols = pl.BlockSpec((pl.Element(rb), pl.Element(part)), lambda i: (i * rb, part - width))
    return pl.pallas_call(
        functools.partial(up_kernel, 1, len(pieces), rows),
        grid=grid,
        in_specs=[SMEM, SMEM, pl.BlockSpec((rb, width), lambda i: (i, 0)), whole(vec.shape)]
        + [ANY] * (len(pieces) + 2),
        out_specs=[cols, cols],
        out_shape=[kept((total, wide), BF16)] * 2,
        input_output_aliases={4 + len(pieces): 0, 5 + len(pieces): 1},
        scratch_shapes=[pltpu.VMEM((width, part), BF16), pltpu.SemaphoreType.DMA((piece_count(pieces),))],
        compiler_params=params(grid, 32),
        cost_estimate=cost(total * width * part * 2, total * width * 20, total * wide),
        name="up_second",
    )(table, count, *far(n2, vec, *pieces, act, slope))


def down_kernel(nup, ndown, rows, table, count, act_ref, gp_ref, mid_ref, cot_ref, gd_ref, vec_ref, *rest):
    ups = rest[:nup]
    downs = rest[nup : nup + ndown]
    (out_ref, gm_ref, gb_ref, ga_ref, gu_ref, sums_ref, ubsum_ref, w, wd, sem, sem_d) = rest[nup + ndown :]
    i = pl.program_id(0)
    rb, width = mid_ref.shape
    wide = act_ref.shape[1]

    @pl.when(i == 0)
    def _():
        first = load_pieces(table, downs, wd, sem_d, rows * (wide // width))
        second = load_pieces(table, ups, w, sem, rows)
        for copy in first + second:
            copy.start()
        for copy in first + second:
            copy.wait()
        sums_ref[...] = jnp.zeros_like(sums_ref)
        ubsum_ref[...] = jnp.zeros_like(ubsum_ref)

    slot = lax.broadcasted_iota(jnp.int32, (rb, 1), 0) + i * rb
    valid = jnp.where(slot < count[0], 1.0, 0.0)
    middle = mid_ref[...]
    cot = cot_ref[...]
    gd = gd_ref[...]
    lowered = nn(act_ref[...], wd[...]) + vec_ref[V_DBIAS : V_DBIAS + 1, :width]
    out_ref[...] = middle + valid * lowered
    step = 1024
    gn2 = jnp.zeros((rb, width), F32)
    for c in range(wide // step):
        cut = pl.ds(c * step, step)
        g = nt(gd, wd[cut, :]) * gp_ref[:, cut].astype(F32)
        g_low = g.astype(BF16)
        gu_ref[:, cut] = g_low
        ubsum_ref[0:1, cut] += jnp.sum(g_low.astype(F32), axis=0, keepdims=True)
        gn2 = gn2 + nt(g_low, w[:, pl.ds(width + c * step, step)])
    xhat, inverse = normalize(middle)
    sums_ref[0:1, :] += jnp.sum(gn2 * xhat, axis=0, keepdims=True)
    sums_ref[1:2, :] += jnp.sum(gn2, axis=0, keepdims=True)
    e = gn2 * vec_ref[V_MGAIN : V_MGAIN + 1, :width]
    back = (e - jnp.mean(e, axis=-1, keepdims=True) - xhat * jnp.mean(e * xhat, axis=-1, keepdims=True)) * inverse
    gmid = cot + back
    gm_ref[...] = gmid
    gb = (valid * gmid).astype(BF16)
    gb_ref[...] = gb
    sums_ref[2:3, :] += jnp.sum(gb.astype(F32), axis=0, keepdims=True)
    sums_ref[3:4, :] += jnp.sum(gd.astype(F32), axis=0, keepdims=True)
    ga_ref[...] = nt(gb, w[:, pl.ds(0, width)]).astype(BF16)


def down(rows, table, count, act, gp, mid, cot, gd, vec, ups, downs, rb=256):
    total, width = mid.shape
    wide = act.shape[1]
    grid = (total // rb,)
    blk = lambda w: pl.BlockSpec((rb, w), lambda i: (i, 0))
    return pl.pallas_call(
        functools.partial(down_kernel, len(ups), len(downs), rows),
        grid=grid,
        in_specs=[SMEM, SMEM, blk(wide), blk(wide), blk(width), blk(width), blk(width), whole(vec.shape)]
        + [ANY] * (len(ups) + len(downs)),
        out_specs=[blk(width), blk(width), blk(width), blk(width), blk(wide), whole((8, width)), whole((8, wide))],
        out_shape=[
            kept((total, width), F32),
            kept((total, width), F32),
            kept((total, width), BF16),
            kept((total, width), BF16),
            kept((total, wide), BF16),
            kept((8, width), F32),
            kept((8, wide), F32),
        ],
        scratch_shapes=[
            pltpu.VMEM((width, width + wide), BF16),
            pltpu.VMEM((wide, width), BF16),
            pltpu.SemaphoreType.DMA((piece_count(ups),)),
            pltpu.SemaphoreType.DMA((piece_count(downs),)),
        ],
        compiler_params=params(grid, 44),
        cost_estimate=cost(total * width * (width + 3 * wide) * 2, total * (width * 20 + wide * 6)),
        name="down",
    )(table, count, *far(act, gp, mid, cot, gd, vec, *ups, *downs))


def grad_kernel(pairs, mids, reps, rows, core, *rest):
    keep_ref, send_ref = rest[-2:]
    part = core[0]

    def spot(parity, mid, rep):
        return jnp.where(parity == 0, mid, rep), jnp.where(parity == 0, rep, mid)

    each = keep_ref.shape[-1]
    offset = 0
    for at, bt in pairs:
        a, b_ref = rest[at][...], rest[bt]
        begin = 0
        while begin < b_ref.shape[1]:
            column = offset + begin
            step = min(b_ref.shape[1] - begin, each - column % each, 768)
            result = tn(a, b_ref[:, pl.ds(begin, step)])
            rep, cut = column // each, pl.ds(column % each, step)
            for pair in range(a.shape[1] // (2 * rows)):
                low = result[pair * 2 * rows : pair * 2 * rows + rows]
                high = result[pair * 2 * rows + rows : (pair + 1) * 2 * rows]
                zz, mid = pair // mids, pair % mids
                one, two = spot(part, mid, rep)
                keep_ref[one, two, zz, :, cut] = jnp.where(part == 0, low, high).astype(BF16)
                one, two = spot(1 - part, mid, rep)
                send_ref[one, two, zz, :, cut] = jnp.where(part == 0, high, low).astype(BF16)
            begin += step
        offset += b_ref.shape[1]


def operands(pairs):
    arrays, index = [], []
    for pair in pairs:
        spots = []
        for array in pair:
            if not any(array is other for other in arrays):
                arrays.append(array)
            spots.append([array is other for other in arrays].index(True))
        index.append(spots)
    lefts = {one for one, _ in index}
    return arrays, index, lefts


def weight_grad(core, pairs, layout, name, lasting=False):
    slow, mids, reps = layout
    arrays, index, lefts = operands(pairs)
    total, height = pairs[0][0].shape
    width = sum(b.shape[1] for _, b in pairs)
    rows = height // (slow * mids * 2)
    chunk = 384 if 384 % (2 * mids * rows) == 0 else 2 * mids * rows
    slows = chunk // (2 * mids * rows)
    grid = (height // chunk,)
    shape = (mids, reps, slow, rows, width // reps)
    out = jax.ShapeDtypeStruct(shape, BF16)
    spec = pl.BlockSpec((mids, reps, slows, rows, width // reps), lambda i: (0, 0, i, 0, 0))
    return pl.pallas_call(
        functools.partial(grad_kernel, index, mids, reps, rows),
        grid=grid,
        in_specs=[SMEM]
        + [
            pl.BlockSpec((total, chunk), lambda i: (0, i)) if n in lefts else whole(a.shape)
            for n, a in enumerate(arrays)
        ],
        out_specs=[spec, spec],
        out_shape=[kept(shape, BF16) if lasting else out, out],
        compiler_params=params(grid, 40),
        cost_estimate=cost(total * height * width * 2, total * (height + width) * 2 + height * width * 2),
        name=name,
    )(core, *far(*arrays))


def plain_grad_kernel(pairs, *rest):
    out_ref = rest[-1]
    offset = 0
    for at, bt in pairs:
        a, b_ref = rest[at][...], rest[bt]
        step = min(b_ref.shape[1], 768)
        for c in range(b_ref.shape[1] // step):
            out_ref[:, pl.ds(offset + c * step, step)] = tn(a, b_ref[:, pl.ds(c * step, step)])
        offset += b_ref.shape[1]


def plain_grad(pairs, name):
    arrays, index, lefts = operands(pairs)
    total, height = pairs[0][0].shape
    width = sum(b.shape[1] for _, b in pairs)
    chunk = 384
    grid = (height // chunk,)
    return pl.pallas_call(
        functools.partial(plain_grad_kernel, index),
        grid=grid,
        in_specs=[
            pl.BlockSpec((total, chunk), lambda i: (0, i)) if n in lefts else whole(a.shape)
            for n, a in enumerate(arrays)
        ],
        out_specs=pl.BlockSpec((chunk, width), lambda i: (i, 0)),
        out_shape=jax.ShapeDtypeStruct((height, width), F32),
        compiler_params=params(grid, 63),
        cost_estimate=cost(total * height * width * 2, total * (height + width) * 2 + height * width * 4),
        name=name,
    )(*arrays)


def unrotate(grad, cosine, sine):
    first, second = grad[:, :HALF], grad[:, HALF:]
    return first * cosine + second * sine, second * cosine - first * sine


def angle_grad(grad, rotated):
    return grad[:, HALF:] * rotated[:, :HALF] - grad[:, :HALF] * rotated[:, HALF:]


def back_kernel(q_ref, k_ref, v_ref, do_ref, lse_ref, wide_ref, aux_ref, cos_ref, sin_ref,
                g_ref, fsum_ref, bsum_ref, ds_s, p_s, dk_s, dv_s):
    r = pl.program_id(0)
    rb, keys = q_ref.shape[0], k_ref.shape[0]
    here = pl.ds(pl.multiple_of(r * rb, rb), rb)
    q = q_ref[...]
    k = k_ref[...]
    v = v_ref[...]
    do = do_ref[...]
    zero = jnp.zeros_like(q)
    product = do.astype(F32) * wide_ref[...]
    high = product.astype(BF16)
    low = (product - high.astype(F32)).astype(BF16)
    lane = lax.broadcasted_iota(jnp.int32, (16, GW), 1)
    pick_head = jnp.where(lane // HD == lax.broadcasted_iota(jnp.int32, (16, GW), 0), 1.0, 0.0).astype(BF16)
    inner = nt(pick_head, high) + nt(pick_head, low)
    key = lax.broadcasted_iota(jnp.int32, (keys, rb), 0)
    query = lax.broadcasted_iota(jnp.int32, (keys, rb), 1) + r * rb
    mask = jnp.where(key == query, 0.0, jnp.broadcast_to(aux_ref[:, 2:3], (keys, rb)))
    dq = jnp.zeros((rb, GW), F32)
    qms, doms = [], []
    for h in range(GH):
        qm = jnp.where(packed_head_mask(h), q, zero)
        dom = jnp.where(natural_head_mask(h), do, zero)
        qms.append(qm)
        doms.append(dom)
        soft = jnp.exp2(nt(k, qm) + mask - lse_ref[h : h + 1, :])
        ds = (soft * (nt(v, dom) - inner[h : h + 1, :])).astype(BF16)
        cut = pl.ds(h * rb, rb)
        ds_s[:, cut] = ds
        p_s[:, cut] = soft.astype(BF16)
        km = jnp.where(packed_head_mask(h), k, jnp.zeros_like(k))
        dq = dq + tn(ds, km)
    dk = nn(ds_s[...], jnp.concatenate(qms, axis=0)) * (1.0 / LOG2E)
    dv = nn(p_s[...], jnp.concatenate(doms, axis=0))

    perm = group_perm(True)
    cosine, sine = cos_ref[here, :], sin_ref[here, :]
    dq = dq * (HD**-0.5)
    ang = angle_grad(dq, q.astype(F32) * (HD**0.5 / LOG2E))
    first, second = unrotate(dq, cosine, sine)
    gq = nn(jnp.concatenate([first.astype(BF16), second.astype(BF16)], axis=1), perm)
    g_ref[here, pl.ds(0, GW)] = gq.astype(BF16)
    col, row = aux_ref[here, 0:1], aux_ref[here, 1:2]
    fcol = jnp.sum(ang * col, axis=0, keepdims=True)
    frow = jnp.sum(ang * row, axis=0, keepdims=True)
    qsum = jnp.sum(gq, axis=0, keepdims=True)

    @pl.when(r == 0)
    def _():
        dk_s[...] = dk
        dv_s[...] = dv
        fsum_ref[...] = jnp.zeros_like(fsum_ref)
        fsum_ref[0:1, pl.ds(0, HALF)] = fcol
        fsum_ref[1:2, pl.ds(0, HALF)] = frow
        bsum_ref[0:1, pl.ds(0, GW)] = qsum

    @pl.when(r > 0)
    def _():
        dk_s[...] += dk
        dv_s[...] += dv
        fsum_ref[0:1, pl.ds(0, HALF)] += fcol
        fsum_ref[1:2, pl.ds(0, HALF)] += frow
        bsum_ref[0:1, pl.ds(0, GW)] += qsum

    @pl.when(r == pl.num_programs(0) - 1)
    def _():
        dkf = dk_s[...]
        angk = angle_grad(dkf, k.astype(F32))
        fsum_ref[0:1, pl.ds(0, HALF)] += jnp.sum(angk * aux_ref[:, 0:1], axis=0, keepdims=True)
        fsum_ref[1:2, pl.ds(0, HALF)] += jnp.sum(angk * aux_ref[:, 1:2], axis=0, keepdims=True)
        one, two = unrotate(dkf, cos_ref[...], sin_ref[...])
        gk = nn(jnp.concatenate([one.astype(BF16), two.astype(BF16)], axis=1), perm)
        g_ref[:, pl.ds(GW, GW)] = gk.astype(BF16)
        bsum_ref[0:1, pl.ds(GW, GW)] = jnp.sum(gk, axis=0, keepdims=True)
        gv = dv_s[...].astype(BF16)
        g_ref[:, pl.ds(2 * GW, GW)] = gv
        lane = lax.broadcasted_iota(jnp.int32, (HALF, 2 * HALF), 1)
        pair = lax.broadcasted_iota(jnp.int32, (HALF, 2 * HALF), 0)
        sums = fsum_ref[:, pl.ds(0, HALF)]
        spread = [
            jnp.dot(sums, jnp.where(lane == 2 * pair + odd, 1.0, 0.0), precision=lax.Precision.HIGHEST)
            for odd in range(2)
        ]
        fsum_ref[0:1, :] = spread[0][0:1] + spread[1][1:2]
        bsum_ref[0:1, pl.ds(2 * GW, GW)] = jnp.sum(gv.astype(F32), axis=0, keepdims=True)


def attend_back(g0, l0, q, k, v, do, lse, wide, aux, cosine, sine, rb=256):
    total = q.shape[0]
    grid = (total // rb,)
    return pl.pallas_call(
        back_kernel,
        grid=grid,
        in_specs=[
            pl.BlockSpec((rb, GW), lambda r: (r, l0)),
            pl.BlockSpec((total, GW), lambda r: (0, l0)),
            pl.BlockSpec((total, GW), lambda r: (0, l0)),
            pl.BlockSpec((rb, GW), lambda r: (r, g0)),
            pl.BlockSpec((None, 8, rb), lambda r: (l0, 0, r)),
            pl.BlockSpec((rb, GW), lambda r: (r, l0)),
            whole((total, 128)),
            pl.BlockSpec((total, HALF), lambda r: (0, g0)),
            pl.BlockSpec((total, HALF), lambda r: (0, g0)),
        ],
        out_specs=[whole((total, 3 * GW)), whole((8, GW)), whole((8, 3 * GW))],
        out_shape=[
            kept((total, 3 * GW), BF16),
            jax.ShapeDtypeStruct((8, GW), F32),
            jax.ShapeDtypeStruct((8, 3 * GW), F32),
        ],
        scratch_shapes=[
            pltpu.VMEM((total, GH * rb), BF16),
            pltpu.VMEM((total, GH * rb), BF16),
            pltpu.VMEM((total, GW), F32),
            pltpu.VMEM((total, GW), F32),
        ],
        compiler_params=params(grid, 48),
        cost_estimate=cost(total * total * GW * 40, total * GW * 20, total * total * GH),
        name="attend_back",
    )(*far(q, k, v, do, lse, wide, aux, cosine, sine))


def final_kernel(count, counts, rows, table_one, table_two, x_ref, gm_ref, vec_ref, *rest):
    grads, place = rest[:count], count
    pieces = []
    for number in counts:
        pieces.append(rest[place : place + number])
        place += number
    out_ref, sums_ref = rest[place : place + 2]
    weights = rest[place + 2 : place + 2 + len(counts)]
    sems = rest[place + 2 + len(counts) :]

    @pl.when(pl.program_id(0) == 0)
    def _():
        copies = []
        for table, p, w, sem in zip((table_one, table_two), pieces, weights, sems):
            copies += load_pieces(table, p, w, sem, rows)
        for copy in copies:
            copy.start()
        for copy in copies:
            copy.wait()
        sums_ref[...] = jnp.zeros_like(sums_ref)

    e = jnp.zeros(x_ref.shape, F32)
    group = 0
    for w in weights:
        for g in range(w.shape[1] // (3 * GW)):
            e = e + nt(grads[group][...], w[:, pl.ds(g * 3 * GW, 3 * GW)])
            group += 1
    xhat, inverse = normalize(x_ref[...])
    sums_ref[0:1, :] += jnp.sum(e * xhat, axis=0, keepdims=True)
    sums_ref[1:2, :] += jnp.sum(e, axis=0, keepdims=True)
    eg = e * vec_ref[V_GAIN : V_GAIN + 1, : x_ref.shape[1]]
    back = (eg - jnp.mean(eg, axis=-1, keepdims=True) - xhat * jnp.mean(eg * xhat, axis=-1, keepdims=True)) * inverse
    out_ref[...] = gm_ref[...] + back


def final(rows, widths, tables, x, gmid, vec, grads, piece_sets, rb=256):
    total, width = x.shape
    grid = (total // rb,)
    blk = lambda w: pl.BlockSpec((rb, w), lambda i: (i, 0))
    pieces = [p for ps in piece_sets for p in ps]
    return pl.pallas_call(
        functools.partial(final_kernel, len(grads), [len(ps) for ps in piece_sets], rows),
        grid=grid,
        in_specs=[SMEM, SMEM, blk(width), blk(width), whole(vec.shape)]
        + [blk(g.shape[1]) for g in grads]
        + [ANY] * len(pieces),
        out_specs=[blk(width), whole((8, width))],
        out_shape=[kept((total, width), F32), jax.ShapeDtypeStruct((8, width), F32)],
        scratch_shapes=[pltpu.VMEM((width, w), BF16) for w in widths]
        + [pltpu.SemaphoreType.DMA((piece_count(ps),)) for ps in piece_sets],
        compiler_params=params(grid, 32),
        cost_estimate=cost(total * width * width * 6, total * width * 20 + width * width * 6),
        name="final",
    )(*tables, *far(x, gmid, vec), *far(*grads), *far(*pieces))


FOLD = (
    ("bias", 0, 0), ("value", 1, 0), ("freqs", 1, 64), ("gain", 2, 0), ("shift", 2, 64),
    ("obias", 3, 0), ("dbias", 3, 64), ("mgain", 4, 0), ("mshift", 4, 64), ("ubias", 5, 0),
)


def fold_kernel(groups, owners, spot, *refs):
    out_ref = refs[-1]
    fsums, bsums = refs[:groups], refs[groups : 2 * groups]
    mid_ref, wide_ref, first_ref = refs[2 * groups : 2 * groups + 3]
    lines = {
        "bias": [(b, 0, part * GW, GW) for part in range(2) for b in bsums],
        "value": [(b, 0, 2 * GW, GW) for b in bsums],
        "freqs": [(f, 0, 0, GW) for f in fsums],
        "gain": [(first_ref, 0, 0, first_ref.shape[1])],
        "shift": [(first_ref, 1, 0, first_ref.shape[1])],
        "mgain": [(mid_ref, 0, 0, mid_ref.shape[1])],
        "mshift": [(mid_ref, 1, 0, mid_ref.shape[1])],
        "obias": [(mid_ref, 2, 0, mid_ref.shape[1])],
        "dbias": [(mid_ref, 3, 0, mid_ref.shape[1])],
        "ubias": [(wide_ref, 0, 0, wide_ref.shape[1])],
    }
    out_ref[...] = jnp.zeros_like(out_ref)
    for name, row, lane in FOLD:
        total = sum(length for _, _, _, length in lines[name])
        each = total // owners
        for owner in range(owners):
            begin, end = owner * each, (owner + 1) * each
            offset = 0
            for ref, line, start, length in lines[name]:
                low, high = max(begin, offset), min(end, offset + length)
                while low < high:
                    place = row * 128 + lane + low - begin
                    at = start + low - offset
                    lead, last = spot(owner)
                    out_ref[(*lead, slice(last, last + 1), slice(place, place + high - low))] = (
                        ref[line : line + 1, at : at + high - low]
                    )
                    low = high
                offset += length


def fold(owners, cube, fsums, bsums, mid, wide, first):
    arrays = [*fsums, *bsums, mid, wide, first]
    shape, spot = (owners, 1024), lambda owner: ((), owner)
    if cube:
        shape, spot = (2, 2, 4, 1024), lambda owner: ((owner % 2, owner // 2 % 2), owner // 4)
    return pl.pallas_call(
        functools.partial(fold_kernel, len(fsums), owners, spot),
        in_specs=[pl.BlockSpec(memory_space=pltpu.VMEM)] * len(arrays),
        out_specs=pl.BlockSpec(memory_space=pltpu.VMEM),
        out_shape=jax.ShapeDtypeStruct(shape, F32),
        cost_estimate=cost(0, 100000),
        name="fold",
    )(*arrays)


def half_column(pair, swap, place, width):
    mine, other = pair
    each = mine.shape[1]
    cut = pl.ds(place % each, width)
    a, b = (mine, other) if place < each else (other, mine)
    return jnp.where(swap, b[:, cut], a[:, cut])


def finish_kernel(rep, *refs):
    outup, downs, (out_ref, up_ref, down_ref) = refs[:2], refs[2:4], refs[4:]
    swap, step, width = rep[0] == 1, GW // 2, out_ref.shape[1]
    for place in range(0, outup[0].shape[1] * 2, step):
        value = half_column(outup, swap, place, step)
        if place < width:
            out_ref[:, pl.ds(place, step)] = value
        else:
            up_ref[:, pl.ds(place - width, step)] = value
    for place in range(0, down_ref.shape[1], step):
        down_ref[:, pl.ds(place, step)] = half_column(downs, swap, place, step)


def finish(rep, outup, downs):
    width = downs[0].shape[1] * 2
    rows = outup[0].shape[0]
    shapes = [(rows, width), (rows, outup[0].shape[1] * 2 - width), (downs[0].shape[0], width)]
    return pl.pallas_call(
        finish_kernel,
        in_specs=[SMEM] + [NEAR] * 4,
        out_specs=[NEAR] * 3,
        out_shape=[jax.ShapeDtypeStruct(shape, F32) for shape in shapes],
        cost_estimate=cost(0, 4000000),
        name="finish",
    )(rep, *outup, *downs)


def finish_inward_kernel(groups, rep, *refs):
    halves, in_ref = refs[:-1], refs[-1]
    swap, step, group, total = rep[0] == 1, GW // 2, 0, in_ref.shape[1] // 3
    for n, count in enumerate(groups):
        for g in range(count):
            for part in range(3):
                for half in range(2):
                    value = half_column(halves[2 * n : 2 * n + 2], swap, (g * 3 + part) * GW + half * step, step)
                    in_ref[:, pl.ds(part * total + group * GW + half * step, step)] = value
            group += 1


def finish_inward(groups, rep, pairs):
    arrays = [a for pair in pairs for a in pair]
    return pl.pallas_call(
        functools.partial(finish_inward_kernel, groups),
        in_specs=[SMEM] + [NEAR] * len(arrays),
        out_specs=NEAR,
        out_shape=jax.ShapeDtypeStruct((arrays[0].shape[0], 3 * GW * sum(groups)), F32),
        cost_estimate=cost(0, 1000000),
        name="finish_inward",
    )(rep, *arrays)


def place():
    me = lax.axis_index("fsdp")
    return lax.axis_index("rep"), me // 4, (me // 2) % 2, me % 2


def move(value, step):
    moves = []
    for i in range(32):
        y, z, x, c = step(i // 16, (i // 4) % 4, (i // 2) % 2, i % 2)
        moves.append((i, y * 16 + z * 4 + x * 2 + c))
    return lax.ppermute(value, ("rep", "fsdp"), moves)


def across_core(value):
    return move(value, lambda y, z, x, c: (y, z, x, 1 - c))


def across_x(value):
    return move(value, lambda y, z, x, c: (y, z, 1 - x, c))


def across_rep(value):
    return move(value, lambda y, z, x, c: (1 - y, z, x, c))


def across_near(value):
    return move(value, lambda y, z, x, c: (y, z ^ 1, x, c))


def across_far(value):
    return move(value, lambda y, z, x, c: (y, z ^ 2, x, c))


def across_third(value):
    return move(value, lambda y, z, x, c: (y, z ^ 3, x, c))


def across_both(value):
    return move(value, lambda y, z, x, c: (1 - y, z, 1 - x, c))


def across_one(value):
    return move(value, lambda y, z, x, c: (y, z, 1 - x, c) if c == 0 else (1 - y, z, x, c))


def across_two(value):
    return move(value, lambda y, z, x, c: (1 - y, z, x, c) if c == 0 else (y, z, 1 - x, c))


def pick(array, index):
    return lax.dynamic_index_in_dim(array, index, 0, keepdims=False)


def pick_two(array, index):
    return lax.dynamic_slice_in_dim(array, 2 * index, 2, 0)


def piece_tables():
    y, z, x, c = place()
    slot = jnp.arange(4, dtype=jnp.int32)
    here, swap = (lambda core, a, b: a), (lambda core, a, b: jnp.where(core == 0, a, b))
    tables = []
    for choose in (here, swap):
        owners, halves = [], []
        for core in (c, 1 - c):
            for mid, half in ((x, y), (choose(core, x, 1 - x), choose(core, 1 - y, y)),
                              (choose(core, 1 - x, x), choose(core, y, 1 - y)), (1 - x, 1 - y)):
                owners.append((z ^ slot) * 4 + mid * 2 + core)
                halves.append(jnp.broadcast_to(half, (4,)))
        tables.append(jnp.concatenate(owners + halves).astype(jnp.int32))
    return tables


def first_of_owner(table, n):
    slots = table.shape[0] // 2
    match = table[None, :slots] == jnp.arange(n, dtype=jnp.int32)[:, None]
    return jnp.min(jnp.where(match, jnp.arange(slots, dtype=jnp.int32)[None, :], slots), axis=1)


class Reduce:
    stages = (across_core, across_one, across_two, across_far, across_near, across_rep)

    def __init__(self, keep, send):
        self.keep, self.first, self.got, self.stage = keep, send, [], 0
        self.out = None

    def sends(self):
        return [(self.stages[self.stage], self.send())]

    def takes(self, values):
        self.take(values[0])

    def base(self, count, one, two=None, cut=None):
        step = lambda a, i: a if i is None else pick(a, i)
        total = None
        for source, used in ((self.keep, 0), (self.got[0], 0), *((g, n + 1) for n, g in enumerate(self.got[1:count]))):
            value = source
            if used < 1:
                value = step(value, one)
            if used < 2:
                value = step(value, two)
            if cut is not None:
                value = cut(value)
            value = value.astype(F32)
            total = value if total is None else total + value
        return total

    def level(self, index):
        return self.base(3, self.i1, self.i2, lambda a: pick(a, index)) + pick(self.got[3], index % 2).astype(F32)

    def send(self):
        y, z, x, c = place()
        self.i1, self.i2 = jnp.where(c == 0, x, y), jnp.where(c == 0, y, x)
        if self.stage == 0:
            return self.first
        if self.stage == 1:
            return self.base(1, 1 - self.i1).astype(BF16)
        if self.stage == 2:
            return self.base(2, self.i1, 1 - self.i2).astype(BF16)
        if self.stage == 3:
            return self.base(3, self.i1, self.i2, lambda a: pick_two(a, 1 - z // 2)).astype(BF16)
        if self.stage == 4:
            return self.level(z ^ 1).astype(BF16)
        self.total = self.level(z) + self.got[4].astype(F32)
        return self.total

    def take(self, value):
        self.stage += 1
        if self.stage == 6:
            self.out = (self.total, value)
        else:
            self.got.append(value)


class SmallReduce:
    stages = (across_core, across_x, across_far, across_near, across_rep)

    def __init__(self, cube):
        self.part, self.stage = cube, 0

    sends, takes = Reduce.sends, Reduce.takes

    def send(self):
        y, z, x, c = place()
        if self.stage == 4:
            self.kept = self.part
            return self.part
        cut = pick_two if self.stage == 2 else pick
        index = (c, x, z // 2, z % 2)[self.stage]
        self.kept = cut(self.part, index)
        return cut(self.part, 1 - index)

    def take(self, value):
        self.stage += 1
        self.part = self.kept + value
        self.out = self.part


class QuickGather:
    def __init__(self, half):
        self.part, self.stage = half, 0

    def sends(self):
        if self.stage == 0:
            return [(f, self.part) for f in (across_near, across_far, across_third)]
        if self.stage == 1:
            return [(f, self.part) for f in (across_rep, across_x, across_both, across_core)]
        return [(across_core, part) for part in self.beside]

    def takes(self, values):
        self.stage += 1
        if self.stage == 1:
            self.part = jnp.concatenate([self.part, *values])
        elif self.stage == 2:
            self.beside, self.other = values[:3], values[3]
        else:
            self.out = [self.part, *self.beside, self.other, *values]


class Gather:
    def __init__(self, half, cuts=()):
        self.part, self.stage, self.cuts, self.got = half, 0, cuts, []

    def sends(self):
        if self.stage == 1 and self.cuts:
            bounds = (0, *self.cuts, self.part.shape[2])
            return [(across_far, self.part[:, :, bounds[len(self.got)] : bounds[len(self.got) + 1]])]
        if self.stage < 3:
            return [((across_near, across_far, across_two)[self.stage], self.part)]
        if self.stage == 3:
            return [(across_one, self.part), (across_one, self.two), (across_core, self.part), (across_core, self.two)]
        return [(across_core, part) for part in self.one]

    def takes(self, values):
        if self.stage == 1:
            self.got += values
            if len(self.got) <= len(self.cuts):
                return
            values = [jnp.concatenate(self.got, axis=2)] if self.cuts else values
        self.stage += 1
        if self.stage < 3:
            self.part = jnp.concatenate([self.part, values[0]])
        elif self.stage == 3:
            self.two = values[0]
        elif self.stage == 4:
            self.one, self.other = values[:2], values[2:]
        else:
            self.out = [self.part, self.two, *self.one, *self.other, *values]


def step(movers, kernel=None, *inputs):
    sends = [m.sends() for m in movers]
    inputs, arrays = lax.optimization_barrier((inputs, [[a for _, a in s] for s in sends]))
    got = [[f(a) for (f, _), a in zip(s, each)] for s, each in zip(sends, arrays)]
    outs = kernel(*inputs) if kernel is not None else ()
    outs, got = lax.optimization_barrier((outs, got))
    for m, g in zip(movers, got):
        m.takes(g)
    return outs


def group_columns(weight, g0, ng, width):
    cuts = []
    for g in range(g0, g0 + ng):
        cuts += [weight[:, part * width + g * GW : part * width + (g + 1) * GW] for part in range(3)]
    return jnp.concatenate(cuts, axis=1)


def small_block(smalls, lanes):
    total = None
    for row, vector in enumerate(smalls):
        block = jnp.pad(vector[None, :], ((row, SMALL_ROWS - 1 - row), (0, lanes - vector.shape[0])))
        total = block if total is None else total + block
    return total


class Done:
    def __init__(self, out):
        self.out = out


def local(tuned, n, tokens, pre_gain, pre_shift, inward_weight, inward_bias, rotary_freqs, outward_weight,
          outward_bias, mlp_gain, mlp_shift, up_weight, up_bias, down_weight, down_bias, keep_mask, kept_counts,
          patch_rows, patch_cols, cotangent):
    total, width = tokens.shape
    groups = width // GW
    wide = up_weight.shape[1]
    rows = width // n
    smalls = [pre_gain, pre_shift, inward_bias, rotary_freqs, outward_bias, mlp_gain, mlp_shift, up_bias, down_bias]
    lengths = [s.shape[0] for s in smalls]
    slot = jnp.arange(total, dtype=jnp.int32)
    count = kept_counts
    key_bias = jnp.where((slot < count[0]) & (keep_mask[0] == 1), 0.0, NEG).astype(F32)
    lines = [patch_cols[0].astype(F32), patch_rows[0].astype(F32), key_bias]
    pos = jnp.stack(lines + [jnp.zeros_like(key_bias)] * 5)
    core = (lax.axis_index("fsdp") % 2).astype(jnp.int32)[None]
    rep = lax.axis_index("rep").astype(jnp.int32)[None]

    if tuned:
        shards = pack(rep, inward_weight, outward_weight, up_weight, down_weight, smalls)
        first, second, outup, downs = QuickGather(shards[0]), Gather(shards[1]), Gather(shards[2], (640,)), Gather(shards[3])
        quick, table = piece_tables()
        order = first_of_owner(quick, n)
        step([first])
        step([first, second])
        step([first])
        load = skip = rows
        small_pieces = first.out
    else:
        gather = lambda a: lax.all_gather(a, "fsdp", axis=0, tiled=True)
        small = small_block(smalls, 3 * GW // 2)
        quick = table = jnp.array([0, 0, 0, 1], jnp.int32)
        order = jnp.arange(n, dtype=jnp.int32)
        load, skip = width, SMALL_ROWS
        small_pieces = [jnp.pad(gather(small[None]), ((0, 0), (skip, 0), (0, 0)))]
        weights = [group_columns(inward_weight, 0, 1, width), group_columns(inward_weight, 1, groups - 1, width),
                   jnp.concatenate([outward_weight, up_weight], axis=1), down_weight]
        first, second, outup, downs = [Done([gather(w)[None]]) for w in weights]
        outup = Done([half[None] for half in jnp.split(outup.out[0][0], 2, axis=1)])

    def run(movers, kernel, *inputs):
        return step(movers, kernel, *inputs) if tuned else kernel(*inputs)

    part = functools.partial
    n1, cosine, sine, vec, aux = run([second, outup], part(prologue, lengths, n, skip), order, tokens, pos, small_pieces)

    q0, k0, v0 = run([second, outup], part(qkv, 0, 1, load), quick, n1, vec, cosine, sine, first.out)
    att, lse0, wide0 = run([second, outup], part(attend, 0, width), q0, k0, v0, pos)
    if tuned:
        step([second])
    q1, k1, v1 = run([outup, downs], part(qkv, 1, groups - 1, load), table, n1, vec, cosine, sine, second.out)
    att, lse1, wide1 = run([outup, downs], part(attend, 1, width), q1, k1, v1, pos, att)
    if tuned:
        step([outup])
    middle, n2, gd, act, slope = run(
        [downs], part(up_first, load, wide), table, count, att, tokens, cotangent, vec, outup.out
    )
    act, slope = run([downs], part(up_second, load), table, count, n2, act, slope, vec, outup.out)

    layout = (n // 4, 2, 2)

    def gradient(name, pairs):
        if tuned:
            return weight_grad(core, pairs, layout, name, name == "in_grad0")
        return lax.psum(lax.psum_scatter(plain_grad(pairs, name), "fsdp", scatter_dimension=0, tiled=True), "rep")

    def reduction(movers, name, pairs):
        out = run(movers, part(gradient, name), pairs)
        return Reduce(*out) if tuned else Done(out)

    r_down = reduction([downs], "down_grad", [(act, gd)])
    outputs, gmid, gb, ga, gu, sums, ubsum = run(
        [r_down], part(down, load), table, count, act, slope, middle, cotangent, gd, vec, outup.out, downs.out
    )
    r_up = reduction([r_down], "up_grad", [(att, gb), (n2, gu)])
    backs = []
    heads = ((0, 0, q0, k0, v0, lse0, wide0), (1, 0, q1, k1, v1, lse1, wide1), (2, 1, q1, k1, v1, lse1, wide1))

    def back(movers, which):
        g0, l0, q, k, v, lse, att_wide = heads[which]
        backs.append(run(movers, part(attend_back, g0, l0), q, k, v, ga, lse, att_wide, aux, cosine, sine))

    def in_gradient(movers, name, which):
        return reduction(movers, name, [(n1, backs[g][0]) for g in which])

    back([r_down, r_up], 0)
    back([r_down, r_up], 1)
    r_in0 = in_gradient([r_down, r_up], "in_grad0", (0, 1))
    if tuned:
        step([r_in0])
    back([r_down, r_up, r_in0], 2)
    r_in1 = in_gradient([r_up, r_in0], "in_grad1", (2,))
    grad_tokens, first_sums = run(
        [r_up, r_in0, r_in1], part(final, load, [3 * GW, 3 * GW * (groups - 1)]),
        (quick, table), tokens, gmid, vec, [b[0] for b in backs], [first.out, second.out]
    )
    small_sums = fold(n, tuned, [b[1] for b in backs], [b[2] for b in backs], sums, ubsum, first_sums)
    if tuned:
        r_small = SmallReduce(small_sums)
        step([r_small, r_in0, r_in1])
        step([r_small, r_in0, r_in1])
        step([r_small, r_in1])
        step([r_small, r_in1])
        d_out, d_up, d_down = step([r_small, r_in1], finish, rep, r_up.out, r_down.out)
        mine = r_small.out
        d_inward = finish_inward((2, 1), rep, [r_in0.out, r_in1.out])
    else:
        mine = lax.psum(lax.psum_scatter(small_sums, "fsdp", scatter_dimension=0, tiled=True), "rep")[0]
        blocks = [r.out[:, 3 * g * GW : 3 * (g + 1) * GW] for r, ng in ((r_in0, 2), (r_in1, 1)) for g in range(ng)]
        d_inward = jnp.concatenate([b[:, p * GW : (p + 1) * GW] for p in range(3) for b in blocks], axis=1)
        d_out, d_up, d_down = r_up.out[:, :width], r_up.out[:, width:], r_down.out
    each = width // n
    line = {name: mine[row * 128 + lane :] for name, row, lane in FOLD}
    o_bias, o_ubias = line["bias"][: 2 * each], line["ubias"][: wide // n]
    o_vbias, o_freqs, o_gain, o_shift, o_obias, o_mgain, o_mshift, o_dbias = [
        line[name][:each] for name in ("value", "freqs", "gain", "shift", "obias", "mgain", "mshift", "dbias")
    ]
    return (outputs, grad_tokens, o_gain, o_shift, d_inward, o_bias, o_vbias, o_freqs, d_out, o_obias,
            o_mgain, o_mshift, d_up, o_ubias, d_down, o_dbias)


def solution(mesh):
    n = mesh.shape["fsdp"]
    tuned = mesh.shape["rep"] == 2 and n == 16
    row = P(("rep", "fsdp"), None)
    vec, mat = P("fsdp"), P("fsdp", None)
    return jax.shard_map(
        functools.partial(local, tuned, n),
        mesh=mesh,
        in_specs=(row, vec, vec, mat, vec, vec, mat, vec, vec, vec, mat, vec, mat, vec, row,
                  P(("rep", "fsdp")), row, row, row),
        out_specs=(row, row, vec, vec, mat, vec, vec, vec, mat, vec, vec, vec, mat, vec, mat, vec),
        check_vma=False,
    )
```

```python
import functools
import math

import jax
import jax.numpy as jnp
from jax import lax
from jax.experimental import pallas as pl
from jax.experimental.pallas import tpu as pltpu
from jax.sharding import PartitionSpec as P

HD = 64
LOG2E = 1.4426950408889634
EPS = 1e-06
NEG = -1e30
F32 = jnp.float32
BF16 = jnp.bfloat16
GH = 4
GW = GH * HD
HALF = GW // 2


def dims(lhs, rhs, lhs_axis, rhs_axis):
    return lax.dot_general(
        lhs, rhs, (((lhs_axis,), (rhs_axis,)), ((), ())), preferred_element_type=F32
    )


def nn(lhs, rhs):
    return dims(lhs, rhs, 1, 0)


def nt(lhs, rhs):
    return dims(lhs, rhs, 1, 1)


def tn(lhs, rhs):
    return dims(lhs, rhs, 0, 0)


def params(grid, mib):
    return pltpu.CompilerParams(
        dimension_semantics=("arbitrary",) * len(grid), vmem_limit_bytes=mib * 2**20
    )


def whole(shape):
    return pl.BlockSpec(shape, lambda *idx: (0,) * len(shape))


ANY = pl.BlockSpec(memory_space=pl.ANY)
SMEM = pl.BlockSpec(memory_space=pltpu.SMEM)
NEAR = pl.BlockSpec(memory_space=pltpu.VMEM)


def kept(shape, dtype):
    return pltpu.HBM(shape, dtype)


def far(*arrays):
    return [pltpu.with_memory_space_constraint(a, pltpu.HBM) for a in arrays]


def cost(flops, bytes_moved, transcendental=0):
    return pl.CostEstimate(
        flops=int(flops), bytes_accessed=int(bytes_moved), transcendentals=int(transcendental)
    )


def group_perm(transposed):
    row = lax.broadcasted_iota(jnp.int32, (GW, GW), 0)
    col = lax.broadcasted_iota(jnp.int32, (GW, GW), 1)
    packed, natural = (row, col) if transposed else (col, row)
    half = packed // HALF
    head = (packed % HALF) // (HD // 2)
    source = head * HD + half * (HD // 2) + packed % (HD // 2)
    return jnp.where(source == natural, 1.0, 0.0).astype(BF16)


def packed_head_mask(head):
    lane = lax.broadcasted_iota(jnp.int32, (1, GW), 1)
    return (lane % HALF) // (HD // 2) == head


def natural_head_mask(head):
    lane = lax.broadcasted_iota(jnp.int32, (1, GW), 1)
    return lane // HD == head


def normalize(values):
    center = values - jnp.mean(values, axis=-1, keepdims=True)
    spread = jnp.mean(center * center, axis=-1, keepdims=True)
    inverse = lax.rsqrt(spread + EPS)
    return center * inverse, inverse


def load_pieces(table, sources, target, sem, rows, column=True):
    copies = []
    slots = table.shape[0] // 2
    for source in sources:
        width = source.shape[2]
        for slot in range(source.shape[0]):
            number = len(copies)
            row = pl.multiple_of(table[number] * rows, rows)
            col = pl.multiple_of(table[slots + number] * width, width) if column else 0
            copies.append(
                pltpu.make_async_copy(
                    source.at[slot, pl.ds(0, rows)], target.at[pl.ds(row, rows), pl.ds(col, width)], sem.at[number]
                )
            )
    return copies


def piece_count(sources):
    return sum(s.shape[0] for s in sources)


SMALL_ROWS = 16


def pack_kernel(rep, in_ref, out_ref, up_ref, down_ref, *rest):
    vectors, (one_ref, two_ref, three_ref, four_ref, small_ref) = rest[:-5], rest[-5:]
    small_ref[...] = jnp.zeros_like(small_ref)
    for row, vector in enumerate(vectors):
        length = vector.shape[0]
        small_ref[row : row + 1, :length] = vector[...].astype(F32).reshape(1, length)

    def write(y):
        rows, third = in_ref.shape[0], in_ref.shape[1] // 3
        groups = third // GW
        cuts = [in_ref[:, pl.ds(part * third + g * GW, GW)] for g in range(groups) for part in range(3)]
        first = jnp.concatenate(cuts[:3], axis=1)
        half = first.shape[1] // 2
        one_ref[0, pl.ds(0, rows), :] = first[:, y * half : (y + 1) * half]
        one_ref[0, pl.ds(rows, SMALL_ROWS), :] = small_ref[...].astype(BF16)
        rest = jnp.concatenate(cuts[3:], axis=1)
        half = rest.shape[1] // 2
        two_ref[0] = rest[:, y * half : (y + 1) * half]
        both = jnp.concatenate([out_ref[...], up_ref[...]], axis=1)
        half = both.shape[1] // 2
        three_ref[0] = both[:, y * half : (y + 1) * half]
        half = down_ref.shape[1] // 2
        four_ref[0] = down_ref[:, pl.ds(y * half, half)]

    @pl.when(rep[0] == 0)
    def _():
        write(0)

    @pl.when(rep[0] == 1)
    def _():
        write(1)


def pack(rep, inward, outward, upward, downward, smalls):
    rows, wide = inward.shape
    width = wide // 3
    shapes = [
        (1, rows + SMALL_ROWS, 3 * GW // 2),
        (1, rows, (wide - 3 * GW) // 2),
        (1, rows, (width + upward.shape[1]) // 2),
        (1, downward.shape[0], width // 2),
    ]
    return pl.pallas_call(
        pack_kernel,
        in_specs=[SMEM] + [pl.BlockSpec(memory_space=pltpu.VMEM)] * (4 + len(smalls)),
        out_specs=[pl.BlockSpec(memory_space=pltpu.VMEM)] * 4,
        out_shape=[jax.ShapeDtypeStruct(shape, BF16) for shape in shapes],
        scratch_shapes=[pltpu.VMEM((SMALL_ROWS, 3 * GW // 2), F32)],
        cost_estimate=cost(0, 2 * rows * width * 24),
        name="pack",
    )(rep, inward, outward, upward, downward, *smalls)


V_GAIN, V_SHIFT, V_BIAS, V_FREQ, V_OBIAS, V_MGAIN, V_MSHIFT, V_UBIAS, V_DBIAS = range(9)


def prologue_kernel(lengths, owners, rows, npieces, order, x_ref, pos_ref, *rest):
    pieces = rest[:npieces]
    n1_ref, cos_ref, sin_ref, vec_ref, aux_ref, got, fc, fr, sem = rest[npieces:]
    width = x_ref.shape[1]

    @pl.when(pl.program_id(0) == 0)
    def _():
        copies = []
        for number, piece in enumerate(pieces):
            slots = piece.shape[0]
            copies.append(
                pltpu.make_async_copy(
                    piece.at[:, pl.ds(rows, SMALL_ROWS)], got.at[pl.ds(number * slots, slots)], sem.at[number]
                )
            )
        for copy in copies:
            copy.start()
        for copy in copies:
            copy.wait()
        vec_ref[...] = jnp.zeros_like(vec_ref)
        for owner in range(owners):
            tile = got[order[owner]].astype(F32)
            for row, length in enumerate(lengths):
                vec_ref[row : row + 1, owner * length : (owner + 1) * length] = tile[row : row + 1, :length]
        freq = jnp.broadcast_to(vec_ref[V_FREQ : V_FREQ + 1, :width], (16, width)).astype(BF16)
        source = lax.broadcasted_iota(jnp.int32, (width, width // 2), 0)
        target = lax.broadcasted_iota(jnp.int32, (width, width // 2), 1)
        fc[...] = nn(freq, jnp.where(source == 2 * target, 1.0, 0.0).astype(BF16))[:8]
        fr[...] = nn(freq, jnp.where(source == 2 * target + 1, 1.0, 0.0).astype(BF16))[:8]

    xhat, _ = normalize(x_ref[...])
    n1_ref[...] = (xhat * vec_ref[V_GAIN : V_GAIN + 1, :width] + vec_ref[V_SHIFT : V_SHIFT + 1, :width]).astype(BF16)
    pos = pos_ref[...]
    aux = jnp.transpose(jnp.concatenate([pos, jnp.zeros((120, pos.shape[1]), F32)], axis=0))
    aux_ref[...] = aux
    angle = aux[:, 0:1] * fc[0:1, :] + aux[:, 1:2] * fr[0:1, :]
    cosine, sine = cos_sin(angle)
    cos_ref[...] = cosine
    sin_ref[...] = sine


def prologue(lengths, owners, rows, order, x, pos, pieces, rb=256):
    total, width = x.shape
    pairs = width // 2
    grid = (total // rb,)
    blk = lambda w: pl.BlockSpec((rb, w), lambda i: (i, 0))
    wide = max(lengths) * owners
    return pl.pallas_call(
        functools.partial(prologue_kernel, lengths, owners, rows, len(pieces)),
        grid=grid,
        in_specs=[SMEM, blk(width), pl.BlockSpec((8, rb), lambda i: (0, i))] + [ANY] * len(pieces),
        out_specs=[blk(width), blk(pairs), blk(pairs), whole((16, wide)), blk(128)],
        out_shape=[
            kept((total, width), BF16),
            kept((total, pairs), F32),
            kept((total, pairs), F32),
            kept((16, wide), F32),
            kept((total, 128), F32),
        ],
        scratch_shapes=[
            pltpu.VMEM((piece_count(pieces), SMALL_ROWS, pieces[0].shape[2]), BF16),
            pltpu.VMEM((8, pairs), F32),
            pltpu.VMEM((8, pairs), F32),
            pltpu.SemaphoreType.DMA((len(pieces),)),
        ],
        compiler_params=params(grid, 24),
        cost_estimate=cost(total * width * 40, total * width * 10),
        name="prologue",
    )(order, *far(x), pos, *far(*pieces))


QUARTER = (1.5703125, 4.837512969970703125e-4, 7.549789948768648e-8)


def cos_sin(angle):
    turns = jnp.floor(angle * 0.6366197723675814 + 0.5)
    r = ((angle - turns * QUARTER[0]) - turns * QUARTER[1]) - turns * QUARTER[2]
    r2 = r * r
    s = r + r * r2 * (-1.6666654611e-1 + r2 * (8.3321608736e-3 - 1.9515295891e-4 * r2))
    c = 1.0 - 0.5 * r2 + r2 * r2 * (4.166664568298827e-2 + r2 * (-1.388731625493765e-3 + 2.443315711809948e-5 * r2))
    quad = turns.astype(jnp.int32)
    odd = (quad & 1) == 1
    cosine = jnp.where(odd, s, c)
    sine = jnp.where(odd, c, s)
    cosine = jnp.where(((quad + 1) & 2) == 2, -cosine, cosine)
    sine = jnp.where((quad & 2) == 2, -sine, sine)
    return cosine, sine


def qkv_kernel(g0, npieces, rows, table, n1_ref, vec_ref, cos_ref, sin_ref, *rest):
    pieces = rest[:npieces]
    q_ref, k_ref, v_ref, w, wp, bp, sem = rest[npieces:]
    width = n1_ref.shape[1]
    groups = w.shape[1] // (3 * GW)
    bias_ref = vec_ref.at[V_BIAS : V_BIAS + 1, :]

    @pl.when(pl.program_id(0) == 0)
    def _():
        copies = load_pieces(table, pieces, w, sem, rows)
        for copy in copies:
            copy.start()
        perm = group_perm(False)
        for copy in copies:
            copy.wait()
        for g in range(groups):
            for part in range(2):
                packed = pl.ds((g * 2 + part) * GW, GW)
                wp[:, packed] = nn(w[:, pl.ds((g * 3 + part) * GW, GW)], perm).astype(BF16)
                natural = pl.ds(part * width + (g0 + g) * GW, GW)
                spread = jnp.broadcast_to(bias_ref[:, natural].astype(BF16), (16, GW))
                bp[:, packed] = nn(spread, perm)[:8]

    n1 = n1_ref[...]
    for g in range(groups):
        cosine = cos_ref[:, pl.ds((g0 + g) * HALF, HALF)]
        sine = sin_ref[:, pl.ds((g0 + g) * HALF, HALF)]
        for part, out, scale in ((0, q_ref, HD**-0.5 * LOG2E), (1, k_ref, 1.0)):
            packed = pl.ds((g * 2 + part) * GW, GW)
            mixed = nn(n1, wp[:, packed]) + bp[0:1, packed]
            a, b = mixed[:, :HALF], mixed[:, HALF:]
            first = a * cosine - b * sine
            second = a * sine + b * cosine
            if scale != 1.0:
                first = first * scale
                second = second * scale
            out[:, pl.ds(g * GW, HALF)] = first.astype(BF16)
            out[:, pl.ds(g * GW + HALF, HALF)] = second.astype(BF16)
        bias = bias_ref[:, pl.ds(2 * width + (g0 + g) * GW, GW)]
        v_ref[:, pl.ds(g * GW, GW)] = (nn(n1, w[:, pl.ds((g * 3 + 2) * GW, GW)]) + bias).astype(BF16)


def qkv(g0, groups, rows, table, n1, vec, cosine, sine, pieces):
    total, width = n1.shape
    rb = 512
    pairs = width // 2
    grid = (total // rb,)
    blk = lambda w: pl.BlockSpec((rb, w), lambda i: (i, 0))
    out = kept((total, groups * GW), BF16)
    copies = piece_count(pieces)
    return pl.pallas_call(
        functools.partial(qkv_kernel, g0, len(pieces), rows),
        grid=grid,
        in_specs=[SMEM, blk(width), whole(vec.shape), blk(pairs), blk(pairs)] + [ANY] * len(pieces),
        out_specs=[blk(groups * GW)] * 3,
        out_shape=[out] * 3,
        scratch_shapes=[
            pltpu.VMEM((width, 3 * groups * GW), BF16),
            pltpu.VMEM((width, 2 * groups * GW), BF16),
            pltpu.VMEM((8, 2 * groups * GW), F32),
            pltpu.SemaphoreType.DMA((copies,)),
        ],
        compiler_params=params(grid, 24),
        cost_estimate=cost(total * width * groups * GW * 6, total * width * 8 + width * groups * GW * 6),
        name="qkv",
    )(table, *far(n1, vec, cosine, sine, *pieces))


def attend_kernel(q_ref, k_ref, v_ref, pos_ref, *rest):
    att_ref, lse_ref, wide_ref, mask = rest[-4:]
    g, r = pl.program_id(0), pl.program_id(1)
    rb, keys = q_ref.shape[0], k_ref.shape[0]
    here = pl.ds(pl.multiple_of(r * rb, rb), rb)

    @pl.when(g == 0)
    def _():
        row = lax.broadcasted_iota(jnp.int32, (rb, keys), 0) + r * rb
        col = lax.broadcasted_iota(jnp.int32, (rb, keys), 1)
        mask[here, :] = jnp.where(row == col, 0.0, jnp.broadcast_to(pos_ref[2:3, :], (rb, keys)))

    q = q_ref[...]
    k = k_ref[...]
    v = v_ref[...]
    total = jnp.zeros((rb, GW), F32)
    lane = lax.broadcasted_iota(jnp.int32, (rb, 128), 1)
    logs = jnp.zeros((rb, 128), F32)
    for h in range(GH):
        qm = jnp.where(packed_head_mask(h), q, jnp.zeros_like(q))
        scores = nt(qm, k) + mask[here, :]
        top = jnp.max(scores, axis=-1, keepdims=True)
        weight = jnp.exp2(scores - top)
        norm = jnp.sum(weight, axis=-1, keepdims=True)
        vm = jnp.where(natural_head_mask(h), v, jnp.zeros_like(v))
        total = total + nn(weight.astype(BF16), vm) * (1.0 / norm)
        logs = jnp.where(lane == h, top + jnp.log2(norm), logs)
    att_ref[...] = total.astype(BF16)
    wide_ref[...] = total
    lse_ref[...] = jnp.transpose(logs)[:8, :]


def attend(g0, full, q, k, v, pos, *att, rb=512):
    total, width = q.shape
    groups = width // GW
    grid = (groups, total // rb)
    return pl.pallas_call(
        attend_kernel,
        grid=grid,
        in_specs=[
            pl.BlockSpec((rb, GW), lambda g, r: (r, g)),
            pl.BlockSpec((total, GW), lambda g, r: (0, g)),
            pl.BlockSpec((total, GW), lambda g, r: (0, g)),
            whole((8, total)),
        ]
        + [ANY] * len(att),
        out_specs=[
            pl.BlockSpec((rb, GW), lambda g, r: (r, g + g0)),
            pl.BlockSpec((None, 8, rb), lambda g, r: (g, 0, r)),
            pl.BlockSpec((rb, GW), lambda g, r: (r, g)),
        ],
        out_shape=[
            kept((total, full), BF16),
            kept((groups, 8, total), F32),
            kept((total, width), F32),
        ],
        input_output_aliases={4: 0} if att else {},
        scratch_shapes=[pltpu.VMEM((total, total), F32)],
        compiler_params=params(grid, 32),
        cost_estimate=cost(total * total * width * 16, total * width * 8, total * total * 12),
        name="attend",
    )(*far(q, k, v, pos, *att))


PHI_SCALE = 0.3989422804014327
TAIL_SCALE = 0.44 * 0.7071067811865476
TAIL = (
    0.12411047596471954,
    0.12443560910041027,
    0.10865662380098591,
    0.10790671631036299,
    -0.010091621907114547,
    0.14834527631989725,
    -0.13897496529649409,
    0.03561197654899638,
)


def gelu_parts(h):
    t = 1.0 / (1.0 + TAIL_SCALE * jnp.abs(h))
    poly = TAIL[-1]
    for coefficient in TAIL[-2::-1]:
        poly = poly * t + coefficient
    bell = jnp.exp2((-0.5 * LOG2E) * (h * h))
    tail = poly * t * bell
    phi = jnp.where(h < 0, tail, 1.0 - tail)
    return h * phi, phi + h * (bell * PHI_SCALE)


def up_kernel(half, npieces, rows, table, count, *refs):
    if half == 0:
        att_ref, x_ref, cot_ref, vec_ref = refs[:4]
        pieces = refs[4 : 4 + npieces]
        mid_ref, n2_ref, gd_ref, act_ref, gp_ref, w, sem = refs[4 + npieces :]
    else:
        n2_ref, vec_ref = refs[:2]
        pieces = refs[2 : 2 + npieces]
        act_ref, gp_ref, w, sem = refs[-4:]
    rb, width = n2_ref.shape

    @pl.when(pl.program_id(0) == 0)
    def _():
        slots = table.shape[0] // 2
        copies = load_pieces(table, pieces, w, sem, rows, column=False)
        for start in (True, False):
            for number, copy in enumerate(copies):

                @pl.when(table[slots + number] == half)
                def _():
                    if start:
                        copy.start()
                    else:
                        copy.wait()

    if half == 0:
        slot = lax.broadcasted_iota(jnp.int32, (rb, 1), 0) + pl.program_id(0) * rb
        valid = jnp.where(slot < count[0], 1.0, 0.0)
        gd_ref[...] = (valid * cot_ref[...]).astype(BF16)
        branch = nn(att_ref[...], w[:, pl.ds(0, width)]) + vec_ref[V_OBIAS : V_OBIAS + 1, :width]
        middle = x_ref[...] + valid * branch
        mid_ref[...] = middle
        xhat, _ = normalize(middle)
        n2 = (xhat * vec_ref[V_MGAIN : V_MGAIN + 1, :width] + vec_ref[V_MSHIFT : V_MSHIFT + 1, :width]).astype(BF16)
        n2_ref[...] = n2
        place = width
    else:
        n2 = n2_ref[...]
        place = 0
    first = half * (w.shape[1] - width)
    step = 384
    for c in range(act_ref.shape[1] // step):
        cut = pl.ds(c * step, step)
        hidden = nn(n2, w[:, pl.ds(place + c * step, step)]) + vec_ref[V_UBIAS : V_UBIAS + 1, pl.ds(first + c * step, step)]
        act, slope = gelu_parts(hidden)
        act_ref[:, cut] = act.astype(BF16)
        gp_ref[:, cut] = slope.astype(BF16)


def up_first(rows, wide, table, count, att, x, cot, vec, pieces, rb=256):
    total, width = x.shape
    part = (width + wide) // 2
    grid = (total // rb,)
    blk = lambda w: pl.BlockSpec((rb, w), lambda i: (i, 0))
    return pl.pallas_call(
        functools.partial(up_kernel, 0, len(pieces), rows),
        grid=grid,
        in_specs=[SMEM, SMEM, blk(width), blk(width), blk(width), whole(vec.shape)] + [ANY] * len(pieces),
        out_specs=[blk(width), blk(width), blk(width), blk(part - width), blk(part - width)],
        out_shape=[
            kept((total, width), F32),
            kept((total, width), BF16),
            kept((total, width), BF16),
            kept((total, wide), BF16),
            kept((total, wide), BF16),
        ],
        scratch_shapes=[pltpu.VMEM((width, part), BF16), pltpu.SemaphoreType.DMA((piece_count(pieces),))],
        compiler_params=params(grid, 32),
        cost_estimate=cost(total * width * part * 2, total * width * 20, total * wide),
        name="up_first",
    )(table, count, *far(att, x, cot, vec, *pieces))


def up_second(rows, table, count, n2, act, slope, vec, pieces, rb=256):
    total, width = n2.shape
    wide = act.shape[1]
    part = (width + wide) // 2
    grid = (total // rb,)
    cols = pl.BlockSpec((pl.Element(rb), pl.Element(part)), lambda i: (i * rb, part - width))
    return pl.pallas_call(
        functools.partial(up_kernel, 1, len(pieces), rows),
        grid=grid,
        in_specs=[SMEM, SMEM, pl.BlockSpec((rb, width), lambda i: (i, 0)), whole(vec.shape)]
        + [ANY] * (len(pieces) + 2),
        out_specs=[cols, cols],
        out_shape=[kept((total, wide), BF16)] * 2,
        input_output_aliases={4 + len(pieces): 0, 5 + len(pieces): 1},
        scratch_shapes=[pltpu.VMEM((width, part), BF16), pltpu.SemaphoreType.DMA((piece_count(pieces),))],
        compiler_params=params(grid, 32),
        cost_estimate=cost(total * width * part * 2, total * width * 20, total * wide),
        name="up_second",
    )(table, count, *far(n2, vec, *pieces, act, slope))


def down_kernel(nup, ndown, rows, table, count, act_ref, gp_ref, mid_ref, cot_ref, gd_ref, vec_ref, *rest):
    ups = rest[:nup]
    downs = rest[nup : nup + ndown]
    (out_ref, gm_ref, gb_ref, ga_ref, gu_ref, sums_ref, ubsum_ref, w, wd, sem, sem_d) = rest[nup + ndown :]
    i = pl.program_id(0)
    rb, width = mid_ref.shape
    wide = act_ref.shape[1]

    @pl.when(i == 0)
    def _():
        first = load_pieces(table, downs, wd, sem_d, rows * (wide // width))
        second = load_pieces(table, ups, w, sem, rows)
        for copy in first + second:
            copy.start()
        for copy in first + second:
            copy.wait()
        sums_ref[...] = jnp.zeros_like(sums_ref)
        ubsum_ref[...] = jnp.zeros_like(ubsum_ref)

    slot = lax.broadcasted_iota(jnp.int32, (rb, 1), 0) + i * rb
    valid = jnp.where(slot < count[0], 1.0, 0.0)
    middle = mid_ref[...]
    cot = cot_ref[...]
    gd = gd_ref[...]
    lowered = nn(act_ref[...], wd[...]) + vec_ref[V_DBIAS : V_DBIAS + 1, :width]
    out_ref[...] = middle + valid * lowered
    step = 1024
    gn2 = jnp.zeros((rb, width), F32)
    for c in range(wide // step):
        cut = pl.ds(c * step, step)
        g = nt(gd, wd[cut, :]) * gp_ref[:, cut].astype(F32)
        g_low = g.astype(BF16)
        gu_ref[:, cut] = g_low
        ubsum_ref[0:1, cut] += jnp.sum(g_low.astype(F32), axis=0, keepdims=True)
        gn2 = gn2 + nt(g_low, w[:, pl.ds(width + c * step, step)])
    xhat, inverse = normalize(middle)
    sums_ref[0:1, :] += jnp.sum(gn2 * xhat, axis=0, keepdims=True)
    sums_ref[1:2, :] += jnp.sum(gn2, axis=0, keepdims=True)
    e = gn2 * vec_ref[V_MGAIN : V_MGAIN + 1, :width]
    back = (e - jnp.mean(e, axis=-1, keepdims=True) - xhat * jnp.mean(e * xhat, axis=-1, keepdims=True)) * inverse
    gmid = cot + back
    gm_ref[...] = gmid
    gb = (valid * gmid).astype(BF16)
    gb_ref[...] = gb
    sums_ref[2:3, :] += jnp.sum(gb.astype(F32), axis=0, keepdims=True)
    sums_ref[3:4, :] += jnp.sum(gd.astype(F32), axis=0, keepdims=True)
    ga_ref[...] = nt(gb, w[:, pl.ds(0, width)]).astype(BF16)


def down(rows, table, count, act, gp, mid, cot, gd, vec, ups, downs, rb=256):
    total, width = mid.shape
    wide = act.shape[1]
    grid = (total // rb,)
    blk = lambda w: pl.BlockSpec((rb, w), lambda i: (i, 0))
    return pl.pallas_call(
        functools.partial(down_kernel, len(ups), len(downs), rows),
        grid=grid,
        in_specs=[SMEM, SMEM, blk(wide), blk(wide), blk(width), blk(width), blk(width), whole(vec.shape)]
        + [ANY] * (len(ups) + len(downs)),
        out_specs=[blk(width), blk(width), blk(width), blk(width), blk(wide), whole((8, width)), whole((8, wide))],
        out_shape=[
            kept((total, width), F32),
            kept((total, width), F32),
            kept((total, width), BF16),
            kept((total, width), BF16),
            kept((total, wide), BF16),
            kept((8, width), F32),
            kept((8, wide), F32),
        ],
        scratch_shapes=[
            pltpu.VMEM((width, width + wide), BF16),
            pltpu.VMEM((wide, width), BF16),
            pltpu.SemaphoreType.DMA((piece_count(ups),)),
            pltpu.SemaphoreType.DMA((piece_count(downs),)),
        ],
        compiler_params=params(grid, 44),
        cost_estimate=cost(total * width * (width + 3 * wide) * 2, total * (width * 20 + wide * 6)),
        name="down",
    )(table, count, *far(act, gp, mid, cot, gd, vec, *ups, *downs))


def grad_kernel(pairs, mids, reps, rows, core, *rest):
    keep_ref, send_ref = rest[-2:]
    part = core[0]

    def spot(parity, mid, rep):
        return jnp.where(parity == 0, mid, rep), jnp.where(parity == 0, rep, mid)

    each = keep_ref.shape[-1]
    offset = 0
    for at, bt in pairs:
        a, b_ref = rest[at][...], rest[bt]
        begin = 0
        while begin < b_ref.shape[1]:
            column = offset + begin
            step = min(b_ref.shape[1] - begin, each - column % each, 768)
            result = tn(a, b_ref[:, pl.ds(begin, step)])
            rep, cut = column // each, pl.ds(column % each, step)
            for pair in range(a.shape[1] // (2 * rows)):
                low = result[pair * 2 * rows : pair * 2 * rows + rows]
                high = result[pair * 2 * rows + rows : (pair + 1) * 2 * rows]
                zz, mid = pair // mids, pair % mids
                one, two = spot(part, mid, rep)
                keep_ref[one, two, zz, :, cut] = jnp.where(part == 0, low, high).astype(BF16)
                one, two = spot(1 - part, mid, rep)
                send_ref[one, two, zz, :, cut] = jnp.where(part == 0, high, low).astype(BF16)
            begin += step
        offset += b_ref.shape[1]


def operands(pairs):
    arrays, index = [], []
    for pair in pairs:
        spots = []
        for array in pair:
            if not any(array is other for other in arrays):
                arrays.append(array)
            spots.append([array is other for other in arrays].index(True))
        index.append(spots)
    lefts = {one for one, _ in index}
    return arrays, index, lefts


def weight_grad(core, pairs, layout, name, lasting=False):
    slow, mids, reps = layout
    arrays, index, lefts = operands(pairs)
    total, height = pairs[0][0].shape
    width = sum(b.shape[1] for _, b in pairs)
    rows = height // (slow * mids * 2)
    chunk = 384 if 384 % (2 * mids * rows) == 0 else 2 * mids * rows
    slows = chunk // (2 * mids * rows)
    grid = (height // chunk,)
    shape = (mids, reps, slow, rows, width // reps)
    out = jax.ShapeDtypeStruct(shape, BF16)
    spec = pl.BlockSpec((mids, reps, slows, rows, width // reps), lambda i: (0, 0, i, 0, 0))
    return pl.pallas_call(
        functools.partial(grad_kernel, index, mids, reps, rows),
        grid=grid,
        in_specs=[SMEM]
        + [
            pl.BlockSpec((total, chunk), lambda i: (0, i)) if n in lefts else whole(a.shape)
            for n, a in enumerate(arrays)
        ],
        out_specs=[spec, spec],
        out_shape=[kept(shape, BF16) if lasting else out, out],
        compiler_params=params(grid, 40),
        cost_estimate=cost(total * height * width * 2, total * (height + width) * 2 + height * width * 2),
        name=name,
    )(core, *far(*arrays))


def plain_grad_kernel(pairs, *rest):
    out_ref = rest[-1]
    offset = 0
    for at, bt in pairs:
        a, b_ref = rest[at][...], rest[bt]
        step = min(b_ref.shape[1], 768)
        for c in range(b_ref.shape[1] // step):
            out_ref[:, pl.ds(offset + c * step, step)] = tn(a, b_ref[:, pl.ds(c * step, step)])
        offset += b_ref.shape[1]


def plain_grad(pairs, name):
    arrays, index, lefts = operands(pairs)
    total, height = pairs[0][0].shape
    width = sum(b.shape[1] for _, b in pairs)
    chunk = 384
    grid = (height // chunk,)
    return pl.pallas_call(
        functools.partial(plain_grad_kernel, index),
        grid=grid,
        in_specs=[
            pl.BlockSpec((total, chunk), lambda i: (0, i)) if n in lefts else whole(a.shape)
            for n, a in enumerate(arrays)
        ],
        out_specs=pl.BlockSpec((chunk, width), lambda i: (i, 0)),
        out_shape=jax.ShapeDtypeStruct((height, width), F32),
        compiler_params=params(grid, 63),
        cost_estimate=cost(total * height * width * 2, total * (height + width) * 2 + height * width * 4),
        name=name,
    )(*arrays)


def unrotate(grad, cosine, sine):
    first, second = grad[:, :HALF], grad[:, HALF:]
    return first * cosine + second * sine, second * cosine - first * sine


def angle_grad(grad, rotated):
    return grad[:, HALF:] * rotated[:, :HALF] - grad[:, :HALF] * rotated[:, HALF:]


def back_kernel(q_ref, k_ref, v_ref, do_ref, lse_ref, wide_ref, aux_ref, cos_ref, sin_ref,
                g_ref, fsum_ref, bsum_ref, ds_s, p_s, dk_s, dv_s):
    r = pl.program_id(0)
    rb, keys = q_ref.shape[0], k_ref.shape[0]
    here = pl.ds(pl.multiple_of(r * rb, rb), rb)
    q = q_ref[...]
    k = k_ref[...]
    v = v_ref[...]
    do = do_ref[...]
    zero = jnp.zeros_like(q)
    product = do.astype(F32) * wide_ref[...]
    high = product.astype(BF16)
    low = (product - high.astype(F32)).astype(BF16)
    lane = lax.broadcasted_iota(jnp.int32, (16, GW), 1)
    pick_head = jnp.where(lane // HD == lax.broadcasted_iota(jnp.int32, (16, GW), 0), 1.0, 0.0).astype(BF16)
    inner = nt(pick_head, high) + nt(pick_head, low)
    key = lax.broadcasted_iota(jnp.int32, (keys, rb), 0)
    query = lax.broadcasted_iota(jnp.int32, (keys, rb), 1) + r * rb
    mask = jnp.where(key == query, 0.0, jnp.broadcast_to(aux_ref[:, 2:3], (keys, rb)))
    dq = jnp.zeros((rb, GW), F32)
    qms, doms = [], []
    for h in range(GH):
        qm = jnp.where(packed_head_mask(h), q, zero)
        dom = jnp.where(natural_head_mask(h), do, zero)
        qms.append(qm)
        doms.append(dom)
        soft = jnp.exp2(nt(k, qm) + mask - lse_ref[h : h + 1, :])
        ds = (soft * (nt(v, dom) - inner[h : h + 1, :])).astype(BF16)
        cut = pl.ds(h * rb, rb)
        ds_s[:, cut] = ds
        p_s[:, cut] = soft.astype(BF16)
        km = jnp.where(packed_head_mask(h), k, jnp.zeros_like(k))
        dq = dq + tn(ds, km)
    dk = nn(ds_s[...], jnp.concatenate(qms, axis=0)) * (1.0 / LOG2E)
    dv = nn(p_s[...], jnp.concatenate(doms, axis=0))

    perm = group_perm(True)
    cosine, sine = cos_ref[here, :], sin_ref[here, :]
    dq = dq * (HD**-0.5)
    ang = angle_grad(dq, q.astype(F32) * (HD**0.5 / LOG2E))
    first, second = unrotate(dq, cosine, sine)
    gq = nn(jnp.concatenate([first.astype(BF16), second.astype(BF16)], axis=1), perm)
    g_ref[here, pl.ds(0, GW)] = gq.astype(BF16)
    col, row = aux_ref[here, 0:1], aux_ref[here, 1:2]
    fcol = jnp.sum(ang * col, axis=0, keepdims=True)
    frow = jnp.sum(ang * row, axis=0, keepdims=True)
    qsum = jnp.sum(gq, axis=0, keepdims=True)

    @pl.when(r == 0)
    def _():
        dk_s[...] = dk
        dv_s[...] = dv
        fsum_ref[...] = jnp.zeros_like(fsum_ref)
        fsum_ref[0:1, pl.ds(0, HALF)] = fcol
        fsum_ref[1:2, pl.ds(0, HALF)] = frow
        bsum_ref[0:1, pl.ds(0, GW)] = qsum

    @pl.when(r > 0)
    def _():
        dk_s[...] += dk
        dv_s[...] += dv
        fsum_ref[0:1, pl.ds(0, HALF)] += fcol
        fsum_ref[1:2, pl.ds(0, HALF)] += frow
        bsum_ref[0:1, pl.ds(0, GW)] += qsum

    @pl.when(r == pl.num_programs(0) - 1)
    def _():
        dkf = dk_s[...]
        angk = angle_grad(dkf, k.astype(F32))
        fsum_ref[0:1, pl.ds(0, HALF)] += jnp.sum(angk * aux_ref[:, 0:1], axis=0, keepdims=True)
        fsum_ref[1:2, pl.ds(0, HALF)] += jnp.sum(angk * aux_ref[:, 1:2], axis=0, keepdims=True)
        one, two = unrotate(dkf, cos_ref[...], sin_ref[...])
        gk = nn(jnp.concatenate([one.astype(BF16), two.astype(BF16)], axis=1), perm)
        g_ref[:, pl.ds(GW, GW)] = gk.astype(BF16)
        bsum_ref[0:1, pl.ds(GW, GW)] = jnp.sum(gk, axis=0, keepdims=True)
        gv = dv_s[...].astype(BF16)
        g_ref[:, pl.ds(2 * GW, GW)] = gv
        lane = lax.broadcasted_iota(jnp.int32, (HALF, 2 * HALF), 1)
        pair = lax.broadcasted_iota(jnp.int32, (HALF, 2 * HALF), 0)
        sums = fsum_ref[:, pl.ds(0, HALF)]
        spread = [
            jnp.dot(sums, jnp.where(lane == 2 * pair + odd, 1.0, 0.0), precision=lax.Precision.HIGHEST)
            for odd in range(2)
        ]
        fsum_ref[0:1, :] = spread[0][0:1] + spread[1][1:2]
        bsum_ref[0:1, pl.ds(2 * GW, GW)] = jnp.sum(gv.astype(F32), axis=0, keepdims=True)


def attend_back(g0, l0, q, k, v, do, lse, wide, aux, cosine, sine, rb=512):
    total = q.shape[0]
    grid = (total // rb,)
    return pl.pallas_call(
        back_kernel,
        grid=grid,
        in_specs=[
            pl.BlockSpec((rb, GW), lambda r: (r, l0)),
            pl.BlockSpec((total, GW), lambda r: (0, l0)),
            pl.BlockSpec((total, GW), lambda r: (0, l0)),
            pl.BlockSpec((rb, GW), lambda r: (r, g0)),
            pl.BlockSpec((None, 8, rb), lambda r: (l0, 0, r)),
            pl.BlockSpec((rb, GW), lambda r: (r, l0)),
            whole((total, 128)),
            pl.BlockSpec((total, HALF), lambda r: (0, g0)),
            pl.BlockSpec((total, HALF), lambda r: (0, g0)),
        ],
        out_specs=[whole((total, 3 * GW)), whole((8, GW)), whole((8, 3 * GW))],
        out_shape=[
            kept((total, 3 * GW), BF16),
            jax.ShapeDtypeStruct((8, GW), F32),
            jax.ShapeDtypeStruct((8, 3 * GW), F32),
        ],
        scratch_shapes=[
            pltpu.VMEM((total, GH * rb), BF16),
            pltpu.VMEM((total, GH * rb), BF16),
            pltpu.VMEM((total, GW), F32),
            pltpu.VMEM((total, GW), F32),
        ],
        compiler_params=params(grid, 48),
        cost_estimate=cost(total * total * GW * 40, total * GW * 20, total * total * GH),
        name="attend_back",
    )(*far(q, k, v, do, lse, wide, aux, cosine, sine))


def final_kernel(count, counts, rows, table_one, table_two, x_ref, gm_ref, vec_ref, *rest):
    grads, place = rest[:count], count
    pieces = []
    for number in counts:
        pieces.append(rest[place : place + number])
        place += number
    out_ref, sums_ref = rest[place : place + 2]
    weights = rest[place + 2 : place + 2 + len(counts)]
    sems = rest[place + 2 + len(counts) :]

    @pl.when(pl.program_id(0) == 0)
    def _():
        copies = []
        for table, p, w, sem in zip((table_one, table_two), pieces, weights, sems):
            copies += load_pieces(table, p, w, sem, rows)
        for copy in copies:
            copy.start()
        for copy in copies:
            copy.wait()
        sums_ref[...] = jnp.zeros_like(sums_ref)

    e = jnp.zeros(x_ref.shape, F32)
    group = 0
    for w in weights:
        for g in range(w.shape[1] // (3 * GW)):
            e = e + nt(grads[group][...], w[:, pl.ds(g * 3 * GW, 3 * GW)])
            group += 1
    xhat, inverse = normalize(x_ref[...])
    sums_ref[0:1, :] += jnp.sum(e * xhat, axis=0, keepdims=True)
    sums_ref[1:2, :] += jnp.sum(e, axis=0, keepdims=True)
    eg = e * vec_ref[V_GAIN : V_GAIN + 1, : x_ref.shape[1]]
    back = (eg - jnp.mean(eg, axis=-1, keepdims=True) - xhat * jnp.mean(eg * xhat, axis=-1, keepdims=True)) * inverse
    out_ref[...] = gm_ref[...] + back


def final(rows, widths, tables, x, gmid, vec, grads, piece_sets, rb=256):
    total, width = x.shape
    grid = (total // rb,)
    blk = lambda w: pl.BlockSpec((rb, w), lambda i: (i, 0))
    pieces = [p for ps in piece_sets for p in ps]
    return pl.pallas_call(
        functools.partial(final_kernel, len(grads), [len(ps) for ps in piece_sets], rows),
        grid=grid,
        in_specs=[SMEM, SMEM, blk(width), blk(width), whole(vec.shape)]
        + [blk(g.shape[1]) for g in grads]
        + [ANY] * len(pieces),
        out_specs=[blk(width), whole((8, width))],
        out_shape=[kept((total, width), F32), jax.ShapeDtypeStruct((8, width), F32)],
        scratch_shapes=[pltpu.VMEM((width, w), BF16) for w in widths]
        + [pltpu.SemaphoreType.DMA((piece_count(ps),)) for ps in piece_sets],
        compiler_params=params(grid, 32),
        cost_estimate=cost(total * width * width * 6, total * width * 20 + width * width * 6),
        name="final",
    )(*tables, *far(x, gmid, vec), *far(*grads), *far(*pieces))


FOLD = (
    ("bias", 0, 0), ("value", 1, 0), ("freqs", 1, 64), ("gain", 2, 0), ("shift", 2, 64),
    ("obias", 3, 0), ("dbias", 3, 64), ("mgain", 4, 0), ("mshift", 4, 64), ("ubias", 5, 0),
)


def fold_kernel(groups, owners, spot, *refs):
    out_ref = refs[-1]
    fsums, bsums = refs[:groups], refs[groups : 2 * groups]
    mid_ref, wide_ref, first_ref = refs[2 * groups : 2 * groups + 3]
    lines = {
        "bias": [(b, 0, part * GW, GW) for part in range(2) for b in bsums],
        "value": [(b, 0, 2 * GW, GW) for b in bsums],
        "freqs": [(f, 0, 0, GW) for f in fsums],
        "gain": [(first_ref, 0, 0, first_ref.shape[1])],
        "shift": [(first_ref, 1, 0, first_ref.shape[1])],
        "mgain": [(mid_ref, 0, 0, mid_ref.shape[1])],
        "mshift": [(mid_ref, 1, 0, mid_ref.shape[1])],
        "obias": [(mid_ref, 2, 0, mid_ref.shape[1])],
        "dbias": [(mid_ref, 3, 0, mid_ref.shape[1])],
        "ubias": [(wide_ref, 0, 0, wide_ref.shape[1])],
    }
    out_ref[...] = jnp.zeros_like(out_ref)
    for name, row, lane in FOLD:
        total = sum(length for _, _, _, length in lines[name])
        each = total // owners
        for owner in range(owners):
            begin, end = owner * each, (owner + 1) * each
            offset = 0
            for ref, line, start, length in lines[name]:
                low, high = max(begin, offset), min(end, offset + length)
                while low < high:
                    place = row * 128 + lane + low - begin
                    at = start + low - offset
                    lead, last = spot(owner)
                    out_ref[(*lead, slice(last, last + 1), slice(place, place + high - low))] = (
                        ref[line : line + 1, at : at + high - low]
                    )
                    low = high
                offset += length


def fold(owners, cube, fsums, bsums, mid, wide, first):
    arrays = [*fsums, *bsums, mid, wide, first]
    shape, spot = (owners, 1024), lambda owner: ((), owner)
    if cube:
        shape, spot = (2, 2, 4, 1024), lambda owner: ((owner % 2, owner // 2 % 2), owner // 4)
    return pl.pallas_call(
        functools.partial(fold_kernel, len(fsums), owners, spot),
        in_specs=[pl.BlockSpec(memory_space=pltpu.VMEM)] * len(arrays),
        out_specs=pl.BlockSpec(memory_space=pltpu.VMEM),
        out_shape=jax.ShapeDtypeStruct(shape, F32),
        cost_estimate=cost(0, 100000),
        name="fold",
    )(*arrays)


def half_column(pair, swap, place, width):
    mine, other = pair
    each = mine.shape[1]
    cut = pl.ds(place % each, width)
    a, b = (mine, other) if place < each else (other, mine)
    return jnp.where(swap, b[:, cut], a[:, cut])


def finish_kernel(rep, *refs):
    outup, downs, (out_ref, up_ref, down_ref) = refs[:2], refs[2:4], refs[4:]
    swap, step, width = rep[0] == 1, GW // 2, out_ref.shape[1]
    for place in range(0, outup[0].shape[1] * 2, step):
        value = half_column(outup, swap, place, step)
        if place < width:
            out_ref[:, pl.ds(place, step)] = value
        else:
            up_ref[:, pl.ds(place - width, step)] = value
    for place in range(0, down_ref.shape[1], step):
        down_ref[:, pl.ds(place, step)] = half_column(downs, swap, place, step)


def finish(rep, outup, downs):
    width = downs[0].shape[1] * 2
    rows = outup[0].shape[0]
    shapes = [(rows, width), (rows, outup[0].shape[1] * 2 - width), (downs[0].shape[0], width)]
    return pl.pallas_call(
        finish_kernel,
        in_specs=[SMEM] + [NEAR] * 4,
        out_specs=[NEAR] * 3,
        out_shape=[jax.ShapeDtypeStruct(shape, F32) for shape in shapes],
        cost_estimate=cost(0, 4000000),
        name="finish",
    )(rep, *outup, *downs)


def finish_inward_kernel(groups, rep, *refs):
    halves, in_ref = refs[:-1], refs[-1]
    swap, step, group, total = rep[0] == 1, GW // 2, 0, in_ref.shape[1] // 3
    for n, count in enumerate(groups):
        for g in range(count):
            for part in range(3):
                for half in range(2):
                    value = half_column(halves[2 * n : 2 * n + 2], swap, (g * 3 + part) * GW + half * step, step)
                    in_ref[:, pl.ds(part * total + group * GW + half * step, step)] = value
            group += 1


def finish_inward(groups, rep, pairs):
    arrays = [a for pair in pairs for a in pair]
    return pl.pallas_call(
        functools.partial(finish_inward_kernel, groups),
        in_specs=[SMEM] + [NEAR] * len(arrays),
        out_specs=NEAR,
        out_shape=jax.ShapeDtypeStruct((arrays[0].shape[0], 3 * GW * sum(groups)), F32),
        cost_estimate=cost(0, 1000000),
        name="finish_inward",
    )(rep, *arrays)


def place():
    me = lax.axis_index("fsdp")
    return lax.axis_index("rep"), me // 4, (me // 2) % 2, me % 2


def move(value, step):
    moves = []
    for i in range(32):
        y, z, x, c = step(i // 16, (i // 4) % 4, (i // 2) % 2, i % 2)
        moves.append((i, y * 16 + z * 4 + x * 2 + c))
    return lax.ppermute(value, ("rep", "fsdp"), moves)


def across_core(value):
    return move(value, lambda y, z, x, c: (y, z, x, 1 - c))


def across_x(value):
    return move(value, lambda y, z, x, c: (y, z, 1 - x, c))


def across_rep(value):
    return move(value, lambda y, z, x, c: (1 - y, z, x, c))


def across_near(value):
    return move(value, lambda y, z, x, c: (y, z ^ 1, x, c))


def across_far(value):
    return move(value, lambda y, z, x, c: (y, z ^ 2, x, c))


def across_third(value):
    return move(value, lambda y, z, x, c: (y, z ^ 3, x, c))


def across_both(value):
    return move(value, lambda y, z, x, c: (1 - y, z, 1 - x, c))


def across_one(value):
    return move(value, lambda y, z, x, c: (y, z, 1 - x, c) if c == 0 else (1 - y, z, x, c))


def across_two(value):
    return move(value, lambda y, z, x, c: (1 - y, z, x, c) if c == 0 else (y, z, 1 - x, c))


def pick(array, index):
    return lax.dynamic_index_in_dim(array, index, 0, keepdims=False)


def pick_two(array, index):
    return lax.dynamic_slice_in_dim(array, 2 * index, 2, 0)


def piece_tables():
    y, z, x, c = place()
    slot = jnp.arange(4, dtype=jnp.int32)
    here, swap = (lambda core, a, b: a), (lambda core, a, b: jnp.where(core == 0, a, b))
    tables = []
    for choose in (here, swap):
        owners, halves = [], []
        for core in (c, 1 - c):
            for mid, half in ((x, y), (choose(core, x, 1 - x), choose(core, 1 - y, y)),
                              (choose(core, 1 - x, x), choose(core, y, 1 - y)), (1 - x, 1 - y)):
                owners.append((z ^ slot) * 4 + mid * 2 + core)
                halves.append(jnp.broadcast_to(half, (4,)))
        tables.append(jnp.concatenate(owners + halves).astype(jnp.int32))
    return tables


def first_of_owner(table, n):
    slots = table.shape[0] // 2
    match = table[None, :slots] == jnp.arange(n, dtype=jnp.int32)[:, None]
    return jnp.min(jnp.where(match, jnp.arange(slots, dtype=jnp.int32)[None, :], slots), axis=1)


class Reduce:
    stages = (across_core, across_one, across_two, across_far, across_near, across_rep)

    def __init__(self, keep, send):
        self.keep, self.first, self.got, self.stage = keep, send, [], 0
        self.out = None

    def sends(self):
        return [(self.stages[self.stage], self.send())]

    def takes(self, values):
        self.take(values[0])

    def base(self, count, one, two=None, cut=None):
        step = lambda a, i: a if i is None else pick(a, i)
        total = None
        for source, used in ((self.keep, 0), (self.got[0], 0), *((g, n + 1) for n, g in enumerate(self.got[1:count]))):
            value = source
            if used < 1:
                value = step(value, one)
            if used < 2:
                value = step(value, two)
            if cut is not None:
                value = cut(value)
            value = value.astype(F32)
            total = value if total is None else total + value
        return total

    def level(self, index):
        return self.base(3, self.i1, self.i2, lambda a: pick(a, index)) + pick(self.got[3], index % 2).astype(F32)

    def send(self):
        y, z, x, c = place()
        self.i1, self.i2 = jnp.where(c == 0, x, y), jnp.where(c == 0, y, x)
        if self.stage == 0:
            return self.first
        if self.stage == 1:
            return self.base(1, 1 - self.i1).astype(BF16)
        if self.stage == 2:
            return self.base(2, self.i1, 1 - self.i2).astype(BF16)
        if self.stage == 3:
            return self.base(3, self.i1, self.i2, lambda a: pick_two(a, 1 - z // 2)).astype(BF16)
        if self.stage == 4:
            return self.level(z ^ 1).astype(BF16)
        self.total = self.level(z) + self.got[4].astype(F32)
        return self.total

    def take(self, value):
        self.stage += 1
        if self.stage == 6:
            self.out = (self.total, value)
        else:
            self.got.append(value)


class SmallReduce:
    stages = (across_core, across_x, across_far, across_near, across_rep)

    def __init__(self, cube):
        self.part, self.stage = cube, 0

    sends, takes = Reduce.sends, Reduce.takes

    def send(self):
        y, z, x, c = place()
        if self.stage == 4:
            self.kept = self.part
            return self.part
        cut = pick_two if self.stage == 2 else pick
        index = (c, x, z // 2, z % 2)[self.stage]
        self.kept = cut(self.part, index)
        return cut(self.part, 1 - index)

    def take(self, value):
        self.stage += 1
        self.part = self.kept + value
        self.out = self.part


class QuickGather:
    def __init__(self, half):
        self.part, self.stage = half, 0

    def sends(self):
        if self.stage == 0:
            return [(f, self.part) for f in (across_near, across_far, across_third)]
        if self.stage == 1:
            return [(f, self.part) for f in (across_rep, across_x, across_both, across_core)]
        return [(across_core, part) for part in self.beside]

    def takes(self, values):
        self.stage += 1
        if self.stage == 1:
            self.part = jnp.concatenate([self.part, *values])
        elif self.stage == 2:
            self.beside, self.other = values[:3], values[3]
        else:
            self.out = [self.part, *self.beside, self.other, *values]


class Gather:
    def __init__(self, half, cuts=()):
        self.part, self.stage, self.cuts, self.got = half, 0, cuts, []

    def sends(self):
        if self.stage == 1 and self.cuts:
            bounds = (0, *self.cuts, self.part.shape[2])
            return [(across_far, self.part[:, :, bounds[len(self.got)] : bounds[len(self.got) + 1]])]
        if self.stage < 3:
            return [((across_near, across_far, across_two)[self.stage], self.part)]
        if self.stage == 3:
            return [(across_one, self.part), (across_one, self.two), (across_core, self.part), (across_core, self.two)]
        return [(across_core, part) for part in self.one]

    def takes(self, values):
        if self.stage == 1:
            self.got += values
            if len(self.got) <= len(self.cuts):
                return
            values = [jnp.concatenate(self.got, axis=2)] if self.cuts else values
        self.stage += 1
        if self.stage < 3:
            self.part = jnp.concatenate([self.part, values[0]])
        elif self.stage == 3:
            self.two = values[0]
        elif self.stage == 4:
            self.one, self.other = values[:2], values[2:]
        else:
            self.out = [self.part, self.two, *self.one, *self.other, *values]


def step(movers, kernel=None, *inputs):
    sends = [m.sends() for m in movers]
    inputs, arrays = lax.optimization_barrier((inputs, [[a for _, a in s] for s in sends]))
    got = [[f(a) for (f, _), a in zip(s, each)] for s, each in zip(sends, arrays)]
    outs = kernel(*inputs) if kernel is not None else ()
    outs, got = lax.optimization_barrier((outs, got))
    for m, g in zip(movers, got):
        m.takes(g)
    return outs


def group_columns(weight, g0, ng, width):
    cuts = []
    for g in range(g0, g0 + ng):
        cuts += [weight[:, part * width + g * GW : part * width + (g + 1) * GW] for part in range(3)]
    return jnp.concatenate(cuts, axis=1)


def small_block(smalls, lanes):
    total = None
    for row, vector in enumerate(smalls):
        block = jnp.pad(vector[None, :], ((row, SMALL_ROWS - 1 - row), (0, lanes - vector.shape[0])))
        total = block if total is None else total + block
    return total


class Done:
    def __init__(self, out):
        self.out = out


def local(tuned, n, tokens, pre_gain, pre_shift, inward_weight, inward_bias, rotary_freqs, outward_weight,
          outward_bias, mlp_gain, mlp_shift, up_weight, up_bias, down_weight, down_bias, keep_mask, kept_counts,
          patch_rows, patch_cols, cotangent):
    total, width = tokens.shape
    groups = width // GW
    wide = up_weight.shape[1]
    rows = width // n
    smalls = [pre_gain, pre_shift, inward_bias, rotary_freqs, outward_bias, mlp_gain, mlp_shift, up_bias, down_bias]
    lengths = [s.shape[0] for s in smalls]
    slot = jnp.arange(total, dtype=jnp.int32)
    count = kept_counts
    key_bias = jnp.where((slot < count[0]) & (keep_mask[0] == 1), 0.0, NEG).astype(F32)
    lines = [patch_cols[0].astype(F32), patch_rows[0].astype(F32), key_bias]
    pos = jnp.stack(lines + [jnp.zeros_like(key_bias)] * 5)
    core = (lax.axis_index("fsdp") % 2).astype(jnp.int32)[None]
    rep = lax.axis_index("rep").astype(jnp.int32)[None]

    if tuned:
        shards = pack(rep, inward_weight, outward_weight, up_weight, down_weight, smalls)
        first, second, outup, downs = QuickGather(shards[0]), Gather(shards[1]), Gather(shards[2], (shards[2].shape[2] // 2,)), Gather(shards[3])
        quick, table = piece_tables()
        order = first_of_owner(quick, n)
        step([first])
        step([first, second])
        step([first])
        load = skip = rows
        small_pieces = first.out
    else:
        gather = lambda a: lax.all_gather(a, "fsdp", axis=0, tiled=True)
        small = small_block(smalls, 3 * GW // 2)
        quick = table = jnp.array([0, 0, 0, 1], jnp.int32)
        order = jnp.arange(n, dtype=jnp.int32)
        load, skip = width, SMALL_ROWS
        small_pieces = [jnp.pad(gather(small[None]), ((0, 0), (skip, 0), (0, 0)))]
        weights = [group_columns(inward_weight, 0, 1, width), group_columns(inward_weight, 1, groups - 1, width),
                   jnp.concatenate([outward_weight, up_weight], axis=1), down_weight]
        first, second, outup, downs = [Done([gather(w)[None]]) for w in weights]
        outup = Done([half[None] for half in jnp.split(outup.out[0][0], 2, axis=1)])

    def run(movers, kernel, *inputs):
        return step(movers, kernel, *inputs) if tuned else kernel(*inputs)

    part = functools.partial
    n1, cosine, sine, vec, aux = run([second, outup], part(prologue, lengths, n, skip), order, tokens, pos, small_pieces)

    q0, k0, v0 = run([second, outup], part(qkv, 0, 1, load), quick, n1, vec, cosine, sine, first.out)
    att, lse0, wide0 = run([second, outup], part(attend, 0, width), q0, k0, v0, pos)
    if tuned:
        step([second])
    q1, k1, v1 = run([outup, downs], part(qkv, 1, groups - 1, load), table, n1, vec, cosine, sine, second.out)
    att, lse1, wide1 = run([outup, downs], part(attend, 1, width), q1, k1, v1, pos, att)
    if tuned:
        step([outup])
    middle, n2, gd, act, slope = run(
        [downs], part(up_first, load, wide), table, count, att, tokens, cotangent, vec, outup.out
    )
    act, slope = run([downs], part(up_second, load), table, count, n2, act, slope, vec, outup.out)

    layout = (n // 4, 2, 2)

    def gradient(name, pairs):
        if tuned:
            return weight_grad(core, pairs, layout, name, name == "in_grad0")
        return lax.psum(lax.psum_scatter(plain_grad(pairs, name), "fsdp", scatter_dimension=0, tiled=True), "rep")

    def reduction(movers, name, pairs):
        out = run(movers, part(gradient, name), pairs)
        return Reduce(*out) if tuned else Done(out)

    r_down = reduction([downs], "down_grad", [(act, gd)])
    outputs, gmid, gb, ga, gu, sums, ubsum = run(
        [r_down], part(down, load), table, count, act, slope, middle, cotangent, gd, vec, outup.out, downs.out
    )
    r_up = reduction([r_down], "up_grad", [(att, gb), (n2, gu)])
    backs = []
    heads = ((0, 0, q0, k0, v0, lse0, wide0), (1, 0, q1, k1, v1, lse1, wide1), (2, 1, q1, k1, v1, lse1, wide1))

    def back(movers, which):
        g0, l0, q, k, v, lse, att_wide = heads[which]
        backs.append(run(movers, part(attend_back, g0, l0), q, k, v, ga, lse, att_wide, aux, cosine, sine))

    def in_gradient(movers, name, which):
        return reduction(movers, name, [(n1, backs[g][0]) for g in which])

    back([r_down, r_up], 0)
    back([r_down, r_up], 1)
    r_in0 = in_gradient([r_down, r_up], "in_grad0", (0, 1))
    if tuned:
        step([r_in0])
    back([r_down, r_up, r_in0], 2)
    r_in1 = in_gradient([r_up, r_in0], "in_grad1", (2,))
    grad_tokens, first_sums = run(
        [r_up, r_in0, r_in1], part(final, load, [3 * GW, 3 * GW * (groups - 1)]),
        (quick, table), tokens, gmid, vec, [b[0] for b in backs], [first.out, second.out]
    )
    small_sums = fold(n, tuned, [b[1] for b in backs], [b[2] for b in backs], sums, ubsum, first_sums)
    if tuned:
        r_small = SmallReduce(small_sums)
        step([r_small, r_in0, r_in1])
        step([r_small, r_in0, r_in1])
        step([r_small, r_in1])
        step([r_small, r_in1])
        d_out, d_up, d_down = step([r_small, r_in1], finish, rep, r_up.out, r_down.out)
        mine = r_small.out
        d_inward = finish_inward((2, 1), rep, [r_in0.out, r_in1.out])
    else:
        mine = lax.psum(lax.psum_scatter(small_sums, "fsdp", scatter_dimension=0, tiled=True), "rep")[0]
        blocks = [r.out[:, 3 * g * GW : 3 * (g + 1) * GW] for r, ng in ((r_in0, 2), (r_in1, 1)) for g in range(ng)]
        d_inward = jnp.concatenate([b[:, p * GW : (p + 1) * GW] for p in range(3) for b in blocks], axis=1)
        d_out, d_up, d_down = r_up.out[:, :width], r_up.out[:, width:], r_down.out
    each = width // n
    line = {name: mine[row * 128 + lane :] for name, row, lane in FOLD}
    o_bias, o_ubias = line["bias"][: 2 * each], line["ubias"][: wide // n]
    o_vbias, o_freqs, o_gain, o_shift, o_obias, o_mgain, o_mshift, o_dbias = [
        line[name][:each] for name in ("value", "freqs", "gain", "shift", "obias", "mgain", "mshift", "dbias")
    ]
    return (outputs, grad_tokens, o_gain, o_shift, d_inward, o_bias, o_vbias, o_freqs, d_out, o_obias,
            o_mgain, o_mshift, d_up, o_ubias, d_down, o_dbias)


def solution(mesh):
    n = mesh.shape["fsdp"]
    tuned = mesh.shape["rep"] == 2 and n == 16
    row = P(("rep", "fsdp"), None)
    vec, mat = P("fsdp"), P("fsdp", None)
    return jax.shard_map(
        functools.partial(local, tuned, n),
        mesh=mesh,
        in_specs=(row, vec, vec, mat, vec, vec, mat, vec, vec, vec, mat, vec, mat, vec, row,
                  P(("rep", "fsdp")), row, row, row),
        out_specs=(row, row, vec, vec, mat, vec, vec, vec, mat, vec, vec, vec, mat, vec, mat, vec),
        check_vma=False,
    )
```

```python
import functools
import math

import jax
import jax.numpy as jnp
from jax import lax
from jax.experimental import pallas as pl
from jax.experimental.pallas import tpu as pltpu
from jax.sharding import PartitionSpec as P

HD = 64
LOG2E = 1.4426950408889634
EPS = 1e-06
NEG = -1e30
F32 = jnp.float32
BF16 = jnp.bfloat16
GH = 4
GW = GH * HD
HALF = GW // 2


def dims(lhs, rhs, lhs_axis, rhs_axis):
    return lax.dot_general(
        lhs, rhs, (((lhs_axis,), (rhs_axis,)), ((), ())), preferred_element_type=F32
    )


def nn(lhs, rhs):
    return dims(lhs, rhs, 1, 0)


def nt(lhs, rhs):
    return dims(lhs, rhs, 1, 1)


def tn(lhs, rhs):
    return dims(lhs, rhs, 0, 0)


def params(grid, mib):
    return pltpu.CompilerParams(
        dimension_semantics=("arbitrary",) * len(grid), vmem_limit_bytes=mib * 2**20
    )


def whole(shape):
    return pl.BlockSpec(shape, lambda *idx: (0,) * len(shape))


ANY = pl.BlockSpec(memory_space=pl.ANY)
SMEM = pl.BlockSpec(memory_space=pltpu.SMEM)
NEAR = pl.BlockSpec(memory_space=pltpu.VMEM)


def kept(shape, dtype):
    return pltpu.HBM(shape, dtype)


def far(*arrays):
    return [pltpu.with_memory_space_constraint(a, pltpu.HBM) for a in arrays]


def cost(flops, bytes_moved, transcendental=0):
    return pl.CostEstimate(
        flops=int(flops), bytes_accessed=int(bytes_moved), transcendentals=int(transcendental)
    )


def group_perm(transposed):
    row = lax.broadcasted_iota(jnp.int32, (GW, GW), 0)
    col = lax.broadcasted_iota(jnp.int32, (GW, GW), 1)
    packed, natural = (row, col) if transposed else (col, row)
    half = packed // HALF
    head = (packed % HALF) // (HD // 2)
    source = head * HD + half * (HD // 2) + packed % (HD // 2)
    return jnp.where(source == natural, 1.0, 0.0).astype(BF16)


def packed_head_mask(head):
    lane = lax.broadcasted_iota(jnp.int32, (1, GW), 1)
    return (lane % HALF) // (HD // 2) == head


def natural_head_mask(head):
    lane = lax.broadcasted_iota(jnp.int32, (1, GW), 1)
    return lane // HD == head


def normalize(values):
    center = values - jnp.mean(values, axis=-1, keepdims=True)
    spread = jnp.mean(center * center, axis=-1, keepdims=True)
    inverse = lax.rsqrt(spread + EPS)
    return center * inverse, inverse


def load_pieces(table, sources, target, sem, rows, column=True):
    copies = []
    slots = table.shape[0] // 2
    for source in sources:
        width = source.shape[2]
        for slot in range(source.shape[0]):
            number = len(copies)
            row = pl.multiple_of(table[number] * rows, rows)
            col = pl.multiple_of(table[slots + number] * width, width) if column else 0
            copies.append(
                pltpu.make_async_copy(
                    source.at[slot, pl.ds(0, rows)], target.at[pl.ds(row, rows), pl.ds(col, width)], sem.at[number]
                )
            )
    return copies


def piece_count(sources):
    return sum(s.shape[0] for s in sources)


SMALL_ROWS = 16


def pack_kernel(rep, in_ref, out_ref, up_ref, down_ref, *rest):
    vectors, (one_ref, two_ref, three_ref, four_ref, small_ref) = rest[:-5], rest[-5:]
    small_ref[...] = jnp.zeros_like(small_ref)
    for row, vector in enumerate(vectors):
        length = vector.shape[0]
        small_ref[row : row + 1, :length] = vector[...].astype(F32).reshape(1, length)

    def write(y):
        rows, third = in_ref.shape[0], in_ref.shape[1] // 3
        groups = third // GW
        cuts = [in_ref[:, pl.ds(part * third + g * GW, GW)] for g in range(groups) for part in range(3)]
        first = jnp.concatenate(cuts[:3], axis=1)
        half = first.shape[1] // 2
        one_ref[0, pl.ds(0, rows), :] = first[:, y * half : (y + 1) * half]
        one_ref[0, pl.ds(rows, SMALL_ROWS), :] = small_ref[...].astype(BF16)
        rest = jnp.concatenate(cuts[3:], axis=1)
        half = rest.shape[1] // 2
        two_ref[0] = rest[:, y * half : (y + 1) * half]
        both = jnp.concatenate([out_ref[...], up_ref[...]], axis=1)
        half = both.shape[1] // 2
        three_ref[0] = both[:, y * half : (y + 1) * half]
        half = down_ref.shape[1] // 2
        four_ref[0] = down_ref[:, pl.ds(y * half, half)]

    @pl.when(rep[0] == 0)
    def _():
        write(0)

    @pl.when(rep[0] == 1)
    def _():
        write(1)


def pack(rep, inward, outward, upward, downward, smalls):
    rows, wide = inward.shape
    width = wide // 3
    shapes = [
        (1, rows + SMALL_ROWS, 3 * GW // 2),
        (1, rows, (wide - 3 * GW) // 2),
        (1, rows, (width + upward.shape[1]) // 2),
        (1, downward.shape[0], width // 2),
    ]
    return pl.pallas_call(
        pack_kernel,
        in_specs=[SMEM] + [pl.BlockSpec(memory_space=pltpu.VMEM)] * (4 + len(smalls)),
        out_specs=[pl.BlockSpec(memory_space=pltpu.VMEM)] * 4,
        out_shape=[jax.ShapeDtypeStruct(shape, BF16) for shape in shapes],
        scratch_shapes=[pltpu.VMEM((SMALL_ROWS, 3 * GW // 2), F32)],
        cost_estimate=cost(0, 2 * rows * width * 24),
        name="pack",
    )(rep, inward, outward, upward, downward, *smalls)


V_GAIN, V_SHIFT, V_BIAS, V_FREQ, V_OBIAS, V_MGAIN, V_MSHIFT, V_UBIAS, V_DBIAS = range(9)


def prologue_kernel(lengths, owners, rows, npieces, order, x_ref, pos_ref, *rest):
    pieces = rest[:npieces]
    n1_ref, cos_ref, sin_ref, vec_ref, aux_ref, got, fc, fr, sem = rest[npieces:]
    width = x_ref.shape[1]

    @pl.when(pl.program_id(0) == 0)
    def _():
        copies = []
        for number, piece in enumerate(pieces):
            slots = piece.shape[0]
            copies.append(
                pltpu.make_async_copy(
                    piece.at[:, pl.ds(rows, SMALL_ROWS)], got.at[pl.ds(number * slots, slots)], sem.at[number]
                )
            )
        for copy in copies:
            copy.start()
        for copy in copies:
            copy.wait()
        vec_ref[...] = jnp.zeros_like(vec_ref)
        for owner in range(owners):
            tile = got[order[owner]].astype(F32)
            for row, length in enumerate(lengths):
                vec_ref[row : row + 1, owner * length : (owner + 1) * length] = tile[row : row + 1, :length]
        freq = jnp.broadcast_to(vec_ref[V_FREQ : V_FREQ + 1, :width], (16, width)).astype(BF16)
        source = lax.broadcasted_iota(jnp.int32, (width, width // 2), 0)
        target = lax.broadcasted_iota(jnp.int32, (width, width // 2), 1)
        fc[...] = nn(freq, jnp.where(source == 2 * target, 1.0, 0.0).astype(BF16))[:8]
        fr[...] = nn(freq, jnp.where(source == 2 * target + 1, 1.0, 0.0).astype(BF16))[:8]

    xhat, _ = normalize(x_ref[...])
    n1_ref[...] = (xhat * vec_ref[V_GAIN : V_GAIN + 1, :width] + vec_ref[V_SHIFT : V_SHIFT + 1, :width]).astype(BF16)
    pos = pos_ref[...]
    aux = jnp.transpose(jnp.concatenate([pos, jnp.zeros((120, pos.shape[1]), F32)], axis=0))
    aux_ref[...] = aux
    angle = aux[:, 0:1] * fc[0:1, :] + aux[:, 1:2] * fr[0:1, :]
    cosine, sine = cos_sin(angle)
    cos_ref[...] = cosine
    sin_ref[...] = sine


def prologue(lengths, owners, rows, order, x, pos, pieces, rb=512):
    total, width = x.shape
    pairs = width // 2
    grid = (total // rb,)
    blk = lambda w: pl.BlockSpec((rb, w), lambda i: (i, 0))
    wide = max(lengths) * owners
    return pl.pallas_call(
        functools.partial(prologue_kernel, lengths, owners, rows, len(pieces)),
        grid=grid,
        in_specs=[SMEM, blk(width), pl.BlockSpec((8, rb), lambda i: (0, i))] + [ANY] * len(pieces),
        out_specs=[blk(width), blk(pairs), blk(pairs), whole((16, wide)), blk(128)],
        out_shape=[
            kept((total, width), BF16),
            kept((total, pairs), F32),
            kept((total, pairs), F32),
            kept((16, wide), F32),
            kept((total, 128), F32),
        ],
        scratch_shapes=[
            pltpu.VMEM((piece_count(pieces), SMALL_ROWS, pieces[0].shape[2]), BF16),
            pltpu.VMEM((8, pairs), F32),
            pltpu.VMEM((8, pairs), F32),
            pltpu.SemaphoreType.DMA((len(pieces),)),
        ],
        compiler_params=params(grid, 24),
        cost_estimate=cost(total * width * 40, total * width * 10),
        name="prologue",
    )(order, *far(x), pos, *far(*pieces))


QUARTER = (1.5703125, 4.837512969970703125e-4, 7.549789948768648e-8)


def cos_sin(angle):
    turns = jnp.floor(angle * 0.6366197723675814 + 0.5)
    r = ((angle - turns * QUARTER[0]) - turns * QUARTER[1]) - turns * QUARTER[2]
    r2 = r * r
    s = r + r * r2 * (-1.6666654611e-1 + r2 * (8.3321608736e-3 - 1.9515295891e-4 * r2))
    c = 1.0 - 0.5 * r2 + r2 * r2 * (4.166664568298827e-2 + r2 * (-1.388731625493765e-3 + 2.443315711809948e-5 * r2))
    quad = turns.astype(jnp.int32)
    odd = (quad & 1) == 1
    cosine = jnp.where(odd, s, c)
    sine = jnp.where(odd, c, s)
    cosine = jnp.where(((quad + 1) & 2) == 2, -cosine, cosine)
    sine = jnp.where((quad & 2) == 2, -sine, sine)
    return cosine, sine


def qkv_kernel(g0, npieces, rows, table, n1_ref, vec_ref, cos_ref, sin_ref, *rest):
    pieces = rest[:npieces]
    q_ref, k_ref, v_ref, w, wp, bp, sem = rest[npieces:]
    width = n1_ref.shape[1]
    groups = w.shape[1] // (3 * GW)
    bias_ref = vec_ref.at[V_BIAS : V_BIAS + 1, :]

    @pl.when(pl.program_id(0) == 0)
    def _():
        copies = load_pieces(table, pieces, w, sem, rows)
        for copy in copies:
            copy.start()
        perm = group_perm(False)
        for copy in copies:
            copy.wait()
        for g in range(groups):
            for part in range(2):
                packed = pl.ds((g * 2 + part) * GW, GW)
                wp[:, packed] = nn(w[:, pl.ds((g * 3 + part) * GW, GW)], perm).astype(BF16)
                natural = pl.ds(part * width + (g0 + g) * GW, GW)
                spread = jnp.broadcast_to(bias_ref[:, natural].astype(BF16), (16, GW))
                bp[:, packed] = nn(spread, perm)[:8]

    n1 = n1_ref[...]
    for g in range(groups):
        cosine = cos_ref[:, pl.ds((g0 + g) * HALF, HALF)]
        sine = sin_ref[:, pl.ds((g0 + g) * HALF, HALF)]
        for part, out, scale in ((0, q_ref, HD**-0.5 * LOG2E), (1, k_ref, 1.0)):
            packed = pl.ds((g * 2 + part) * GW, GW)
            mixed = nn(n1, wp[:, packed]) + bp[0:1, packed]
            a, b = mixed[:, :HALF], mixed[:, HALF:]
            first = a * cosine - b * sine
            second = a * sine + b * cosine
            if scale != 1.0:
                first = first * scale
                second = second * scale
            out[:, pl.ds(g * GW, HALF)] = first.astype(BF16)
            out[:, pl.ds(g * GW + HALF, HALF)] = second.astype(BF16)
        bias = bias_ref[:, pl.ds(2 * width + (g0 + g) * GW, GW)]
        v_ref[:, pl.ds(g * GW, GW)] = (nn(n1, w[:, pl.ds((g * 3 + 2) * GW, GW)]) + bias).astype(BF16)


def qkv(g0, groups, rows, table, n1, vec, cosine, sine, pieces):
    total, width = n1.shape
    rb = 512
    pairs = width // 2
    grid = (total // rb,)
    blk = lambda w: pl.BlockSpec((rb, w), lambda i: (i, 0))
    out = kept((total, groups * GW), BF16)
    copies = piece_count(pieces)
    return pl.pallas_call(
        functools.partial(qkv_kernel, g0, len(pieces), rows),
        grid=grid,
        in_specs=[SMEM, blk(width), whole(vec.shape), blk(pairs), blk(pairs)] + [ANY] * len(pieces),
        out_specs=[blk(groups * GW)] * 3,
        out_shape=[out] * 3,
        scratch_shapes=[
            pltpu.VMEM((width, 3 * groups * GW), BF16),
            pltpu.VMEM((width, 2 * groups * GW), BF16),
            pltpu.VMEM((8, 2 * groups * GW), F32),
            pltpu.SemaphoreType.DMA((copies,)),
        ],
        compiler_params=params(grid, 24),
        cost_estimate=cost(total * width * groups * GW * 6, total * width * 8 + width * groups * GW * 6),
        name="qkv",
    )(table, *far(n1, vec, cosine, sine, *pieces))


def attend_kernel(q_ref, k_ref, v_ref, pos_ref, *rest):
    att_ref, lse_ref, wide_ref, mask = rest[-4:]
    g, r = pl.program_id(0), pl.program_id(1)
    rb, keys = q_ref.shape[0], k_ref.shape[0]
    here = pl.ds(pl.multiple_of(r * rb, rb), rb)

    @pl.when(g == 0)
    def _():
        row = lax.broadcasted_iota(jnp.int32, (rb, keys), 0) + r * rb
        col = lax.broadcasted_iota(jnp.int32, (rb, keys), 1)
        mask[here, :] = jnp.where(row == col, 0.0, jnp.broadcast_to(pos_ref[2:3, :], (rb, keys)))

    q = q_ref[...]
    k = k_ref[...]
    v = v_ref[...]
    total = jnp.zeros((rb, GW), F32)
    lane = lax.broadcasted_iota(jnp.int32, (rb, 128), 1)
    logs = jnp.zeros((rb, 128), F32)
    for h in range(GH):
        qm = jnp.where(packed_head_mask(h), q, jnp.zeros_like(q))
        scores = nt(qm, k) + mask[here, :]
        top = jnp.max(scores, axis=-1, keepdims=True)
        weight = jnp.exp2(scores - top)
        norm = jnp.sum(weight, axis=-1, keepdims=True)
        vm = jnp.where(natural_head_mask(h), v, jnp.zeros_like(v))
        total = total + nn(weight.astype(BF16), vm) * (1.0 / norm)
        logs = jnp.where(lane == h, top + jnp.log2(norm), logs)
    att_ref[...] = total.astype(BF16)
    wide_ref[...] = total
    lse_ref[...] = jnp.transpose(logs)[:8, :]


def attend(g0, full, q, k, v, pos, *att, rb=512):
    total, width = q.shape
    groups = width // GW
    grid = (groups, total // rb)
    return pl.pallas_call(
        attend_kernel,
        grid=grid,
        in_specs=[
            pl.BlockSpec((rb, GW), lambda g, r: (r, g)),
            pl.BlockSpec((total, GW), lambda g, r: (0, g)),
            pl.BlockSpec((total, GW), lambda g, r: (0, g)),
            whole((8, total)),
        ]
        + [ANY] * len(att),
        out_specs=[
            pl.BlockSpec((rb, GW), lambda g, r: (r, g + g0)),
            pl.BlockSpec((None, 8, rb), lambda g, r: (g, 0, r)),
            pl.BlockSpec((rb, GW), lambda g, r: (r, g)),
        ],
        out_shape=[
            kept((total, full), BF16),
            kept((groups, 8, total), F32),
            kept((total, width), F32),
        ],
        input_output_aliases={4: 0} if att else {},
        scratch_shapes=[pltpu.VMEM((total, total), F32)],
        compiler_params=params(grid, 32),
        cost_estimate=cost(total * total * width * 16, total * width * 8, total * total * 12),
        name="attend",
    )(*far(q, k, v, pos, *att))


PHI_SCALE = 0.3989422804014327
TAIL_SCALE = 0.44 * 0.7071067811865476
TAIL = (
    0.12411047596471954,
    0.12443560910041027,
    0.10865662380098591,
    0.10790671631036299,
    -0.010091621907114547,
    0.14834527631989725,
    -0.13897496529649409,
    0.03561197654899638,
)


def gelu_parts(h):
    t = 1.0 / (1.0 + TAIL_SCALE * jnp.abs(h))
    poly = TAIL[-1]
    for coefficient in TAIL[-2::-1]:
        poly = poly * t + coefficient
    bell = jnp.exp2((-0.5 * LOG2E) * (h * h))
    tail = poly * t * bell
    phi = jnp.where(h < 0, tail, 1.0 - tail)
    return h * phi, phi + h * (bell * PHI_SCALE)


def up_kernel(half, npieces, rows, table, count, *refs):
    if half == 0:
        att_ref, x_ref, cot_ref, vec_ref = refs[:4]
        pieces = refs[4 : 4 + npieces]
        mid_ref, n2_ref, gd_ref, act_ref, gp_ref, w, sem = refs[4 + npieces :]
    else:
        n2_ref, vec_ref = refs[:2]
        pieces = refs[2 : 2 + npieces]
        act_ref, gp_ref, w, sem = refs[-4:]
    rb, width = n2_ref.shape

    @pl.when(pl.program_id(0) == 0)
    def _():
        slots = table.shape[0] // 2
        copies = load_pieces(table, pieces, w, sem, rows, column=False)
        for start in (True, False):
            for number, copy in enumerate(copies):

                @pl.when(table[slots + number] == half)
                def _():
                    if start:
                        copy.start()
                    else:
                        copy.wait()

    if half == 0:
        slot = lax.broadcasted_iota(jnp.int32, (rb, 1), 0) + pl.program_id(0) * rb
        valid = jnp.where(slot < count[0], 1.0, 0.0)
        gd_ref[...] = (valid * cot_ref[...]).astype(BF16)
        branch = nn(att_ref[...], w[:, pl.ds(0, width)]) + vec_ref[V_OBIAS : V_OBIAS + 1, :width]
        middle = x_ref[...] + valid * branch
        mid_ref[...] = middle
        xhat, _ = normalize(middle)
        n2 = (xhat * vec_ref[V_MGAIN : V_MGAIN + 1, :width] + vec_ref[V_MSHIFT : V_MSHIFT + 1, :width]).astype(BF16)
        n2_ref[...] = n2
        place = width
    else:
        n2 = n2_ref[...]
        place = 0
    first = half * (w.shape[1] - width)
    step = 384
    for c in range(act_ref.shape[1] // step):
        cut = pl.ds(c * step, step)
        hidden = nn(n2, w[:, pl.ds(place + c * step, step)]) + vec_ref[V_UBIAS : V_UBIAS + 1, pl.ds(first + c * step, step)]
        act, slope = gelu_parts(hidden)
        act_ref[:, cut] = act.astype(BF16)
        gp_ref[:, cut] = slope.astype(BF16)


def up_first(rows, wide, table, count, att, x, cot, vec, pieces, rb=256):
    total, width = x.shape
    part = (width + wide) // 2
    grid = (total // rb,)
    blk = lambda w: pl.BlockSpec((rb, w), lambda i: (i, 0))
    return pl.pallas_call(
        functools.partial(up_kernel, 0, len(pieces), rows),
        grid=grid,
        in_specs=[SMEM, SMEM, blk(width), blk(width), blk(width), whole(vec.shape)] + [ANY] * len(pieces),
        out_specs=[blk(width), blk(width), blk(width), blk(part - width), blk(part - width)],
        out_shape=[
            kept((total, width), F32),
            kept((total, width), BF16),
            kept((total, width), BF16),
            kept((total, wide), BF16),
            kept((total, wide), BF16),
        ],
        scratch_shapes=[pltpu.VMEM((width, part), BF16), pltpu.SemaphoreType.DMA((piece_count(pieces),))],
        compiler_params=params(grid, 32),
        cost_estimate=cost(total * width * part * 2, total * width * 20, total * wide),
        name="up_first",
    )(table, count, *far(att, x, cot, vec, *pieces))


def up_second(rows, table, count, n2, act, slope, vec, pieces, rb=256):
    total, width = n2.shape
    wide = act.shape[1]
    part = (width + wide) // 2
    grid = (total // rb,)
    cols = pl.BlockSpec((pl.Element(rb), pl.Element(part)), lambda i: (i * rb, part - width))
    return pl.pallas_call(
        functools.partial(up_kernel, 1, len(pieces), rows),
        grid=grid,
        in_specs=[SMEM, SMEM, pl.BlockSpec((rb, width), lambda i: (i, 0)), whole(vec.shape)]
        + [ANY] * (len(pieces) + 2),
        out_specs=[cols, cols],
        out_shape=[kept((total, wide), BF16)] * 2,
        input_output_aliases={4 + len(pieces): 0, 5 + len(pieces): 1},
        scratch_shapes=[pltpu.VMEM((width, part), BF16), pltpu.SemaphoreType.DMA((piece_count(pieces),))],
        compiler_params=params(grid, 32),
        cost_estimate=cost(total * width * part * 2, total * width * 20, total * wide),
        name="up_second",
    )(table, count, *far(n2, vec, *pieces, act, slope))


def down_kernel(nup, ndown, rows, table, count, act_ref, gp_ref, mid_ref, cot_ref, gd_ref, vec_ref, *rest):
    ups = rest[:nup]
    downs = rest[nup : nup + ndown]
    (out_ref, gm_ref, gb_ref, ga_ref, gu_ref, sums_ref, ubsum_ref, w, wd, sem, sem_d) = rest[nup + ndown :]
    i = pl.program_id(0)
    rb, width = mid_ref.shape
    wide = act_ref.shape[1]

    @pl.when(i == 0)
    def _():
        first = load_pieces(table, downs, wd, sem_d, rows * (wide // width))
        second = load_pieces(table, ups, w, sem, rows)
        for copy in first + second:
            copy.start()
        for copy in first + second:
            copy.wait()
        sums_ref[...] = jnp.zeros_like(sums_ref)
        ubsum_ref[...] = jnp.zeros_like(ubsum_ref)

    slot = lax.broadcasted_iota(jnp.int32, (rb, 1), 0) + i * rb
    valid = jnp.where(slot < count[0], 1.0, 0.0)
    middle = mid_ref[...]
    cot = cot_ref[...]
    gd = gd_ref[...]
    lowered = nn(act_ref[...], wd[...]) + vec_ref[V_DBIAS : V_DBIAS + 1, :width]
    out_ref[...] = middle + valid * lowered
    step = 1024
    gn2 = jnp.zeros((rb, width), F32)
    for c in range(wide // step):
        cut = pl.ds(c * step, step)
        g = nt(gd, wd[cut, :]) * gp_ref[:, cut].astype(F32)
        g_low = g.astype(BF16)
        gu_ref[:, cut] = g_low
        ubsum_ref[0:1, cut] += jnp.sum(g_low.astype(F32), axis=0, keepdims=True)
        gn2 = gn2 + nt(g_low, w[:, pl.ds(width + c * step, step)])
    xhat, inverse = normalize(middle)
    sums_ref[0:1, :] += jnp.sum(gn2 * xhat, axis=0, keepdims=True)
    sums_ref[1:2, :] += jnp.sum(gn2, axis=0, keepdims=True)
    e = gn2 * vec_ref[V_MGAIN : V_MGAIN + 1, :width]
    back = (e - jnp.mean(e, axis=-1, keepdims=True) - xhat * jnp.mean(e * xhat, axis=-1, keepdims=True)) * inverse
    gmid = cot + back
    gm_ref[...] = gmid
    gb = (valid * gmid).astype(BF16)
    gb_ref[...] = gb
    sums_ref[2:3, :] += jnp.sum(gb.astype(F32), axis=0, keepdims=True)
    sums_ref[3:4, :] += jnp.sum(gd.astype(F32), axis=0, keepdims=True)
    ga_ref[...] = nt(gb, w[:, pl.ds(0, width)]).astype(BF16)


def down(rows, table, count, act, gp, mid, cot, gd, vec, ups, downs, rb=256):
    total, width = mid.shape
    wide = act.shape[1]
    grid = (total // rb,)
    blk = lambda w: pl.BlockSpec((rb, w), lambda i: (i, 0))
    return pl.pallas_call(
        functools.partial(down_kernel, len(ups), len(downs), rows),
        grid=grid,
        in_specs=[SMEM, SMEM, blk(wide), blk(wide), blk(width), blk(width), blk(width), whole(vec.shape)]
        + [ANY] * (len(ups) + len(downs)),
        out_specs=[blk(width), blk(width), blk(width), blk(width), blk(wide), whole((8, width)), whole((8, wide))],
        out_shape=[
            kept((total, width), F32),
            kept((total, width), F32),
            kept((total, width), BF16),
            kept((total, width), BF16),
            kept((total, wide), BF16),
            kept((8, width), F32),
            kept((8, wide), F32),
        ],
        scratch_shapes=[
            pltpu.VMEM((width, width + wide), BF16),
            pltpu.VMEM((wide, width), BF16),
            pltpu.SemaphoreType.DMA((piece_count(ups),)),
            pltpu.SemaphoreType.DMA((piece_count(downs),)),
        ],
        compiler_params=params(grid, 44),
        cost_estimate=cost(total * width * (width + 3 * wide) * 2, total * (width * 20 + wide * 6)),
        name="down",
    )(table, count, *far(act, gp, mid, cot, gd, vec, *ups, *downs))


def grad_kernel(pairs, mids, reps, rows, core, *rest):
    keep_ref, send_ref = rest[-2:]
    part = core[0]

    def spot(parity, mid, rep):
        return jnp.where(parity == 0, mid, rep), jnp.where(parity == 0, rep, mid)

    each = keep_ref.shape[-1]
    offset = 0
    for at, bt in pairs:
        a, b_ref = rest[at][...], rest[bt]
        begin = 0
        while begin < b_ref.shape[1]:
            column = offset + begin
            step = min(b_ref.shape[1] - begin, each - column % each, 768)
            result = tn(a, b_ref[:, pl.ds(begin, step)])
            rep, cut = column // each, pl.ds(column % each, step)
            for pair in range(a.shape[1] // (2 * rows)):
                low = result[pair * 2 * rows : pair * 2 * rows + rows]
                high = result[pair * 2 * rows + rows : (pair + 1) * 2 * rows]
                zz, mid = pair // mids, pair % mids
                one, two = spot(part, mid, rep)
                keep_ref[one, two, zz, :, cut] = jnp.where(part == 0, low, high).astype(BF16)
                one, two = spot(1 - part, mid, rep)
                send_ref[one, two, zz, :, cut] = jnp.where(part == 0, high, low).astype(BF16)
            begin += step
        offset += b_ref.shape[1]


def operands(pairs):
    arrays, index = [], []
    for pair in pairs:
        spots = []
        for array in pair:
            if not any(array is other for other in arrays):
                arrays.append(array)
            spots.append([array is other for other in arrays].index(True))
        index.append(spots)
    lefts = {one for one, _ in index}
    return arrays, index, lefts


def weight_grad(core, pairs, layout, name, lasting=False):
    slow, mids, reps = layout
    arrays, index, lefts = operands(pairs)
    total, height = pairs[0][0].shape
    width = sum(b.shape[1] for _, b in pairs)
    rows = height // (slow * mids * 2)
    chunk = 384 if 384 % (2 * mids * rows) == 0 else 2 * mids * rows
    slows = chunk // (2 * mids * rows)
    grid = (height // chunk,)
    shape = (mids, reps, slow, rows, width // reps)
    out = jax.ShapeDtypeStruct(shape, BF16)
    spec = pl.BlockSpec((mids, reps, slows, rows, width // reps), lambda i: (0, 0, i, 0, 0))
    return pl.pallas_call(
        functools.partial(grad_kernel, index, mids, reps, rows),
        grid=grid,
        in_specs=[SMEM]
        + [
            pl.BlockSpec((total, chunk), lambda i: (0, i)) if n in lefts else whole(a.shape)
            for n, a in enumerate(arrays)
        ],
        out_specs=[spec, spec],
        out_shape=[kept(shape, BF16) if lasting else out, out],
        compiler_params=params(grid, 40),
        cost_estimate=cost(total * height * width * 2, total * (height + width) * 2 + height * width * 2),
        name=name,
    )(core, *far(*arrays))


def plain_grad_kernel(pairs, *rest):
    out_ref = rest[-1]
    offset = 0
    for at, bt in pairs:
        a, b_ref = rest[at][...], rest[bt]
        step = min(b_ref.shape[1], 768)
        for c in range(b_ref.shape[1] // step):
            out_ref[:, pl.ds(offset + c * step, step)] = tn(a, b_ref[:, pl.ds(c * step, step)])
        offset += b_ref.shape[1]


def plain_grad(pairs, name):
    arrays, index, lefts = operands(pairs)
    total, height = pairs[0][0].shape
    width = sum(b.shape[1] for _, b in pairs)
    chunk = 384
    grid = (height // chunk,)
    return pl.pallas_call(
        functools.partial(plain_grad_kernel, index),
        grid=grid,
        in_specs=[
            pl.BlockSpec((total, chunk), lambda i: (0, i)) if n in lefts else whole(a.shape)
            for n, a in enumerate(arrays)
        ],
        out_specs=pl.BlockSpec((chunk, width), lambda i: (i, 0)),
        out_shape=jax.ShapeDtypeStruct((height, width), F32),
        compiler_params=params(grid, 63),
        cost_estimate=cost(total * height * width * 2, total * (height + width) * 2 + height * width * 4),
        name=name,
    )(*arrays)


def unrotate(grad, cosine, sine):
    first, second = grad[:, :HALF], grad[:, HALF:]
    return first * cosine + second * sine, second * cosine - first * sine


def angle_grad(grad, rotated):
    return grad[:, HALF:] * rotated[:, :HALF] - grad[:, :HALF] * rotated[:, HALF:]


def back_kernel(q_ref, k_ref, v_ref, do_ref, lse_ref, wide_ref, aux_ref, cos_ref, sin_ref,
                g_ref, fsum_ref, bsum_ref, ds_s, p_s, dk_s, dv_s):
    r = pl.program_id(0)
    rb, keys = q_ref.shape[0], k_ref.shape[0]
    here = pl.ds(pl.multiple_of(r * rb, rb), rb)
    q = q_ref[...]
    k = k_ref[...]
    v = v_ref[...]
    do = do_ref[...]
    zero = jnp.zeros_like(q)
    product = do.astype(F32) * wide_ref[...]
    high = product.astype(BF16)
    low = (product - high.astype(F32)).astype(BF16)
    lane = lax.broadcasted_iota(jnp.int32, (16, GW), 1)
    pick_head = jnp.where(lane // HD == lax.broadcasted_iota(jnp.int32, (16, GW), 0), 1.0, 0.0).astype(BF16)
    inner = nt(pick_head, high) + nt(pick_head, low)
    key = lax.broadcasted_iota(jnp.int32, (keys, rb), 0)
    query = lax.broadcasted_iota(jnp.int32, (keys, rb), 1) + r * rb
    mask = jnp.where(key == query, 0.0, jnp.broadcast_to(aux_ref[:, 2:3], (keys, rb)))
    dq = jnp.zeros((rb, GW), F32)
    qms, doms = [], []
    for h in range(GH):
        qm = jnp.where(packed_head_mask(h), q, zero)
        dom = jnp.where(natural_head_mask(h), do, zero)
        qms.append(qm)
        doms.append(dom)
        soft = jnp.exp2(nt(k, qm) + mask - lse_ref[h : h + 1, :])
        ds = (soft * (nt(v, dom) - inner[h : h + 1, :])).astype(BF16)
        cut = pl.ds(h * rb, rb)
        ds_s[:, cut] = ds
        p_s[:, cut] = soft.astype(BF16)
        km = jnp.where(packed_head_mask(h), k, jnp.zeros_like(k))
        dq = dq + tn(ds, km)
    dk = nn(ds_s[...], jnp.concatenate(qms, axis=0)) * (1.0 / LOG2E)
    dv = nn(p_s[...], jnp.concatenate(doms, axis=0))

    perm = group_perm(True)
    cosine, sine = cos_ref[here, :], sin_ref[here, :]
    dq = dq * (HD**-0.5)
    ang = angle_grad(dq, q.astype(F32) * (HD**0.5 / LOG2E))
    first, second = unrotate(dq, cosine, sine)
    gq = nn(jnp.concatenate([first.astype(BF16), second.astype(BF16)], axis=1), perm)
    g_ref[here, pl.ds(0, GW)] = gq.astype(BF16)
    col, row = aux_ref[here, 0:1], aux_ref[here, 1:2]
    fcol = jnp.sum(ang * col, axis=0, keepdims=True)
    frow = jnp.sum(ang * row, axis=0, keepdims=True)
    qsum = jnp.sum(gq, axis=0, keepdims=True)

    @pl.when(r == 0)
    def _():
        dk_s[...] = dk
        dv_s[...] = dv
        fsum_ref[...] = jnp.zeros_like(fsum_ref)
        fsum_ref[0:1, pl.ds(0, HALF)] = fcol
        fsum_ref[1:2, pl.ds(0, HALF)] = frow
        bsum_ref[0:1, pl.ds(0, GW)] = qsum

    @pl.when(r > 0)
    def _():
        dk_s[...] += dk
        dv_s[...] += dv
        fsum_ref[0:1, pl.ds(0, HALF)] += fcol
        fsum_ref[1:2, pl.ds(0, HALF)] += frow
        bsum_ref[0:1, pl.ds(0, GW)] += qsum

    @pl.when(r == pl.num_programs(0) - 1)
    def _():
        dkf = dk_s[...]
        angk = angle_grad(dkf, k.astype(F32))
        fsum_ref[0:1, pl.ds(0, HALF)] += jnp.sum(angk * aux_ref[:, 0:1], axis=0, keepdims=True)
        fsum_ref[1:2, pl.ds(0, HALF)] += jnp.sum(angk * aux_ref[:, 1:2], axis=0, keepdims=True)
        one, two = unrotate(dkf, cos_ref[...], sin_ref[...])
        gk = nn(jnp.concatenate([one.astype(BF16), two.astype(BF16)], axis=1), perm)
        g_ref[:, pl.ds(GW, GW)] = gk.astype(BF16)
        bsum_ref[0:1, pl.ds(GW, GW)] = jnp.sum(gk, axis=0, keepdims=True)
        gv = dv_s[...].astype(BF16)
        g_ref[:, pl.ds(2 * GW, GW)] = gv
        lane = lax.broadcasted_iota(jnp.int32, (HALF, 2 * HALF), 1)
        pair = lax.broadcasted_iota(jnp.int32, (HALF, 2 * HALF), 0)
        sums = fsum_ref[:, pl.ds(0, HALF)]
        spread = [
            jnp.dot(sums, jnp.where(lane == 2 * pair + odd, 1.0, 0.0), precision=lax.Precision.HIGHEST)
            for odd in range(2)
        ]
        fsum_ref[0:1, :] = spread[0][0:1] + spread[1][1:2]
        bsum_ref[0:1, pl.ds(2 * GW, GW)] = jnp.sum(gv.astype(F32), axis=0, keepdims=True)


def attend_back(g0, l0, q, k, v, do, lse, wide, aux, cosine, sine, rb=512):
    total = q.shape[0]
    grid = (total // rb,)
    return pl.pallas_call(
        back_kernel,
        grid=grid,
        in_specs=[
            pl.BlockSpec((rb, GW), lambda r: (r, l0)),
            pl.BlockSpec((total, GW), lambda r: (0, l0)),
            pl.BlockSpec((total, GW), lambda r: (0, l0)),
            pl.BlockSpec((rb, GW), lambda r: (r, g0)),
            pl.BlockSpec((None, 8, rb), lambda r: (l0, 0, r)),
            pl.BlockSpec((rb, GW), lambda r: (r, l0)),
            whole((total, 128)),
            pl.BlockSpec((total, HALF), lambda r: (0, g0)),
            pl.BlockSpec((total, HALF), lambda r: (0, g0)),
        ],
        out_specs=[whole((total, 3 * GW)), whole((8, GW)), whole((8, 3 * GW))],
        out_shape=[
            kept((total, 3 * GW), BF16),
            jax.ShapeDtypeStruct((8, GW), F32),
            jax.ShapeDtypeStruct((8, 3 * GW), F32),
        ],
        scratch_shapes=[
            pltpu.VMEM((total, GH * rb), BF16),
            pltpu.VMEM((total, GH * rb), BF16),
            pltpu.VMEM((total, GW), F32),
            pltpu.VMEM((total, GW), F32),
        ],
        compiler_params=params(grid, 48),
        cost_estimate=cost(total * total * GW * 40, total * GW * 20, total * total * GH),
        name="attend_back",
    )(*far(q, k, v, do, lse, wide, aux, cosine, sine))


def final_kernel(count, counts, rows, table_one, table_two, x_ref, gm_ref, vec_ref, *rest):
    grads, place = rest[:count], count
    pieces = []
    for number in counts:
        pieces.append(rest[place : place + number])
        place += number
    out_ref, sums_ref = rest[place : place + 2]
    weights = rest[place + 2 : place + 2 + len(counts)]
    sems = rest[place + 2 + len(counts) :]

    @pl.when(pl.program_id(0) == 0)
    def _():
        copies = []
        for table, p, w, sem in zip((table_one, table_two), pieces, weights, sems):
            copies += load_pieces(table, p, w, sem, rows)
        for copy in copies:
            copy.start()
        for copy in copies:
            copy.wait()
        sums_ref[...] = jnp.zeros_like(sums_ref)

    e = jnp.zeros(x_ref.shape, F32)
    group = 0
    for w in weights:
        for g in range(w.shape[1] // (3 * GW)):
            e = e + nt(grads[group][...], w[:, pl.ds(g * 3 * GW, 3 * GW)])
            group += 1
    xhat, inverse = normalize(x_ref[...])
    sums_ref[0:1, :] += jnp.sum(e * xhat, axis=0, keepdims=True)
    sums_ref[1:2, :] += jnp.sum(e, axis=0, keepdims=True)
    eg = e * vec_ref[V_GAIN : V_GAIN + 1, : x_ref.shape[1]]
    back = (eg - jnp.mean(eg, axis=-1, keepdims=True) - xhat * jnp.mean(eg * xhat, axis=-1, keepdims=True)) * inverse
    out_ref[...] = gm_ref[...] + back


def final(rows, widths, tables, x, gmid, vec, grads, piece_sets, rb=256):
    total, width = x.shape
    grid = (total // rb,)
    blk = lambda w: pl.BlockSpec((rb, w), lambda i: (i, 0))
    pieces = [p for ps in piece_sets for p in ps]
    return pl.pallas_call(
        functools.partial(final_kernel, len(grads), [len(ps) for ps in piece_sets], rows),
        grid=grid,
        in_specs=[SMEM, SMEM, blk(width), blk(width), whole(vec.shape)]
        + [blk(g.shape[1]) for g in grads]
        + [ANY] * len(pieces),
        out_specs=[blk(width), whole((8, width))],
        out_shape=[kept((total, width), F32), jax.ShapeDtypeStruct((8, width), F32)],
        scratch_shapes=[pltpu.VMEM((width, w), BF16) for w in widths]
        + [pltpu.SemaphoreType.DMA((piece_count(ps),)) for ps in piece_sets],
        compiler_params=params(grid, 32),
        cost_estimate=cost(total * width * width * 6, total * width * 20 + width * width * 6),
        name="final",
    )(*tables, *far(x, gmid, vec), *far(*grads), *far(*pieces))


FOLD = (
    ("bias", 0, 0), ("value", 1, 0), ("freqs", 1, 64), ("gain", 2, 0), ("shift", 2, 64),
    ("obias", 3, 0), ("dbias", 3, 64), ("mgain", 4, 0), ("mshift", 4, 64), ("ubias", 5, 0),
)


def fold_kernel(groups, owners, spot, *refs):
    out_ref = refs[-1]
    fsums, bsums = refs[:groups], refs[groups : 2 * groups]
    mid_ref, wide_ref, first_ref = refs[2 * groups : 2 * groups + 3]
    lines = {
        "bias": [(b, 0, part * GW, GW) for part in range(2) for b in bsums],
        "value": [(b, 0, 2 * GW, GW) for b in bsums],
        "freqs": [(f, 0, 0, GW) for f in fsums],
        "gain": [(first_ref, 0, 0, first_ref.shape[1])],
        "shift": [(first_ref, 1, 0, first_ref.shape[1])],
        "mgain": [(mid_ref, 0, 0, mid_ref.shape[1])],
        "mshift": [(mid_ref, 1, 0, mid_ref.shape[1])],
        "obias": [(mid_ref, 2, 0, mid_ref.shape[1])],
        "dbias": [(mid_ref, 3, 0, mid_ref.shape[1])],
        "ubias": [(wide_ref, 0, 0, wide_ref.shape[1])],
    }
    out_ref[...] = jnp.zeros_like(out_ref)
    for name, row, lane in FOLD:
        total = sum(length for _, _, _, length in lines[name])
        each = total // owners
        for owner in range(owners):
            begin, end = owner * each, (owner + 1) * each
            offset = 0
            for ref, line, start, length in lines[name]:
                low, high = max(begin, offset), min(end, offset + length)
                while low < high:
                    place = row * 128 + lane + low - begin
                    at = start + low - offset
                    lead, last = spot(owner)
                    out_ref[(*lead, slice(last, last + 1), slice(place, place + high - low))] = (
                        ref[line : line + 1, at : at + high - low]
                    )
                    low = high
                offset += length


def fold(owners, cube, fsums, bsums, mid, wide, first):
    arrays = [*fsums, *bsums, mid, wide, first]
    shape, spot = (owners, 1024), lambda owner: ((), owner)
    if cube:
        shape, spot = (2, 2, 4, 1024), lambda owner: ((owner % 2, owner // 2 % 2), owner // 4)
    return pl.pallas_call(
        functools.partial(fold_kernel, len(fsums), owners, spot),
        in_specs=[pl.BlockSpec(memory_space=pltpu.VMEM)] * len(arrays),
        out_specs=pl.BlockSpec(memory_space=pltpu.VMEM),
        out_shape=jax.ShapeDtypeStruct(shape, F32),
        cost_estimate=cost(0, 100000),
        name="fold",
    )(*arrays)


def half_column(pair, swap, place, width):
    mine, other = pair
    each = mine.shape[1]
    cut = pl.ds(place % each, width)
    a, b = (mine, other) if place < each else (other, mine)
    return jnp.where(swap, b[:, cut], a[:, cut])


def finish_kernel(rep, *refs):
    outup, downs, (out_ref, up_ref, down_ref) = refs[:2], refs[2:4], refs[4:]
    swap, step, width = rep[0] == 1, GW // 2, out_ref.shape[1]
    for place in range(0, outup[0].shape[1] * 2, step):
        value = half_column(outup, swap, place, step)
        if place < width:
            out_ref[:, pl.ds(place, step)] = value
        else:
            up_ref[:, pl.ds(place - width, step)] = value
    for place in range(0, down_ref.shape[1], step):
        down_ref[:, pl.ds(place, step)] = half_column(downs, swap, place, step)


def finish(rep, outup, downs):
    width = downs[0].shape[1] * 2
    rows = outup[0].shape[0]
    shapes = [(rows, width), (rows, outup[0].shape[1] * 2 - width), (downs[0].shape[0], width)]
    return pl.pallas_call(
        finish_kernel,
        in_specs=[SMEM] + [NEAR] * 4,
        out_specs=[NEAR] * 3,
        out_shape=[jax.ShapeDtypeStruct(shape, F32) for shape in shapes],
        cost_estimate=cost(0, 4000000),
        name="finish",
    )(rep, *outup, *downs)


def finish_inward_kernel(groups, rep, *refs):
    halves, in_ref = refs[:-1], refs[-1]
    swap, step, group, total = rep[0] == 1, GW // 2, 0, in_ref.shape[1] // 3
    for n, count in enumerate(groups):
        for g in range(count):
            for part in range(3):
                for half in range(2):
                    value = half_column(halves[2 * n : 2 * n + 2], swap, (g * 3 + part) * GW + half * step, step)
                    in_ref[:, pl.ds(part * total + group * GW + half * step, step)] = value
            group += 1


def finish_inward(groups, rep, pairs):
    arrays = [a for pair in pairs for a in pair]
    return pl.pallas_call(
        functools.partial(finish_inward_kernel, groups),
        in_specs=[SMEM] + [NEAR] * len(arrays),
        out_specs=NEAR,
        out_shape=jax.ShapeDtypeStruct((arrays[0].shape[0], 3 * GW * sum(groups)), F32),
        cost_estimate=cost(0, 1000000),
        name="finish_inward",
    )(rep, *arrays)


def place():
    me = lax.axis_index("fsdp")
    return lax.axis_index("rep"), me // 4, (me // 2) % 2, me % 2


def move(value, step):
    moves = []
    for i in range(32):
        y, z, x, c = step(i // 16, (i // 4) % 4, (i // 2) % 2, i % 2)
        moves.append((i, y * 16 + z * 4 + x * 2 + c))
    return lax.ppermute(value, ("rep", "fsdp"), moves)


def across_core(value):
    return move(value, lambda y, z, x, c: (y, z, x, 1 - c))


def across_x(value):
    return move(value, lambda y, z, x, c: (y, z, 1 - x, c))


def across_rep(value):
    return move(value, lambda y, z, x, c: (1 - y, z, x, c))


def across_near(value):
    return move(value, lambda y, z, x, c: (y, z ^ 1, x, c))


def across_far(value):
    return move(value, lambda y, z, x, c: (y, z ^ 2, x, c))


def across_third(value):
    return move(value, lambda y, z, x, c: (y, z ^ 3, x, c))


def across_both(value):
    return move(value, lambda y, z, x, c: (1 - y, z, 1 - x, c))


def across_one(value):
    return move(value, lambda y, z, x, c: (y, z, 1 - x, c) if c == 0 else (1 - y, z, x, c))


def across_two(value):
    return move(value, lambda y, z, x, c: (1 - y, z, x, c) if c == 0 else (y, z, 1 - x, c))


def pick(array, index):
    return lax.dynamic_index_in_dim(array, index, 0, keepdims=False)


def pick_two(array, index):
    return lax.dynamic_slice_in_dim(array, 2 * index, 2, 0)


def piece_tables():
    y, z, x, c = place()
    slot = jnp.arange(4, dtype=jnp.int32)
    here, swap = (lambda core, a, b: a), (lambda core, a, b: jnp.where(core == 0, a, b))
    tables = []
    for choose in (here, swap):
        owners, halves = [], []
        for core in (c, 1 - c):
            for mid, half in ((x, y), (choose(core, x, 1 - x), choose(core, 1 - y, y)),
                              (choose(core, 1 - x, x), choose(core, y, 1 - y)), (1 - x, 1 - y)):
                owners.append((z ^ slot) * 4 + mid * 2 + core)
                halves.append(jnp.broadcast_to(half, (4,)))
        tables.append(jnp.concatenate(owners + halves).astype(jnp.int32))
    return tables


def first_of_owner(table, n):
    slots = table.shape[0] // 2
    match = table[None, :slots] == jnp.arange(n, dtype=jnp.int32)[:, None]
    return jnp.min(jnp.where(match, jnp.arange(slots, dtype=jnp.int32)[None, :], slots), axis=1)


class Reduce:
    stages = (across_core, across_one, across_two, across_far, across_near, across_rep)

    def __init__(self, keep, send):
        self.keep, self.first, self.got, self.stage = keep, send, [], 0
        self.out = None

    def sends(self):
        return [(self.stages[self.stage], self.send())]

    def takes(self, values):
        self.take(values[0])

    def base(self, count, one, two=None, cut=None):
        step = lambda a, i: a if i is None else pick(a, i)
        total = None
        for source, used in ((self.keep, 0), (self.got[0], 0), *((g, n + 1) for n, g in enumerate(self.got[1:count]))):
            value = source
            if used < 1:
                value = step(value, one)
            if used < 2:
                value = step(value, two)
            if cut is not None:
                value = cut(value)
            value = value.astype(F32)
            total = value if total is None else total + value
        return total

    def level(self, index):
        return self.base(3, self.i1, self.i2, lambda a: pick(a, index)) + pick(self.got[3], index % 2).astype(F32)

    def send(self):
        y, z, x, c = place()
        self.i1, self.i2 = jnp.where(c == 0, x, y), jnp.where(c == 0, y, x)
        if self.stage == 0:
            return self.first
        if self.stage == 1:
            return self.base(1, 1 - self.i1).astype(BF16)
        if self.stage == 2:
            return self.base(2, self.i1, 1 - self.i2).astype(BF16)
        if self.stage == 3:
            return self.base(3, self.i1, self.i2, lambda a: pick_two(a, 1 - z // 2)).astype(BF16)
        if self.stage == 4:
            return self.level(z ^ 1).astype(BF16)
        self.total = self.level(z) + self.got[4].astype(F32)
        return self.total

    def take(self, value):
        self.stage += 1
        if self.stage == 6:
            self.out = (self.total, value)
        else:
            self.got.append(value)


class SmallReduce:
    stages = (across_core, across_x, across_far, across_near, across_rep)

    def __init__(self, cube):
        self.part, self.stage = cube, 0

    sends, takes = Reduce.sends, Reduce.takes

    def send(self):
        y, z, x, c = place()
        if self.stage == 4:
            self.kept = self.part
            return self.part
        cut = pick_two if self.stage == 2 else pick
        index = (c, x, z // 2, z % 2)[self.stage]
        self.kept = cut(self.part, index)
        return cut(self.part, 1 - index)

    def take(self, value):
        self.stage += 1
        self.part = self.kept + value
        self.out = self.part


class QuickGather:
    def __init__(self, half):
        self.part, self.stage = half, 0

    def sends(self):
        if self.stage == 0:
            return [(f, self.part) for f in (across_near, across_far, across_third)]
        if self.stage == 1:
            return [(f, self.part) for f in (across_rep, across_x, across_both, across_core)]
        return [(across_core, part) for part in self.beside]

    def takes(self, values):
        self.stage += 1
        if self.stage == 1:
            self.part = jnp.concatenate([self.part, *values])
        elif self.stage == 2:
            self.beside, self.other = values[:3], values[3]
        else:
            self.out = [self.part, *self.beside, self.other, *values]


class Gather:
    def __init__(self, half, cuts=()):
        self.part, self.stage, self.cuts, self.got = half, 0, cuts, []

    def sends(self):
        if self.stage == 1 and self.cuts:
            bounds = (0, *self.cuts, self.part.shape[2])
            return [(across_far, self.part[:, :, bounds[len(self.got)] : bounds[len(self.got) + 1]])]
        if self.stage < 3:
            return [((across_near, across_far, across_two)[self.stage], self.part)]
        if self.stage == 3:
            return [(across_one, self.part), (across_one, self.two), (across_core, self.part), (across_core, self.two)]
        return [(across_core, part) for part in self.one]

    def takes(self, values):
        if self.stage == 1:
            self.got += values
            if len(self.got) <= len(self.cuts):
                return
            values = [jnp.concatenate(self.got, axis=2)] if self.cuts else values
        self.stage += 1
        if self.stage < 3:
            self.part = jnp.concatenate([self.part, values[0]])
        elif self.stage == 3:
            self.two = values[0]
        elif self.stage == 4:
            self.one, self.other = values[:2], values[2:]
        else:
            self.out = [self.part, self.two, *self.one, *self.other, *values]


def step(movers, kernel=None, *inputs):
    sends = [m.sends() for m in movers]
    inputs, arrays = lax.optimization_barrier((inputs, [[a for _, a in s] for s in sends]))
    got = [[f(a) for (f, _), a in zip(s, each)] for s, each in zip(sends, arrays)]
    outs = kernel(*inputs) if kernel is not None else ()
    outs, got = lax.optimization_barrier((outs, got))
    for m, g in zip(movers, got):
        m.takes(g)
    return outs


def group_columns(weight, g0, ng, width):
    cuts = []
    for g in range(g0, g0 + ng):
        cuts += [weight[:, part * width + g * GW : part * width + (g + 1) * GW] for part in range(3)]
    return jnp.concatenate(cuts, axis=1)


def small_block(smalls, lanes):
    total = None
    for row, vector in enumerate(smalls):
        block = jnp.pad(vector[None, :], ((row, SMALL_ROWS - 1 - row), (0, lanes - vector.shape[0])))
        total = block if total is None else total + block
    return total


class Done:
    def __init__(self, out):
        self.out = out


def local(tuned, n, tokens, pre_gain, pre_shift, inward_weight, inward_bias, rotary_freqs, outward_weight,
          outward_bias, mlp_gain, mlp_shift, up_weight, up_bias, down_weight, down_bias, keep_mask, kept_counts,
          patch_rows, patch_cols, cotangent):
    total, width = tokens.shape
    groups = width // GW
    wide = up_weight.shape[1]
    rows = width // n
    smalls = [pre_gain, pre_shift, inward_bias, rotary_freqs, outward_bias, mlp_gain, mlp_shift, up_bias, down_bias]
    lengths = [s.shape[0] for s in smalls]
    slot = jnp.arange(total, dtype=jnp.int32)
    count = kept_counts
    key_bias = jnp.where((slot < count[0]) & (keep_mask[0] == 1), 0.0, NEG).astype(F32)
    lines = [patch_cols[0].astype(F32), patch_rows[0].astype(F32), key_bias]
    pos = jnp.stack(lines + [jnp.zeros_like(key_bias)] * 5)
    core = (lax.axis_index("fsdp") % 2).astype(jnp.int32)[None]
    rep = lax.axis_index("rep").astype(jnp.int32)[None]

    if tuned:
        shards = pack(rep, inward_weight, outward_weight, up_weight, down_weight, smalls)
        first, second, outup, downs = QuickGather(shards[0]), Gather(shards[1]), Gather(shards[2], (768,)), Gather(shards[3])
        quick, table = piece_tables()
        order = first_of_owner(quick, n)
        step([first])
        step([first, second])
        step([first])
        load = skip = rows
        small_pieces = first.out
    else:
        gather = lambda a: lax.all_gather(a, "fsdp", axis=0, tiled=True)
        small = small_block(smalls, 3 * GW // 2)
        quick = table = jnp.array([0, 0, 0, 1], jnp.int32)
        order = jnp.arange(n, dtype=jnp.int32)
        load, skip = width, SMALL_ROWS
        small_pieces = [jnp.pad(gather(small[None]), ((0, 0), (skip, 0), (0, 0)))]
        weights = [group_columns(inward_weight, 0, 1, width), group_columns(inward_weight, 1, groups - 1, width),
                   jnp.concatenate([outward_weight, up_weight], axis=1), down_weight]
        first, second, outup, downs = [Done([gather(w)[None]]) for w in weights]
        outup = Done([half[None] for half in jnp.split(outup.out[0][0], 2, axis=1)])

    def run(movers, kernel, *inputs):
        return step(movers, kernel, *inputs) if tuned else kernel(*inputs)

    part = functools.partial
    n1, cosine, sine, vec, aux = run([second, outup], part(prologue, lengths, n, skip), order, tokens, pos, small_pieces)

    q0, k0, v0 = run([second, outup], part(qkv, 0, 1, load), quick, n1, vec, cosine, sine, first.out)
    att, lse0, wide0 = run([second, outup], part(attend, 0, width), q0, k0, v0, pos)
    if tuned:
        step([second])
    q1, k1, v1 = run([outup, downs], part(qkv, 1, groups - 1, load), table, n1, vec, cosine, sine, second.out)
    att, lse1, wide1 = run([outup, downs], part(attend, 1, width), q1, k1, v1, pos, att)
    if tuned:
        step([outup])
    middle, n2, gd, act, slope = run(
        [downs], part(up_first, load, wide), table, count, att, tokens, cotangent, vec, outup.out
    )
    act, slope = run([downs], part(up_second, load), table, count, n2, act, slope, vec, outup.out)

    layout = (n // 4, 2, 2)

    def gradient(name, pairs):
        if tuned:
            return weight_grad(core, pairs, layout, name, name == "in_grad0")
        return lax.psum(lax.psum_scatter(plain_grad(pairs, name), "fsdp", scatter_dimension=0, tiled=True), "rep")

    def reduction(movers, name, pairs):
        out = run(movers, part(gradient, name), pairs)
        return Reduce(*out) if tuned else Done(out)

    r_down = reduction([downs], "down_grad", [(act, gd)])
    outputs, gmid, gb, ga, gu, sums, ubsum = run(
        [r_down], part(down, load), table, count, act, slope, middle, cotangent, gd, vec, outup.out, downs.out
    )
    r_up = reduction([r_down], "up_grad", [(att, gb), (n2, gu)])
    backs = []
    heads = ((0, 0, q0, k0, v0, lse0, wide0), (1, 0, q1, k1, v1, lse1, wide1), (2, 1, q1, k1, v1, lse1, wide1))

    def back(movers, which):
        g0, l0, q, k, v, lse, att_wide = heads[which]
        backs.append(run(movers, part(attend_back, g0, l0), q, k, v, ga, lse, att_wide, aux, cosine, sine))

    def in_gradient(movers, name, which):
        return reduction(movers, name, [(n1, backs[g][0]) for g in which])

    back([r_down, r_up], 0)
    back([r_down, r_up], 1)
    r_in0 = in_gradient([r_down, r_up], "in_grad0", (0, 1))
    if tuned:
        step([r_in0])
    back([r_down, r_up, r_in0], 2)
    r_in1 = in_gradient([r_up, r_in0], "in_grad1", (2,))
    grad_tokens, first_sums = run(
        [r_up, r_in0, r_in1], part(final, load, [3 * GW, 3 * GW * (groups - 1)]),
        (quick, table), tokens, gmid, vec, [b[0] for b in backs], [first.out, second.out]
    )
    small_sums = fold(n, tuned, [b[1] for b in backs], [b[2] for b in backs], sums, ubsum, first_sums)
    if tuned:
        r_small = SmallReduce(small_sums)
        step([r_small, r_in0, r_in1])
        step([r_small, r_in0, r_in1])
        step([r_small, r_in1])
        step([r_small, r_in1])
        d_out, d_up, d_down = step([r_small, r_in1], finish, rep, r_up.out, r_down.out)
        mine = r_small.out
        d_inward = finish_inward((2, 1), rep, [r_in0.out, r_in1.out])
    else:
        mine = lax.psum(lax.psum_scatter(small_sums, "fsdp", scatter_dimension=0, tiled=True), "rep")[0]
        blocks = [r.out[:, 3 * g * GW : 3 * (g + 1) * GW] for r, ng in ((r_in0, 2), (r_in1, 1)) for g in range(ng)]
        d_inward = jnp.concatenate([b[:, p * GW : (p + 1) * GW] for p in range(3) for b in blocks], axis=1)
        d_out, d_up, d_down = r_up.out[:, :width], r_up.out[:, width:], r_down.out
    each = width // n
    line = {name: mine[row * 128 + lane :] for name, row, lane in FOLD}
    o_bias, o_ubias = line["bias"][: 2 * each], line["ubias"][: wide // n]
    o_vbias, o_freqs, o_gain, o_shift, o_obias, o_mgain, o_mshift, o_dbias = [
        line[name][:each] for name in ("value", "freqs", "gain", "shift", "obias", "mgain", "mshift", "dbias")
    ]
    return (outputs, grad_tokens, o_gain, o_shift, d_inward, o_bias, o_vbias, o_freqs, d_out, o_obias,
            o_mgain, o_mshift, d_up, o_ubias, d_down, o_dbias)


def solution(mesh):
    n = mesh.shape["fsdp"]
    tuned = mesh.shape["rep"] == 2 and n == 16
    row = P(("rep", "fsdp"), None)
    vec, mat = P("fsdp"), P("fsdp", None)
    return jax.shard_map(
        functools.partial(local, tuned, n),
        mesh=mesh,
        in_specs=(row, vec, vec, mat, vec, vec, mat, vec, vec, vec, mat, vec, mat, vec, row,
                  P(("rep", "fsdp")), row, row, row),
        out_specs=(row, row, vec, vec, mat, vec, vec, vec, mat, vec, vec, vec, mat, vec, mat, vec),
        check_vma=False,
    )
```
